32 devices in a mesh: dp: 8 (over z, y), fsdp: 4 (over x, core).
Axes of the slice: x: 2, y: 2, z: 4, core: 2. Of those that a mesh axis runs over, the one named last changes fastest.
Arguments:
- states: bfloat16 [20480, 1280], P(('dp', 'fsdp')), may hold values from -0.1796875 to 0.1796875
- teacher: float32 [20480, 1280], P(('dp', 'fsdp')), may hold values from -0.18 to 0.18
- parent_ids: int32 [160], P('dp'), may hold values from -1 to 159, as said below
- valid_mask: int32 [20480], P(('dp', 'fsdp')), may hold values from 0 to 1, as said below
- w_query: bfloat16 [1280, 1280], P(('dp', 'fsdp')), may hold values from -0.15625 to 0.15625
- w_key: bfloat16 [1280, 1280], P(('dp', 'fsdp')), may hold values from -0.15625 to 0.15625
- w_value: bfloat16 [1280, 1280], P(('dp', 'fsdp')), may hold values from -0.15625 to 0.15625
- w_out: bfloat16 [1280, 1280], P(('dp', 'fsdp')), may hold values from -0.15625 to 0.15625
- w_up: bfloat16 [1280, 5120], P(('dp', 'fsdp')), may hold values from -0.15625 to 0.15625
- w_gate: bfloat16 [1280, 5120], P(('dp', 'fsdp')), may hold values from -0.15625 to 0.15625
- w_down: bfloat16 [5120, 1280], P(('dp', 'fsdp')), may hold values from -0.078125 to 0.078125
- qk_scale: bfloat16 [1280], P(('dp', 'fsdp')), may hold values from 0.69921875 to 1.5
- attn_rate: bfloat16 [1280], P(('dp', 'fsdp')), may hold values from 0.099609375 to 0.59765625
- mlp_rate: bfloat16 [1280], P(('dp', 'fsdp')), may hold values from 0.099609375 to 0.59765625
- up_scale: bfloat16 [5120], P(('dp', 'fsdp')), may hold values from 0.5 to 2
- gate_scale: bfloat16 [5120], P(('dp', 'fsdp')), may hold values from 0.5 to 2
Outputs:
- out_states: bfloat16 [20480, 1280], P(('dp', 'fsdp'))
- loss: float32 [], replicated
- grad_states: float32 [20480, 1280], P(('dp', 'fsdp'))
- grad_query: float32 [1280, 1280], P(('dp', 'fsdp'))
- grad_key: float32 [1280, 1280], P(('dp', 'fsdp'))
- grad_value: float32 [1280, 1280], P(('dp', 'fsdp'))
- grad_out: float32 [1280, 1280], P(('dp', 'fsdp'))
- grad_up: float32 [1280, 5120], P(('dp', 'fsdp'))
- grad_gate: float32 [1280, 5120], P(('dp', 'fsdp'))
- grad_down: float32 [5120, 1280], P(('dp', 'fsdp'))
- grad_qk_scale: float32 [1280], P(('dp', 'fsdp'))
- grad_attn_rate: float32 [1280], P(('dp', 'fsdp'))
- grad_mlp_rate: float32 [1280], P(('dp', 'fsdp'))
- grad_up_scale: float32 [5120], P(('dp', 'fsdp'))
- grad_gate_scale: float32 [5120], P(('dp', 'fsdp'))
The draws below stay inside these ranges and needn't reach their ends.
Inputs may be any that keep to these rules, and one draw needn't show every extreme that they name: `parent_ids`: the blocks form runs of 20 in order; a parent is a block of the same run. Each run holds 1 trees of 20 blocks placed at random: a chain of 8 trunk blocks, four branch blocks whose parent is the trunk's last, and two leaf blocks under each branch; every other block has no parent. `valid_mask`: 1 on a leading part of each block, never empty, 0 after it.
All inputs are finite; a program needn't handle non-finite values.
Results may differ from the reference program's by a relative error of at most 0.017.
Values may be sent and summed in bfloat16 or wider, within the bound.
A program may use at most 576 MiB of HBM per device.

```python
import math
import jax
import jax.numpy as jnp
import numpy as np
from jax import lax

D = 1280
HEADS = 20
HEAD_DIM = 64
FF = 5120
BLOCK = 128
TRUNK = 8
TREE_BLOCKS = 20
DEPTH = 10
BLK_GRP = 20
TREES_GRP = 1
NB = 160
TOKENS = 20480


def tree_tables():
    parent_slot = np.full(BLK_GRP, -1, np.int32)
    kind_slot = np.zeros(BLK_GRP, np.int32)
    for slot in range(TREES_GRP * TREE_BLOCKS):
        first = slot // TREE_BLOCKS * TREE_BLOCKS
        rank = slot % TREE_BLOCKS
        kind_slot[slot] = 1
        if rank == 0:
            parent_slot[slot] = -1
        elif rank < TRUNK:
            parent_slot[slot] = slot - 1
        elif rank < TRUNK + 4:
            parent_slot[slot] = first + TRUNK - 1
        else:
            parent_slot[slot] = first + TRUNK + (rank - TRUNK - 4) // 2
            kind_slot[slot] = 2
    return (parent_slot, kind_slot)


def tree_layout(key):
    groups = NB // BLK_GRP
    parent_slot, kind_slot = tree_tables()
    parent_slot = jnp.asarray(parent_slot)
    kind_slot = jnp.asarray(kind_slot)
    group_keys = jax.random.split(jax.random.fold_in(key, 7), groups)
    perms = jax.vmap(lambda item: jax.random.permutation(item, BLK_GRP))(group_keys).astype(jnp.int32)
    offsets = (jnp.arange(groups, dtype=jnp.int32) * BLK_GRP)[:, None]
    parent_block = jnp.where(parent_slot[None, :] >= 0, perms[:, jnp.maximum(parent_slot, 0)] + offsets, -1).astype(jnp.int32)

    def place(perm, parent_row):
        parents = jnp.zeros((BLK_GRP,), jnp.int32).at[perm].set(parent_row)
        kinds = jnp.zeros((BLK_GRP,), jnp.int32).at[perm].set(kind_slot)
        return (parents, kinds)
    parents, kinds = jax.vmap(place)(perms, parent_block)
    return parents.reshape(NB)


def draw_parent_ids(key, part):
    parents = tree_layout(key)
    return parents


def draw_valid_mask(key, part):
    block_ids = jnp.arange(NB, dtype=jnp.int32)
    ramp = BLOCK // 4 + 3 * BLOCK // 4 * block_ids // NB
    jitter = jax.random.randint(jax.random.fold_in(key, 11), (NB,), 0, BLOCK // 8 + 1).astype(jnp.int32)
    block_len = jnp.minimum(ramp + jitter, BLOCK).astype(jnp.int32)
    marks = (jnp.arange(BLOCK, dtype=jnp.int32)[None, :] < block_len[:, None]).astype(jnp.int32)
    return marks.reshape(TOKENS)


def level_of(stream_key, dims, cuts, least, largest):
    factor_of = 1.0
    for dim, shards_of in cuts:
        heights = jax.random.uniform(jax.random.fold_in(jax.random.fold_in(stream_key, 6), dim), (shards_of,), jnp.float32, least / len(cuts), largest / len(cuts))
        factor_of = factor_of * jnp.repeat(jnp.exp(heights), dims[dim] // shards_of).reshape((-1,) + (1,) * (len(dims) - 1 - dim))
    return factor_of


def normal_values(key, extent, width, most, cuts=(), kind=jnp.bfloat16):
    level = level_of(key, extent, cuts, -0.22, 0.18) if cuts else 1.0
    array = jax.random.normal(key, extent, jnp.float32) * width * level
    return jnp.minimum(jnp.maximum(array, -most), most).astype(kind)


def setup_inputs(seed: int = 0) -> dict:
    splits = jax.random.split(jax.random.key(seed), 17)
    return {
        "states": normal_values(splits[0], (TOKENS, D), 0.03, 0.1796875, ((0, 32),)),
        "teacher": normal_values(splits[1], (TOKENS, D), 0.03, 0.18, ((0, 32),), jnp.float32),
        "parent_ids": draw_parent_ids(jax.random.fold_in(splits[16], 71), 0),
        "valid_mask": draw_valid_mask(jax.random.fold_in(splits[16], 71), 0),
        "w_query": normal_values(splits[4], (D, D), D ** -0.5, 0.15625, ((0, 32),)),
        "w_key": normal_values(splits[5], (D, D), D ** -0.5, 0.15625, ((0, 32),)),
        "w_value": normal_values(splits[6], (D, D), D ** -0.5, 0.15625, ((0, 32),)),
        "w_out": normal_values(splits[7], (D, D), D ** -0.5, 0.15625, ((0, 32),)),
        "w_up": normal_values(splits[8], (D, FF), D ** -0.5, 0.15625, ((0, 32),)),
        "w_gate": normal_values(splits[9], (D, FF), D ** -0.5, 0.15625, ((0, 32),)),
        "w_down": normal_values(splits[10], (FF, D), FF ** -0.5, 0.078125, ((0, 32),)),
        "qk_scale": jnp.clip(jnp.exp(math.log(1.5) - 0.7632567 * jax.random.uniform(splits[11], (D,), jnp.float32) ** level_of(splits[11], (D,), ((0, 32),), -0.2, 0.2)), 0.69921875, 1.5).astype(jnp.bfloat16),
        "attn_rate": jnp.clip(jnp.exp(math.log(0.59765625) - 1.7917595 * jax.random.uniform(splits[12], (D,), jnp.float32) ** level_of(splits[12], (D,), ((0, 32),), -0.2, 0.2)), 0.099609375, 0.59765625).astype(jnp.bfloat16),
        "mlp_rate": jnp.clip(jnp.exp(math.log(0.59765625) - 1.7917595 * jax.random.uniform(splits[13], (D,), jnp.float32) ** level_of(splits[13], (D,), ((0, 32),), -0.2, 0.2)), 0.099609375, 0.59765625).astype(jnp.bfloat16),
        "up_scale": jnp.clip(jnp.exp(math.log(2.0) - 1.3862944 * jax.random.uniform(splits[14], (FF,), jnp.float32) ** level_of(splits[14], (FF,), ((0, 32),), -0.2, 0.2)), 0.5, 2.0).astype(jnp.bfloat16),
        "gate_scale": jnp.clip(jnp.exp(math.log(2.0) - 1.3862944 * jax.random.uniform(splits[15], (FF,), jnp.float32) ** level_of(splits[15], (FF,), ((0, 32),), -0.2, 0.2)), 0.5, 2.0).astype(jnp.bfloat16),
    }


@jax.custom_vjp
def low(v):
    return lax.optimization_barrier(v.astype(jnp.bfloat16)).astype(jnp.float32)

@jax.custom_vjp
def low_back(v):
    return v

def low_keep(v):
    return (low(v), None)

def low_pass(kept, grad):
    return (grad,)

def back_keep(v):
    return (v, None)

def back_low(kept, grad):
    return (low(grad),)
low.defvjp(low_keep, low_pass)
low_back.defvjp(back_keep, back_low)
EPS = 1e-06

def unit_norm(vector):
    return vector * lax.rsqrt(lax.optimization_barrier(jnp.sum(vector * vector, axis=-1, keepdims=True)) + EPS)

def precise(left, right):
    return jnp.dot(left, right, precision=lax.Precision.HIGHEST, preferred_element_type=jnp.float32)

def ancestors(local_parent):
    column = jnp.arange(local_parent.shape[0], dtype=jnp.int32)
    columns = [column]
    for depth_step in range(DEPTH - 1):
        column = jnp.where(column >= 0, local_parent[jnp.maximum(column, 0)], -1).astype(jnp.int32)
        columns.append(column)
    return jnp.stack(columns, axis=1)

def head_unit(vector):
    shaped = vector.reshape(vector.shape[0], HEADS, HEAD_DIM)
    return unit_norm(shaped).reshape(vector.shape)

def layer(inputs, params, paths):
    w_query, w_key, w_value, w_out, w_up, w_gate, w_down, qk_scale, attn_rate, mlp_rate, up_scale, gate_scale = params
    query_raw = low_back(precise(inputs, w_query))
    key_raw = low_back(precise(inputs, w_key))
    values = low(low_back(precise(inputs, w_value)))
    query_n = low(head_unit(query_raw) * qk_scale)
    key_n = low(head_unit(key_raw) * qk_scale)
    rows_all = inputs.shape[0]
    blocks = rows_all // BLOCK
    key_blocks = key_n.reshape(blocks, BLOCK, D)
    value_blocks = values.reshape(blocks, BLOCK, D)
    span = DEPTH * BLOCK
    slot_of = jnp.arange(span, dtype=jnp.int32) // BLOCK
    offset = jnp.arange(span, dtype=jnp.int32) % BLOCK
    row_pos = jnp.arange(BLOCK, dtype=jnp.int32)
    causal = offset[None, :] <= row_pos[:, None]
    factor = math.sqrt(HEAD_DIM)

    def one_block(query_block, path_row):
        safe_paths = jnp.maximum(path_row, 0)
        key_rows = key_blocks[safe_paths].reshape(span, HEADS, HEAD_DIM)
        value_rows = value_blocks[safe_paths].reshape(span, HEADS, HEAD_DIM)
        query_heads = query_block.reshape(BLOCK, HEADS, HEAD_DIM)
        scores = factor * jnp.einsum('qhd,khd->hqk', query_heads, key_rows, precision=lax.Precision.HIGHEST)
        scores = low_back(scores)
        is_live = path_row[slot_of] >= 0
        allowed = jnp.where(slot_of[None, :] == 0, causal, is_live[None, :])
        scores = jnp.where(allowed[None], scores, jnp.float32(-1e+30))
        row_max = lax.optimization_barrier(jnp.max(scores, axis=-1, keepdims=True))
        powers = jnp.exp(scores - row_max)
        probs = powers / lax.optimization_barrier(jnp.sum(powers, axis=-1, keepdims=True))
        mixed_block = jnp.einsum('hqk,khd->qhd', low(probs), value_rows, precision=lax.Precision.HIGHEST)
        return mixed_block.reshape(BLOCK, D)
    checked = jax.checkpoint(one_block)
    mixed = lax.map(lambda pair: checked(pair[0], pair[1]), (query_n.reshape(blocks, BLOCK, D), paths))
    mixed = low(low_back(mixed.reshape(rows_all, D)))
    attn = low_back(precise(mixed, w_out))
    hidden = unit_norm(inputs + attn_rate * (unit_norm(attn) - inputs))
    hidden_b = low(hidden)
    up_proj = low_back(precise(hidden_b, w_up))
    gate_proj = low_back(precise(hidden_b, w_gate))
    gated = gate_proj * gate_scale * math.sqrt(D)
    act = low(up_proj * up_scale * (gated * jax.nn.sigmoid(gated)))
    down = low_back(precise(act, w_down))
    return unit_norm(hidden + mlp_rate * (unit_norm(down) - hidden))

def reference(states, teacher, parent_ids, valid_mask, w_query, w_key, w_value, w_out, w_up, w_gate, w_down, qk_scale, attn_rate, mlp_rate, up_scale, gate_scale):
    groups = NB // BLK_GRP
    group_tok = BLK_GRP * BLOCK
    valid_count = jnp.sum(valid_mask.astype(jnp.float32))
    params = tuple((item.astype(jnp.float32) for item in (w_query, w_key, w_value, w_out, w_up, w_gate, w_down, qk_scale, attn_rate, mlp_rate, up_scale, gate_scale)))
    inputs_all = (states.astype(jnp.float32).reshape(groups, group_tok, D), teacher.reshape(groups, group_tok, D), parent_ids.reshape(groups, BLK_GRP), valid_mask.astype(jnp.float32).reshape(groups, group_tok), jnp.arange(groups, dtype=jnp.int32))

    def per_group(totals, item):
        inputs, target, parents, weights_mask, group_idx = item
        local = jnp.where(parents >= 0, parents - group_idx * BLK_GRP, -1).astype(jnp.int32)
        paths = ancestors(local)

        def loss_of(inputs_in, *param_in):
            result = layer(inputs_in, param_in, paths)
            part = jnp.sum(weights_mask[:, None] * (result - target) ** 2) / valid_count
            return (part, result)
        part, pull, result = jax.vjp(loss_of, inputs, *params, has_aux=True)
        grads = pull(jnp.float32(1.0))
        totals = tuple((acc + grad for acc, grad in zip(totals, grads[1:])))
        return (totals, (result.astype(jnp.bfloat16), part, grads[0]))
    zeros = tuple((jnp.zeros_like(item) for item in params))
    totals, (results, parts, grad_in) = lax.scan(per_group, zeros, inputs_all)
    return (results.reshape(TOKENS, D), jnp.sum(parts), grad_in.reshape(TOKENS, D), totals[0], totals[1], totals[2], totals[3], totals[4], totals[5], totals[6], totals[7], totals[8], totals[9], totals[10], totals[11])
```

```python
import functools
import math

import jax
import jax.numpy as jnp
from jax import lax
from jax.experimental import pallas as pl
from jax.experimental.pallas import tpu as pltpu
from jax.sharding import PartitionSpec as P


D = 1280
HEADS = 20
HEAD_DIM = 64
FF = 5120
BLOCK = 128
DEPTH = 10


EPS = 1e-06


def unit_rows(vector):
    inverse = lax.rsqrt(jnp.sum(vector * vector, axis=-1, keepdims=True) + EPS)
    return (vector * inverse, inverse)


def unit_back(grad, unit, inverse):
    return (grad - unit * jnp.sum(grad * unit, axis=-1, keepdims=True)) * inverse


def project(left, right):
    return jnp.dot(left, right, preferred_element_type=jnp.float32)


def project_back(grad, weight):
    return jnp.einsum("te,de->td", grad, weight, preferred_element_type=jnp.float32)


def ancestors(local_parent):
    column = jnp.arange(local_parent.shape[0], dtype=jnp.int32)
    columns = [column]
    for depth_step in range(DEPTH - 1):
        column = jnp.where(column >= 0, local_parent[jnp.maximum(column, 0)], -1)
        columns.append(column)
    return jnp.stack(columns, axis=1)


def head_back(grad_flat, unit, inverse, scale):
    scaled = (grad_flat * scale).reshape(unit.shape)
    raw = unit_back(scaled, unit, inverse).reshape(grad_flat.shape)
    scale_grad = jnp.sum(grad_flat * unit.reshape(grad_flat.shape), axis=0)
    return (raw, scale_grad)


def general(
    states,
    teacher,
    parent_ids,
    valid_mask,
    w_query,
    w_key,
    w_value,
    w_out,
    w_up,
    w_gate,
    w_down,
    qk_scale,
    attn_rate,
    mlp_rate,
    up_scale,
    gate_scale,
):
    rows_dev = states.shape[0]
    blocks_dev = rows_dev // BLOCK
    width_rows = w_query.shape[0]
    span = DEPTH * BLOCK
    factor = math.sqrt(HEAD_DIM)
    root_width = math.sqrt(D)
    mask_f = valid_mask.astype(jnp.float32)
    qkv_local = jnp.concatenate((w_query, w_key, w_value), axis=1)
    scal_width_local = jnp.stack((qk_scale, attn_rate, mlp_rate), axis=1)
    piece_qkv = lax.all_gather(qkv_local, ("dp", "fsdp"), axis=0, tiled=True)
    piece_out = lax.all_gather(w_out, ("dp", "fsdp"), axis=0, tiled=True)
    piece_scal = lax.all_gather(scal_width_local, ("dp", "fsdp"), axis=0, tiled=True)
    lefts = states
    total = jnp.dot(lefts, piece_qkv, preferred_element_type=jnp.float32)
    scal_whole = piece_scal
    qkv_raw = total
    scal_width = scal_whole
    scale_qk = scal_width[:, 0].astype(jnp.float32)
    rate_attn = scal_width[:, 1].astype(jnp.float32)
    rate_mlp = scal_width[:, 2].astype(jnp.float32)
    query_raw = qkv_raw[:, :D]
    key_raw = qkv_raw[:, D : 2 * D]
    values = qkv_raw[:, 2 * D :].astype(jnp.bfloat16)
    query_unit, query_inv = unit_rows(query_raw.reshape(rows_dev, HEADS, HEAD_DIM))
    key_unit, key_inv = unit_rows(key_raw.reshape(rows_dev, HEADS, HEAD_DIM))
    query_n = (query_unit.reshape(rows_dev, D) * scale_qk).astype(jnp.bfloat16)
    key_n = (key_unit.reshape(rows_dev, D) * scale_qk).astype(jnp.bfloat16)
    key_group, value_group = (
        lax.all_gather(key_n, "fsdp", axis=0, tiled=True),
        lax.all_gather(values, "fsdp", axis=0, tiled=True),
    )
    group_blocks = parent_ids.shape[0]
    group_base = lax.axis_index("dp") * group_blocks
    local_parent = jnp.where(parent_ids >= 0, parent_ids - group_base, -1)
    paths_all = ancestors(local_parent)
    own_first = lax.axis_index("fsdp") * blocks_dev
    paths = lax.dynamic_slice_in_dim(paths_all, own_first, blocks_dev, 0)
    safe_paths = jnp.maximum(paths, 0)
    key_rows = key_group.reshape(group_blocks, BLOCK, D)[safe_paths].reshape(
        blocks_dev, span, HEADS, HEAD_DIM
    )
    value_rows = value_group.reshape(group_blocks, BLOCK, D)[safe_paths].reshape(
        blocks_dev, span, HEADS, HEAD_DIM
    )
    slot_of = jnp.arange(span, dtype=jnp.int32) // BLOCK
    offset = jnp.arange(span, dtype=jnp.int32) % BLOCK
    row_pos = jnp.arange(BLOCK, dtype=jnp.int32)
    causal = offset[None, :] <= row_pos[:, None]
    is_live = jnp.take(paths, slot_of, axis=1) >= 0
    allowed = jnp.where(slot_of[None, None, :] == 0, causal[None], is_live[:, None, :])[:, None]
    query_heads = query_n.reshape(blocks_dev, BLOCK, HEADS, HEAD_DIM)
    scores = factor * jnp.einsum(
        "bqhd,bkhd->bhqk", query_heads, key_rows, preferred_element_type=jnp.float32
    )
    scores = jnp.where(allowed, scores, jnp.float32(-1e30))
    row_max = jnp.max(scores, axis=-1, keepdims=True)
    powers = jnp.exp(scores - row_max)
    row_sum = jnp.sum(powers, axis=-1, keepdims=True)
    probs_b = (powers / row_sum).astype(jnp.bfloat16)
    log_total = row_max + jnp.log(row_sum)
    mixed = jnp.einsum("bhqk,bkhd->bqhd", probs_b, value_rows, preferred_element_type=jnp.float32)
    mixed = mixed.reshape(rows_dev, D).astype(jnp.bfloat16)
    inputs = states.astype(jnp.float32)
    attn = project(mixed, piece_out)
    attn_unit, attn_inv = unit_rows(attn)
    hidden, hidden_inv = unit_rows(inputs + rate_attn * (attn_unit - inputs))
    hidden_b = hidden.astype(jnp.bfloat16)
    ffn_local = jnp.concatenate((w_up, w_gate), axis=1)
    scal_hidden_local = jnp.concatenate(
        (up_scale.reshape(width_rows, 4), gate_scale.reshape(width_rows, 4)), axis=1
    )
    piece_ffn = lax.all_gather(ffn_local, ("dp", "fsdp"), axis=0, tiled=True)
    piece_scal = lax.all_gather(scal_hidden_local, ("dp", "fsdp"), axis=0, tiled=True)
    lefts = hidden_b
    total = jnp.dot(lefts, piece_ffn, preferred_element_type=jnp.float32)
    scal_whole = piece_scal
    scale_up = scal_whole[:, :4].reshape(FF).astype(jnp.float32)
    scale_gate = scal_whole[:, 4:].reshape(FF).astype(jnp.float32)
    up_proj = total[:, :FF]
    gate_proj = total[:, FF:]
    upscaled = up_proj * scale_up
    gated = gate_proj * scale_gate * root_width
    sigmoid_gate = jax.nn.sigmoid(gated)
    act = (upscaled * (gated * sigmoid_gate)).astype(jnp.bfloat16)
    lefts = act
    down = jnp.dot(
        lefts,
        lax.all_gather(w_down, ("dp", "fsdp"), axis=0, tiled=True),
        preferred_element_type=jnp.float32,
    )
    down_unit, down_inv = unit_rows(down)
    result, result_inv = unit_rows(hidden + rate_mlp * (down_unit - hidden))
    loss_local = jnp.sum(mask_f[:, None] * (result - teacher) ** 2)
    valid_count, loss_sum = lax.psum((jnp.sum(mask_f), loss_local), ("dp", "fsdp"))
    loss = loss_sum / valid_count
    g_result = 2.0 * mask_f[:, None] * (result - teacher) / valid_count
    g_last = unit_back(g_result, result, result_inv)
    g_hidden = g_last * (1.0 - rate_mlp)
    g_rate_mlp = jnp.sum(g_last * (down_unit - hidden), axis=0)
    g_down = unit_back(g_last * rate_mlp, down_unit, down_inv).astype(jnp.bfloat16)
    g_act = jnp.einsum(
        "te,fe->tf",
        g_down,
        lax.all_gather(w_down, ("dp", "fsdp"), axis=0, tiled=True),
        preferred_element_type=jnp.float32,
    )
    g_upscaled = g_act * (gated * sigmoid_gate)
    g_gated = g_act * upscaled * sigmoid_gate * (1.0 + gated * (1.0 - sigmoid_gate))
    grad_up_scale = jnp.sum(g_upscaled * up_proj, axis=0)
    grad_gate_scale = jnp.sum(g_gated * gate_proj * root_width, axis=0)
    g_up = (g_upscaled * scale_up).astype(jnp.bfloat16)
    g_gate = (g_gated * scale_gate * root_width).astype(jnp.bfloat16)
    g_both = jnp.concatenate((g_up, g_gate), axis=1)
    g_hidden = g_hidden + jnp.einsum(
        "tc,dc->td",
        g_both,
        lax.all_gather(ffn_local, ("dp", "fsdp"), axis=0, tiled=True),
        preferred_element_type=jnp.float32,
    )
    scal_terms = jnp.concatenate(
        (grad_up_scale.reshape(D, 4), grad_gate_scale.reshape(D, 4)), axis=1
    )
    lefts = hidden_b
    main = jnp.einsum("td,tc->dc", lefts, g_both, preferred_element_type=jnp.float32)
    ffn_share = lax.psum_scatter(
        jnp.concatenate((main, scal_terms), axis=1), ("dp", "fsdp"), scatter_dimension=0, tiled=True
    )
    lefts = act
    grad_down = lax.psum_scatter(
        jnp.einsum("tf,te->fe", lefts, g_down, preferred_element_type=jnp.float32),
        ("dp", "fsdp"),
        scatter_dimension=0,
        tiled=True,
    )
    g_pre = unit_back(g_hidden, hidden, hidden_inv)
    g_states = g_pre * (1.0 - rate_attn)
    g_rate_attn = jnp.sum(g_pre * (attn_unit - inputs), axis=0)
    g_attn = unit_back(g_pre * rate_attn, attn_unit, attn_inv).astype(jnp.bfloat16)
    g_mixed = project_back(g_attn, piece_out).astype(jnp.bfloat16)
    scores = factor * jnp.einsum(
        "bqhd,bkhd->bhqk", query_heads, key_rows, preferred_element_type=jnp.float32
    )
    probs = jnp.where(allowed, jnp.exp(scores - log_total), jnp.float32(0.0))
    probs_again = probs.astype(jnp.bfloat16)
    g_heads = g_mixed.reshape(blocks_dev, BLOCK, HEADS, HEAD_DIM)
    g_probs = jnp.einsum("bqhd,bkhd->bhqk", g_heads, value_rows, preferred_element_type=jnp.float32)
    delta = jnp.sum(probs * g_probs, axis=-1, keepdims=True)
    g_scores = (probs * (g_probs - delta)).astype(jnp.bfloat16)
    g_query_n = factor * jnp.einsum(
        "bhqk,bkhd->bqhd", g_scores, key_rows, preferred_element_type=jnp.float32
    )
    g_key_rows = factor * jnp.einsum(
        "bhqk,bqhd->bkhd", g_scores, query_heads, preferred_element_type=jnp.float32
    )
    g_value_rows = jnp.einsum(
        "bhqk,bqhd->bkhd", probs_again, g_heads, preferred_element_type=jnp.float32
    )
    flat_paths = safe_paths.reshape(blocks_dev * DEPTH)
    g_key_group = (
        jnp.zeros((group_blocks, BLOCK, D), jnp.float32)
        .at[flat_paths]
        .add(g_key_rows.reshape(blocks_dev * DEPTH, BLOCK, D))
    )
    g_value_group = (
        jnp.zeros((group_blocks, BLOCK, D), jnp.float32)
        .at[flat_paths]
        .add(g_value_rows.reshape(blocks_dev * DEPTH, BLOCK, D))
    )
    g_key_n, g_values = (
        lax.psum_scatter(
            g_key_group.reshape(group_blocks * BLOCK, D).astype(jnp.bfloat16),
            "fsdp",
            scatter_dimension=0,
            tiled=True,
        ).astype(jnp.float32),
        lax.psum_scatter(
            g_value_group.reshape(group_blocks * BLOCK, D).astype(jnp.bfloat16),
            "fsdp",
            scatter_dimension=0,
            tiled=True,
        ).astype(jnp.float32),
    )
    g_query_raw, scale_from_query = head_back(
        g_query_n.reshape(rows_dev, D), query_unit, query_inv, scale_qk
    )
    g_key_raw, scale_from_key = head_back(g_key_n, key_unit, key_inv, scale_qk)
    grad_qk_scale = scale_from_query + scale_from_key
    g_qkv = jnp.concatenate(
        (
            g_query_raw.astype(jnp.bfloat16),
            g_key_raw.astype(jnp.bfloat16),
            g_values.astype(jnp.bfloat16),
        ),
        axis=1,
    )
    g_states = g_states + jnp.einsum(
        "tc,dc->td",
        g_qkv,
        lax.all_gather(qkv_local, ("dp", "fsdp"), axis=0, tiled=True),
        preferred_element_type=jnp.float32,
    )
    vector_terms = jnp.stack((grad_qk_scale, g_rate_attn, g_rate_mlp), axis=1)
    lefts = states
    main = jnp.einsum("td,tc->dc", lefts, g_qkv, preferred_element_type=jnp.float32)
    outer = jnp.einsum("td,tc->dc", mixed, g_attn, preferred_element_type=jnp.float32)
    attn_share = lax.psum_scatter(
        jnp.concatenate((main, outer, vector_terms), axis=1),
        ("dp", "fsdp"),
        scatter_dimension=0,
        tiled=True,
    )
    return (
        result.astype(jnp.bfloat16),
        loss,
        g_states,
        attn_share[:, :D],
        attn_share[:, D : 2 * D],
        attn_share[:, 2 * D : 3 * D],
        attn_share[:, 3 * D : 4 * D],
        ffn_share[:, :FF],
        ffn_share[:, FF : 2 * FF],
        grad_down,
        attn_share[:, 4 * D],
        attn_share[:, 4 * D + 1],
        attn_share[:, 4 * D + 2],
        ffn_share[:, 2 * FF : 2 * FF + 4].reshape(-1),
        ffn_share[:, 2 * FF + 4 : 2 * FF + 8].reshape(-1),
    )

TRUNK = 8
NB = 20
TOK = NB * BLOCK
F32 = jnp.float32
BF = jnp.bfloat16


def head_norm(raw):
    inv = lax.rsqrt(jnp.sum(raw * raw, axis=0, keepdims=True) + EPS)
    return raw * inv, inv

def tri(size):
    key = lax.broadcasted_iota(jnp.int32, (size, size), 0)
    query = lax.broadcasted_iota(jnp.int32, (size, size), 1)
    return key, query

def chunks():
    out = []
    for j in range(TRUNK // 2):
        parts = [(0, 256 * j, "all")] if j else []
        out.append((256 * j, parts + [(256 * j, 256, "causal")]))
    for j in range(2):
        start = TRUNK * BLOCK + 256 * j
        out.append((start, [(0, 1024, "all"), (start, 256, "pair")]))
    for j in range(4):
        start = (TRUNK + 4) * BLOCK + 256 * j
        out.append((start, [(0, 1024, "all"), ((TRUNK + j) * BLOCK, 128, "all"), (start, 256, "pair")]))
    return out

def masked(kind, value):
    if kind == "all":
        return value
    key, query = tri(256)
    keep = key <= query
    if kind == "pair":
        keep = keep & ((key < 128) == (query < 128))
    return jnp.where(keep, value, jnp.zeros_like(value))

def nn(a, b):
    return lax.dot_general(a, b, (((1,), (0,)), ((), ())), preferred_element_type=F32)

def fwd_kernel(perm_ref, qkv_ref, scale_ref, mixed_ref, sum_ref, qs, ks, vs):
    scale = scale_ref[0]
    for i in range(NB):
        lanes = pl.ds(pl.multiple_of(perm_ref[i] * BLOCK, BLOCK), BLOCK)
        here = slice(i * BLOCK, (i + 1) * BLOCK)
        q_unit, _ = head_norm(qkv_ref[0, :, lanes])
        k_unit, _ = head_norm(qkv_ref[1, :, lanes])
        qs[:, here] = (q_unit * scale).astype(BF) * BF(8.0)
        ks[here, :] = (k_unit * scale).astype(BF).T
        vs[0:64, here] = qkv_ref[2, :, lanes].astype(BF)
    vs[64:80, :] = jnp.ones((16, TOK), BF)
    for start, parts in chunks():
        query = qs[:, start:start + 256]
        acc = jnp.zeros((80, 256), F32)
        for kstart, count, kind in parts:
            scores = nn(ks[kstart:kstart + count, :], query)
            powers = masked(kind, jnp.exp(scores)).astype(BF)
            acc = acc + nn(vs[:, kstart:kstart + count], powers)
        total = acc[64:65, :]
        result = (acc[0:64, :] / total).astype(BF)
        for half in range(2):
            lanes = pl.ds(pl.multiple_of(perm_ref[start // BLOCK + half] * BLOCK, BLOCK), BLOCK)
            cut = slice(half * BLOCK, (half + 1) * BLOCK)
            mixed_ref[:, lanes] = result[:, cut]
            sum_ref[0, :, lanes] = jnp.broadcast_to(1.0 / total[:, cut], (8, BLOCK))

def attn_fwd(perm, qkv, scale):
    heads = qkv.shape[1] // HEAD_DIM
    return pl.pallas_call(
        fwd_kernel,
        grid_spec=pltpu.PrefetchScalarGridSpec(
            num_scalar_prefetch=1,
            grid=(heads,),
            in_specs=[
                pl.BlockSpec((3, HEAD_DIM, TOK), lambda h, p: (0, h, 0)),
                pl.BlockSpec((1, HEAD_DIM, 1), lambda h, p: (h, 0, 0)),
            ],
            out_specs=[
                pl.BlockSpec((HEAD_DIM, TOK), lambda h, p: (h, 0)),
                pl.BlockSpec((1, 8, TOK), lambda h, p: (h, 0, 0)),
            ],
            scratch_shapes=[
                pltpu.VMEM((HEAD_DIM, TOK), BF),
                pltpu.VMEM((TOK, HEAD_DIM), BF),
                pltpu.VMEM((80, TOK), BF),
            ],
        ),
        out_shape=[
            jax.ShapeDtypeStruct((heads * HEAD_DIM, TOK), BF),
            jax.ShapeDtypeStruct((heads, 8, TOK), F32),
        ],
        compiler_params=pltpu.CompilerParams(vmem_limit_bytes=48 << 20),
        name="tree_attention",
        cost_estimate=pl.CostEstimate(flops=heads * 2 * 2 * 64 * 256 * 10752, bytes_accessed=12 << 20, transcendentals=heads * 256 * 10752),
    )(perm, qkv, scale)

def bwd_kernel(perm_ref, qkv_ref, scale_ref, sum_ref, mixed_ref, g_ref, out_ref, gscale_ref,
               qT, q, k, kT, v, gT, g, dq, dk, dv, delta, inv):
    scale = scale_ref[0]
    for i in range(NB):
        lanes = pl.ds(pl.multiple_of(perm_ref[i] * BLOCK, BLOCK), BLOCK)
        here = slice(i * BLOCK, (i + 1) * BLOCK)
        q_unit, _ = head_norm(qkv_ref[0, :, lanes])
        k_unit, _ = head_norm(qkv_ref[1, :, lanes])
        q8 = (q_unit * scale).astype(BF) * BF(8.0)
        qT[:, here] = q8
        q[here, :] = q8.T
        kn = (k_unit * scale).astype(BF)
        kT[:, here] = kn
        k[here, :] = kn.T
        v[here, :] = qkv_ref[2, :, lanes].astype(BF).T
        gh = g_ref[:, lanes]
        gT[:, here] = gh
        g[here, :] = gh.T
        delta[:, here] = jnp.sum(gh.astype(F32) * mixed_ref[:, lanes].astype(F32), axis=0, keepdims=True)
        inv[:, here] = sum_ref[0, 0:1, lanes]
    dk[...] = jnp.zeros_like(dk)
    dv[...] = jnp.zeros_like(dv)
    for start, parts in chunks():
        span = slice(start, start + 256)
        query, grad = qT[:, span], gT[:, span]
        query_rows, grad_rows = q[span, :], g[span, :]
        scale_row, delta_row = inv[:, span], delta[:, span]
        acc = jnp.zeros((64, 256), F32)
        for kstart, count, kind in parts:
            keys = slice(kstart, kstart + count)
            probs = masked(kind, jnp.exp(nn(k[keys, :], query)) * scale_row)
            g_probs = nn(v[keys, :], grad)
            g_scores = (probs * (g_probs - delta_row)).astype(BF)
            dv[keys, :] += nn(probs.astype(BF), grad_rows)
            dk[keys, :] += nn(g_scores, query_rows)
            acc = acc + nn(kT[:, keys], g_scores)
        dq[:, span] = acc * 8.0
    g_scale = jnp.zeros((64, BLOCK), F32)
    for i in range(NB):
        lanes = pl.ds(pl.multiple_of(perm_ref[i] * BLOCK, BLOCK), BLOCK)
        here = slice(i * BLOCK, (i + 1) * BLOCK)
        for which, grad in ((0, dq[:, here]), (1, dk[here, :].T)):
            unit, inverse = head_norm(qkv_ref[which, :, lanes])
            g_scale = g_scale + grad * unit
            scaled = grad * scale
            raw = (scaled - unit * jnp.sum(scaled * unit, axis=0, keepdims=True)) * inverse
            out_ref[which, :, lanes] = raw.astype(BF)
        out_ref[2, :, lanes] = dv[here, :].T.astype(BF)
    gscale_ref[0] = jnp.sum(g_scale, axis=1, keepdims=True)

def attn_bwd(perm, qkv, scale, sums, mixed, g_mixed):
    heads = qkv.shape[1] // HEAD_DIM
    row = lambda h, p: (h, 0)
    return pl.pallas_call(
        bwd_kernel,
        grid_spec=pltpu.PrefetchScalarGridSpec(
            num_scalar_prefetch=1,
            grid=(heads,),
            in_specs=[
                pl.BlockSpec((3, HEAD_DIM, TOK), lambda h, p: (0, h, 0)),
                pl.BlockSpec((1, HEAD_DIM, 1), lambda h, p: (h, 0, 0)),
                pl.BlockSpec((1, 8, TOK), lambda h, p: (h, 0, 0)),
                pl.BlockSpec((HEAD_DIM, TOK), row),
                pl.BlockSpec((HEAD_DIM, TOK), row),
            ],
            out_specs=[
                pl.BlockSpec((3, HEAD_DIM, TOK), lambda h, p: (0, h, 0)),
                pl.BlockSpec((1, HEAD_DIM, 1), lambda h, p: (h, 0, 0)),
            ],
            scratch_shapes=[
                pltpu.VMEM((HEAD_DIM, TOK), BF),
                pltpu.VMEM((TOK, HEAD_DIM), BF),
                pltpu.VMEM((TOK, HEAD_DIM), BF),
                pltpu.VMEM((HEAD_DIM, TOK), BF),
                pltpu.VMEM((TOK, HEAD_DIM), BF),
                pltpu.VMEM((HEAD_DIM, TOK), BF),
                pltpu.VMEM((TOK, HEAD_DIM), BF),
                pltpu.VMEM((HEAD_DIM, TOK), F32),
                pltpu.VMEM((TOK, HEAD_DIM), F32),
                pltpu.VMEM((TOK, HEAD_DIM), F32),
                pltpu.VMEM((1, TOK), F32),
                pltpu.VMEM((1, TOK), F32),
            ],
        ),
        out_shape=[
            jax.ShapeDtypeStruct((3, heads * HEAD_DIM, TOK), BF),
            jax.ShapeDtypeStruct((heads, HEAD_DIM, 1), F32),
        ],
        compiler_params=pltpu.CompilerParams(vmem_limit_bytes=48 << 20),
        name="tree_attention_grad",
        cost_estimate=pl.CostEstimate(flops=heads * 5 * 2 * 64 * 256 * 10752, bytes_accessed=20 << 20, transcendentals=heads * 256 * 10752),
    )(perm, qkv, scale, sums, mixed, g_mixed)


def order_kernel(where_ref, parent_ref, perm_ref, branch_ref, leaf_ref):
    base, me = where_ref[0], where_ref[1]

    def parent_of(block):
        return jnp.where(block >= 0, parent_ref[jnp.maximum(block, 0)] - base, -1)

    def depth_of(block):
        def climb(step, state):
            at, depth = state
            at = jnp.where(at >= 0, jnp.maximum(parent_of(at), -1), -1)
            return at, depth + (at >= 0).astype(jnp.int32)

        return lax.fori_loop(0, DEPTH - 1, climb, (block, jnp.int32(0)))[1]

    def relative(block):
        return jnp.bitwise_xor(block // 5, me) * 5 + block % 5

    def first(block, count):
        depth = depth_of(block)
        is_branch = depth == TRUNK
        branch_ref[block] = count
        leaf_ref[block] = 0

        @pl.when(depth <= TRUNK)
        def _():
            perm_ref[jnp.where(is_branch, TRUNK + count, depth)] = relative(block)

        return count + is_branch.astype(jnp.int32)

    lax.fori_loop(0, NB, first, jnp.int32(0))

    def second(block, carry):
        @pl.when(depth_of(block) > TRUNK)
        def _():
            parent = jnp.maximum(parent_of(block), 0)
            seen = leaf_ref[parent]
            perm_ref[TRUNK + 4 + 2 * branch_ref[parent] + seen] = relative(block)
            leaf_ref[parent] = seen + 1

        return carry

    lax.fori_loop(0, NB, second, jnp.int32(0))


def tree_order(where, parents):
    smem = pl.BlockSpec(memory_space=pltpu.SMEM)
    return pl.pallas_call(
        order_kernel,
        in_specs=[smem, smem],
        out_specs=smem,
        out_shape=jax.ShapeDtypeStruct((NB,), jnp.int32),
        scratch_shapes=[pltpu.SMEM((NB,), jnp.int32), pltpu.SMEM((NB,), jnp.int32)],
        name="tree_order",
    )(where, parents)


def swap(value, step):
    return lax.ppermute(value, "fsdp", [(i, i ^ step) for i in range(4)])


def gather_tokens(mine):
    across = swap(mine, 2)
    return jnp.concatenate((mine, swap(mine, 1), across, swap(across, 1)), axis=0)


def reduce_tokens(share):
    rows = share.shape[0] // 4
    part = [share[i * rows : (i + 1) * rows] for i in range(4)]
    other = swap(jnp.concatenate((part[3], part[1]), axis=0).astype(BF), 1)
    far = part[2] + other[:rows]
    near = part[0] + other[rows:]
    return near + swap(far.astype(BF), 2)


def dot(left, right, contract):
    return lax.dot_general(left, right, ((contract[:1], contract[1:]), ((), ())), preferred_element_type=F32)


def local(
    states,
    teacher,
    parent_ids,
    valid_mask,
    w_query,
    w_key,
    w_value,
    w_out,
    w_up,
    w_gate,
    w_down,
    qk_scale,
    attn_rate,
    mlp_rate,
    up_scale,
    gate_scale,
):
    both = ("dp", "fsdp")
    dps, tps = 8, 4
    rows_w = w_query.shape[0]
    cols = D // tps
    hid = FF // tps
    ff_rows = FF // (dps * tps)
    me = lax.axis_index("fsdp")
    root_width = math.sqrt(D)
    mask_f = valid_mask.astype(F32)
    group_base = lax.axis_index("dp") * NB
    perm = tree_order(jnp.stack((group_base, me)).astype(jnp.int32), parent_ids)

    tokens = gather_tokens(states)

    count = jnp.sum(valid_mask)
    first_row = jnp.arange(rows_w, dtype=jnp.int32) == 0
    small = jnp.stack(
        (
            qk_scale,
            attn_rate,
            mlp_rate,
            jnp.where(first_row, count // 128, 0).astype(BF),
            jnp.where(first_row, count % 128, 0).astype(BF),
        ),
        axis=1,
    )
    qkv_send = jnp.concatenate(
        [w.reshape(rows_w, tps, cols).transpose(1, 0, 2) for w in (w_query, w_key, w_value)]
        + [jnp.broadcast_to(small[None], (tps, rows_w, 5))],
        axis=2,
    )
    qkv_group = lax.all_to_all(qkv_send, "fsdp", 0, 0, tiled=True).reshape(tps * rows_w, 3 * cols + 5)
    qkv_group = jnp.concatenate(
        (qkv_group, up_scale[:, None], gate_scale[:, None], jnp.zeros((tps * rows_w, 57), BF)), axis=1
    )
    first = lax.all_gather(qkv_group, "dp", axis=0, tiled=True)
    ug_send = jnp.concatenate(
        [
            w.reshape(rows_w, dps, tps, ff_rows).transpose(2, 0, 1, 3).reshape(tps, rows_w, hid)
            for w in (w_up, w_gate)
        ],
        axis=2,
    )
    ug_group = lax.all_to_all(ug_send, "fsdp", 0, 0, tiled=True).reshape(tps * rows_w, 2 * hid)
    spread = [(j, tps * (j % dps) + j // dps) for j in range(dps * tps)]
    out_mine = lax.ppermute(w_out, both, spread)
    w_ug = lax.all_gather(ug_group, "dp", axis=0, tiled=True)
    w_o = lax.all_gather(out_mine, "dp", axis=0, tiled=True)
    w_d = lax.all_gather(w_down, "dp", axis=0, tiled=True)

    w_qkv = first[:, : 3 * cols]
    small_all = first[:, 3 * cols :].astype(F32)
    rate_attn = small_all[:, 1]
    rate_mlp = small_all[:, 2]
    valid_count = 128.0 * jnp.sum(small_all[:, 3]) + jnp.sum(small_all[:, 4])
    scale_up = small_all[:, 5]
    scale_gate = small_all[:, 6]
    scale_qk = lax.dynamic_slice_in_dim(small_all[:, 0], me * cols, cols).reshape(cols // HEAD_DIM, HEAD_DIM, 1)

    qkv = dot(w_qkv, tokens, (0, 1)).reshape(3, cols, TOK)
    mixed, sums = attn_fwd(perm, qkv, scale_qk)
    attn = reduce_tokens(dot(mixed, w_o, (0, 0)))
    inputs = states.astype(F32)
    attn_unit, attn_inv = unit_rows(attn)
    hidden, hidden_inv = unit_rows(inputs + rate_attn * (attn_unit - inputs))
    hidden_all = gather_tokens(hidden.astype(BF))
    raw = dot(hidden_all, w_ug, (1, 0))
    up_proj, gate_proj = raw[:, :hid], raw[:, hid:]
    upscaled = up_proj * scale_up
    gated = gate_proj * scale_gate * root_width
    sigmoid_gate = jax.nn.sigmoid(gated)
    act = (upscaled * (gated * sigmoid_gate)).astype(BF)
    down = reduce_tokens(dot(act, w_d, (1, 0)))
    down_unit, down_inv = unit_rows(down)
    result, result_inv = unit_rows(hidden + rate_mlp * (down_unit - hidden))
    loss_local = jnp.sum(mask_f[:, None] * (result - teacher) ** 2)
    loss_parts = lax.all_gather(jnp.broadcast_to(loss_local, (1, 128)), both, axis=0, tiled=True)
    loss = jnp.sum(loss_parts[:, 0]) / valid_count

    g_result = 2.0 * mask_f[:, None] * (result - teacher) / valid_count
    g_last = unit_back(g_result, result, result_inv)
    g_rate_mlp = jnp.sum(g_last * (down_unit - hidden), axis=0)
    g_down = unit_back(g_last * rate_mlp, down_unit, down_inv).astype(BF)
    g_down_all = gather_tokens(g_down)
    g_act = dot(g_down_all, w_d, (1, 1))
    g_upscaled = g_act * (gated * sigmoid_gate)
    g_gated = g_act * upscaled * sigmoid_gate * (1.0 + gated * (1.0 - sigmoid_gate))
    grad_up_scale = jnp.sum(g_upscaled * up_proj, axis=0)
    grad_gate_scale = jnp.sum(g_gated * gate_proj * root_width, axis=0)
    g_ug = jnp.concatenate(
        ((g_upscaled * scale_up).astype(BF), (g_gated * scale_gate * root_width).astype(BF)), axis=1
    )
    g_hidden = g_last * (1.0 - rate_mlp) + reduce_tokens(dot(g_ug, w_ug, (1, 1)))
    grad_down = lax.psum_scatter(
        dot(act, g_down_all, (0, 0)).astype(BF), "dp", scatter_dimension=0, tiled=True
    ).astype(F32)
    grad_ug = lax.psum_scatter(dot(hidden_all, g_ug, (0, 0)).astype(BF), "dp", scatter_dimension=0, tiled=True)

    g_pre = unit_back(g_hidden, hidden, hidden_inv)
    g_rate_attn = jnp.sum(g_pre * (attn_unit - inputs), axis=0)
    g_attn = unit_back(g_pre * rate_attn, attn_unit, attn_inv).astype(BF)
    g_attn_all = gather_tokens(g_attn)
    g_mixed = dot(w_o, g_attn_all, (1, 1)).astype(BF)
    g_qkv, g_scale = attn_bwd(perm, qkv, scale_qk, sums, mixed, g_mixed)
    g_qkv = g_qkv.reshape(3 * cols, TOK)
    grad_states = g_pre * (1.0 - rate_attn) + reduce_tokens(dot(g_qkv, w_qkv, (0, 1)))
    grad_out = lax.psum_scatter(dot(mixed, g_attn_all, (1, 0)).astype(BF), "dp", scatter_dimension=0, tiled=True)
    grad_qkv = lax.psum_scatter(dot(tokens, g_qkv, (0, 1)).astype(BF), "dp", scatter_dimension=0, tiled=True)

    slot = jnp.arange(tps, dtype=jnp.int32) == me
    qk_rows = jnp.where(slot[:, None], g_scale.reshape(1, cols), 0.0).reshape(dps * tps, rows_w)
    ff_terms = [
        jnp.where(slot[None, :, None], term.reshape(dps, 1, ff_rows), 0.0).reshape(dps * tps, ff_rows)
        for term in (grad_up_scale, grad_gate_scale)
    ]
    vectors = jnp.concatenate(
        [g_rate_attn.reshape(dps * tps, rows_w), g_rate_mlp.reshape(dps * tps, rows_w), qk_rows]
        + ff_terms
        + [jnp.zeros((dps * tps, 512 - 3 * rows_w - 2 * ff_rows), F32)],
        axis=1,
    )
    vector_share = lax.psum_scatter(vectors, both, scatter_dimension=0, tiled=True)[0]

    grad_out = lax.ppermute(grad_out, both, [(b, a) for a, b in spread]).astype(F32)
    ug_back = lax.all_to_all(grad_ug, "fsdp", 0, 0, tiled=True).reshape(tps, rows_w, 2, dps, ff_rows)
    ug_back = ug_back.transpose(2, 1, 3, 0, 4).reshape(2, rows_w, FF).astype(F32)
    qkv_back = lax.all_to_all(grad_qkv, "fsdp", 0, 0, tiled=True).reshape(tps, rows_w, 3, cols)
    qkv_back = qkv_back.transpose(2, 1, 0, 3).reshape(3, rows_w, D).astype(F32)
    cuts = (0, rows_w, 2 * rows_w, 3 * rows_w, 3 * rows_w + ff_rows, 3 * rows_w + 2 * ff_rows)
    v = [vector_share[a:b] for a, b in zip(cuts, cuts[1:])]
    return (
        result.astype(BF),
        loss,
        grad_states,
        qkv_back[0],
        qkv_back[1],
        qkv_back[2],
        grad_out,
        ug_back[0],
        ug_back[1],
        grad_down,
        v[2],
        v[0],
        v[1],
        v[3],
        v[4],
    )


def solution(mesh):
    placed = (
        P(("dp", "fsdp"), None),
        P(("dp", "fsdp"), None),
        P("dp"),
        P(("dp", "fsdp")),
        P(("dp", "fsdp"), None),
        P(("dp", "fsdp"), None),
        P(("dp", "fsdp"), None),
        P(("dp", "fsdp"), None),
        P(("dp", "fsdp"), None),
        P(("dp", "fsdp"), None),
        P(("dp", "fsdp"), None),
        P(("dp", "fsdp")),
        P(("dp", "fsdp")),
        P(("dp", "fsdp")),
        P(("dp", "fsdp")),
        P(("dp", "fsdp")),
    )
    quick = mesh.shape["fsdp"] == 4 and mesh.shape["dp"] == 8
    return jax.shard_map(
        local if quick else general,
        mesh=mesh,
        in_specs=placed,
        out_specs=(
            P(("dp", "fsdp"), None),
            P(),
            P(("dp", "fsdp"), None),
            P(("dp", "fsdp"), None),
            P(("dp", "fsdp"), None),
            P(("dp", "fsdp"), None),
            P(("dp", "fsdp"), None),
            P(("dp", "fsdp"), None),
            P(("dp", "fsdp"), None),
            P(("dp", "fsdp"), None),
            P(("dp", "fsdp")),
            P(("dp", "fsdp")),
            P(("dp", "fsdp")),
            P(("dp", "fsdp")),
            P(("dp", "fsdp")),
        ),
        check_vma=False,
    )
```

```python
import functools
import math

import jax
import jax.numpy as jnp
from jax import lax
from jax.experimental import pallas as pl
from jax.experimental.pallas import tpu as pltpu
from jax.sharding import PartitionSpec as P


D = 1280
HEADS = 20
HEAD_DIM = 64
FF = 5120
BLOCK = 128
DEPTH = 10


EPS = 1e-06


def unit_rows(vector):
    inverse = lax.rsqrt(jnp.sum(vector * vector, axis=-1, keepdims=True) + EPS)
    return (vector * inverse, inverse)


def unit_back(grad, unit, inverse):
    return (grad - unit * jnp.sum(grad * unit, axis=-1, keepdims=True)) * inverse


def project(left, right):
    return jnp.dot(left, right, preferred_element_type=jnp.float32)


def project_back(grad, weight):
    return jnp.einsum("te,de->td", grad, weight, preferred_element_type=jnp.float32)


def ancestors(local_parent):
    column = jnp.arange(local_parent.shape[0], dtype=jnp.int32)
    columns = [column]
    for depth_step in range(DEPTH - 1):
        column = jnp.where(column >= 0, local_parent[jnp.maximum(column, 0)], -1)
        columns.append(column)
    return jnp.stack(columns, axis=1)


def head_back(grad_flat, unit, inverse, scale):
    scaled = (grad_flat * scale).reshape(unit.shape)
    raw = unit_back(scaled, unit, inverse).reshape(grad_flat.shape)
    scale_grad = jnp.sum(grad_flat * unit.reshape(grad_flat.shape), axis=0)
    return (raw, scale_grad)


def general(
    states,
    teacher,
    parent_ids,
    valid_mask,
    w_query,
    w_key,
    w_value,
    w_out,
    w_up,
    w_gate,
    w_down,
    qk_scale,
    attn_rate,
    mlp_rate,
    up_scale,
    gate_scale,
):
    rows_dev = states.shape[0]
    blocks_dev = rows_dev // BLOCK
    width_rows = w_query.shape[0]
    span = DEPTH * BLOCK
    factor = math.sqrt(HEAD_DIM)
    root_width = math.sqrt(D)
    mask_f = valid_mask.astype(jnp.float32)
    qkv_local = jnp.concatenate((w_query, w_key, w_value), axis=1)
    scal_width_local = jnp.stack((qk_scale, attn_rate, mlp_rate), axis=1)
    piece_qkv = lax.all_gather(qkv_local, ("dp", "fsdp"), axis=0, tiled=True)
    piece_out = lax.all_gather(w_out, ("dp", "fsdp"), axis=0, tiled=True)
    piece_scal = lax.all_gather(scal_width_local, ("dp", "fsdp"), axis=0, tiled=True)
    lefts = states
    total = jnp.dot(lefts, piece_qkv, preferred_element_type=jnp.float32)
    scal_whole = piece_scal
    qkv_raw = total
    scal_width = scal_whole
    scale_qk = scal_width[:, 0].astype(jnp.float32)
    rate_attn = scal_width[:, 1].astype(jnp.float32)
    rate_mlp = scal_width[:, 2].astype(jnp.float32)
    query_raw = qkv_raw[:, :D]
    key_raw = qkv_raw[:, D : 2 * D]
    values = qkv_raw[:, 2 * D :].astype(jnp.bfloat16)
    query_unit, query_inv = unit_rows(query_raw.reshape(rows_dev, HEADS, HEAD_DIM))
    key_unit, key_inv = unit_rows(key_raw.reshape(rows_dev, HEADS, HEAD_DIM))
    query_n = (query_unit.reshape(rows_dev, D) * scale_qk).astype(jnp.bfloat16)
    key_n = (key_unit.reshape(rows_dev, D) * scale_qk).astype(jnp.bfloat16)
    key_group, value_group = (
        lax.all_gather(key_n, "fsdp", axis=0, tiled=True),
        lax.all_gather(values, "fsdp", axis=0, tiled=True),
    )
    group_blocks = parent_ids.shape[0]
    group_base = lax.axis_index("dp") * group_blocks
    local_parent = jnp.where(parent_ids >= 0, parent_ids - group_base, -1)
    paths_all = ancestors(local_parent)
    own_first = lax.axis_index("fsdp") * blocks_dev
    paths = lax.dynamic_slice_in_dim(paths_all, own_first, blocks_dev, 0)
    safe_paths = jnp.maximum(paths, 0)
    key_rows = key_group.reshape(group_blocks, BLOCK, D)[safe_paths].reshape(
        blocks_dev, span, HEADS, HEAD_DIM
    )
    value_rows = value_group.reshape(group_blocks, BLOCK, D)[safe_paths].reshape(
        blocks_dev, span, HEADS, HEAD_DIM
    )
    slot_of = jnp.arange(span, dtype=jnp.int32) // BLOCK
    offset = jnp.arange(span, dtype=jnp.int32) % BLOCK
    row_pos = jnp.arange(BLOCK, dtype=jnp.int32)
    causal = offset[None, :] <= row_pos[:, None]
    is_live = jnp.take(paths, slot_of, axis=1) >= 0
    allowed = jnp.where(slot_of[None, None, :] == 0, causal[None], is_live[:, None, :])[:, None]
    query_heads = query_n.reshape(blocks_dev, BLOCK, HEADS, HEAD_DIM)
    scores = factor * jnp.einsum(
        "bqhd,bkhd->bhqk", query_heads, key_rows, preferred_element_type=jnp.float32
    )
    scores = jnp.where(allowed, scores, jnp.float32(-1e30))
    row_max = jnp.max(scores, axis=-1, keepdims=True)
    powers = jnp.exp(scores - row_max)
    row_sum = jnp.sum(powers, axis=-1, keepdims=True)
    probs_b = (powers / row_sum).astype(jnp.bfloat16)
    log_total = row_max + jnp.log(row_sum)
    mixed = jnp.einsum("bhqk,bkhd->bqhd", probs_b, value_rows, preferred_element_type=jnp.float32)
    mixed = mixed.reshape(rows_dev, D).astype(jnp.bfloat16)
    inputs = states.astype(jnp.float32)
    attn = project(mixed, piece_out)
    attn_unit, attn_inv = unit_rows(attn)
    hidden, hidden_inv = unit_rows(inputs + rate_attn * (attn_unit - inputs))
    hidden_b = hidden.astype(jnp.bfloat16)
    ffn_local = jnp.concatenate((w_up, w_gate), axis=1)
    scal_hidden_local = jnp.concatenate(
        (up_scale.reshape(width_rows, 4), gate_scale.reshape(width_rows, 4)), axis=1
    )
    piece_ffn = lax.all_gather(ffn_local, ("dp", "fsdp"), axis=0, tiled=True)
    piece_scal = lax.all_gather(scal_hidden_local, ("dp", "fsdp"), axis=0, tiled=True)
    lefts = hidden_b
    total = jnp.dot(lefts, piece_ffn, preferred_element_type=jnp.float32)
    scal_whole = piece_scal
    scale_up = scal_whole[:, :4].reshape(FF).astype(jnp.float32)
    scale_gate = scal_whole[:, 4:].reshape(FF).astype(jnp.float32)
    up_proj = total[:, :FF]
    gate_proj = total[:, FF:]
    upscaled = up_proj * scale_up
    gated = gate_proj * scale_gate * root_width
    sigmoid_gate = jax.nn.sigmoid(gated)
    act = (upscaled * (gated * sigmoid_gate)).astype(jnp.bfloat16)
    lefts = act
    down = jnp.dot(
        lefts,
        lax.all_gather(w_down, ("dp", "fsdp"), axis=0, tiled=True),
        preferred_element_type=jnp.float32,
    )
    down_unit, down_inv = unit_rows(down)
    result, result_inv = unit_rows(hidden + rate_mlp * (down_unit - hidden))
    loss_local = jnp.sum(mask_f[:, None] * (result - teacher) ** 2)
    valid_count, loss_sum = lax.psum((jnp.sum(mask_f), loss_local), ("dp", "fsdp"))
    loss = loss_sum / valid_count
    g_result = 2.0 * mask_f[:, None] * (result - teacher) / valid_count
    g_last = unit_back(g_result, result, result_inv)
    g_hidden = g_last * (1.0 - rate_mlp)
    g_rate_mlp = jnp.sum(g_last * (down_unit - hidden), axis=0)
    g_down = unit_back(g_last * rate_mlp, down_unit, down_inv).astype(jnp.bfloat16)
    g_act = jnp.einsum(
        "te,fe->tf",
        g_down,
        lax.all_gather(w_down, ("dp", "fsdp"), axis=0, tiled=True),
        preferred_element_type=jnp.float32,
    )
    g_upscaled = g_act * (gated * sigmoid_gate)
    g_gated = g_act * upscaled * sigmoid_gate * (1.0 + gated * (1.0 - sigmoid_gate))
    grad_up_scale = jnp.sum(g_upscaled * up_proj, axis=0)
    grad_gate_scale = jnp.sum(g_gated * gate_proj * root_width, axis=0)
    g_up = (g_upscaled * scale_up).astype(jnp.bfloat16)
    g_gate = (g_gated * scale_gate * root_width).astype(jnp.bfloat16)
    g_both = jnp.concatenate((g_up, g_gate), axis=1)
    g_hidden = g_hidden + jnp.einsum(
        "tc,dc->td",
        g_both,
        lax.all_gather(ffn_local, ("dp", "fsdp"), axis=0, tiled=True),
        preferred_element_type=jnp.float32,
    )
    scal_terms = jnp.concatenate(
        (grad_up_scale.reshape(D, 4), grad_gate_scale.reshape(D, 4)), axis=1
    )
    lefts = hidden_b
    main = jnp.einsum("td,tc->dc", lefts, g_both, preferred_element_type=jnp.float32)
    ffn_share = lax.psum_scatter(
        jnp.concatenate((main, scal_terms), axis=1), ("dp", "fsdp"), scatter_dimension=0, tiled=True
    )
    lefts = act
    grad_down = lax.psum_scatter(
        jnp.einsum("tf,te->fe", lefts, g_down, preferred_element_type=jnp.float32),
        ("dp", "fsdp"),
        scatter_dimension=0,
        tiled=True,
    )
    g_pre = unit_back(g_hidden, hidden, hidden_inv)
    g_states = g_pre * (1.0 - rate_attn)
    g_rate_attn = jnp.sum(g_pre * (attn_unit - inputs), axis=0)
    g_attn = unit_back(g_pre * rate_attn, attn_unit, attn_inv).astype(jnp.bfloat16)
    g_mixed = project_back(g_attn, piece_out).astype(jnp.bfloat16)
    scores = factor * jnp.einsum(
        "bqhd,bkhd->bhqk", query_heads, key_rows, preferred_element_type=jnp.float32
    )
    probs = jnp.where(allowed, jnp.exp(scores - log_total), jnp.float32(0.0))
    probs_again = probs.astype(jnp.bfloat16)
    g_heads = g_mixed.reshape(blocks_dev, BLOCK, HEADS, HEAD_DIM)
    g_probs = jnp.einsum("bqhd,bkhd->bhqk", g_heads, value_rows, preferred_element_type=jnp.float32)
    delta = jnp.sum(probs * g_probs, axis=-1, keepdims=True)
    g_scores = (probs * (g_probs - delta)).astype(jnp.bfloat16)
    g_query_n = factor * jnp.einsum(
        "bhqk,bkhd->bqhd", g_scores, key_rows, preferred_element_type=jnp.float32
    )
    g_key_rows = factor * jnp.einsum(
        "bhqk,bqhd->bkhd", g_scores, query_heads, preferred_element_type=jnp.float32
    )
    g_value_rows = jnp.einsum(
        "bhqk,bqhd->bkhd", probs_again, g_heads, preferred_element_type=jnp.float32
    )
    flat_paths = safe_paths.reshape(blocks_dev * DEPTH)
    g_key_group = (
        jnp.zeros((group_blocks, BLOCK, D), jnp.float32)
        .at[flat_paths]
        .add(g_key_rows.reshape(blocks_dev * DEPTH, BLOCK, D))
    )
    g_value_group = (
        jnp.zeros((group_blocks, BLOCK, D), jnp.float32)
        .at[flat_paths]
        .add(g_value_rows.reshape(blocks_dev * DEPTH, BLOCK, D))
    )
    g_key_n, g_values = (
        lax.psum_scatter(
            g_key_group.reshape(group_blocks * BLOCK, D).astype(jnp.bfloat16),
            "fsdp",
            scatter_dimension=0,
            tiled=True,
        ).astype(jnp.float32),
        lax.psum_scatter(
            g_value_group.reshape(group_blocks * BLOCK, D).astype(jnp.bfloat16),
            "fsdp",
            scatter_dimension=0,
            tiled=True,
        ).astype(jnp.float32),
    )
    g_query_raw, scale_from_query = head_back(
        g_query_n.reshape(rows_dev, D), query_unit, query_inv, scale_qk
    )
    g_key_raw, scale_from_key = head_back(g_key_n, key_unit, key_inv, scale_qk)
    grad_qk_scale = scale_from_query + scale_from_key
    g_qkv = jnp.concatenate(
        (
            g_query_raw.astype(jnp.bfloat16),
            g_key_raw.astype(jnp.bfloat16),
            g_values.astype(jnp.bfloat16),
        ),
        axis=1,
    )
    g_states = g_states + jnp.einsum(
        "tc,dc->td",
        g_qkv,
        lax.all_gather(qkv_local, ("dp", "fsdp"), axis=0, tiled=True),
        preferred_element_type=jnp.float32,
    )
    vector_terms = jnp.stack((grad_qk_scale, g_rate_attn, g_rate_mlp), axis=1)
    lefts = states
    main = jnp.einsum("td,tc->dc", lefts, g_qkv, preferred_element_type=jnp.float32)
    outer = jnp.einsum("td,tc->dc", mixed, g_attn, preferred_element_type=jnp.float32)
    attn_share = lax.psum_scatter(
        jnp.concatenate((main, outer, vector_terms), axis=1),
        ("dp", "fsdp"),
        scatter_dimension=0,
        tiled=True,
    )
    return (
        result.astype(jnp.bfloat16),
        loss,
        g_states,
        attn_share[:, :D],
        attn_share[:, D : 2 * D],
        attn_share[:, 2 * D : 3 * D],
        attn_share[:, 3 * D : 4 * D],
        ffn_share[:, :FF],
        ffn_share[:, FF : 2 * FF],
        grad_down,
        attn_share[:, 4 * D],
        attn_share[:, 4 * D + 1],
        attn_share[:, 4 * D + 2],
        ffn_share[:, 2 * FF : 2 * FF + 4].reshape(-1),
        ffn_share[:, 2 * FF + 4 : 2 * FF + 8].reshape(-1),
    )

TRUNK = 8
NB = 20
TOK = NB * BLOCK
F32 = jnp.float32
BF = jnp.bfloat16


def head_norm(raw):
    inv = lax.rsqrt(jnp.sum(raw * raw, axis=0, keepdims=True) + EPS)
    return raw * inv, inv

def tri(size):
    key = lax.broadcasted_iota(jnp.int32, (size, size), 0)
    query = lax.broadcasted_iota(jnp.int32, (size, size), 1)
    return key, query

def chunks():
    out = []
    for j in range(TRUNK // 2):
        parts = [(0, 256 * j, "all")] if j else []
        out.append((256 * j, parts + [(256 * j, 256, "causal")]))
    for j in range(2):
        start = TRUNK * BLOCK + 256 * j
        out.append((start, [(0, 1024, "all"), (start, 256, "pair")]))
    for j in range(4):
        start = (TRUNK + 4) * BLOCK + 256 * j
        out.append((start, [(0, 1024, "all"), ((TRUNK + j) * BLOCK, 128, "all"), (start, 256, "pair")]))
    return out

def masked(kind, value):
    if kind == "all":
        return value
    key, query = tri(256)
    keep = key <= query
    if kind == "pair":
        keep = keep & ((key < 128) == (query < 128))
    return jnp.where(keep, value, jnp.zeros_like(value))

def nn(a, b):
    return lax.dot_general(a, b, (((1,), (0,)), ((), ())), preferred_element_type=F32)

def fwd_kernel(perm_ref, qkv_ref, scale_ref, mixed_ref, sum_ref, qs, ks, vs):
    scale = scale_ref[0]
    for i in range(NB):
        lanes = pl.ds(pl.multiple_of(perm_ref[i] * BLOCK, BLOCK), BLOCK)
        here = slice(i * BLOCK, (i + 1) * BLOCK)
        q_unit, _ = head_norm(qkv_ref[0, :, lanes])
        k_unit, _ = head_norm(qkv_ref[1, :, lanes])
        qs[:, here] = (q_unit * scale).astype(BF) * BF(8.0)
        ks[here, :] = (k_unit * scale).astype(BF).T
        vs[0:64, here] = qkv_ref[2, :, lanes].astype(BF)
    vs[64:80, :] = jnp.ones((16, TOK), BF)
    for start, parts in chunks():
        query = qs[:, start:start + 256]
        acc = jnp.zeros((80, 256), F32)
        for kstart, count, kind in parts:
            scores = nn(ks[kstart:kstart + count, :], query)
            powers = masked(kind, jnp.exp(scores)).astype(BF)
            acc = acc + nn(vs[:, kstart:kstart + count], powers)
        total = acc[64:65, :]
        result = (acc[0:64, :] / total).astype(BF)
        for half in range(2):
            lanes = pl.ds(pl.multiple_of(perm_ref[start // BLOCK + half] * BLOCK, BLOCK), BLOCK)
            cut = slice(half * BLOCK, (half + 1) * BLOCK)
            mixed_ref[:, lanes] = result[:, cut]
            sum_ref[0, :, lanes] = jnp.broadcast_to(1.0 / total[:, cut], (8, BLOCK))

def attn_fwd(perm, qkv, scale):
    heads = qkv.shape[1] // HEAD_DIM
    return pl.pallas_call(
        fwd_kernel,
        grid_spec=pltpu.PrefetchScalarGridSpec(
            num_scalar_prefetch=1,
            grid=(heads,),
            in_specs=[
                pl.BlockSpec((3, HEAD_DIM, TOK), lambda h, p: (0, h, 0)),
                pl.BlockSpec((1, HEAD_DIM, 1), lambda h, p: (h, 0, 0)),
            ],
            out_specs=[
                pl.BlockSpec((HEAD_DIM, TOK), lambda h, p: (h, 0)),
                pl.BlockSpec((1, 8, TOK), lambda h, p: (h, 0, 0)),
            ],
            scratch_shapes=[
                pltpu.VMEM((HEAD_DIM, TOK), BF),
                pltpu.VMEM((TOK, HEAD_DIM), BF),
                pltpu.VMEM((80, TOK), BF),
            ],
        ),
        out_shape=[
            jax.ShapeDtypeStruct((heads * HEAD_DIM, TOK), BF),
            jax.ShapeDtypeStruct((heads, 8, TOK), F32),
        ],
        compiler_params=pltpu.CompilerParams(vmem_limit_bytes=48 << 20),
        name="tree_attention",
        cost_estimate=pl.CostEstimate(flops=heads * 2 * 2 * 64 * 256 * 10752, bytes_accessed=12 << 20, transcendentals=heads * 256 * 10752),
    )(perm, qkv, scale)

def bwd_kernel(perm_ref, qkv_ref, scale_ref, sum_ref, mixed_ref, g_ref, out_ref, gscale_ref,
               qT, q, k, kT, v, gT, g, dq, dk, dv, delta, inv):
    scale = scale_ref[0]
    for i in range(NB):
        lanes = pl.ds(pl.multiple_of(perm_ref[i] * BLOCK, BLOCK), BLOCK)
        here = slice(i * BLOCK, (i + 1) * BLOCK)
        q_unit, _ = head_norm(qkv_ref[0, :, lanes])
        k_unit, _ = head_norm(qkv_ref[1, :, lanes])
        q8 = (q_unit * scale).astype(BF) * BF(8.0)
        qT[:, here] = q8
        q[here, :] = q8.T
        kn = (k_unit * scale).astype(BF)
        kT[:, here] = kn
        k[here, :] = kn.T
        v[here, :] = qkv_ref[2, :, lanes].astype(BF).T
        gh = g_ref[:, lanes]
        gT[:, here] = gh
        g[here, :] = gh.T
        delta[:, here] = jnp.sum(gh.astype(F32) * mixed_ref[:, lanes].astype(F32), axis=0, keepdims=True)
        inv[:, here] = sum_ref[0, 0:1, lanes]
    dk[...] = jnp.zeros_like(dk)
    dv[...] = jnp.zeros_like(dv)
    for start, parts in chunks():
        span = slice(start, start + 256)
        query, grad = qT[:, span], gT[:, span]
        query_rows, grad_rows = q[span, :], g[span, :]
        scale_row, delta_row = inv[:, span], delta[:, span]
        acc = jnp.zeros((64, 256), F32)
        for kstart, count, kind in parts:
            keys = slice(kstart, kstart + count)
            probs = masked(kind, jnp.exp(nn(k[keys, :], query)) * scale_row)
            g_probs = nn(v[keys, :], grad)
            g_scores = (probs * (g_probs - delta_row)).astype(BF)
            dv[keys, :] += nn(probs.astype(BF), grad_rows)
            dk[keys, :] += nn(g_scores, query_rows)
            acc = acc + nn(kT[:, keys], g_scores)
        dq[:, span] = acc * 8.0
    g_scale = jnp.zeros((64, BLOCK), F32)
    for i in range(NB):
        lanes = pl.ds(pl.multiple_of(perm_ref[i] * BLOCK, BLOCK), BLOCK)
        here = slice(i * BLOCK, (i + 1) * BLOCK)
        for which, grad in ((0, dq[:, here]), (1, dk[here, :].T)):
            unit, inverse = head_norm(qkv_ref[which, :, lanes])
            g_scale = g_scale + grad * unit
            scaled = grad * scale
            raw = (scaled - unit * jnp.sum(scaled * unit, axis=0, keepdims=True)) * inverse
            out_ref[which, :, lanes] = raw.astype(BF)
        out_ref[2, :, lanes] = dv[here, :].T.astype(BF)
    gscale_ref[0] = jnp.sum(g_scale, axis=1, keepdims=True)

def attn_bwd(perm, qkv, scale, sums, mixed, g_mixed):
    heads = qkv.shape[1] // HEAD_DIM
    row = lambda h, p: (h, 0)
    return pl.pallas_call(
        bwd_kernel,
        grid_spec=pltpu.PrefetchScalarGridSpec(
            num_scalar_prefetch=1,
            grid=(heads,),
            in_specs=[
                pl.BlockSpec((3, HEAD_DIM, TOK), lambda h, p: (0, h, 0)),
                pl.BlockSpec((1, HEAD_DIM, 1), lambda h, p: (h, 0, 0)),
                pl.BlockSpec((1, 8, TOK), lambda h, p: (h, 0, 0)),
                pl.BlockSpec((HEAD_DIM, TOK), row),
                pl.BlockSpec((HEAD_DIM, TOK), row),
            ],
            out_specs=[
                pl.BlockSpec((3, HEAD_DIM, TOK), lambda h, p: (0, h, 0)),
                pl.BlockSpec((1, HEAD_DIM, 1), lambda h, p: (h, 0, 0)),
            ],
            scratch_shapes=[
                pltpu.VMEM((HEAD_DIM, TOK), BF),
                pltpu.VMEM((TOK, HEAD_DIM), BF),
                pltpu.VMEM((TOK, HEAD_DIM), BF),
                pltpu.VMEM((HEAD_DIM, TOK), BF),
                pltpu.VMEM((TOK, HEAD_DIM), BF),
                pltpu.VMEM((HEAD_DIM, TOK), BF),
                pltpu.VMEM((TOK, HEAD_DIM), BF),
                pltpu.VMEM((HEAD_DIM, TOK), F32),
                pltpu.VMEM((TOK, HEAD_DIM), F32),
                pltpu.VMEM((TOK, HEAD_DIM), F32),
                pltpu.VMEM((1, TOK), F32),
                pltpu.VMEM((1, TOK), F32),
            ],
        ),
        out_shape=[
            jax.ShapeDtypeStruct((3, heads * HEAD_DIM, TOK), BF),
            jax.ShapeDtypeStruct((heads, HEAD_DIM, 1), F32),
        ],
        compiler_params=pltpu.CompilerParams(vmem_limit_bytes=48 << 20),
        name="tree_attention_grad",
        cost_estimate=pl.CostEstimate(flops=heads * 5 * 2 * 64 * 256 * 10752, bytes_accessed=20 << 20, transcendentals=heads * 256 * 10752),
    )(perm, qkv, scale, sums, mixed, g_mixed)


MESH = pl.DeviceIdType.MESH


def ring_place():
    dp = lax.axis_index("dp")
    z, y = dp // 2, dp % 2
    return z + y * (7 - 2 * z)


def ring_dp(place):
    place = (place + 16) % 8
    y = place // 4
    return 2 * (place + y * (7 - 2 * place)) + y


def greet(peers):
    barrier = pltpu.get_barrier_semaphore()
    for peer in peers:
        pl.semaphore_signal(barrier, inc=1, device_id=peer, device_id_type=MESH)
    pl.semaphore_wait(barrier, len(peers))


def group_peers():
    me = lax.axis_index("fsdp")
    core = 1 - 2 * (me % 2)
    chip = 2 - 4 * (me // 2)
    return {"fsdp": me + core}, {"fsdp": me + chip}, {"fsdp": me + core + chip}


def send(src, dst, send_sem, recv_sem, peer):
    return pltpu.make_async_remote_copy(
        src_ref=src, dst_ref=dst, send_sem=send_sem, recv_sem=recv_sem, device_id=peer, device_id_type=MESH
    )


def first_kernel(states, qkv_send, extra, out_piece, tokens, weights, out_w, own_sem, tok_send, tok_recv,
                 a2a_send, a2a_recv, ring_send, ring_recv):
    me, dp = lax.axis_index("fsdp"), lax.axis_index("dp")
    place = ring_place()
    sibling, across, corner = group_peers()
    right, left = {"dp": ring_dp(place + 1)}, {"dp": ring_dp(place - 1)}
    greet([sibling, across, corner, right, left])
    rows = states.shape[0] // 2
    halves = [pl.ds(0, rows), pl.ds(rows, rows)]

    exchange = []
    for i, peer in enumerate((sibling, across, corner)):
        copy = send(qkv_send.at[peer["fsdp"]], weights.at[dp, me], a2a_send.at[i], a2a_recv.at[i], peer)
        copy.start()
        exchange.append(copy)
    far = []
    for i, half in enumerate(halves):
        copy = send(states.at[half], tokens.at[2, half], tok_send.at[i], tok_recv.at[i], across)
        copy.start()
        far.append(copy)
    near = send(states, tokens.at[1], tok_send.at[2], tok_recv.at[2], sibling)
    near.start()
    own = pltpu.make_async_copy(states, tokens.at[0], own_sem.at[0])
    own.start()
    weights[dp, me] = qkv_send[me]
    out_w[dp] = out_piece[...]
    for copy in exchange:
        copy.wait()
    lanes = pl.ds(weights.shape[3] - 128, 128)
    weights[dp, :, :, lanes] = weights[dp, :, :, lanes] + extra[...]

    def hop(step, carry):
        to_right, to_left = ring_dp(place - step), ring_dp(place + step)
        copies = [
            send(weights.at[to_right, pl.ds(0, 2)], weights.at[to_right, pl.ds(0, 2)],
                 ring_send.at[0, step], ring_recv.at[0, step], right),
            send(weights.at[to_left, pl.ds(2, 2)], weights.at[to_left, pl.ds(2, 2)],
                 ring_send.at[1, step], ring_recv.at[1, step], left),
            send(out_w.at[to_right, :, pl.ds(0, 640)], out_w.at[to_right, :, pl.ds(0, 640)],
                 ring_send.at[2, step], ring_recv.at[2, step], right),
            send(out_w.at[to_left, :, pl.ds(640, 640)], out_w.at[to_left, :, pl.ds(640, 640)],
                 ring_send.at[3, step], ring_recv.at[3, step], left),
        ]
        for copy in copies:
            copy.start()
        for copy in copies:
            copy.wait()
        return carry

    lax.fori_loop(0, 4, hop, 0)
    passed = []
    for i, half in enumerate(halves):
        far[i].wait()
        copy = send(tokens.at[2, half], tokens.at[3, half], tok_send.at[3 + i], tok_recv.at[3 + i], sibling)
        copy.start()
        passed.append(copy)
    lax.fori_loop(4, 7, hop, 0)
    near.wait()
    own.wait()
    for copy in passed:
        copy.wait()


def first_exchange(states, qkv_send, extra, out_piece):
    tps, rows_w, width = qkv_send.shape
    vmem, hbm = pl.BlockSpec(memory_space=pltpu.VMEM), pl.BlockSpec(memory_space=pl.ANY)
    return pl.pallas_call(
        first_kernel,
        in_specs=[hbm, vmem, vmem, vmem],
        out_specs=[hbm, vmem, vmem],
        out_shape=[
            jax.ShapeDtypeStruct((4,) + states.shape, BF),
            jax.ShapeDtypeStruct((8, tps, rows_w, width), BF),
            jax.ShapeDtypeStruct((8,) + out_piece.shape, BF),
        ],
        scratch_shapes=[
            pltpu.SemaphoreType.DMA((1,)),
            pltpu.SemaphoreType.DMA((5,)),
            pltpu.SemaphoreType.DMA((5,)),
            pltpu.SemaphoreType.DMA((3,)),
            pltpu.SemaphoreType.DMA((3,)),
            pltpu.SemaphoreType.DMA((4, 7)),
            pltpu.SemaphoreType.DMA((4, 7)),
        ],
        compiler_params=pltpu.CompilerParams(
            collective_id=1, has_side_effects=True, vmem_limit_bytes=32 << 20
        ),
        cost_estimate=pl.CostEstimate(flops=0, bytes_accessed=150 << 20, transcendentals=0),
        name="first_exchange",
    )(states, qkv_send, extra, out_piece)


def last_kernel(share, base, grads, vectors, g_states, qkv_rows, out_rows, vec_own,
                core_buf, far_buf, x_buf, ring_buf, vec_buf, row_buf, vec_part, vec_in,
                core_send, core_recv, x_send, x_recv, ring_send, ring_recv, a2a_send, a2a_recv):
    me, dp = lax.axis_index("fsdp"), lax.axis_index("dp")
    place = ring_place()
    sibling, across, corner = group_peers()
    right, left = {"dp": ring_dp(place + 1)}, {"dp": ring_dp(place - 1)}
    greet([sibling, across, corner, right, left])
    half = grads.shape[1] // 2
    rows = share.shape[1] // 4

    def first_hop():
        to_right, to_left = ring_dp(place - 1), ring_dp(place + 1)
        return [
            send(grads.at[to_right, pl.ds(0, half)], ring_buf.at[0, 0], ring_send.at[0, 0], ring_recv.at[0, 0], right),
            send(grads.at[to_left, pl.ds(half, half)], ring_buf.at[1, 0], ring_send.at[1, 0], ring_recv.at[1, 0], left),
            send(vectors.at[to_right], vec_buf.at[0], ring_send.at[2, 0], ring_recv.at[2, 0], right),
        ]

    def later_hop(step):
        return [
            send(ring_buf.at[0, step - 1], ring_buf.at[0, step], ring_send.at[0, step], ring_recv.at[0, step], right),
            send(ring_buf.at[1, step - 1], ring_buf.at[1, step], ring_send.at[1, step], ring_recv.at[1, step], left),
            send(vec_buf.at[step - 1], vec_buf.at[step], ring_send.at[2, step], ring_recv.at[2, step], right),
        ]

    core = [
        send(share.at[3], core_buf.at[0], core_send.at[0], core_recv.at[0], sibling),
        send(share.at[1], core_buf.at[1], core_send.at[1], core_recv.at[1], sibling),
    ]
    core[0].start()
    opening = first_hop()
    for copy in opening:
        copy.start()
    core[1].start()
    core[0].wait()
    far = []
    for i in range(4):
        span = pl.ds(i * rows, rows)
        far_buf[span] = (share[2, span].astype(F32) + core_buf[0, span].astype(F32)).astype(BF)
        copy = send(far_buf.at[span], x_buf.at[span], x_send.at[i], x_recv.at[i], across)
        copy.start()
        far.append(copy)
    for copy in opening:
        copy.wait()

    def hop(step, carry):
        to_right, to_left = ring_dp(place - 1 - step), ring_dp(place + 1 + step)
        ring_buf[0, step - 1] = (
            ring_buf[0, step - 1].astype(F32) + grads[to_right, pl.ds(0, half)].astype(F32)
        ).astype(BF)
        ring_buf[1, step - 1] = (
            ring_buf[1, step - 1].astype(F32) + grads[to_left, pl.ds(half, half)].astype(F32)
        ).astype(BF)
        vec_buf[step - 1] = vec_buf[step - 1] + vectors[to_right]
        copies = later_hop(step)
        for copy in copies:
            copy.start()
        for copy in copies:
            copy.wait()
        return carry

    lax.fori_loop(1, 7, hop, 0)
    quarter = half // 2
    for side in range(2):
        total = ring_buf[side, 6].astype(F32) + grads[dp, pl.ds(side * half, half)].astype(F32)
        for i in range(2):
            piece = total[i * quarter : (i + 1) * quarter]
            row_buf[2 * side + i] = piece.astype(BF)
            out_rows[2 * side + i] = piece
    vec_part[...] = vec_buf[6] + vectors[dp]
    exchange = []
    for i, peer in enumerate((sibling, across, corner)):
        to = peer["fsdp"]
        copies = [
            send(row_buf.at[to], qkv_rows.at[me], a2a_send.at[i], a2a_recv.at[i], peer),
            send(vec_part.at[to], vec_in.at[me], a2a_send.at[3 + i], a2a_recv.at[3 + i], peer),
        ]
        for copy in copies:
            copy.start()
        exchange += copies
    qkv_rows[me] = row_buf[me]
    vec_in[me] = vec_part[me]
    core[1].wait()
    for i in range(4):
        span = pl.ds(i * rows, rows)
        far[i].wait()
        g_states[span] = base[span] + (
            share[0, span].astype(F32) + core_buf[1, span].astype(F32) + x_buf[span].astype(F32)
        )
    for copy in exchange:
        copy.wait()
    vec_own[...] = vec_in[0] + vec_in[1] + vec_in[2] + vec_in[3]


def last_exchange(share, base, grads, vectors):
    half, cols = grads.shape[1] // 2, grads.shape[2]
    rows_w = grads.shape[1] // 4
    vmem = pl.BlockSpec(memory_space=pltpu.VMEM)
    return pl.pallas_call(
        last_kernel,
        in_specs=[vmem] * 4,
        out_specs=[vmem] * 4,
        out_shape=[
            jax.ShapeDtypeStruct(base.shape, F32),
            jax.ShapeDtypeStruct((4, rows_w, cols), BF),
            jax.ShapeDtypeStruct((4, rows_w, cols), F32),
            jax.ShapeDtypeStruct(vectors.shape[2:], F32),
        ],
        scratch_shapes=[
            pltpu.VMEM((2,) + share.shape[1:], BF),
            pltpu.VMEM(share.shape[1:], BF),
            pltpu.VMEM(share.shape[1:], BF),
            pltpu.VMEM((2, 7, half, cols), BF),
            pltpu.VMEM((7,) + vectors.shape[1:], F32),
            pltpu.VMEM((4, rows_w, cols), BF),
            pltpu.VMEM(vectors.shape[1:], F32),
            pltpu.VMEM(vectors.shape[1:], F32),
            pltpu.SemaphoreType.DMA((2,)),
            pltpu.SemaphoreType.DMA((2,)),
            pltpu.SemaphoreType.DMA((4,)),
            pltpu.SemaphoreType.DMA((4,)),
            pltpu.SemaphoreType.DMA((3, 7)),
            pltpu.SemaphoreType.DMA((3, 7)),
            pltpu.SemaphoreType.DMA((6,)),
            pltpu.SemaphoreType.DMA((6,)),
        ],
        compiler_params=pltpu.CompilerParams(
            collective_id=2, has_side_effects=True, vmem_limit_bytes=52 << 20
        ),
        cost_estimate=pl.CostEstimate(flops=0, bytes_accessed=150 << 20, transcendentals=0),
        name="last_exchange",
    )(share, base, grads, vectors)


def order_kernel(where_ref, parent_ref, perm_ref, branch_ref, leaf_ref):
    base, me = where_ref[0], where_ref[1]

    def parent_of(block):
        return jnp.where(block >= 0, parent_ref[jnp.maximum(block, 0)] - base, -1)

    def depth_of(block):
        def climb(step, state):
            at, depth = state
            at = jnp.where(at >= 0, jnp.maximum(parent_of(at), -1), -1)
            return at, depth + (at >= 0).astype(jnp.int32)

        return lax.fori_loop(0, DEPTH - 1, climb, (block, jnp.int32(0)))[1]

    def relative(block):
        return jnp.bitwise_xor(block // 5, me) * 5 + block % 5

    def first(block, count):
        depth = depth_of(block)
        is_branch = depth == TRUNK
        branch_ref[block] = count
        leaf_ref[block] = 0

        @pl.when(depth <= TRUNK)
        def _():
            perm_ref[jnp.where(is_branch, TRUNK + count, depth)] = relative(block)

        return count + is_branch.astype(jnp.int32)

    lax.fori_loop(0, NB, first, jnp.int32(0))

    def second(block, carry):
        @pl.when(depth_of(block) > TRUNK)
        def _():
            parent = jnp.maximum(parent_of(block), 0)
            seen = leaf_ref[parent]
            perm_ref[TRUNK + 4 + 2 * branch_ref[parent] + seen] = relative(block)
            leaf_ref[parent] = seen + 1

        return carry

    lax.fori_loop(0, NB, second, jnp.int32(0))


def tree_order(where, parents):
    smem = pl.BlockSpec(memory_space=pltpu.SMEM)
    return pl.pallas_call(
        order_kernel,
        in_specs=[smem, smem],
        out_specs=smem,
        out_shape=jax.ShapeDtypeStruct((NB,), jnp.int32),
        scratch_shapes=[pltpu.SMEM((NB,), jnp.int32), pltpu.SMEM((NB,), jnp.int32)],
        name="tree_order",
    )(where, parents)


def swap(value, step):
    return lax.ppermute(value, "fsdp", [(i, i ^ step) for i in range(4)])


def gather_tokens(mine):
    across = swap(mine, 2)
    return jnp.concatenate((mine, swap(mine, 1), across, swap(across, 1)), axis=0)


def reduce_tokens(share):
    rows = share.shape[0] // 4
    part = [share[i * rows : (i + 1) * rows] for i in range(4)]
    other = swap(jnp.concatenate((part[3], part[1]), axis=0).astype(BF), 1)
    far = part[2] + other[:rows]
    near = part[0] + other[rows:]
    return near + swap(far.astype(BF), 2)


def dot(left, right, contract):
    return lax.dot_general(left, right, ((contract[:1], contract[1:]), ((), ())), preferred_element_type=F32)


def local(
    states,
    teacher,
    parent_ids,
    valid_mask,
    w_query,
    w_key,
    w_value,
    w_out,
    w_up,
    w_gate,
    w_down,
    qk_scale,
    attn_rate,
    mlp_rate,
    up_scale,
    gate_scale,
):
    both = ("dp", "fsdp")
    dps, tps = 8, 4
    rows_w = w_query.shape[0]
    cols = D // tps
    hid = FF // tps
    ff_rows = FF // (dps * tps)
    me = lax.axis_index("fsdp")
    root_width = math.sqrt(D)
    mask_f = valid_mask.astype(F32)
    group_base = lax.axis_index("dp") * NB
    perm = tree_order(jnp.stack((group_base, me)).astype(jnp.int32), parent_ids)

    count = jnp.sum(valid_mask)
    first_row = jnp.arange(rows_w, dtype=jnp.int32) == 0
    small = jnp.stack(
        (
            qk_scale,
            attn_rate,
            mlp_rate,
            jnp.where(first_row, count // 128, 0).astype(BF),
            jnp.where(first_row, count % 128, 0).astype(BF),
        ),
        axis=1,
    )
    small = jnp.pad(small, ((0, 0), (0, 59)))
    qkv_send = jnp.concatenate(
        [w.reshape(rows_w, tps, cols).transpose(1, 0, 2) for w in (w_query, w_key, w_value)]
        + [jnp.broadcast_to(small[None], (tps, rows_w, 64))],
        axis=2,
    )
    extra = jnp.pad(jnp.stack((up_scale, gate_scale), axis=1), ((0, 0), (69, 57))).reshape(tps, rows_w, 128)
    spread = [(j, tps * (j % dps) + j // dps) for j in range(dps * tps)]
    tokens, first, w_o = first_exchange(states, qkv_send, extra, lax.ppermute(w_out, both, spread))
    tokens = tokens.reshape(TOK, D)
    first = first.reshape(D, 1024)
    w_o = w_o.reshape(cols, D)
    ug_send = jnp.concatenate(
        [
            w.reshape(rows_w, dps, tps, ff_rows).transpose(2, 0, 1, 3).reshape(tps, rows_w, hid)
            for w in (w_up, w_gate)
        ],
        axis=2,
    )
    ug_group = lax.all_to_all(ug_send, "fsdp", 0, 0, tiled=True).reshape(tps * rows_w, 2 * hid)
    w_ug = lax.all_gather(ug_group, "dp", axis=0, tiled=True)
    w_d = lax.all_gather(w_down, "dp", axis=0, tiled=True)

    w_qkv = first[:, : 3 * cols]
    small_all = first[:, 3 * cols :].astype(F32)
    rate_attn = small_all[:, 1]
    rate_mlp = small_all[:, 2]
    valid_count = 128.0 * jnp.sum(small_all[:, 3]) + jnp.sum(small_all[:, 4])
    scale_up = small_all[:, 5]
    scale_gate = small_all[:, 6]
    scale_qk = lax.dynamic_slice_in_dim(small_all[:, 0], me * cols, cols).reshape(cols // HEAD_DIM, HEAD_DIM, 1)

    qkv = dot(w_qkv, tokens, (0, 1)).reshape(3, cols, TOK)
    mixed, sums = attn_fwd(perm, qkv, scale_qk)
    attn = reduce_tokens(dot(mixed, w_o, (0, 0)))
    inputs = states.astype(F32)
    attn_unit, attn_inv = unit_rows(attn)
    hidden, hidden_inv = unit_rows(inputs + rate_attn * (attn_unit - inputs))
    hidden_all = gather_tokens(hidden.astype(BF))
    raw = dot(hidden_all, w_ug, (1, 0))
    up_proj, gate_proj = raw[:, :hid], raw[:, hid:]
    upscaled = up_proj * scale_up
    gated = gate_proj * scale_gate * root_width
    sigmoid_gate = jax.nn.sigmoid(gated)
    act = (upscaled * (gated * sigmoid_gate)).astype(BF)
    down = reduce_tokens(dot(act, w_d, (1, 0)))
    down_unit, down_inv = unit_rows(down)
    result, result_inv = unit_rows(hidden + rate_mlp * (down_unit - hidden))
    loss_local = jnp.sum(mask_f[:, None] * (result - teacher) ** 2)

    g_result = 2.0 * mask_f[:, None] * (result - teacher) / valid_count
    g_last = unit_back(g_result, result, result_inv)
    g_rate_mlp = jnp.sum(g_last * (down_unit - hidden), axis=0)
    g_down = unit_back(g_last * rate_mlp, down_unit, down_inv).astype(BF)
    g_down_all = gather_tokens(g_down)
    g_act = dot(g_down_all, w_d, (1, 1))
    g_upscaled = g_act * (gated * sigmoid_gate)
    g_gated = g_act * upscaled * sigmoid_gate * (1.0 + gated * (1.0 - sigmoid_gate))
    grad_up_scale = jnp.sum(g_upscaled * up_proj, axis=0)
    grad_gate_scale = jnp.sum(g_gated * gate_proj * root_width, axis=0)
    g_ug = jnp.concatenate(
        ((g_upscaled * scale_up).astype(BF), (g_gated * scale_gate * root_width).astype(BF)), axis=1
    )
    back_hidden, part_down, part_ug = lax.optimization_barrier(
        (
            reduce_tokens(dot(g_ug, w_ug, (1, 1))),
            dot(act, g_down_all, (0, 0)).astype(BF),
            dot(hidden_all, g_ug, (0, 0)).astype(BF),
        )
    )
    g_hidden = g_last * (1.0 - rate_mlp) + back_hidden
    grad_ug = lax.psum_scatter(part_ug, "dp", scatter_dimension=0, tiled=True)
    grad_down = lax.psum_scatter(part_down, "dp", scatter_dimension=0, tiled=True).astype(F32)

    g_pre = unit_back(g_hidden, hidden, hidden_inv)
    g_rate_attn = jnp.sum(g_pre * (attn_unit - inputs), axis=0)
    g_attn = unit_back(g_pre * rate_attn, attn_unit, attn_inv).astype(BF)
    g_attn_all = gather_tokens(g_attn)
    g_mixed = dot(w_o, g_attn_all, (1, 1)).astype(BF)
    g_qkv, g_scale = attn_bwd(perm, qkv, scale_qk, sums, mixed, g_mixed)
    g_qkv = g_qkv.reshape(3 * cols, TOK)
    slot = jnp.arange(tps, dtype=jnp.int32) == me
    qk_rows = jnp.where(slot[:, None], g_scale.reshape(1, cols), 0.0).reshape(dps * tps, rows_w)
    ff_terms = [
        jnp.where(slot[None, :, None], term.reshape(dps, 1, ff_rows), 0.0).reshape(dps * tps, ff_rows)
        for term in (grad_up_scale, grad_gate_scale)
    ]
    vectors = jnp.concatenate(
        [g_rate_attn.reshape(dps * tps, rows_w), g_rate_mlp.reshape(dps * tps, rows_w), qk_rows]
        + ff_terms
        + [jnp.broadcast_to(loss_local, (dps * tps, 512 - 3 * rows_w - 2 * ff_rows))],
        axis=1,
    ).reshape(dps, tps, 4, 128)
    share = dot(g_qkv, w_qkv, (0, 1)).astype(BF).reshape(tps, TOK // tps, D)
    part_out = dot(mixed, g_attn_all, (1, 0)).astype(BF).reshape(dps, rows_w, tps, cols).transpose(0, 2, 1, 3)
    part_qkv = dot(tokens, g_qkv, (0, 1)).astype(BF).reshape(dps, tps * rows_w, 3 * cols)
    parts = jnp.concatenate((part_qkv, part_out.reshape(dps, tps * rows_w, cols)), axis=2)
    grad_states, qkv_back, out_back, vector_share = last_exchange(share, g_pre * (1.0 - rate_attn), parts, vectors)
    vector_share = vector_share.reshape(512)
    out_back = out_back[:, :, 3 * cols :].transpose(1, 0, 2).reshape(rows_w, D)
    grad_out = lax.ppermute(out_back, both, [(b, a) for a, b in spread])
    ug_back = lax.all_to_all(grad_ug, "fsdp", 0, 0, tiled=True).reshape(tps, rows_w, 2, dps, ff_rows)
    ug_back = ug_back.transpose(2, 1, 3, 0, 4).reshape(2, rows_w, FF).astype(F32)
    qkv_back = qkv_back[:, :, : 3 * cols].reshape(tps, rows_w, 3, cols)
    qkv_back = qkv_back.transpose(2, 1, 0, 3).reshape(3, rows_w, D).astype(F32)
    cuts = (0, rows_w, 2 * rows_w, 3 * rows_w, 3 * rows_w + ff_rows, 3 * rows_w + 2 * ff_rows)
    v = [vector_share[a:b] for a, b in zip(cuts, cuts[1:])]
    return (
        result.astype(BF),
        vector_share[-1] / valid_count,
        grad_states,
        qkv_back[0],
        qkv_back[1],
        qkv_back[2],
        grad_out,
        ug_back[0],
        ug_back[1],
        grad_down,
        v[2],
        v[0],
        v[1],
        v[3],
        v[4],
    )


def solution(mesh):
    placed = (
        P(("dp", "fsdp"), None),
        P(("dp", "fsdp"), None),
        P("dp"),
        P(("dp", "fsdp")),
        P(("dp", "fsdp"), None),
        P(("dp", "fsdp"), None),
        P(("dp", "fsdp"), None),
        P(("dp", "fsdp"), None),
        P(("dp", "fsdp"), None),
        P(("dp", "fsdp"), None),
        P(("dp", "fsdp"), None),
        P(("dp", "fsdp")),
        P(("dp", "fsdp")),
        P(("dp", "fsdp")),
        P(("dp", "fsdp")),
        P(("dp", "fsdp")),
    )
    quick = mesh.shape["fsdp"] == 4 and mesh.shape["dp"] == 8
    return jax.shard_map(
        local if quick else general,
        mesh=mesh,
        in_specs=placed,
        out_specs=(
            P(("dp", "fsdp"), None),
            P(),
            P(("dp", "fsdp"), None),
            P(("dp", "fsdp"), None),
            P(("dp", "fsdp"), None),
            P(("dp", "fsdp"), None),
            P(("dp", "fsdp"), None),
            P(("dp", "fsdp"), None),
            P(("dp", "fsdp"), None),
            P(("dp", "fsdp"), None),
            P(("dp", "fsdp")),
            P(("dp", "fsdp")),
            P(("dp", "fsdp")),
            P(("dp", "fsdp")),
            P(("dp", "fsdp")),
        ),
        check_vma=False,
    )
```

```python
import functools
import math

import jax
import jax.numpy as jnp
from jax import lax
from jax.experimental import pallas as pl
from jax.experimental.pallas import tpu as pltpu
from jax.sharding import PartitionSpec as P


D = 1280
HEADS = 20
HEAD_DIM = 64
FF = 5120
BLOCK = 128
DEPTH = 10


EPS = 1e-06


def unit_rows(vector):
    inverse = lax.rsqrt(jnp.sum(vector * vector, axis=-1, keepdims=True) + EPS)
    return (vector * inverse, inverse)


def unit_back(grad, unit, inverse):
    return (grad - unit * jnp.sum(grad * unit, axis=-1, keepdims=True)) * inverse


def project(left, right):
    return jnp.dot(left, right, preferred_element_type=jnp.float32)


def project_back(grad, weight):
    return jnp.einsum("te,de->td", grad, weight, preferred_element_type=jnp.float32)


def ancestors(local_parent):
    column = jnp.arange(local_parent.shape[0], dtype=jnp.int32)
    columns = [column]
    for depth_step in range(DEPTH - 1):
        column = jnp.where(column >= 0, local_parent[jnp.maximum(column, 0)], -1)
        columns.append(column)
    return jnp.stack(columns, axis=1)


def head_back(grad_flat, unit, inverse, scale):
    scaled = (grad_flat * scale).reshape(unit.shape)
    raw = unit_back(scaled, unit, inverse).reshape(grad_flat.shape)
    scale_grad = jnp.sum(grad_flat * unit.reshape(grad_flat.shape), axis=0)
    return (raw, scale_grad)


def general(
    states,
    teacher,
    parent_ids,
    valid_mask,
    w_query,
    w_key,
    w_value,
    w_out,
    w_up,
    w_gate,
    w_down,
    qk_scale,
    attn_rate,
    mlp_rate,
    up_scale,
    gate_scale,
):
    rows_dev = states.shape[0]
    blocks_dev = rows_dev // BLOCK
    width_rows = w_query.shape[0]
    span = DEPTH * BLOCK
    factor = math.sqrt(HEAD_DIM)
    root_width = math.sqrt(D)
    mask_f = valid_mask.astype(jnp.float32)
    qkv_local = jnp.concatenate((w_query, w_key, w_value), axis=1)
    scal_width_local = jnp.stack((qk_scale, attn_rate, mlp_rate), axis=1)
    piece_qkv = lax.all_gather(qkv_local, ("dp", "fsdp"), axis=0, tiled=True)
    piece_out = lax.all_gather(w_out, ("dp", "fsdp"), axis=0, tiled=True)
    piece_scal = lax.all_gather(scal_width_local, ("dp", "fsdp"), axis=0, tiled=True)
    lefts = states
    total = jnp.dot(lefts, piece_qkv, preferred_element_type=jnp.float32)
    scal_whole = piece_scal
    qkv_raw = total
    scal_width = scal_whole
    scale_qk = scal_width[:, 0].astype(jnp.float32)
    rate_attn = scal_width[:, 1].astype(jnp.float32)
    rate_mlp = scal_width[:, 2].astype(jnp.float32)
    query_raw = qkv_raw[:, :D]
    key_raw = qkv_raw[:, D : 2 * D]
    values = qkv_raw[:, 2 * D :].astype(jnp.bfloat16)
    query_unit, query_inv = unit_rows(query_raw.reshape(rows_dev, HEADS, HEAD_DIM))
    key_unit, key_inv = unit_rows(key_raw.reshape(rows_dev, HEADS, HEAD_DIM))
    query_n = (query_unit.reshape(rows_dev, D) * scale_qk).astype(jnp.bfloat16)
    key_n = (key_unit.reshape(rows_dev, D) * scale_qk).astype(jnp.bfloat16)
    key_group, value_group = (
        lax.all_gather(key_n, "fsdp", axis=0, tiled=True),
        lax.all_gather(values, "fsdp", axis=0, tiled=True),
    )
    group_blocks = parent_ids.shape[0]
    group_base = lax.axis_index("dp") * group_blocks
    local_parent = jnp.where(parent_ids >= 0, parent_ids - group_base, -1)
    paths_all = ancestors(local_parent)
    own_first = lax.axis_index("fsdp") * blocks_dev
    paths = lax.dynamic_slice_in_dim(paths_all, own_first, blocks_dev, 0)
    safe_paths = jnp.maximum(paths, 0)
    key_rows = key_group.reshape(group_blocks, BLOCK, D)[safe_paths].reshape(
        blocks_dev, span, HEADS, HEAD_DIM
    )
    value_rows = value_group.reshape(group_blocks, BLOCK, D)[safe_paths].reshape(
        blocks_dev, span, HEADS, HEAD_DIM
    )
    slot_of = jnp.arange(span, dtype=jnp.int32) // BLOCK
    offset = jnp.arange(span, dtype=jnp.int32) % BLOCK
    row_pos = jnp.arange(BLOCK, dtype=jnp.int32)
    causal = offset[None, :] <= row_pos[:, None]
    is_live = jnp.take(paths, slot_of, axis=1) >= 0
    allowed = jnp.where(slot_of[None, None, :] == 0, causal[None], is_live[:, None, :])[:, None]
    query_heads = query_n.reshape(blocks_dev, BLOCK, HEADS, HEAD_DIM)
    scores = factor * jnp.einsum(
        "bqhd,bkhd->bhqk", query_heads, key_rows, preferred_element_type=jnp.float32
    )
    scores = jnp.where(allowed, scores, jnp.float32(-1e30))
    row_max = jnp.max(scores, axis=-1, keepdims=True)
    powers = jnp.exp(scores - row_max)
    row_sum = jnp.sum(powers, axis=-1, keepdims=True)
    probs_b = (powers / row_sum).astype(jnp.bfloat16)
    log_total = row_max + jnp.log(row_sum)
    mixed = jnp.einsum("bhqk,bkhd->bqhd", probs_b, value_rows, preferred_element_type=jnp.float32)
    mixed = mixed.reshape(rows_dev, D).astype(jnp.bfloat16)
    inputs = states.astype(jnp.float32)
    attn = project(mixed, piece_out)
    attn_unit, attn_inv = unit_rows(attn)
    hidden, hidden_inv = unit_rows(inputs + rate_attn * (attn_unit - inputs))
    hidden_b = hidden.astype(jnp.bfloat16)
    ffn_local = jnp.concatenate((w_up, w_gate), axis=1)
    scal_hidden_local = jnp.concatenate(
        (up_scale.reshape(width_rows, 4), gate_scale.reshape(width_rows, 4)), axis=1
    )
    piece_ffn = lax.all_gather(ffn_local, ("dp", "fsdp"), axis=0, tiled=True)
    piece_scal = lax.all_gather(scal_hidden_local, ("dp", "fsdp"), axis=0, tiled=True)
    lefts = hidden_b
    total = jnp.dot(lefts, piece_ffn, preferred_element_type=jnp.float32)
    scal_whole = piece_scal
    scale_up = scal_whole[:, :4].reshape(FF).astype(jnp.float32)
    scale_gate = scal_whole[:, 4:].reshape(FF).astype(jnp.float32)
    up_proj = total[:, :FF]
    gate_proj = total[:, FF:]
    upscaled = up_proj * scale_up
    gated = gate_proj * scale_gate * root_width
    sigmoid_gate = jax.nn.sigmoid(gated)
    act = (upscaled * (gated * sigmoid_gate)).astype(jnp.bfloat16)
    lefts = act
    down = jnp.dot(
        lefts,
        lax.all_gather(w_down, ("dp", "fsdp"), axis=0, tiled=True),
        preferred_element_type=jnp.float32,
    )
    down_unit, down_inv = unit_rows(down)
    result, result_inv = unit_rows(hidden + rate_mlp * (down_unit - hidden))
    loss_local = jnp.sum(mask_f[:, None] * (result - teacher) ** 2)
    valid_count, loss_sum = lax.psum((jnp.sum(mask_f), loss_local), ("dp", "fsdp"))
    loss = loss_sum / valid_count
    g_result = 2.0 * mask_f[:, None] * (result - teacher) / valid_count
    g_last = unit_back(g_result, result, result_inv)
    g_hidden = g_last * (1.0 - rate_mlp)
    g_rate_mlp = jnp.sum(g_last * (down_unit - hidden), axis=0)
    g_down = unit_back(g_last * rate_mlp, down_unit, down_inv).astype(jnp.bfloat16)
    g_act = jnp.einsum(
        "te,fe->tf",
        g_down,
        lax.all_gather(w_down, ("dp", "fsdp"), axis=0, tiled=True),
        preferred_element_type=jnp.float32,
    )
    g_upscaled = g_act * (gated * sigmoid_gate)
    g_gated = g_act * upscaled * sigmoid_gate * (1.0 + gated * (1.0 - sigmoid_gate))
    grad_up_scale = jnp.sum(g_upscaled * up_proj, axis=0)
    grad_gate_scale = jnp.sum(g_gated * gate_proj * root_width, axis=0)
    g_up = (g_upscaled * scale_up).astype(jnp.bfloat16)
    g_gate = (g_gated * scale_gate * root_width).astype(jnp.bfloat16)
    g_both = jnp.concatenate((g_up, g_gate), axis=1)
    g_hidden = g_hidden + jnp.einsum(
        "tc,dc->td",
        g_both,
        lax.all_gather(ffn_local, ("dp", "fsdp"), axis=0, tiled=True),
        preferred_element_type=jnp.float32,
    )
    scal_terms = jnp.concatenate(
        (grad_up_scale.reshape(D, 4), grad_gate_scale.reshape(D, 4)), axis=1
    )
    lefts = hidden_b
    main = jnp.einsum("td,tc->dc", lefts, g_both, preferred_element_type=jnp.float32)
    ffn_share = lax.psum_scatter(
        jnp.concatenate((main, scal_terms), axis=1), ("dp", "fsdp"), scatter_dimension=0, tiled=True
    )
    lefts = act
    grad_down = lax.psum_scatter(
        jnp.einsum("tf,te->fe", lefts, g_down, preferred_element_type=jnp.float32),
        ("dp", "fsdp"),
        scatter_dimension=0,
        tiled=True,
    )
    g_pre = unit_back(g_hidden, hidden, hidden_inv)
    g_states = g_pre * (1.0 - rate_attn)
    g_rate_attn = jnp.sum(g_pre * (attn_unit - inputs), axis=0)
    g_attn = unit_back(g_pre * rate_attn, attn_unit, attn_inv).astype(jnp.bfloat16)
    g_mixed = project_back(g_attn, piece_out).astype(jnp.bfloat16)
    scores = factor * jnp.einsum(
        "bqhd,bkhd->bhqk", query_heads, key_rows, preferred_element_type=jnp.float32
    )
    probs = jnp.where(allowed, jnp.exp(scores - log_total), jnp.float32(0.0))
    probs_again = probs.astype(jnp.bfloat16)
    g_heads = g_mixed.reshape(blocks_dev, BLOCK, HEADS, HEAD_DIM)
    g_probs = jnp.einsum("bqhd,bkhd->bhqk", g_heads, value_rows, preferred_element_type=jnp.float32)
    delta = jnp.sum(probs * g_probs, axis=-1, keepdims=True)
    g_scores = (probs * (g_probs - delta)).astype(jnp.bfloat16)
    g_query_n = factor * jnp.einsum(
        "bhqk,bkhd->bqhd", g_scores, key_rows, preferred_element_type=jnp.float32
    )
    g_key_rows = factor * jnp.einsum(
        "bhqk,bqhd->bkhd", g_scores, query_heads, preferred_element_type=jnp.float32
    )
    g_value_rows = jnp.einsum(
        "bhqk,bqhd->bkhd", probs_again, g_heads, preferred_element_type=jnp.float32
    )
    flat_paths = safe_paths.reshape(blocks_dev * DEPTH)
    g_key_group = (
        jnp.zeros((group_blocks, BLOCK, D), jnp.float32)
        .at[flat_paths]
        .add(g_key_rows.reshape(blocks_dev * DEPTH, BLOCK, D))
    )
    g_value_group = (
        jnp.zeros((group_blocks, BLOCK, D), jnp.float32)
        .at[flat_paths]
        .add(g_value_rows.reshape(blocks_dev * DEPTH, BLOCK, D))
    )
    g_key_n, g_values = (
        lax.psum_scatter(
            g_key_group.reshape(group_blocks * BLOCK, D).astype(jnp.bfloat16),
            "fsdp",
            scatter_dimension=0,
            tiled=True,
        ).astype(jnp.float32),
        lax.psum_scatter(
            g_value_group.reshape(group_blocks * BLOCK, D).astype(jnp.bfloat16),
            "fsdp",
            scatter_dimension=0,
            tiled=True,
        ).astype(jnp.float32),
    )
    g_query_raw, scale_from_query = head_back(
        g_query_n.reshape(rows_dev, D), query_unit, query_inv, scale_qk
    )
    g_key_raw, scale_from_key = head_back(g_key_n, key_unit, key_inv, scale_qk)
    grad_qk_scale = scale_from_query + scale_from_key
    g_qkv = jnp.concatenate(
        (
            g_query_raw.astype(jnp.bfloat16),
            g_key_raw.astype(jnp.bfloat16),
            g_values.astype(jnp.bfloat16),
        ),
        axis=1,
    )
    g_states = g_states + jnp.einsum(
        "tc,dc->td",
        g_qkv,
        lax.all_gather(qkv_local, ("dp", "fsdp"), axis=0, tiled=True),
        preferred_element_type=jnp.float32,
    )
    vector_terms = jnp.stack((grad_qk_scale, g_rate_attn, g_rate_mlp), axis=1)
    lefts = states
    main = jnp.einsum("td,tc->dc", lefts, g_qkv, preferred_element_type=jnp.float32)
    outer = jnp.einsum("td,tc->dc", mixed, g_attn, preferred_element_type=jnp.float32)
    attn_share = lax.psum_scatter(
        jnp.concatenate((main, outer, vector_terms), axis=1),
        ("dp", "fsdp"),
        scatter_dimension=0,
        tiled=True,
    )
    return (
        result.astype(jnp.bfloat16),
        loss,
        g_states,
        attn_share[:, :D],
        attn_share[:, D : 2 * D],
        attn_share[:, 2 * D : 3 * D],
        attn_share[:, 3 * D : 4 * D],
        ffn_share[:, :FF],
        ffn_share[:, FF : 2 * FF],
        grad_down,
        attn_share[:, 4 * D],
        attn_share[:, 4 * D + 1],
        attn_share[:, 4 * D + 2],
        ffn_share[:, 2 * FF : 2 * FF + 4].reshape(-1),
        ffn_share[:, 2 * FF + 4 : 2 * FF + 8].reshape(-1),
    )

TRUNK = 8
NB = 20
TOK = NB * BLOCK
F32 = jnp.float32
BF = jnp.bfloat16


def head_norm(raw):
    inv = lax.rsqrt(jnp.sum(raw * raw, axis=0, keepdims=True) + EPS)
    return raw * inv, inv

def tri(size):
    key = lax.broadcasted_iota(jnp.int32, (size, size), 0)
    query = lax.broadcasted_iota(jnp.int32, (size, size), 1)
    return key, query

def chunks():
    out = []
    for j in range(TRUNK // 2):
        parts = [(0, 256 * j, "all")] if j else []
        out.append((256 * j, parts + [(256 * j, 256, "causal")]))
    for j in range(2):
        start = TRUNK * BLOCK + 256 * j
        out.append((start, [(0, 1024, "all"), (start, 256, "pair")]))
    for j in range(4):
        start = (TRUNK + 4) * BLOCK + 256 * j
        out.append((start, [(0, 1024, "all"), ((TRUNK + j) * BLOCK, 128, "all"), (start, 256, "pair")]))
    return out

def masked(kind, value):
    if kind == "all":
        return value
    key, query = tri(256)
    keep = key <= query
    if kind == "pair":
        keep = keep & ((key < 128) == (query < 128))
    return jnp.where(keep, value, jnp.zeros_like(value))

def nn(a, b):
    return lax.dot_general(a, b, (((1,), (0,)), ((), ())), preferred_element_type=F32)

def fwd_kernel(perm_ref, qkv_ref, scale_ref, mixed_ref, sum_ref, qs, ks, vs):
    scale = scale_ref[0]
    for i in range(NB):
        lanes = pl.ds(pl.multiple_of(perm_ref[i] * BLOCK, BLOCK), BLOCK)
        here = slice(i * BLOCK, (i + 1) * BLOCK)
        q_unit, _ = head_norm(qkv_ref[0, :, lanes])
        k_unit, _ = head_norm(qkv_ref[1, :, lanes])
        qs[:, here] = (q_unit * scale).astype(BF) * BF(8.0)
        ks[here, :] = (k_unit * scale).astype(BF).T
        vs[0:64, here] = qkv_ref[2, :, lanes].astype(BF)
    vs[64:80, :] = jnp.ones((16, TOK), BF)
    for start, parts in chunks():
        query = qs[:, start:start + 256]
        acc = jnp.zeros((80, 256), F32)
        for kstart, count, kind in parts:
            scores = nn(ks[kstart:kstart + count, :], query)
            powers = masked(kind, jnp.exp(scores)).astype(BF)
            acc = acc + nn(vs[:, kstart:kstart + count], powers)
        total = acc[64:65, :]
        result = (acc[0:64, :] / total).astype(BF)
        for half in range(2):
            lanes = pl.ds(pl.multiple_of(perm_ref[start // BLOCK + half] * BLOCK, BLOCK), BLOCK)
            cut = slice(half * BLOCK, (half + 1) * BLOCK)
            mixed_ref[:, lanes] = result[:, cut]
            sum_ref[0, :, lanes] = jnp.broadcast_to(1.0 / total[:, cut], (8, BLOCK))

def attn_fwd(perm, qkv, scale):
    heads = qkv.shape[1] // HEAD_DIM
    return pl.pallas_call(
        fwd_kernel,
        grid_spec=pltpu.PrefetchScalarGridSpec(
            num_scalar_prefetch=1,
            grid=(heads,),
            in_specs=[
                pl.BlockSpec((3, HEAD_DIM, TOK), lambda h, p: (0, h, 0)),
                pl.BlockSpec((1, HEAD_DIM, 1), lambda h, p: (h, 0, 0)),
            ],
            out_specs=[
                pl.BlockSpec((HEAD_DIM, TOK), lambda h, p: (h, 0)),
                pl.BlockSpec((1, 8, TOK), lambda h, p: (h, 0, 0)),
            ],
            scratch_shapes=[
                pltpu.VMEM((HEAD_DIM, TOK), BF),
                pltpu.VMEM((TOK, HEAD_DIM), BF),
                pltpu.VMEM((80, TOK), BF),
            ],
        ),
        out_shape=[
            jax.ShapeDtypeStruct((heads * HEAD_DIM, TOK), BF),
            jax.ShapeDtypeStruct((heads, 8, TOK), F32),
        ],
        compiler_params=pltpu.CompilerParams(vmem_limit_bytes=48 << 20),
        name="tree_attention",
        cost_estimate=pl.CostEstimate(flops=heads * 2 * 2 * 64 * 256 * 10752, bytes_accessed=12 << 20, transcendentals=heads * 256 * 10752),
    )(perm, qkv, scale)

def bwd_kernel(perm_ref, qkv_ref, scale_ref, sum_ref, mixed_ref, g_ref, out_ref, gscale_ref,
               qT, q, k, kT, v, gT, g, dq, dk, dv, delta, inv):
    scale = scale_ref[0]
    for i in range(NB):
        lanes = pl.ds(pl.multiple_of(perm_ref[i] * BLOCK, BLOCK), BLOCK)
        here = slice(i * BLOCK, (i + 1) * BLOCK)
        q_unit, _ = head_norm(qkv_ref[0, :, lanes])
        k_unit, _ = head_norm(qkv_ref[1, :, lanes])
        q8 = (q_unit * scale).astype(BF) * BF(8.0)
        qT[:, here] = q8
        q[here, :] = q8.T
        kn = (k_unit * scale).astype(BF)
        kT[:, here] = kn
        k[here, :] = kn.T
        v[here, :] = qkv_ref[2, :, lanes].astype(BF).T
        gh = g_ref[:, lanes]
        gT[:, here] = gh
        g[here, :] = gh.T
        delta[:, here] = jnp.sum(gh.astype(F32) * mixed_ref[:, lanes].astype(F32), axis=0, keepdims=True)
        inv[:, here] = sum_ref[0, 0:1, lanes]
    dk[...] = jnp.zeros_like(dk)
    dv[...] = jnp.zeros_like(dv)
    for start, parts in chunks():
        span = slice(start, start + 256)
        query, grad = qT[:, span], gT[:, span]
        query_rows, grad_rows = q[span, :], g[span, :]
        scale_row, delta_row = inv[:, span], delta[:, span]
        acc = jnp.zeros((64, 256), F32)
        for kstart, count, kind in parts:
            keys = slice(kstart, kstart + count)
            probs = masked(kind, jnp.exp(nn(k[keys, :], query)) * scale_row)
            g_probs = nn(v[keys, :], grad)
            g_scores = (probs * (g_probs - delta_row)).astype(BF)
            dv[keys, :] += nn(probs.astype(BF), grad_rows)
            dk[keys, :] += nn(g_scores, query_rows)
            acc = acc + nn(kT[:, keys], g_scores)
        dq[:, span] = acc * 8.0
    g_scale = jnp.zeros((64, BLOCK), F32)
    for i in range(NB):
        lanes = pl.ds(pl.multiple_of(perm_ref[i] * BLOCK, BLOCK), BLOCK)
        here = slice(i * BLOCK, (i + 1) * BLOCK)
        for which, grad in ((0, dq[:, here]), (1, dk[here, :].T)):
            unit, inverse = head_norm(qkv_ref[which, :, lanes])
            g_scale = g_scale + grad * unit
            scaled = grad * scale
            raw = (scaled - unit * jnp.sum(scaled * unit, axis=0, keepdims=True)) * inverse
            out_ref[which, :, lanes] = raw.astype(BF)
        out_ref[2, :, lanes] = dv[here, :].T.astype(BF)
    gscale_ref[0] = jnp.sum(g_scale, axis=1, keepdims=True)

def attn_bwd(perm, qkv, scale, sums, mixed, g_mixed):
    heads = qkv.shape[1] // HEAD_DIM
    row = lambda h, p: (h, 0)
    return pl.pallas_call(
        bwd_kernel,
        grid_spec=pltpu.PrefetchScalarGridSpec(
            num_scalar_prefetch=1,
            grid=(heads,),
            in_specs=[
                pl.BlockSpec((3, HEAD_DIM, TOK), lambda h, p: (0, h, 0)),
                pl.BlockSpec((1, HEAD_DIM, 1), lambda h, p: (h, 0, 0)),
                pl.BlockSpec((1, 8, TOK), lambda h, p: (h, 0, 0)),
                pl.BlockSpec((HEAD_DIM, TOK), row),
                pl.BlockSpec((HEAD_DIM, TOK), row),
            ],
            out_specs=[
                pl.BlockSpec((3, HEAD_DIM, TOK), lambda h, p: (0, h, 0)),
                pl.BlockSpec((1, HEAD_DIM, 1), lambda h, p: (h, 0, 0)),
            ],
            scratch_shapes=[
                pltpu.VMEM((HEAD_DIM, TOK), BF),
                pltpu.VMEM((TOK, HEAD_DIM), BF),
                pltpu.VMEM((TOK, HEAD_DIM), BF),
                pltpu.VMEM((HEAD_DIM, TOK), BF),
                pltpu.VMEM((TOK, HEAD_DIM), BF),
                pltpu.VMEM((HEAD_DIM, TOK), BF),
                pltpu.VMEM((TOK, HEAD_DIM), BF),
                pltpu.VMEM((HEAD_DIM, TOK), F32),
                pltpu.VMEM((TOK, HEAD_DIM), F32),
                pltpu.VMEM((TOK, HEAD_DIM), F32),
                pltpu.VMEM((1, TOK), F32),
                pltpu.VMEM((1, TOK), F32),
            ],
        ),
        out_shape=[
            jax.ShapeDtypeStruct((3, heads * HEAD_DIM, TOK), BF),
            jax.ShapeDtypeStruct((heads, HEAD_DIM, 1), F32),
        ],
        compiler_params=pltpu.CompilerParams(vmem_limit_bytes=48 << 20),
        name="tree_attention_grad",
        cost_estimate=pl.CostEstimate(flops=heads * 5 * 2 * 64 * 256 * 10752, bytes_accessed=20 << 20, transcendentals=heads * 256 * 10752),
    )(perm, qkv, scale, sums, mixed, g_mixed)


MESH = pl.DeviceIdType.MESH


def ring_place():
    dp = lax.axis_index("dp")
    z, y = dp // 2, dp % 2
    return z + y * (7 - 2 * z)


def ring_dp(place):
    place = (place + 16) % 8
    y = place // 4
    return 2 * (place + y * (7 - 2 * place)) + y


def greet(peers):
    barrier = pltpu.get_barrier_semaphore()
    for peer in peers:
        pl.semaphore_signal(barrier, inc=1, device_id=peer, device_id_type=MESH)
    pl.semaphore_wait(barrier, len(peers))


def group_peers():
    me = lax.axis_index("fsdp")
    core = 1 - 2 * (me % 2)
    chip = 2 - 4 * (me // 2)
    return {"fsdp": me + core}, {"fsdp": me + chip}, {"fsdp": me + core + chip}


def send(src, dst, send_sem, recv_sem, peer):
    return pltpu.make_async_remote_copy(
        src_ref=src, dst_ref=dst, send_sem=send_sem, recv_sem=recv_sem, device_id=peer, device_id_type=MESH
    )


def first_kernel(states, qkv_send, extra, out_piece, tokens, weights, out_w, own_sem, tok_send, tok_recv,
                 a2a_send, a2a_recv, ring_send, ring_recv):
    me, dp = lax.axis_index("fsdp"), lax.axis_index("dp")
    place = ring_place()
    sibling, across, corner = group_peers()
    right, left = {"dp": ring_dp(place + 1)}, {"dp": ring_dp(place - 1)}
    greet([sibling, across, corner, right, left])
    rows = states.shape[0] // 2
    halves = [pl.ds(0, rows), pl.ds(rows, rows)]

    exchange = []
    for i, peer in enumerate((sibling, across, corner)):
        copy = send(qkv_send.at[peer["fsdp"]], weights.at[dp, me], a2a_send.at[i], a2a_recv.at[i], peer)
        copy.start()
        exchange.append(copy)
    far = []
    for i, half in enumerate(halves):
        copy = send(states.at[half], tokens.at[2, half], tok_send.at[i], tok_recv.at[i], across)
        copy.start()
        far.append(copy)
    near = send(states, tokens.at[1], tok_send.at[2], tok_recv.at[2], sibling)
    near.start()
    own = pltpu.make_async_copy(states, tokens.at[0], own_sem.at[0])
    own.start()
    weights[dp, me] = qkv_send[me]
    out_w[dp] = out_piece[...]
    for copy in exchange:
        copy.wait()
    lanes = pl.ds(weights.shape[3] - 128, 128)
    weights[dp, :, :, lanes] = weights[dp, :, :, lanes] + extra[...]

    def hop(step, carry):
        to_right, to_left = ring_dp(place - step), ring_dp(place + step)
        copies = [
            send(weights.at[to_right, pl.ds(0, 2)], weights.at[to_right, pl.ds(0, 2)],
                 ring_send.at[0, step], ring_recv.at[0, step], right),
            send(weights.at[to_left, pl.ds(2, 2)], weights.at[to_left, pl.ds(2, 2)],
                 ring_send.at[1, step], ring_recv.at[1, step], left),
            send(out_w.at[to_right, :, pl.ds(0, 640)], out_w.at[to_right, :, pl.ds(0, 640)],
                 ring_send.at[2, step], ring_recv.at[2, step], right),
            send(out_w.at[to_left, :, pl.ds(640, 640)], out_w.at[to_left, :, pl.ds(640, 640)],
                 ring_send.at[3, step], ring_recv.at[3, step], left),
        ]
        for copy in copies:
            copy.start()
        for copy in copies:
            copy.wait()
        return carry

    lax.fori_loop(0, 4, hop, 0)
    passed = []
    for i, half in enumerate(halves):
        far[i].wait()
        copy = send(tokens.at[2, half], tokens.at[3, half], tok_send.at[3 + i], tok_recv.at[3 + i], sibling)
        copy.start()
        passed.append(copy)
    lax.fori_loop(4, 7, hop, 0)
    near.wait()
    own.wait()
    for copy in passed:
        copy.wait()


def first_exchange(states, qkv_send, extra, out_piece):
    tps, rows_w, width = qkv_send.shape
    vmem, hbm = pl.BlockSpec(memory_space=pltpu.VMEM), pl.BlockSpec(memory_space=pl.ANY)
    return pl.pallas_call(
        first_kernel,
        in_specs=[hbm, vmem, vmem, vmem],
        out_specs=[hbm, vmem, vmem],
        out_shape=[
            jax.ShapeDtypeStruct((4,) + states.shape, BF),
            jax.ShapeDtypeStruct((8, tps, rows_w, width), BF),
            jax.ShapeDtypeStruct((8,) + out_piece.shape, BF),
        ],
        scratch_shapes=[
            pltpu.SemaphoreType.DMA((1,)),
            pltpu.SemaphoreType.DMA((5,)),
            pltpu.SemaphoreType.DMA((5,)),
            pltpu.SemaphoreType.DMA((3,)),
            pltpu.SemaphoreType.DMA((3,)),
            pltpu.SemaphoreType.DMA((4, 7)),
            pltpu.SemaphoreType.DMA((4, 7)),
        ],
        compiler_params=pltpu.CompilerParams(
            collective_id=1, has_side_effects=True, vmem_limit_bytes=32 << 20
        ),
        cost_estimate=pl.CostEstimate(flops=0, bytes_accessed=150 << 20, transcendentals=0),
        name="first_exchange",
    )(states, qkv_send, extra, out_piece)


def last_kernel(share, base, grads, down, vectors, g_states, qkv_rows, out_rows, down_rows, vec_own,
                core_buf, far_buf, x_buf, ring_buf, vec_buf, row_buf, vec_part, vec_in,
                core_send, core_recv, x_send, x_recv, ring_send, ring_recv, a2a_send, a2a_recv):
    me, dp = lax.axis_index("fsdp"), lax.axis_index("dp")
    place = ring_place()
    sibling, across, corner = group_peers()
    right, left = {"dp": ring_dp(place + 1)}, {"dp": ring_dp(place - 1)}
    greet([sibling, across, corner, right, left])
    rows = share.shape[1] // 4

    def first_hop():
        to_right, to_left = ring_dp(place - 1), ring_dp(place + 1)
        return [
            send(grads.at[to_right], ring_buf.at[0, 0], ring_send.at[0, 0], ring_recv.at[0, 0], right),
            send(down.at[to_left], ring_buf.at[1, 0], ring_send.at[1, 0], ring_recv.at[1, 0], left),
            send(vectors.at[to_right], vec_buf.at[0], ring_send.at[2, 0], ring_recv.at[2, 0], right),
        ]

    def later_hop(step):
        return [
            send(ring_buf.at[0, step - 1], ring_buf.at[0, step], ring_send.at[0, step], ring_recv.at[0, step], right),
            send(ring_buf.at[1, step - 1], ring_buf.at[1, step], ring_send.at[1, step], ring_recv.at[1, step], left),
            send(vec_buf.at[step - 1], vec_buf.at[step], ring_send.at[2, step], ring_recv.at[2, step], right),
        ]

    core = [
        send(share.at[3], core_buf.at[0], core_send.at[0], core_recv.at[0], sibling),
        send(share.at[1], core_buf.at[1], core_send.at[1], core_recv.at[1], sibling),
    ]
    core[0].start()
    opening = first_hop()
    for copy in opening:
        copy.start()
    core[1].start()
    core[0].wait()
    far = []
    for i in range(4):
        span = pl.ds(i * rows, rows)
        far_buf[span] = (share[2, span].astype(F32) + core_buf[0, span].astype(F32)).astype(BF)
        copy = send(far_buf.at[span], x_buf.at[span], x_send.at[i], x_recv.at[i], across)
        copy.start()
        far.append(copy)
    for copy in opening:
        copy.wait()

    def hop(step, carry):
        to_right, to_left = ring_dp(place - 1 - step), ring_dp(place + 1 + step)
        ring_buf[0, step - 1] = (
            ring_buf[0, step - 1].astype(F32) + grads[to_right].astype(F32)
        ).astype(BF)
        ring_buf[1, step - 1] = (
            ring_buf[1, step - 1].astype(F32) + down[to_left].astype(F32)
        ).astype(BF)
        vec_buf[step - 1] = vec_buf[step - 1] + vectors[to_right]
        copies = later_hop(step)
        for copy in copies:
            copy.start()
        for copy in copies:
            copy.wait()
        return carry

    lax.fori_loop(1, 7, hop, 0)
    total = ring_buf[0, 6].astype(F32) + grads[dp].astype(F32)
    quarter = total.shape[0] // 4
    for i in range(4):
        piece = total[i * quarter : (i + 1) * quarter]
        row_buf[i] = piece.astype(BF)
        out_rows[i] = piece
    down_rows[...] = ring_buf[1, 6].astype(F32) + down[dp].astype(F32)
    vec_part[...] = vec_buf[6] + vectors[dp]
    exchange = []
    for i, peer in enumerate((sibling, across, corner)):
        to = peer["fsdp"]
        copies = [
            send(row_buf.at[to], qkv_rows.at[me], a2a_send.at[i], a2a_recv.at[i], peer),
            send(vec_part.at[to], vec_in.at[me], a2a_send.at[3 + i], a2a_recv.at[3 + i], peer),
        ]
        for copy in copies:
            copy.start()
        exchange += copies
    qkv_rows[me] = row_buf[me]
    vec_in[me] = vec_part[me]
    core[1].wait()
    for i in range(4):
        span = pl.ds(i * rows, rows)
        far[i].wait()
        g_states[span] = base[span] + (
            share[0, span].astype(F32) + core_buf[1, span].astype(F32) + x_buf[span].astype(F32)
        )
    for copy in exchange:
        copy.wait()
    vec_own[...] = vec_in[0] + vec_in[1] + vec_in[2] + vec_in[3]


def last_exchange(share, base, grads, down, vectors):
    cols = grads.shape[2]
    rows_w = grads.shape[1] // 4
    vmem = pl.BlockSpec(memory_space=pltpu.VMEM)
    return pl.pallas_call(
        last_kernel,
        in_specs=[vmem] * 5,
        out_specs=[vmem] * 5,
        out_shape=[
            jax.ShapeDtypeStruct(base.shape, F32),
            jax.ShapeDtypeStruct((4, rows_w, cols), BF),
            jax.ShapeDtypeStruct((4, rows_w, cols), F32),
            jax.ShapeDtypeStruct(down.shape[1:], F32),
            jax.ShapeDtypeStruct(vectors.shape[2:], F32),
        ],
        scratch_shapes=[
            pltpu.VMEM((2,) + share.shape[1:], BF),
            pltpu.VMEM(share.shape[1:], BF),
            pltpu.VMEM(share.shape[1:], BF),
            pltpu.VMEM((2, 7) + grads.shape[1:], BF),
            pltpu.VMEM((7,) + vectors.shape[1:], F32),
            pltpu.VMEM((4, rows_w, cols), BF),
            pltpu.VMEM(vectors.shape[1:], F32),
            pltpu.VMEM(vectors.shape[1:], F32),
            pltpu.SemaphoreType.DMA((2,)),
            pltpu.SemaphoreType.DMA((2,)),
            pltpu.SemaphoreType.DMA((4,)),
            pltpu.SemaphoreType.DMA((4,)),
            pltpu.SemaphoreType.DMA((3, 7)),
            pltpu.SemaphoreType.DMA((3, 7)),
            pltpu.SemaphoreType.DMA((6,)),
            pltpu.SemaphoreType.DMA((6,)),
        ],
        compiler_params=pltpu.CompilerParams(
            collective_id=2, has_side_effects=True, vmem_limit_bytes=52 << 20
        ),
        cost_estimate=pl.CostEstimate(flops=0, bytes_accessed=150 << 20, transcendentals=0),
        name="last_exchange",
    )(share, base, grads, down, vectors)


CHUNK = 128
TILE = 256


def tile(index, base=0):
    return pl.ds(pl.multiple_of(base + index * TILE, TILE), TILE)


def nt(a, b):
    return lax.dot_general(a, b, (((1,), (1,)), ((), ())), preferred_element_type=F32)


def middle_kernel(share, states, teacher, weight, mask, w_all, rates, scales,
                  out_states, hidden, attn_unit, back, attn_inv, hidden_inv, sums, gd_all, ht_all, act_all, ug_all,
                  part, core, x_buf, tok, gd, act, ug, ht,
                  ld_sem, core_send, core_recv, x_send, x_recv, tok_send, tok_recv, gd_send, gd_recv, gd_own,
                  out_sem):
    sibling, across, _ = group_peers()
    count = part.shape[0]
    width = hidden.shape[1]
    rate_attn, rate_mlp = rates[0:1], rates[1:2]

    def rows(i):
        return pl.ds(pl.multiple_of(i * CHUNK, CHUNK), CHUNK)

    def load(i):
        return pltpu.make_async_copy(share.at[:, rows(i)], part.at[i], ld_sem.at[i])

    def core_a(stage, i):
        return send(part.at[i, 3], core.at[0, i], core_send.at[stage, 0, i], core_recv.at[stage, 0, i], sibling)

    def core_b(stage, i):
        return send(part.at[i, 1], core.at[1, i], core_send.at[stage, 1, i], core_recv.at[stage, 1, i], sibling)

    def chip(stage, i):
        return send(part.at[i, 2], x_buf.at[i], x_send.at[stage, i], x_recv.at[stage, i], across)

    def spread(buf, own, sems, recvs, i):
        return [
            send(own, buf.at[i, 1], sems.at[0, i], recvs.at[0, i], sibling),
            send(own, buf.at[i, 2], sems.at[1, i], recvs.at[1, i], across),
            send(buf.at[i, 2], buf.at[i, 3], sems.at[2, i], recvs.at[2, i], sibling),
        ]

    def tok_copies(i):
        return spread(tok, tok.at[i, 0], tok_send, tok_recv, i)

    def gd_copies(i):
        return spread(gd_all, gd.at[i], gd_send, gd_recv, i)

    def gd_local(i):
        return pltpu.make_async_copy(gd.at[i], gd_all.at[i, 0], gd_own.at[i])

    def outs(i):
        slot = i % 2
        return [
            pltpu.make_async_copy(ht.at[slot], ht_all.at[i], out_sem.at[0, slot]),
            pltpu.make_async_copy(act.at[slot], act_all.at[i], out_sem.at[1, slot]),
            pltpu.make_async_copy(ug.at[slot], ug_all.at[i], out_sem.at[2, slot]),
        ]

    def forward_far(stage, i):
        core_a(stage, i).wait_recv()
        part[i, 2] = (part[i, 2].astype(F32) + core[0, i].astype(F32)).astype(BF)
        chip(stage, i).start()

    def reduced(stage, i):
        core_b(stage, i).wait_recv()
        chip(stage, i).wait_recv()
        total = part[i, 0].astype(F32) + core[1, i].astype(F32) + x_buf[i].astype(F32)
        core_a(stage, i).wait_send()
        core_b(stage, i).wait_send()
        chip(stage, i).wait_send()
        return total

    sums[...] = jnp.zeros_like(sums)
    lax.fori_loop(0, count, lambda i, c: (load(i).start(), c)[1], 0)
    greet([sibling, across])

    def open_core(i, carry):
        load(i).wait()
        core_a(0, i).start()
        core_b(0, i).start()
        return carry

    lax.fori_loop(0, count, open_core, 0)
    lax.fori_loop(0, count, lambda i, c: (forward_far(0, i), c)[1], 0)

    def norm_hidden(i):
        unit, inverse = unit_rows(reduced(0, i))
        own = states[rows(i)].astype(F32)
        value, value_inv = unit_rows(own + rate_attn * (unit - own))
        hidden[rows(i)] = value
        attn_unit[rows(i)] = unit.astype(BF)
        attn_inv[rows(i)] = inverse
        hidden_inv[rows(i)] = value_inv
        tok[i, 0] = value.astype(BF)
        copies = tok_copies(i)
        copies[0].start()
        copies[1].start()

    def pass_tokens(i):
        copies = tok_copies(i)
        copies[1].wait_recv()
        copies[2].start()

    def feed(i):
        copies = tok_copies(i)
        copies[0].wait()
        copies[1].wait_send()
        copies[2].wait()
        slot = i % 2

        @pl.when(i >= 2)
        def _():
            for copy in outs(i - 2):
                copy.wait()

        def up(n, carry):
            here = tok[i].reshape(4 * CHUNK, width)
            up_proj = nn(here, w_all[:, tile(n)])
            gate_proj = nn(here, w_all[:, tile(n, width)])
            gated = gate_proj * scales[1:2, tile(n)]
            value = up_proj * scales[0:1, tile(n)] * (gated * jax.nn.sigmoid(gated))
            act[slot, :, tile(n)] = value.astype(BF)
            ug[slot, :, tile(n)] = up_proj.astype(BF)
            ug[slot, :, tile(n, width)] = gate_proj.astype(BF)
            return carry

        lax.fori_loop(0, width // TILE, up, 0)

        def down(n, carry):
            value = nn(act[slot], w_all[:, tile(n, 2 * width)])
            part[i, :, :, tile(n)] = value.astype(BF).reshape(4, CHUNK, TILE)
            ht[slot, tile(n)] = tok[i, :, :, tile(n)].reshape(4 * CHUNK, TILE).T
            return carry

        lax.fori_loop(0, width // TILE, down, 0)
        core_a(1, i).start()
        core_b(1, i).start()
        for copy in outs(i):
            copy.start()
        forward_far(1, i)

    def finish(i):
        unit, inverse = unit_rows(reduced(1, i))
        own = hidden[rows(i)]
        result, result_inv = unit_rows(own + rate_mlp * (unit - own))
        out_states[rows(i)] = result.astype(BF)
        diff = result - teacher[rows(i)]
        sums[1:2] = sums[1:2] + jnp.sum(mask[rows(i)] * (diff * diff), axis=0, keepdims=True)
        g_last = unit_back(weight[rows(i)] * diff, result, result_inv)
        sums[0:1] = sums[0:1] + jnp.sum(g_last * (unit - own), axis=0, keepdims=True)
        back[rows(i)] = g_last * (1.0 - rate_mlp)
        gd[i] = unit_back(g_last * rate_mlp, unit, inverse).astype(BF)
        copies = gd_copies(i)
        copies[0].start()
        copies[1].start()
        gd_local(i).start()

    def pass_grads(i):
        copies = gd_copies(i)
        copies[1].wait_recv()
        copies[2].start()

    stages = (norm_hidden, pass_tokens, feed, finish, pass_grads)

    def step(t, carry):
        for lag, stage in enumerate(stages):
            pl.when((t >= lag) & (t < lag + count))(functools.partial(stage, t - lag))
        return carry

    lax.fori_loop(0, count + len(stages) - 1, step, 0)

    def close(i, carry):
        copies = gd_copies(i)
        copies[0].wait()
        copies[1].wait_send()
        copies[2].wait()
        gd_local(i).wait()
        return carry

    lax.fori_loop(0, count, close, 0)
    for i in (count - 2, count - 1):
        for copy in outs(i):
            copy.wait()


def middle(share, states, teacher, weight, mask, w_all, rates, scales):
    rows, width = states.shape
    count = rows // CHUNK
    vmem, hbm = pl.BlockSpec(memory_space=pltpu.VMEM), pl.BlockSpec(memory_space=pl.ANY)
    dma = pltpu.SemaphoreType.DMA
    return pl.pallas_call(
        middle_kernel,
        in_specs=[hbm] + [vmem] * 7,
        out_specs=[vmem] * 7 + [hbm] * 4,
        out_shape=[
            jax.ShapeDtypeStruct((rows, width), BF),
            jax.ShapeDtypeStruct((rows, width), F32),
            jax.ShapeDtypeStruct((rows, width), BF),
            jax.ShapeDtypeStruct((rows, width), F32),
            jax.ShapeDtypeStruct((rows, 1), F32),
            jax.ShapeDtypeStruct((rows, 1), F32),
            jax.ShapeDtypeStruct((2, width), F32),
            jax.ShapeDtypeStruct((count, 4, CHUNK, width), BF),
            jax.ShapeDtypeStruct((count, width, 4 * CHUNK), BF),
            jax.ShapeDtypeStruct((count, 4 * CHUNK, width), BF),
            jax.ShapeDtypeStruct((count, 4 * CHUNK, 2 * width), BF),
        ],
        scratch_shapes=[
            pltpu.VMEM((count, 4, CHUNK, width), BF),
            pltpu.VMEM((2, count, CHUNK, width), BF),
            pltpu.VMEM((count, CHUNK, width), BF),
            pltpu.VMEM((count, 4, CHUNK, width), BF),
            pltpu.VMEM((count, CHUNK, width), BF),
            pltpu.VMEM((2, 4 * CHUNK, width), BF),
            pltpu.VMEM((2, 4 * CHUNK, 2 * width), BF),
            pltpu.VMEM((2, width, 4 * CHUNK), BF),
            dma((count,)),
            dma((2, 2, count)),
            dma((2, 2, count)),
            dma((2, count)),
            dma((2, count)),
            dma((3, count)),
            dma((3, count)),
            dma((3, count)),
            dma((3, count)),
            dma((count,)),
            dma((3, 2)),
        ],
        compiler_params=pltpu.CompilerParams(
            collective_id=3, has_side_effects=True, vmem_limit_bytes=60 << 20
        ),
        cost_estimate=pl.CostEstimate(flops=26 * 10**9, bytes_accessed=400 << 20, transcendentals=4 << 20),
        name="middle",
    )(share, states, teacher, weight, mask, w_all, rates, scales)


def middle_back_kernel(gd_all, ht_all, ug_all, hidden, attn_unit, states, back, attn_inv, hidden_inv, w_all, rates,
                       scales, base, ga_all, grad_ug, sums, ff_sums,
                       part, core, x_buf, ga, gd, ht, ug, gug, acc, stage_buf, own_f, own_b, base_buf,
                       in_sem, own_sem, core_send, core_recv, x_send, x_recv, ga_send, ga_recv, ga_own, base_sem,
                       out_sem):
    sibling, across, _ = group_peers()
    count = core.shape[1]
    width = w_all.shape[0]
    rate_attn = rates[0:1]

    def rows(i):
        return pl.ds(pl.multiple_of(i * CHUNK, CHUNK), CHUNK)

    def stream(i):
        slot = i % 2
        return [
            pltpu.make_async_copy(gd_all.at[i], gd.at[slot], in_sem.at[0, slot]),
            pltpu.make_async_copy(ht_all.at[i], ht.at[slot], in_sem.at[1, slot]),
            pltpu.make_async_copy(ug_all.at[i], ug.at[slot], in_sem.at[2, slot]),
        ]

    def own_rows(i):
        return [
            pltpu.make_async_copy(hidden.at[rows(i)], own_f.at[0], own_sem.at[0]),
            pltpu.make_async_copy(back.at[rows(i)], own_f.at[1], own_sem.at[1]),
            pltpu.make_async_copy(attn_unit.at[rows(i)], own_b.at[0], own_sem.at[2]),
            pltpu.make_async_copy(states.at[rows(i)], own_b.at[1], own_sem.at[3]),
        ]

    def core_a(i):
        return send(part.at[i % 3, 3], core.at[0, i], core_send.at[0, i], core_recv.at[0, i], sibling)

    def core_b(i):
        return send(part.at[i % 3, 1], core.at[1, i], core_send.at[1, i], core_recv.at[1, i], sibling)

    def chip(i):
        return send(part.at[i % 3, 2], x_buf.at[i], x_send.at[i], x_recv.at[i], across)

    def ga_copies(i):
        return [
            send(ga.at[i], ga_all.at[1, rows(i)], ga_send.at[0, i], ga_recv.at[0, i], sibling),
            send(ga.at[i], ga_all.at[2, rows(i)], ga_send.at[1, i], ga_recv.at[1, i], across),
            send(ga_all.at[2, rows(i)], ga_all.at[3, rows(i)], ga_send.at[2, i], ga_recv.at[2, i], sibling),
        ]

    def ga_local(i):
        return pltpu.make_async_copy(ga.at[i], ga_all.at[0, rows(i)], ga_own.at[i])

    def base_copy(i):
        return pltpu.make_async_copy(base_buf.at[i % 2], base.at[rows(i)], base_sem.at[i % 2])

    for copy in stream(0) + own_rows(0):
        copy.start()
    sums[...] = jnp.zeros_like(sums)
    ff_sums[...] = jnp.zeros_like(ff_sums)
    acc[...] = jnp.zeros_like(acc)
    greet([sibling, across])

    def feed(i):
        slot = i % 2
        for copy in stream(i):
            copy.wait()

        @pl.when(i + 1 < count)
        def _():
            for copy in stream(i + 1):
                copy.start()

        def grads(n, carry):
            g_act = nt(gd[slot].reshape(4 * CHUNK, width), w_all[tile(n), pl.ds(2 * width, width)])
            up_proj = ug[slot, :, tile(n)].astype(F32)
            gate_proj = ug[slot, :, tile(n, width)].astype(F32)
            scale_up, scale_gate = scales[0:1, tile(n)], scales[1:2, tile(n)]
            gated = gate_proj * scale_gate
            sigmoid = jax.nn.sigmoid(gated)
            g_upscaled = g_act * (gated * sigmoid)
            g_gated = g_act * (up_proj * scale_up) * sigmoid * (1.0 + gated * (1.0 - sigmoid))
            ff_sums[0:1, tile(n)] = ff_sums[0:1, tile(n)] + jnp.sum(g_upscaled * up_proj, axis=0, keepdims=True)
            ff_sums[1:2, tile(n)] = ff_sums[1:2, tile(n)] + jnp.sum(g_gated * gate_proj, axis=0, keepdims=True)
            gug[:, tile(n)] = (g_upscaled * scale_up).astype(BF)
            gug[:, tile(n, width)] = (g_gated * scale_gate).astype(BF)
            return carry

        lax.fori_loop(0, width // TILE, grads, 0)

        def through(n, carry):
            value = nt(gug[...], w_all[tile(n), pl.ds(0, 2 * width)])
            part[i % 3, :, :, tile(n)] = value.astype(BF).reshape(4, CHUNK, TILE)
            return carry

        lax.fori_loop(0, width // TILE, through, 0)
        core_a(i).start()
        core_b(i).start()
        core_a(i).wait_recv()
        part[i % 3, 2] = (part[i % 3, 2].astype(F32) + core[0, i].astype(F32)).astype(BF)
        chip(i).start()

        def outer(n, carry):
            acc[:, tile(n)] = acc[:, tile(n)] + nn(ht[slot], gug[:, tile(n)])
            return carry

        lax.fori_loop(0, 2 * width // TILE, outer, 0)

    def finish(i):
        core_b(i).wait_recv()
        chip(i).wait_recv()
        through = part[i % 3, 0].astype(F32) + core[1, i].astype(F32) + x_buf[i].astype(F32)
        core_a(i).wait_send()
        core_b(i).wait_send()
        chip(i).wait_send()
        for copy in own_rows(i):
            copy.wait()
        value, unit, own = own_f[0], own_b[0].astype(F32), own_b[1].astype(F32)
        g_pre = unit_back(own_f[1] + through, value, hidden_inv[rows(i)])

        @pl.when(i + 1 < count)
        def _():
            for copy in own_rows(i + 1):
                copy.start()

        @pl.when(i >= 2)
        def _():
            base_copy(i - 2).wait()

        base_buf[i % 2] = g_pre * (1.0 - rate_attn)
        base_copy(i).start()
        sums[0:1] = sums[0:1] + jnp.sum(g_pre * (unit - own), axis=0, keepdims=True)
        ga[i] = unit_back(g_pre * rate_attn, unit, attn_inv[rows(i)]).astype(BF)
        copies = ga_copies(i)
        copies[0].start()
        copies[1].start()
        ga_local(i).start()

    def pass_grads(i):
        copies = ga_copies(i)
        copies[1].wait_recv()
        copies[2].start()

    stages = (feed, finish, pass_grads)

    def step(t, carry):
        for lag, stage in enumerate(stages):
            pl.when((t >= lag) & (t < lag + count))(functools.partial(stage, t - lag))
        return carry

    lax.fori_loop(0, count + len(stages) - 1, step, 0)

    def out_copy(n):
        return pltpu.make_async_copy(stage_buf.at[n % 2], grad_ug.at[tile(n)], out_sem.at[n % 2])

    def store(n, carry):
        @pl.when(n >= 2)
        def _():
            out_copy(n - 2).wait()

        stage_buf[n % 2] = acc[tile(n)].astype(BF)
        out_copy(n).start()
        return carry

    blocks = width // TILE
    lax.fori_loop(0, blocks, store, 0)

    def close(i, carry):
        copies = ga_copies(i)
        copies[0].wait()
        copies[1].wait_send()
        copies[2].wait()
        ga_local(i).wait()
        return carry

    lax.fori_loop(0, count, close, 0)
    for i in (count - 2, count - 1):
        base_copy(i).wait()
    for n in (blocks - 2, blocks - 1):
        out_copy(n).wait()


def middle_back(gd_all, ht_all, ug_all, hidden, attn_unit, states, back, attn_inv, hidden_inv, w_all, rates, scales):
    rows, width = states.shape
    count = rows // CHUNK
    vmem, hbm = pl.BlockSpec(memory_space=pltpu.VMEM), pl.BlockSpec(memory_space=pl.ANY)
    dma = pltpu.SemaphoreType.DMA
    return pl.pallas_call(
        middle_back_kernel,
        in_specs=[hbm] * 7 + [vmem] * 5,
        out_specs=[hbm, hbm, hbm, vmem, vmem],
        out_shape=[
            jax.ShapeDtypeStruct((rows, width), F32),
            jax.ShapeDtypeStruct((4, rows, width), BF),
            jax.ShapeDtypeStruct((width, 2 * width), BF),
            jax.ShapeDtypeStruct((1, width), F32),
            jax.ShapeDtypeStruct((2, width), F32),
        ],
        scratch_shapes=[
            pltpu.VMEM((3, 4, CHUNK, width), BF),
            pltpu.VMEM((2, count, CHUNK, width), BF),
            pltpu.VMEM((count, CHUNK, width), BF),
            pltpu.VMEM((count, CHUNK, width), BF),
            pltpu.VMEM((2, 4, CHUNK, width), BF),
            pltpu.VMEM((2, width, 4 * CHUNK), BF),
            pltpu.VMEM((2, 4 * CHUNK, 2 * width), BF),
            pltpu.VMEM((4 * CHUNK, 2 * width), BF),
            pltpu.VMEM((width, 2 * width), F32),
            pltpu.VMEM((2, TILE, 2 * width), BF),
            pltpu.VMEM((2, CHUNK, width), F32),
            pltpu.VMEM((2, CHUNK, width), BF),
            pltpu.VMEM((2, CHUNK, width), F32),
            dma((3, 2)),
            dma((4,)),
            dma((2, count)),
            dma((2, count)),
            dma((count,)),
            dma((count,)),
            dma((3, count)),
            dma((3, count)),
            dma((count,)),
            dma((2,)),
            dma((2,)),
        ],
        compiler_params=pltpu.CompilerParams(
            collective_id=4, has_side_effects=True, vmem_limit_bytes=60 << 20
        ),
        cost_estimate=pl.CostEstimate(flops=42 * 10**9, bytes_accessed=200 << 20, transcendentals=4 << 20),
        name="middle_back",
    )(gd_all, ht_all, ug_all, hidden, attn_unit, states, back, attn_inv, hidden_inv, w_all, rates, scales)


def order_kernel(where_ref, parent_ref, perm_ref, branch_ref, leaf_ref):
    base, me = where_ref[0], where_ref[1]

    def parent_of(block):
        return jnp.where(block >= 0, parent_ref[jnp.maximum(block, 0)] - base, -1)

    def depth_of(block):
        def climb(step, state):
            at, depth = state
            at = jnp.where(at >= 0, jnp.maximum(parent_of(at), -1), -1)
            return at, depth + (at >= 0).astype(jnp.int32)

        return lax.fori_loop(0, DEPTH - 1, climb, (block, jnp.int32(0)))[1]

    def relative(block):
        return jnp.bitwise_xor(block // 5, me) * 5 + block % 5

    def first(block, count):
        depth = depth_of(block)
        is_branch = depth == TRUNK
        branch_ref[block] = count
        leaf_ref[block] = 0

        @pl.when(depth <= TRUNK)
        def _():
            perm_ref[jnp.where(is_branch, TRUNK + count, depth)] = relative(block)

        return count + is_branch.astype(jnp.int32)

    lax.fori_loop(0, NB, first, jnp.int32(0))

    def second(block, carry):
        @pl.when(depth_of(block) > TRUNK)
        def _():
            parent = jnp.maximum(parent_of(block), 0)
            seen = leaf_ref[parent]
            perm_ref[TRUNK + 4 + 2 * branch_ref[parent] + seen] = relative(block)
            leaf_ref[parent] = seen + 1

        return carry

    lax.fori_loop(0, NB, second, jnp.int32(0))


def tree_order(where, parents):
    smem = pl.BlockSpec(memory_space=pltpu.SMEM)
    return pl.pallas_call(
        order_kernel,
        in_specs=[smem, smem],
        out_specs=smem,
        out_shape=jax.ShapeDtypeStruct((NB,), jnp.int32),
        scratch_shapes=[pltpu.SMEM((NB,), jnp.int32), pltpu.SMEM((NB,), jnp.int32)],
        name="tree_order",
    )(where, parents)


def dot(left, right, contract):
    return lax.dot_general(left, right, ((contract[:1], contract[1:]), ((), ())), preferred_element_type=F32)


def local(
    states,
    teacher,
    parent_ids,
    valid_mask,
    w_query,
    w_key,
    w_value,
    w_out,
    w_up,
    w_gate,
    w_down,
    qk_scale,
    attn_rate,
    mlp_rate,
    up_scale,
    gate_scale,
):
    both = ("dp", "fsdp")
    dps, tps = 8, 4
    rows_w = w_query.shape[0]
    cols = D // tps
    hid = FF // tps
    ff_rows = FF // (dps * tps)
    me = lax.axis_index("fsdp")
    root_width = math.sqrt(D)
    mask_f = valid_mask.astype(F32)
    group_base = lax.axis_index("dp") * NB
    perm = tree_order(jnp.stack((group_base, me)).astype(jnp.int32), parent_ids)

    count = jnp.sum(valid_mask)
    first_row = jnp.arange(rows_w, dtype=jnp.int32) == 0
    small = jnp.stack(
        (
            qk_scale,
            attn_rate,
            mlp_rate,
            jnp.where(first_row, count // 128, 0).astype(BF),
            jnp.where(first_row, count % 128, 0).astype(BF),
        ),
        axis=1,
    )
    small = jnp.pad(small, ((0, 0), (0, 59)))
    qkv_send = jnp.concatenate(
        [w.reshape(rows_w, tps, cols).transpose(1, 0, 2) for w in (w_query, w_key, w_value)]
        + [jnp.broadcast_to(small[None], (tps, rows_w, 64))],
        axis=2,
    )
    extra = jnp.pad(jnp.stack((up_scale, gate_scale), axis=1), ((0, 0), (69, 57))).reshape(tps, rows_w, 128)
    spread = [(j, tps * (j % dps) + j // dps) for j in range(dps * tps)]
    tokens, first, w_o = first_exchange(states, qkv_send, extra, lax.ppermute(w_out, both, spread))
    tokens = tokens.reshape(TOK, D)
    first = first.reshape(D, 1024)
    w_o = w_o.reshape(cols, D)
    ug_send = jnp.concatenate(
        [
            w.reshape(rows_w, dps, tps, ff_rows).transpose(2, 0, 1, 3).reshape(tps, rows_w, hid)
            for w in (w_up, w_gate)
        ],
        axis=2,
    )
    ug_group = lax.all_to_all(ug_send, "fsdp", 0, 0, tiled=True).reshape(tps * rows_w, 2 * hid)
    w_all = lax.all_gather(jnp.concatenate((ug_group, w_down), axis=1), "dp", axis=0, tiled=True)

    w_qkv = first[:, : 3 * cols]
    small_all = first[:, 3 * cols :].astype(F32)
    rate_attn = small_all[:, 1]
    rate_mlp = small_all[:, 2]
    valid_count = 128.0 * jnp.sum(small_all[:, 3]) + jnp.sum(small_all[:, 4])
    scale_up = small_all[:, 5]
    scale_gate = small_all[:, 6]
    scale_qk = lax.dynamic_slice_in_dim(small_all[:, 0], me * cols, cols).reshape(cols // HEAD_DIM, HEAD_DIM, 1)

    qkv = dot(w_qkv, tokens, (0, 1)).reshape(3, cols, TOK)
    mixed, sums = attn_fwd(perm, qkv, scale_qk)
    rates = jnp.stack((rate_attn, rate_mlp))
    scales = jnp.stack((scale_up, scale_gate * root_width))
    share = dot(mixed, w_o, (0, 0)).astype(BF).reshape(tps, TOK // tps, D)
    mask_col = mask_f[:, None]
    out_states, hidden, attn_unit, back, attn_inv, hidden_inv, sums_mid, gd_all, ht_all, act_all, ug_all = middle(
        share, states, teacher, mask_col * (2.0 / valid_count), mask_col, w_all, rates, scales
    )
    base, ga_all, part_ug, sums_back, ff_sums = middle_back(
        gd_all, ht_all, ug_all, hidden, attn_unit, states, back, attn_inv, hidden_inv, w_all, rates, scales
    )
    grad_ug = lax.psum_scatter(part_ug, "dp", scatter_dimension=0, tiled=True)
    part_down = dot(act_all.reshape(TOK, hid), gd_all.reshape(TOK, D), (0, 0)).astype(BF)
    loss_local = jnp.sum(sums_mid[1])
    g_rate_mlp, g_rate_attn = sums_mid[0], sums_back[0]
    grad_up_scale, grad_gate_scale = ff_sums[0], ff_sums[1] * root_width
    g_attn_all = ga_all.reshape(TOK, D)
    g_mixed = dot(w_o, g_attn_all, (1, 1)).astype(BF)
    g_qkv, g_scale = attn_bwd(perm, qkv, scale_qk, sums, mixed, g_mixed)
    g_qkv = g_qkv.reshape(3 * cols, TOK)
    slot = jnp.arange(tps, dtype=jnp.int32) == me
    qk_rows = jnp.where(slot[:, None], g_scale.reshape(1, cols), 0.0).reshape(dps * tps, rows_w)
    ff_terms = [
        jnp.where(slot[None, :, None], term.reshape(dps, 1, ff_rows), 0.0).reshape(dps * tps, ff_rows)
        for term in (grad_up_scale, grad_gate_scale)
    ]
    vectors = jnp.concatenate(
        [g_rate_attn.reshape(dps * tps, rows_w), g_rate_mlp.reshape(dps * tps, rows_w), qk_rows]
        + ff_terms
        + [jnp.broadcast_to(loss_local, (dps * tps, 512 - 3 * rows_w - 2 * ff_rows))],
        axis=1,
    ).reshape(dps, tps, 4, 128)
    share = dot(g_qkv, w_qkv, (0, 1)).astype(BF).reshape(tps, TOK // tps, D)
    part_out = dot(mixed, g_attn_all, (1, 0)).astype(BF).reshape(dps, rows_w, tps, cols).transpose(0, 2, 1, 3)
    part_qkv = dot(tokens, g_qkv, (0, 1)).astype(BF).reshape(dps, tps * rows_w, 3 * cols)
    parts = jnp.concatenate((part_qkv, part_out.reshape(dps, tps * rows_w, cols)), axis=2)
    grad_states, qkv_back, out_back, grad_down, vector_share = last_exchange(
        share, base, parts, part_down.reshape(dps, ff_rows, D), vectors
    )
    vector_share = vector_share.reshape(512)
    out_back = out_back[:, :, 3 * cols :].transpose(1, 0, 2).reshape(rows_w, D)
    grad_out = lax.ppermute(out_back, both, [(b, a) for a, b in spread])
    ug_back = lax.all_to_all(grad_ug, "fsdp", 0, 0, tiled=True).reshape(tps, rows_w, 2, dps, ff_rows)
    ug_back = ug_back.transpose(2, 1, 3, 0, 4).reshape(2, rows_w, FF).astype(F32)
    qkv_back = qkv_back[:, :, : 3 * cols].reshape(tps, rows_w, 3, cols)
    qkv_back = qkv_back.transpose(2, 1, 0, 3).reshape(3, rows_w, D).astype(F32)
    cuts = (0, rows_w, 2 * rows_w, 3 * rows_w, 3 * rows_w + ff_rows, 3 * rows_w + 2 * ff_rows)
    v = [vector_share[a:b] for a, b in zip(cuts, cuts[1:])]
    return (
        out_states,
        vector_share[-1] / valid_count,
        grad_states,
        qkv_back[0],
        qkv_back[1],
        qkv_back[2],
        grad_out,
        ug_back[0],
        ug_back[1],
        grad_down,
        v[2],
        v[0],
        v[1],
        v[3],
        v[4],
    )


def solution(mesh):
    placed = (
        P(("dp", "fsdp"), None),
        P(("dp", "fsdp"), None),
        P("dp"),
        P(("dp", "fsdp")),
        P(("dp", "fsdp"), None),
        P(("dp", "fsdp"), None),
        P(("dp", "fsdp"), None),
        P(("dp", "fsdp"), None),
        P(("dp", "fsdp"), None),
        P(("dp", "fsdp"), None),
        P(("dp", "fsdp"), None),
        P(("dp", "fsdp")),
        P(("dp", "fsdp")),
        P(("dp", "fsdp")),
        P(("dp", "fsdp")),
        P(("dp", "fsdp")),
    )
    quick = mesh.shape["fsdp"] == 4 and mesh.shape["dp"] == 8
    return jax.shard_map(
        local if quick else general,
        mesh=mesh,
        in_specs=placed,
        out_specs=(
            P(("dp", "fsdp"), None),
            P(),
            P(("dp", "fsdp"), None),
            P(("dp", "fsdp"), None),
            P(("dp", "fsdp"), None),
            P(("dp", "fsdp"), None),
            P(("dp", "fsdp"), None),
            P(("dp", "fsdp"), None),
            P(("dp", "fsdp"), None),
            P(("dp", "fsdp"), None),
            P(("dp", "fsdp")),
            P(("dp", "fsdp")),
            P(("dp", "fsdp")),
            P(("dp", "fsdp")),
            P(("dp", "fsdp")),
        ),
        check_vma=False,
    )
```

```python
import functools
import math

import jax
import jax.numpy as jnp
from jax import lax
from jax.experimental import pallas as pl
from jax.experimental.pallas import tpu as pltpu
from jax.sharding import PartitionSpec as P


D = 1280
HEADS = 20
HEAD_DIM = 64
FF = 5120
BLOCK = 128
DEPTH = 10


EPS = 1e-06


def unit_rows(vector):
    inverse = lax.rsqrt(jnp.sum(vector * vector, axis=-1, keepdims=True) + EPS)
    return (vector * inverse, inverse)


def unit_back(grad, unit, inverse):
    return (grad - unit * jnp.sum(grad * unit, axis=-1, keepdims=True)) * inverse


def project(left, right):
    return jnp.dot(left, right, preferred_element_type=jnp.float32)


def project_back(grad, weight):
    return jnp.einsum("te,de->td", grad, weight, preferred_element_type=jnp.float32)


def ancestors(local_parent):
    column = jnp.arange(local_parent.shape[0], dtype=jnp.int32)
    columns = [column]
    for depth_step in range(DEPTH - 1):
        column = jnp.where(column >= 0, local_parent[jnp.maximum(column, 0)], -1)
        columns.append(column)
    return jnp.stack(columns, axis=1)


def head_back(grad_flat, unit, inverse, scale):
    scaled = (grad_flat * scale).reshape(unit.shape)
    raw = unit_back(scaled, unit, inverse).reshape(grad_flat.shape)
    scale_grad = jnp.sum(grad_flat * unit.reshape(grad_flat.shape), axis=0)
    return (raw, scale_grad)


def general(
    states,
    teacher,
    parent_ids,
    valid_mask,
    w_query,
    w_key,
    w_value,
    w_out,
    w_up,
    w_gate,
    w_down,
    qk_scale,
    attn_rate,
    mlp_rate,
    up_scale,
    gate_scale,
):
    rows_dev = states.shape[0]
    blocks_dev = rows_dev // BLOCK
    width_rows = w_query.shape[0]
    span = DEPTH * BLOCK
    factor = math.sqrt(HEAD_DIM)
    root_width = math.sqrt(D)
    mask_f = valid_mask.astype(jnp.float32)
    qkv_local = jnp.concatenate((w_query, w_key, w_value), axis=1)
    scal_width_local = jnp.stack((qk_scale, attn_rate, mlp_rate), axis=1)
    piece_qkv = lax.all_gather(qkv_local, ("dp", "fsdp"), axis=0, tiled=True)
    piece_out = lax.all_gather(w_out, ("dp", "fsdp"), axis=0, tiled=True)
    piece_scal = lax.all_gather(scal_width_local, ("dp", "fsdp"), axis=0, tiled=True)
    lefts = states
    total = jnp.dot(lefts, piece_qkv, preferred_element_type=jnp.float32)
    scal_whole = piece_scal
    qkv_raw = total
    scal_width = scal_whole
    scale_qk = scal_width[:, 0].astype(jnp.float32)
    rate_attn = scal_width[:, 1].astype(jnp.float32)
    rate_mlp = scal_width[:, 2].astype(jnp.float32)
    query_raw = qkv_raw[:, :D]
    key_raw = qkv_raw[:, D : 2 * D]
    values = qkv_raw[:, 2 * D :].astype(jnp.bfloat16)
    query_unit, query_inv = unit_rows(query_raw.reshape(rows_dev, HEADS, HEAD_DIM))
    key_unit, key_inv = unit_rows(key_raw.reshape(rows_dev, HEADS, HEAD_DIM))
    query_n = (query_unit.reshape(rows_dev, D) * scale_qk).astype(jnp.bfloat16)
    key_n = (key_unit.reshape(rows_dev, D) * scale_qk).astype(jnp.bfloat16)
    key_group, value_group = (
        lax.all_gather(key_n, "fsdp", axis=0, tiled=True),
        lax.all_gather(values, "fsdp", axis=0, tiled=True),
    )
    group_blocks = parent_ids.shape[0]
    group_base = lax.axis_index("dp") * group_blocks
    local_parent = jnp.where(parent_ids >= 0, parent_ids - group_base, -1)
    paths_all = ancestors(local_parent)
    own_first = lax.axis_index("fsdp") * blocks_dev
    paths = lax.dynamic_slice_in_dim(paths_all, own_first, blocks_dev, 0)
    safe_paths = jnp.maximum(paths, 0)
    key_rows = key_group.reshape(group_blocks, BLOCK, D)[safe_paths].reshape(
        blocks_dev, span, HEADS, HEAD_DIM
    )
    value_rows = value_group.reshape(group_blocks, BLOCK, D)[safe_paths].reshape(
        blocks_dev, span, HEADS, HEAD_DIM
    )
    slot_of = jnp.arange(span, dtype=jnp.int32) // BLOCK
    offset = jnp.arange(span, dtype=jnp.int32) % BLOCK
    row_pos = jnp.arange(BLOCK, dtype=jnp.int32)
    causal = offset[None, :] <= row_pos[:, None]
    is_live = jnp.take(paths, slot_of, axis=1) >= 0
    allowed = jnp.where(slot_of[None, None, :] == 0, causal[None], is_live[:, None, :])[:, None]
    query_heads = query_n.reshape(blocks_dev, BLOCK, HEADS, HEAD_DIM)
    scores = factor * jnp.einsum(
        "bqhd,bkhd->bhqk", query_heads, key_rows, preferred_element_type=jnp.float32
    )
    scores = jnp.where(allowed, scores, jnp.float32(-1e30))
    row_max = jnp.max(scores, axis=-1, keepdims=True)
    powers = jnp.exp(scores - row_max)
    row_sum = jnp.sum(powers, axis=-1, keepdims=True)
    probs_b = (powers / row_sum).astype(jnp.bfloat16)
    log_total = row_max + jnp.log(row_sum)
    mixed = jnp.einsum("bhqk,bkhd->bqhd", probs_b, value_rows, preferred_element_type=jnp.float32)
    mixed = mixed.reshape(rows_dev, D).astype(jnp.bfloat16)
    inputs = states.astype(jnp.float32)
    attn = project(mixed, piece_out)
    attn_unit, attn_inv = unit_rows(attn)
    hidden, hidden_inv = unit_rows(inputs + rate_attn * (attn_unit - inputs))
    hidden_b = hidden.astype(jnp.bfloat16)
    ffn_local = jnp.concatenate((w_up, w_gate), axis=1)
    scal_hidden_local = jnp.concatenate(
        (up_scale.reshape(width_rows, 4), gate_scale.reshape(width_rows, 4)), axis=1
    )
    piece_ffn = lax.all_gather(ffn_local, ("dp", "fsdp"), axis=0, tiled=True)
    piece_scal = lax.all_gather(scal_hidden_local, ("dp", "fsdp"), axis=0, tiled=True)
    lefts = hidden_b
    total = jnp.dot(lefts, piece_ffn, preferred_element_type=jnp.float32)
    scal_whole = piece_scal
    scale_up = scal_whole[:, :4].reshape(FF).astype(jnp.float32)
    scale_gate = scal_whole[:, 4:].reshape(FF).astype(jnp.float32)
    up_proj = total[:, :FF]
    gate_proj = total[:, FF:]
    upscaled = up_proj * scale_up
    gated = gate_proj * scale_gate * root_width
    sigmoid_gate = jax.nn.sigmoid(gated)
    act = (upscaled * (gated * sigmoid_gate)).astype(jnp.bfloat16)
    lefts = act
    down = jnp.dot(
        lefts,
        lax.all_gather(w_down, ("dp", "fsdp"), axis=0, tiled=True),
        preferred_element_type=jnp.float32,
    )
    down_unit, down_inv = unit_rows(down)
    result, result_inv = unit_rows(hidden + rate_mlp * (down_unit - hidden))
    loss_local = jnp.sum(mask_f[:, None] * (result - teacher) ** 2)
    valid_count, loss_sum = lax.psum((jnp.sum(mask_f), loss_local), ("dp", "fsdp"))
    loss = loss_sum / valid_count
    g_result = 2.0 * mask_f[:, None] * (result - teacher) / valid_count
    g_last = unit_back(g_result, result, result_inv)
    g_hidden = g_last * (1.0 - rate_mlp)
    g_rate_mlp = jnp.sum(g_last * (down_unit - hidden), axis=0)
    g_down = unit_back(g_last * rate_mlp, down_unit, down_inv).astype(jnp.bfloat16)
    g_act = jnp.einsum(
        "te,fe->tf",
        g_down,
        lax.all_gather(w_down, ("dp", "fsdp"), axis=0, tiled=True),
        preferred_element_type=jnp.float32,
    )
    g_upscaled = g_act * (gated * sigmoid_gate)
    g_gated = g_act * upscaled * sigmoid_gate * (1.0 + gated * (1.0 - sigmoid_gate))
    grad_up_scale = jnp.sum(g_upscaled * up_proj, axis=0)
    grad_gate_scale = jnp.sum(g_gated * gate_proj * root_width, axis=0)
    g_up = (g_upscaled * scale_up).astype(jnp.bfloat16)
    g_gate = (g_gated * scale_gate * root_width).astype(jnp.bfloat16)
    g_both = jnp.concatenate((g_up, g_gate), axis=1)
    g_hidden = g_hidden + jnp.einsum(
        "tc,dc->td",
        g_both,
        lax.all_gather(ffn_local, ("dp", "fsdp"), axis=0, tiled=True),
        preferred_element_type=jnp.float32,
    )
    scal_terms = jnp.concatenate(
        (grad_up_scale.reshape(D, 4), grad_gate_scale.reshape(D, 4)), axis=1
    )
    lefts = hidden_b
    main = jnp.einsum("td,tc->dc", lefts, g_both, preferred_element_type=jnp.float32)
    ffn_share = lax.psum_scatter(
        jnp.concatenate((main, scal_terms), axis=1), ("dp", "fsdp"), scatter_dimension=0, tiled=True
    )
    lefts = act
    grad_down = lax.psum_scatter(
        jnp.einsum("tf,te->fe", lefts, g_down, preferred_element_type=jnp.float32),
        ("dp", "fsdp"),
        scatter_dimension=0,
        tiled=True,
    )
    g_pre = unit_back(g_hidden, hidden, hidden_inv)
    g_states = g_pre * (1.0 - rate_attn)
    g_rate_attn = jnp.sum(g_pre * (attn_unit - inputs), axis=0)
    g_attn = unit_back(g_pre * rate_attn, attn_unit, attn_inv).astype(jnp.bfloat16)
    g_mixed = project_back(g_attn, piece_out).astype(jnp.bfloat16)
    scores = factor * jnp.einsum(
        "bqhd,bkhd->bhqk", query_heads, key_rows, preferred_element_type=jnp.float32
    )
    probs = jnp.where(allowed, jnp.exp(scores - log_total), jnp.float32(0.0))
    probs_again = probs.astype(jnp.bfloat16)
    g_heads = g_mixed.reshape(blocks_dev, BLOCK, HEADS, HEAD_DIM)
    g_probs = jnp.einsum("bqhd,bkhd->bhqk", g_heads, value_rows, preferred_element_type=jnp.float32)
    delta = jnp.sum(probs * g_probs, axis=-1, keepdims=True)
    g_scores = (probs * (g_probs - delta)).astype(jnp.bfloat16)
    g_query_n = factor * jnp.einsum(
        "bhqk,bkhd->bqhd", g_scores, key_rows, preferred_element_type=jnp.float32
    )
    g_key_rows = factor * jnp.einsum(
        "bhqk,bqhd->bkhd", g_scores, query_heads, preferred_element_type=jnp.float32
    )
    g_value_rows = jnp.einsum(
        "bhqk,bqhd->bkhd", probs_again, g_heads, preferred_element_type=jnp.float32
    )
    flat_paths = safe_paths.reshape(blocks_dev * DEPTH)
    g_key_group = (
        jnp.zeros((group_blocks, BLOCK, D), jnp.float32)
        .at[flat_paths]
        .add(g_key_rows.reshape(blocks_dev * DEPTH, BLOCK, D))
    )
    g_value_group = (
        jnp.zeros((group_blocks, BLOCK, D), jnp.float32)
        .at[flat_paths]
        .add(g_value_rows.reshape(blocks_dev * DEPTH, BLOCK, D))
    )
    g_key_n, g_values = (
        lax.psum_scatter(
            g_key_group.reshape(group_blocks * BLOCK, D).astype(jnp.bfloat16),
            "fsdp",
            scatter_dimension=0,
            tiled=True,
        ).astype(jnp.float32),
        lax.psum_scatter(
            g_value_group.reshape(group_blocks * BLOCK, D).astype(jnp.bfloat16),
            "fsdp",
            scatter_dimension=0,
            tiled=True,
        ).astype(jnp.float32),
    )
    g_query_raw, scale_from_query = head_back(
        g_query_n.reshape(rows_dev, D), query_unit, query_inv, scale_qk
    )
    g_key_raw, scale_from_key = head_back(g_key_n, key_unit, key_inv, scale_qk)
    grad_qk_scale = scale_from_query + scale_from_key
    g_qkv = jnp.concatenate(
        (
            g_query_raw.astype(jnp.bfloat16),
            g_key_raw.astype(jnp.bfloat16),
            g_values.astype(jnp.bfloat16),
        ),
        axis=1,
    )
    g_states = g_states + jnp.einsum(
        "tc,dc->td",
        g_qkv,
        lax.all_gather(qkv_local, ("dp", "fsdp"), axis=0, tiled=True),
        preferred_element_type=jnp.float32,
    )
    vector_terms = jnp.stack((grad_qk_scale, g_rate_attn, g_rate_mlp), axis=1)
    lefts = states
    main = jnp.einsum("td,tc->dc", lefts, g_qkv, preferred_element_type=jnp.float32)
    outer = jnp.einsum("td,tc->dc", mixed, g_attn, preferred_element_type=jnp.float32)
    attn_share = lax.psum_scatter(
        jnp.concatenate((main, outer, vector_terms), axis=1),
        ("dp", "fsdp"),
        scatter_dimension=0,
        tiled=True,
    )
    return (
        result.astype(jnp.bfloat16),
        loss,
        g_states,
        attn_share[:, :D],
        attn_share[:, D : 2 * D],
        attn_share[:, 2 * D : 3 * D],
        attn_share[:, 3 * D : 4 * D],
        ffn_share[:, :FF],
        ffn_share[:, FF : 2 * FF],
        grad_down,
        attn_share[:, 4 * D],
        attn_share[:, 4 * D + 1],
        attn_share[:, 4 * D + 2],
        ffn_share[:, 2 * FF : 2 * FF + 4].reshape(-1),
        ffn_share[:, 2 * FF + 4 : 2 * FF + 8].reshape(-1),
    )

TRUNK = 8
NB = 20
TOK = NB * BLOCK
F32 = jnp.float32
BF = jnp.bfloat16


def head_norm(raw):
    inv = lax.rsqrt(jnp.sum(raw * raw, axis=0, keepdims=True) + EPS)
    return raw * inv, inv


def lanes_at(start, size):
    return pl.ds(pl.multiple_of(start, 128), size)


def rows_at(start, size):
    return pl.ds(pl.multiple_of(start, 16), size)


def each_chunk(visit):
    for j in range(TRUNK // 2):
        parts = [(0, 256 * j, "all")] if j else []
        visit(256 * j, parts + [(256 * j, 256, "causal")])
    trunk = TRUNK * BLOCK

    def branches(j, carry):
        start = trunk + 256 * j
        visit(start, [(0, trunk, "all"), (start, 256, "pair")])
        return carry

    def leaves(j, carry):
        start = trunk + 4 * BLOCK + 256 * j
        visit(start, [(0, trunk, "all"), (trunk + BLOCK * j, BLOCK, "all"), (start, 256, "pair")])
        return carry

    for j in range(2):
        branches(j, 0)
    for j in range(4):
        leaves(j, 0)


def masked(kind, value):
    if kind == "all":
        return value
    key = lax.broadcasted_iota(jnp.int32, (256, 256), 0)
    query = lax.broadcasted_iota(jnp.int32, (256, 256), 1)
    keep = key <= query
    if kind == "pair":
        keep = keep & ((key < 128) == (query < 128))
    return jnp.where(keep, value, jnp.zeros_like(value))


def nn(a, b):
    return lax.dot_general(a, b, (((1,), (0,)), ((), ())), preferred_element_type=F32)


def nt(a, b):
    return lax.dot_general(a, b, (((1,), (1,)), ((), ())), preferred_element_type=F32)


def attention_back_kernel(order, qkv, scales, sums, mixed, ga_all, w_o, ht_all, gug_all,
                          g_qkv, g_scale, part_out, g_up, g_gate,
                          ga_b, ga, gm, raw, out_b, qT, q, k, kT, v, gT, g, dq, dk, dv, delta, inv,
                          gug_b, ht_r, ht_l, ring_r, ring_l, next_r, next_l, hid_buf, hid_in,
                          ga_sem, gug_sem, row_sem, raw_sem, out_sem, ring_send, ring_recv, a2a_send, a2a_recv):
    me = lax.axis_index("fsdp")
    place = ring_place()
    peers = group_peers()
    right, left = {"dp": ring_dp(place + 1)}, {"dp": ring_dp(place - 1)}
    count, chunk, side = gug_b.shape[0], ring_r.shape[1], ring_r.shape[2]
    heads = g_scale.shape[0]
    rows_w = hid_buf.shape[1]

    def slices(step):
        slot = step % 2
        cut_r = rows_at(ring_dp(place - 1 - step) * chunk, chunk)
        cut_l = rows_at(ring_dp(place + 1 + step) * chunk, chunk)
        return [
            pltpu.make_async_copy(ht_all.at[:, cut_r], ht_r.at[slot], row_sem.at[0, slot]),
            pltpu.make_async_copy(ht_all.at[:, cut_l], ht_l.at[slot], row_sem.at[1, slot]),
        ]

    def raw_copy(head):
        slot = head % 2
        return pltpu.make_async_copy(
            qkv.at[:, rows_at(head * HEAD_DIM, HEAD_DIM)], raw.at[slot], raw_sem.at[slot]
        )

    def out_copy(head):
        slot = head % 2
        return pltpu.make_async_copy(
            out_b.at[slot], g_qkv.at[:, rows_at(head * HEAD_DIM, HEAD_DIM)], out_sem.at[slot]
        )

    load_ga = pltpu.make_async_copy(ga_all, ga_b, ga_sem.at[0])
    load_ga.start()
    raw_copy(0).start()
    for copy in slices(0):
        copy.start()
    loads = [pltpu.make_async_copy(gug_all.at[i], gug_b.at[i], gug_sem.at[i]) for i in range(count)]
    for copy in loads:
        copy.start()
    for copy in slices(1):
        copy.start()
    greet([*peers, right, left])
    load_ga.wait()

    def pick(i, carry):
        ga[lanes_at(i * BLOCK, BLOCK)] = ga_b[order[0, i]]
        return carry

    lax.fori_loop(0, NB, pick, 0)

    def back(n, carry):
        gm[:, tile(n)] = nt(w_o[...], ga[tile(n)]).astype(BF)
        return carry

    lax.fori_loop(0, TOK // TILE, back, 0)

    def outer(n, carry):
        part_out[:, tile(n)] = nn(mixed[...], ga[:, tile(n)]).astype(BF)
        return carry

    lax.fori_loop(0, D // TILE, outer, 0)

    def parts(step):
        slot = step % 2
        for copy in slices(step):
            copy.wait()
        next_r[...] = jnp.zeros_like(next_r)
        next_l[...] = jnp.zeros_like(next_l)

        def add(i, carry):
            next_r[...] = next_r[...] + nn(ht_r[slot, i], gug_b[i, :, pl.ds(0, side)])
            next_l[...] = next_l[...] + nn(ht_l[slot, i], gug_b[i, :, pl.ds(side, side)])
            return carry

        lax.fori_loop(0, count, add, 0)

        @pl.when(step + 2 < 8)
        def _():
            for copy in slices(step + 2):
                copy.start()

    def hop_copies(step):
        return [
            send(ring_r.at[step], ring_r.at[step + 1], ring_send.at[0, step], ring_recv.at[0, step], right),
            send(ring_l.at[step], ring_l.at[step + 1], ring_send.at[1, step], ring_recv.at[1, step], left),
        ]

    def exchange():
        return [
            send(hid_buf.at[peer["fsdp"]], hid_in.at[me], a2a_send.at[i], a2a_recv.at[i], peer)
            for i, peer in enumerate(peers)
        ]

    def hop(step):
        parts(step + 1)
        for copy in hop_copies(step):
            copy.wait()

        @pl.when(step < 6)
        def _():
            ring_r[step + 1] = (ring_r[step + 1].astype(F32) + next_r[...]).astype(BF)
            ring_l[step + 1] = (ring_l[step + 1].astype(F32) + next_l[...]).astype(BF)
            for copy in hop_copies(step + 1):
                copy.start()

        @pl.when(step == 6)
        def _():
            for start, ring, own in ((0, ring_r, next_r), (side, ring_l, next_l)):
                total = ring[7].astype(F32) + own[...]
                for i in range(4):
                    hid_buf[i, :, start : start + side] = total[i * rows_w : (i + 1) * rows_w].astype(BF)
            for copy in exchange():
                copy.start()

    for copy in loads:
        copy.wait()
    parts(0)
    ring_r[0] = next_r[...].astype(BF)
    ring_l[0] = next_l[...].astype(BF)
    for copy in hop_copies(0):
        copy.start()

    def open_head(head):
        slot = head % 2
        raw_copy(head).wait()

        @pl.when(head + 1 < heads)
        def _():
            raw_copy(head + 1).start()

        @pl.when(head >= 2)
        def _():
            out_copy(head - 2).wait()

        scale = scales[head]
        mine = rows_at(head * HEAD_DIM, HEAD_DIM)

        for i in range(NB):
            here = slice(i * BLOCK, (i + 1) * BLOCK)
            q_unit, _ = head_norm(raw[slot, 0, :, here])
            k_unit, _ = head_norm(raw[slot, 1, :, here])
            q8 = (q_unit * scale).astype(BF) * BF(8.0)
            qT[:, here] = q8
            q[here, :] = q8.T
            kn = (k_unit * scale).astype(BF)
            kT[:, here] = kn
            k[here, :] = kn.T
            v[here, :] = raw[slot, 2, :, here].astype(BF).T
            gh = gm[mine, here]
            gT[:, here] = gh
            g[here, :] = gh.T
            delta[:, here] = jnp.sum(gh.astype(F32) * mixed[mine, here].astype(F32), axis=0, keepdims=True)
            inv[:, here] = sums[head, 0:1, here]
        dk[...] = jnp.zeros_like(dk)
        dv[...] = jnp.zeros_like(dv)

    def close_head(head):
        slot = head % 2
        scale = scales[head]

        def visit(start, pieces):
            span = lanes_at(start, 256)
            query, grad = qT[:, span], gT[:, span]
            query_rows, grad_rows = q[span, :], g[span, :]
            scale_row, delta_row = inv[:, span], delta[:, span]
            acc = jnp.zeros((64, 256), F32)
            for kstart, size, kind in pieces:
                keys = lanes_at(kstart, size)
                probs = masked(kind, jnp.exp(nn(k[keys, :], query)) * scale_row)
                g_probs = nn(v[keys, :], grad)
                g_scores = (probs * (g_probs - delta_row)).astype(BF)
                dv[keys, :] += nn(probs.astype(BF), grad_rows)
                dk[keys, :] += nn(g_scores, query_rows)
                acc = acc + nn(kT[:, keys], g_scores)
            dq[:, span] = acc * 8.0

        each_chunk(visit)
        total = jnp.zeros((64, BLOCK), F32)
        for i in range(NB):
            here = slice(i * BLOCK, (i + 1) * BLOCK)
            for which, grad in ((0, dq[:, here]), (1, dk[here, :].T)):
                unit, inverse = head_norm(raw[slot, which, :, here])
                total = total + grad * unit
                scaled = grad * scale
                value = (scaled - unit * jnp.sum(scaled * unit, axis=0, keepdims=True)) * inverse
                out_b[slot, which, :, here] = value.astype(BF)
            out_b[slot, 2, :, here] = dv[here, :].T.astype(BF)
        g_scale[head] = jnp.sum(total, axis=1, keepdims=True)
        out_copy(head).start()

    def work(i, carry):
        pl.when(i % 2 == 0)(functools.partial(open_head, i // 2))
        pl.when(i % 2 == 1)(functools.partial(close_head, i // 2))
        pl.when(i < 7)(functools.partial(hop, i))
        return carry

    lax.fori_loop(0, 2 * heads, work, 0)
    for copy in exchange():
        copy.wait()
    hid_in[me] = hid_buf[me]
    size = g_up.shape[1] // 32
    for which, out in enumerate((g_up, g_gate)):
        for d in range(8):
            start = (8 * which + d) * size
            block = [hid_in[i, :, start : start + size].astype(F32) for i in range(4)]
            out[:, d * 4 * size : (d + 1) * 4 * size] = jnp.concatenate(block, axis=1)
    for head in (heads - 2, heads - 1):
        out_copy(head).wait()


def attention_back(order, qkv, scales, sums, mixed, ga_all, w_o, ht_all, gug_all):
    heads = scales.shape[0]
    count, tokens, hidden_width = gug_all.shape
    chunk = ht_all.shape[1] // 8
    side = hidden_width // 2
    rows_w = chunk // 4
    vmem, hbm = pl.BlockSpec(memory_space=pltpu.VMEM), pl.BlockSpec(memory_space=pl.ANY)
    smem = pl.BlockSpec(memory_space=pltpu.SMEM)
    dma = pltpu.SemaphoreType.DMA
    return pl.pallas_call(
        attention_back_kernel,
        in_specs=[smem, hbm, vmem, vmem, vmem, hbm, vmem, hbm, hbm],
        out_specs=[hbm, vmem, vmem, vmem, vmem],
        out_shape=[
            jax.ShapeDtypeStruct(qkv.shape, BF),
            jax.ShapeDtypeStruct(scales.shape, F32),
            jax.ShapeDtypeStruct(w_o.shape, BF),
            jax.ShapeDtypeStruct((rows_w, 2 * hidden_width), F32),
            jax.ShapeDtypeStruct((rows_w, 2 * hidden_width), F32),
        ],
        scratch_shapes=[
            pltpu.VMEM(ga_all.shape, BF),
            pltpu.VMEM((TOK, w_o.shape[1]), BF),
            pltpu.VMEM(mixed.shape, BF),
            pltpu.VMEM((2, 3, HEAD_DIM, TOK), F32),
            pltpu.VMEM((2, 3, HEAD_DIM, TOK), BF),
            pltpu.VMEM((HEAD_DIM, TOK), BF),
            pltpu.VMEM((TOK, HEAD_DIM), BF),
            pltpu.VMEM((TOK, HEAD_DIM), BF),
            pltpu.VMEM((HEAD_DIM, TOK), BF),
            pltpu.VMEM((TOK, HEAD_DIM), BF),
            pltpu.VMEM((HEAD_DIM, TOK), BF),
            pltpu.VMEM((TOK, HEAD_DIM), BF),
            pltpu.VMEM((HEAD_DIM, TOK), F32),
            pltpu.VMEM((TOK, HEAD_DIM), F32),
            pltpu.VMEM((TOK, HEAD_DIM), F32),
            pltpu.VMEM((1, TOK), F32),
            pltpu.VMEM((1, TOK), F32),
            pltpu.VMEM(gug_all.shape, BF),
            pltpu.VMEM((2, count, chunk, tokens), BF),
            pltpu.VMEM((2, count, chunk, tokens), BF),
            pltpu.VMEM((8, chunk, side), BF),
            pltpu.VMEM((8, chunk, side), BF),
            pltpu.VMEM((chunk, side), F32),
            pltpu.VMEM((chunk, side), F32),
            pltpu.VMEM((4, rows_w, hidden_width), BF),
            pltpu.VMEM((4, rows_w, hidden_width), BF),
            dma((1,)),
            dma((count,)),
            dma((2, 2)),
            dma((2,)),
            dma((2,)),
            dma((2, 7)),
            dma((2, 7)),
            dma((3,)),
            dma((3,)),
        ],
        compiler_params=pltpu.CompilerParams(
            collective_id=5, has_side_effects=True, vmem_limit_bytes=62 << 20
        ),
        name="attention_back",
        cost_estimate=pl.CostEstimate(flops=40 * 10**9, bytes_accessed=60 << 20, transcendentals=14 << 20),
    )(order, qkv, scales, sums, mixed, ga_all, w_o, ht_all, gug_all)


MESH = pl.DeviceIdType.MESH


def ring_place():
    dp = lax.axis_index("dp")
    z, y = dp // 2, dp % 2
    return z + y * (7 - 2 * z)


def ring_dp(place):
    place = (place + 16) % 8
    y = place // 4
    return 2 * (place + y * (7 - 2 * place)) + y


def greet(peers):
    barrier = pltpu.get_barrier_semaphore()
    for peer in peers:
        pl.semaphore_signal(barrier, inc=1, device_id=peer, device_id_type=MESH)
    pl.semaphore_wait(barrier, len(peers))


def group_peers():
    me = lax.axis_index("fsdp")
    core = 1 - 2 * (me % 2)
    chip = 2 - 4 * (me // 2)
    return {"fsdp": me + core}, {"fsdp": me + chip}, {"fsdp": me + core + chip}


def send(src, dst, send_sem, recv_sem, peer):
    return pltpu.make_async_remote_copy(
        src_ref=src, dst_ref=dst, send_sem=send_sem, recv_sem=recv_sem, device_id=peer, device_id_type=MESH
    )


def forward_kernel(order, states, qkv_send, extra, out_piece, ug_send,
                   tokens_t, w_t, w_o, w_ug, qkv, mixed, sums, share,
                   land, weights, tok, turned, tok_t, out_w, ug_land, ug_own, raw, qs, ks, vs, blocks, stage,
                   tok_send, tok_recv, a2a_send, a2a_recv, ring_send, ring_recv, ug_s, ug_r, local_sem, raw_sem,
                   stage_sem):
    me, dp = lax.axis_index("fsdp"), lax.axis_index("dp")
    place = ring_place()
    sibling, across, corner = group_peers()
    right, left = {"dp": ring_dp(place + 1)}, {"dp": ring_dp(place - 1)}
    rows, width = states.shape
    piece = land.shape[1]
    chunk = 4 * piece
    half = chunk // 2
    cols = mixed.shape[0]
    heads = cols // HEAD_DIM
    greet([sibling, across, corner, right, left])

    exchange, ug_exchange = [], []
    for i, peer in enumerate((sibling, across, corner)):
        copy = send(qkv_send.at[peer["fsdp"]], land.at[me], a2a_send.at[i], a2a_recv.at[i], peer)
        copy.start()
        exchange.append(copy)
    far = []
    for i in range(2):
        part = pl.ds(i * (rows // 2), rows // 2)
        here = pl.ds(2 * rows + i * (rows // 2), rows // 2)
        copy = send(states.at[part], tok.at[here], tok_send.at[i], tok_recv.at[i], across)
        copy.start()
        far.append(copy)
    near = send(states, tok.at[pl.ds(rows, rows)], tok_send.at[2], tok_recv.at[2], sibling)
    near.start()
    own = pltpu.make_async_copy(states, tok.at[pl.ds(0, rows)], local_sem.at[0])
    own.start()
    for i, peer in enumerate((sibling, across, corner)):
        copy = send(ug_send.at[peer["fsdp"]], ug_land.at[me], a2a_send.at[3 + i], a2a_recv.at[3 + i], peer)
        copy.start()
        ug_exchange.append(copy)
    land[me] = qkv_send[me]
    ug_land[me] = ug_send[me]
    out_w[dp] = out_piece[...]
    vs[HEAD_DIM:, :] = jnp.ones((vs.shape[0] - HEAD_DIM, TOK), BF)
    for copy in exchange:
        copy.wait()
    weights[rows_at(dp * chunk, chunk)] = jnp.concatenate([land[i].astype(F32) for i in range(4)], axis=0).astype(BF)
    last = pl.ds(weights.shape[1] - 128, 128)
    weights[rows_at(dp * chunk, chunk), last] = weights[rows_at(dp * chunk, chunk), last] + extra[...]

    def hop(step, carry):
        to_right, to_left = ring_dp(place - step), ring_dp(place + step)
        first, second = rows_at(to_right * chunk, half), rows_at(to_left * chunk + half, half)
        copies = [
            send(weights.at[first], weights.at[first], ring_send.at[0, step], ring_recv.at[0, step], right),
            send(weights.at[second], weights.at[second], ring_send.at[1, step], ring_recv.at[1, step], left),
            send(out_w.at[to_right, :, pl.ds(0, 640)], out_w.at[to_right, :, pl.ds(0, 640)],
                 ring_send.at[2, step], ring_recv.at[2, step], right),
            send(out_w.at[to_left, :, pl.ds(640, 640)], out_w.at[to_left, :, pl.ds(640, 640)],
                 ring_send.at[3, step], ring_recv.at[3, step], left),
        ]
        for copy in copies:
            copy.start()
        for copy in copies:
            copy.wait()
        return carry

    def ug_copies(step):
        first = rows_at(ring_dp(place - step) * chunk, half)
        second = rows_at(ring_dp(place + step) * chunk + half, half)
        return [
            send(w_ug.at[first], w_ug.at[first], ug_s.at[0, step], ug_r.at[0, step], right),
            send(w_ug.at[second], w_ug.at[second], ug_s.at[1, step], ug_r.at[1, step], left),
        ]

    def ug_hop(step):
        for copy in ug_copies(step):
            copy.wait()

        @pl.when(step < 6)
        def _():
            for copy in ug_copies(step + 1):
                copy.start()

    def turn(i, carry):
        turned[i] = tok[lanes_at(i * BLOCK, BLOCK)].T
        return carry

    lax.fori_loop(0, 1, hop, 0)
    near.wait()
    own.wait()
    lax.fori_loop(0, 4, turn, 0)
    lax.fori_loop(1, 2, hop, 0)
    lax.fori_loop(4, 7, turn, 0)
    lax.fori_loop(2, 3, hop, 0)
    lax.fori_loop(7, 10, turn, 0)
    lax.fori_loop(3, 5, hop, 0)
    passed = []
    for i in range(2):
        far[i].wait()
        here = pl.ds(2 * rows + i * (rows // 2), rows // 2)
        there = pl.ds(3 * rows + i * (rows // 2), rows // 2)
        copy = send(tok.at[here], tok.at[there], tok_send.at[3 + i], tok_recv.at[3 + i], sibling)
        copy.start()
        passed.append(copy)
    for copy in ug_exchange:
        copy.wait()
    ug_own[...] = jnp.concatenate([ug_land[i].astype(F32) for i in range(4)], axis=0).astype(BF)
    ug_store = pltpu.make_async_copy(ug_own, w_ug.at[rows_at(dp * chunk, chunk)], local_sem.at[1])
    ug_store.start()
    lax.fori_loop(5, 6, hop, 0)
    lax.fori_loop(10, 15, turn, 0)
    lax.fori_loop(6, 7, hop, 0)
    ug_store.wait()
    for copy in ug_copies(0):
        copy.start()
    for copy in passed:
        copy.wait()

    lax.fori_loop(15, NB, turn, 0)

    def arrange(i, carry):
        tok_t[:, lanes_at(i * BLOCK, BLOCK)] = turned[order[0, i]]
        return carry

    lax.fori_loop(0, NB, arrange, 0)
    keep = pltpu.make_async_copy(tok_t, tokens_t, local_sem.at[2])
    keep.start()

    def turn_weights(i, carry):
        w_t[:, lanes_at(i * BLOCK, BLOCK)] = weights[rows_at(i * BLOCK, BLOCK)].T
        return carry

    lax.fori_loop(0, width // BLOCK, turn_weights, 0)
    w_o[...] = jnp.concatenate([out_w[i].astype(F32) for i in range(8)], axis=0).astype(BF)

    def raw_copies(head):
        slot = head % 2
        return [
            pltpu.make_async_copy(
                raw.at[slot, pl.ds(which * HEAD_DIM, HEAD_DIM)],
                qkv.at[which, rows_at(head * HEAD_DIM, HEAD_DIM)],
                raw_sem.at[slot, which],
            )
            for which in range(3)
        ]

    def attend(head, carry):
        slot = head % 2

        @pl.when(head >= 2)
        def _():
            for copy in raw_copies(head - 2):
                copy.wait()

        left_rows = jnp.concatenate(
            [w_t[rows_at(which * cols + head * HEAD_DIM, HEAD_DIM)] for which in range(3)], axis=0
        )

        def project_tile(n, carry):
            raw[slot, :, tile(n)] = nn(left_rows, tok_t[:, tile(n)])
            return carry

        lax.fori_loop(0, TOK // TILE, project_tile, 0, unroll=2)
        for copy in raw_copies(head):
            copy.start()
        scale = weights[rows_at(me * cols + head * HEAD_DIM, HEAD_DIM), last][:, HEAD_DIM : HEAD_DIM + 1].astype(F32)

        def prepare(i, carry):
            here = lanes_at(i * BLOCK, BLOCK)
            q_unit, _ = head_norm(raw[slot, pl.ds(0, HEAD_DIM), here])
            k_unit, _ = head_norm(raw[slot, pl.ds(HEAD_DIM, HEAD_DIM), here])
            qs[:, here] = (q_unit * scale).astype(BF) * BF(8.0)
            ks[here, :] = (k_unit * scale).astype(BF).T
            vs[0:HEAD_DIM, here] = raw[slot, pl.ds(2 * HEAD_DIM, HEAD_DIM), here].astype(BF)
            return carry

        lax.fori_loop(0, NB, prepare, 0, unroll=NB)

        def visit(start, parts):
            span = lanes_at(start, 256)
            query = qs[:, span]
            acc = jnp.zeros((vs.shape[0], 256), F32)
            for kstart, count, kind in parts:
                keys = lanes_at(kstart, count)
                powers = masked(kind, jnp.exp(nn(ks[keys, :], query))).astype(BF)
                acc = acc + nn(vs[:, keys], powers)
            total = 1.0 / acc[HEAD_DIM : HEAD_DIM + 1, :]
            mixed[rows_at(head * HEAD_DIM, HEAD_DIM), span] = (acc[0:HEAD_DIM, :] * total).astype(BF)
            sums[head, :, span] = jnp.broadcast_to(total, (8, 256))

        each_chunk(visit)

        @pl.when(head % 2 == 1)
        def _():
            ug_hop(head // 2)

        return carry

    lax.fori_loop(0, heads, attend, 0)
    ug_hop(2)

    def share_copy(b):
        slot = b % 2
        return pltpu.make_async_copy(
            stage.at[slot], share.at[b // 5, lanes_at((b % 5) * BLOCK, BLOCK)], stage_sem.at[slot]
        )

    def split(i, carry):
        blocks[i] = mixed[:, lanes_at(i * BLOCK, BLOCK)]
        return carry

    lax.fori_loop(0, NB, split, 0)

    def out_project(b, carry):
        @pl.when(b >= 2)
        def _():
            share_copy(b - 2).wait()

        stage[b % 2] = nn(blocks[order[1, b]].T, w_o[...]).astype(BF)
        share_copy(b).start()
        return carry

    lax.fori_loop(0, NB, out_project, 0, unroll=4)
    lax.fori_loop(3, 7, lambda step, c: (ug_hop(step), c)[1], 0)
    keep.wait()
    for b in (NB - 2, NB - 1):
        share_copy(b).wait()
    for head in (heads - 2, heads - 1):
        for copy in raw_copies(head):
            copy.wait()


def forward(order, states, qkv_send, extra, out_piece, ug_send):
    tps, rows_w, packed = qkv_send.shape
    tokens, width = states.shape
    hidden_width = ug_send.shape[2]
    cols = 8 * rows_w
    vmem, hbm = pl.BlockSpec(memory_space=pltpu.VMEM), pl.BlockSpec(memory_space=pl.ANY)
    smem = pl.BlockSpec(memory_space=pltpu.SMEM)
    dma = pltpu.SemaphoreType.DMA
    return pl.pallas_call(
        forward_kernel,
        in_specs=[smem, hbm] + [vmem] * 4,
        out_specs=[hbm, vmem, vmem, hbm, hbm, vmem, vmem, hbm],
        out_shape=[
            jax.ShapeDtypeStruct((width, TOK), BF),
            jax.ShapeDtypeStruct((packed, width), BF),
            jax.ShapeDtypeStruct((cols, width), BF),
            jax.ShapeDtypeStruct((width, hidden_width), BF),
            jax.ShapeDtypeStruct((3, cols, TOK), F32),
            jax.ShapeDtypeStruct((cols, TOK), BF),
            jax.ShapeDtypeStruct((cols // HEAD_DIM, 8, TOK), F32),
            jax.ShapeDtypeStruct((tps, tokens, width), BF),
        ],
        scratch_shapes=[
            pltpu.VMEM((tps, rows_w, packed), BF),
            pltpu.VMEM((width, packed), BF),
            pltpu.VMEM((TOK, width), BF),
            pltpu.VMEM((NB, width, BLOCK), BF),
            pltpu.VMEM((width, TOK), BF),
            pltpu.VMEM((8, rows_w, width), BF),
            pltpu.VMEM((tps, rows_w, hidden_width), BF),
            pltpu.VMEM((tps * rows_w, hidden_width), BF),
            pltpu.VMEM((2, 3 * HEAD_DIM, TOK), F32),
            pltpu.VMEM((HEAD_DIM, TOK), BF),
            pltpu.VMEM((TOK, HEAD_DIM), BF),
            pltpu.VMEM((HEAD_DIM + 16, TOK), BF),
            pltpu.VMEM((NB, cols, BLOCK), BF),
            pltpu.VMEM((2, BLOCK, width), BF),
            dma((5,)),
            dma((5,)),
            dma((6,)),
            dma((6,)),
            dma((4, 7)),
            dma((4, 7)),
            dma((2, 7)),
            dma((2, 7)),
            dma((3,)),
            dma((2, 3)),
            dma((2,)),
        ],
        compiler_params=pltpu.CompilerParams(
            collective_id=1, has_side_effects=True, vmem_limit_bytes=56 << 20
        ),
        cost_estimate=pl.CostEstimate(flops=12 * 10**9, bytes_accessed=200 << 20, transcendentals=14 << 20),
        name="forward",
    )(order, states, qkv_send, extra, out_piece, ug_send)


def last_kernel(order, base, tokens_t, g_qkv, w_t, part_out, vectors,
                g_states, g_query, g_key, g_value, out_rows, vec_own,
                gq_b, blocks, tok_r, tok_l, share, turned, core_buf, x_buf, base_b, gs_b,
                ring_r, ring_l, ring_o, ring_v, next_r, next_l, row_buf, row_in, vec_part, vec_in,
                in_sem, row_sem, base_sem, core_send, core_recv, x_send, x_recv,
                ring_send, ring_recv, a2a_send, a2a_recv):
    me, dp = lax.axis_index("fsdp"), lax.axis_index("dp")
    place = ring_place()
    sibling, across, corner = group_peers()
    right, left = {"dp": ring_dp(place + 1)}, {"dp": ring_dp(place - 1)}
    chunk, side = ring_r.shape[1], ring_r.shape[2]
    rows = share.shape[1]
    quarter = rows // 4
    width = w_t.shape[1]
    heads_width = gq_b.shape[0]
    rows_w = row_buf.shape[1]

    def slices(step):
        slot = step % 2
        cut_r = rows_at(ring_dp(place - 1 - step) * chunk, chunk)
        cut_l = rows_at(ring_dp(place + 1 + step) * chunk, chunk)
        return [
            pltpu.make_async_copy(tokens_t.at[cut_r], tok_r.at[slot], row_sem.at[0, slot]),
            pltpu.make_async_copy(tokens_t.at[cut_l], tok_l.at[slot], row_sem.at[1, slot]),
        ]

    def base_copy(i):
        return pltpu.make_async_copy(base.at[pl.ds(i * quarter, quarter)], base_b.at[i % 2], base_sem.at[0, i % 2])

    def gs_copy(i):
        return pltpu.make_async_copy(gs_b.at[i % 2], g_states.at[pl.ds(i * quarter, quarter)], base_sem.at[1, i % 2])

    load_q = pltpu.make_async_copy(g_qkv, gq_b, in_sem.at[0])
    load_q.start()
    for step in (0, 1):
        for copy in slices(step):
            copy.start()
    greet([sibling, across, corner, right, left])

    def parts(step):
        slot = step % 2
        for copy in slices(step):
            copy.wait()
        next_r[...] = nt(tok_r[slot], gq_b[pl.ds(0, side)])
        next_l[...] = nt(tok_l[slot], gq_b[pl.ds(side, heads_width - side)])

        @pl.when(step + 2 < 8)
        def _():
            for copy in slices(step + 2):
                copy.start()

    def hop_copies(step):
        return [
            send(ring.at[step], ring.at[step + 1], ring_send.at[i, step], ring_recv.at[i, step], peer)
            for i, (ring, peer) in enumerate(((ring_r, right), (ring_l, left), (ring_o, left), (ring_v, right)))
        ]

    def through(r, slot):
        for i in range(rows // BLOCK):
            turned[i * BLOCK : (i + 1) * BLOCK] = blocks[order[1, r * (rows // BLOCK) + i]].T

        def one(n, carry):
            share[slot, :, tile(n)] = nn(turned[...], w_t[pl.ds(0, heads_width), tile(n)]).astype(BF)
            return carry

        lax.fori_loop(0, width // TILE, one, 0)

    core = [
        send(share.at[0], core_buf.at[0], core_send.at[0], core_recv.at[0], sibling),
        send(share.at[2], core_buf.at[1], core_send.at[1], core_recv.at[1], sibling),
    ]
    far = [
        send(share.at[1, pl.ds(i * quarter, quarter)], x_buf.at[pl.ds(i * quarter, quarter)], x_send.at[i],
             x_recv.at[i], across)
        for i in range(4)
    ]
    load_q.wait()

    def split(i, carry):
        blocks[i] = gq_b[:, lanes_at(i * BLOCK, BLOCK)]
        return carry

    def hop(step, carry):
        parts(step)

        @pl.when(step == 0)
        def _():
            ring_r[0] = next_r[...].astype(BF)
            ring_l[0] = next_l[...].astype(BF)
            ring_o[0] = part_out[ring_dp(place + 1)]
            ring_v[0] = vectors[ring_dp(place - 1)]

        @pl.when(step > 0)
        def _():
            for copy in hop_copies(step - 1):
                copy.wait()
            ring_r[step] = (ring_r[step].astype(F32) + next_r[...]).astype(BF)
            ring_l[step] = (ring_l[step].astype(F32) + next_l[...]).astype(BF)
            ring_o[step] = (ring_o[step].astype(F32) + part_out[ring_dp(place + 1 + step)].astype(F32)).astype(BF)
            ring_v[step] = ring_v[step] + vectors[ring_dp(place - 1 - step)]

        for copy in hop_copies(step):
            copy.start()
        @pl.when(step == 0)
        def _():
            lax.fori_loop(0, NB, split, 0)

        pl.when(step < 4)(functools.partial(through, 3 - step, step % 3))

        @pl.when(step == 0)
        def _():
            core[0].start()

        @pl.when(step == 1)
        def _():
            core[0].wait()
            for i in range(4):
                span = pl.ds(i * quarter, quarter)
                share[1, span] = (share[1, span].astype(F32) + core_buf[0, span].astype(F32)).astype(BF)
                far[i].start()

        @pl.when(step == 2)
        def _():
            core[1].start()

        return carry

    lax.fori_loop(0, 7, hop, 0)
    base_copy(0).start()
    base_copy(1).start()
    parts(7)
    for copy in hop_copies(6):
        copy.wait()
    total = jnp.concatenate((ring_r[7].astype(F32) + next_r[...], ring_l[7].astype(F32) + next_l[...]), axis=1)
    for i in range(4):
        row_buf[i] = total[i * rows_w : (i + 1) * rows_w].astype(BF)
    vec_part[...] = ring_v[7] + vectors[dp]
    exchange = []
    for i, peer in enumerate((sibling, across, corner)):
        to = peer["fsdp"]
        copies = [
            send(row_buf.at[to], row_in.at[me], a2a_send.at[i], a2a_recv.at[i], peer),
            send(vec_part.at[to], vec_in.at[me], a2a_send.at[3 + i], a2a_recv.at[3 + i], peer),
        ]
        for copy in copies:
            copy.start()
        exchange += copies
    row_in[me] = row_buf[me]
    vec_in[me] = vec_part[me]
    out_rows[...] = ring_o[7].astype(F32) + part_out[dp].astype(F32)
    core[1].wait()
    for i in range(4):
        span = pl.ds(i * quarter, quarter)
        far[i].wait()
        base_copy(i).wait()
        if i >= 2:
            gs_copy(i - 2).wait()
        gs_b[i % 2] = base_b[i % 2] + (
            share[0, span].astype(F32) + core_buf[1, span].astype(F32) + x_buf[span].astype(F32)
        )
        gs_copy(i).start()
        if i < 2:
            base_copy(i + 2).start()
    for copy in exchange:
        copy.wait()
    vec_own[...] = vec_in[0] + vec_in[1] + vec_in[2] + vec_in[3]
    cols = heads_width // 3
    for which, out in enumerate((g_query, g_key, g_value)):
        out[...] = jnp.concatenate(
            [row_in[i, :, which * cols : (which + 1) * cols].astype(F32) for i in range(4)], axis=1
        )
    for i in (2, 3):
        gs_copy(i).wait()


def last_exchange(order, base, tokens_t, g_qkv, w_t, part_out, vectors):
    rows, width = base.shape
    heads_width = g_qkv.shape[0]
    rows_w = part_out.shape[1]
    chunk = 4 * rows_w
    side = 2 * heads_width // 3
    vmem, hbm = pl.BlockSpec(memory_space=pltpu.VMEM), pl.BlockSpec(memory_space=pl.ANY)
    dma = pltpu.SemaphoreType.DMA
    return pl.pallas_call(
        last_kernel,
        in_specs=[pl.BlockSpec(memory_space=pltpu.SMEM), hbm, hbm, hbm, vmem, vmem, vmem],
        out_specs=[hbm] + [vmem] * 5,
        out_shape=[jax.ShapeDtypeStruct((rows, width), F32)]
        + [jax.ShapeDtypeStruct((rows_w, width), F32)] * 4
        + [jax.ShapeDtypeStruct(vectors.shape[2:], F32)],
        scratch_shapes=[
            pltpu.VMEM(g_qkv.shape, BF),
            pltpu.VMEM((NB, heads_width, BLOCK), BF),
            pltpu.VMEM((2, chunk, tokens_t.shape[1]), BF),
            pltpu.VMEM((2, chunk, tokens_t.shape[1]), BF),
            pltpu.VMEM((3, rows, width), BF),
            pltpu.VMEM((rows, heads_width), BF),
            pltpu.VMEM((2, rows, width), BF),
            pltpu.VMEM((rows, width), BF),
            pltpu.VMEM((2, rows // 4, width), F32),
            pltpu.VMEM((2, rows // 4, width), F32),
            pltpu.VMEM((8, chunk, side), BF),
            pltpu.VMEM((8, chunk, heads_width - side), BF),
            pltpu.VMEM((8, rows_w, width), BF),
            pltpu.VMEM(vectors.shape, F32),
            pltpu.VMEM((chunk, side), F32),
            pltpu.VMEM((chunk, heads_width - side), F32),
            pltpu.VMEM((4, rows_w, heads_width), BF),
            pltpu.VMEM((4, rows_w, heads_width), BF),
            pltpu.VMEM(vectors.shape[1:], F32),
            pltpu.VMEM(vectors.shape[1:], F32),
            dma((1,)),
            dma((2, 2)),
            dma((2, 2)),
            dma((2,)),
            dma((2,)),
            dma((4,)),
            dma((4,)),
            dma((4, 7)),
            dma((4, 7)),
            dma((6,)),
            dma((6,)),
        ],
        compiler_params=pltpu.CompilerParams(
            collective_id=2, has_side_effects=True, vmem_limit_bytes=48 << 20
        ),
        cost_estimate=pl.CostEstimate(flops=13 * 10**9, bytes_accessed=100 << 20, transcendentals=0),
        name="last_exchange",
    )(order, base, tokens_t, g_qkv, w_t, part_out, vectors)


CHUNK = 128
TILE = 256


def tile(index, base=0):
    return pl.ds(pl.multiple_of(base + index * TILE, TILE), TILE)


def nt(a, b):
    return lax.dot_general(a, b, (((1,), (1,)), ((), ())), preferred_element_type=F32)


def middle_kernel(share, states, teacher, weight, mask, w_ug, w_own, rates, scales,
                  w_d, out_states, hidden, attn_unit, back, attn_inv, hidden_inv, sums, gd_all, ht_all, act_all, ug_all,
                  part, core, x_buf, tok, gd, act, act_t, ug, ht,
                  ld_sem, core_send, core_recv, x_send, x_recv, tok_send, tok_recv, gd_send, gd_recv, gd_own,
                  out_sem, ring_send, ring_recv):
    sibling, across, _ = group_peers()
    dp, place = lax.axis_index("dp"), ring_place()
    right, left = {"dp": ring_dp(place + 1)}, {"dp": ring_dp(place - 1)}
    piece = w_own.shape[0]
    count = part.shape[0]
    width = hidden.shape[1]
    rate_attn, rate_mlp = rates[0:1], rates[1:2]

    def rows(i):
        return pl.ds(pl.multiple_of(i * CHUNK, CHUNK), CHUNK)

    def load(i):
        return pltpu.make_async_copy(share.at[:, rows(i)], part.at[i], ld_sem.at[i])

    def core_a(stage, i):
        return send(part.at[i, 3], core.at[0, i], core_send.at[stage, 0, i], core_recv.at[stage, 0, i], sibling)

    def core_b(stage, i):
        return send(part.at[i, 1], core.at[1, i], core_send.at[stage, 1, i], core_recv.at[stage, 1, i], sibling)

    def chip(stage, i):
        return send(part.at[i, 2], x_buf.at[i], x_send.at[stage, i], x_recv.at[stage, i], across)

    def spread(buf, own, sems, recvs, i):
        return [
            send(own, buf.at[i, 1], sems.at[0, i], recvs.at[0, i], sibling),
            send(own, buf.at[i, 2], sems.at[1, i], recvs.at[1, i], across),
            send(buf.at[i, 2], buf.at[i, 3], sems.at[2, i], recvs.at[2, i], sibling),
        ]

    def tok_copies(i):
        return spread(tok, tok.at[i, 0], tok_send, tok_recv, i)

    def gd_copies(i):
        return spread(gd_all, gd.at[i], gd_send, gd_recv, i)

    def gd_local(i):
        return pltpu.make_async_copy(gd.at[i], gd_all.at[i, 0], gd_own.at[i])

    def outs(i):
        slot = i % 2
        return [
            pltpu.make_async_copy(ht.at[slot], ht_all.at[i], out_sem.at[0, slot]),
            pltpu.make_async_copy(act_t.at[slot], act_all.at[i], out_sem.at[1, slot]),
            pltpu.make_async_copy(ug.at[slot], ug_all.at[i], out_sem.at[2, slot]),
        ]

    def ring(step):
        first = rows_at(ring_dp(place - step) * piece, piece // 2)
        second = rows_at(ring_dp(place + step) * piece + piece // 2, piece // 2)
        return [
            send(w_d.at[first], w_d.at[first], ring_send.at[0, step], ring_recv.at[0, step], right),
            send(w_d.at[second], w_d.at[second], ring_send.at[1, step], ring_recv.at[1, step], left),
        ]

    def hop(step, carry):
        for copy in ring(step):
            copy.wait()

        @pl.when(step < 6)
        def _():
            for copy in ring(step + 1):
                copy.start()

        return carry

    def forward_far(stage, i):
        core_a(stage, i).wait_recv()
        part[i, 2] = (part[i, 2].astype(F32) + core[0, i].astype(F32)).astype(BF)
        chip(stage, i).start()

    def reduced(stage, i):
        core_b(stage, i).wait_recv()
        chip(stage, i).wait_recv()
        total = part[i, 0].astype(F32) + core[1, i].astype(F32) + x_buf[i].astype(F32)
        core_a(stage, i).wait_send()
        core_b(stage, i).wait_send()
        chip(stage, i).wait_send()
        return total

    sums[...] = jnp.zeros_like(sums)
    lax.fori_loop(0, count, lambda i, c: (load(i).start(), c)[1], 0)
    w_d[rows_at(dp * piece, piece)] = w_own[...]
    greet([sibling, across, right, left])
    for copy in ring(0):
        copy.start()

    def open_core(i, carry):
        load(i).wait()
        core_a(0, i).start()
        core_b(0, i).start()
        return carry

    lax.fori_loop(0, count, open_core, 0)
    lax.fori_loop(0, count, lambda i, c: (forward_far(0, i), c)[1], 0)

    def norm_hidden(i):
        unit, inverse = unit_rows(reduced(0, i))
        own = states[rows(i)].astype(F32)
        value, value_inv = unit_rows(own + rate_attn * (unit - own))
        hidden[rows(i)] = value
        attn_unit[rows(i)] = unit.astype(BF)
        attn_inv[rows(i)] = inverse
        hidden_inv[rows(i)] = value_inv
        tok[i, 0] = value.astype(BF)
        copies = tok_copies(i)
        copies[0].start()
        copies[1].start()

    def pass_tokens(i):
        copies = tok_copies(i)
        copies[1].wait_recv()
        copies[2].start()

    def feed(i):
        copies = tok_copies(i)
        copies[0].wait()
        copies[1].wait_send()
        copies[2].wait()
        slot = i % 2

        @pl.when(i >= 2)
        def _():
            for copy in outs(i - 2):
                copy.wait()

        def up(n, carry):
            here = tok[i].reshape(4 * CHUNK, width)
            up_proj = nn(here, w_ug[:, tile(n)])
            gate_proj = nn(here, w_ug[:, tile(n, width)])
            gated = gate_proj * scales[1:2, tile(n)]
            value = up_proj * scales[0:1, tile(n)] * (gated * jax.nn.sigmoid(gated))
            act[:, tile(n)] = value.astype(BF)
            act_t[slot, tile(n)] = value.astype(BF).T
            ug[slot, :, tile(n)] = up_proj.astype(BF)
            ug[slot, :, tile(n, width)] = gate_proj.astype(BF)
            return carry

        lax.fori_loop(0, width // TILE, up, 0)

        @pl.when(i == 0)
        def _():
            lax.fori_loop(4, 7, hop, 0)

        def down(n, carry):
            value = nn(act[...], w_d[:, tile(n)])
            part[i, :, :, tile(n)] = value.astype(BF).reshape(4, CHUNK, TILE)
            ht[slot, tile(n)] = tok[i, :, :, tile(n)].reshape(4 * CHUNK, TILE).T
            return carry

        lax.fori_loop(0, width // TILE, down, 0)
        core_a(1, i).start()
        core_b(1, i).start()
        for copy in outs(i):
            copy.start()
        forward_far(1, i)

    def finish(i):
        unit, inverse = unit_rows(reduced(1, i))
        own = hidden[rows(i)]
        result, result_inv = unit_rows(own + rate_mlp * (unit - own))
        out_states[rows(i)] = result.astype(BF)
        diff = result - teacher[rows(i)]
        sums[1:2] = sums[1:2] + jnp.sum(mask[rows(i)] * (diff * diff), axis=0, keepdims=True)
        g_last = unit_back(weight[rows(i)] * diff, result, result_inv)
        sums[0:1] = sums[0:1] + jnp.sum(g_last * (unit - own), axis=0, keepdims=True)
        back[rows(i)] = g_last * (1.0 - rate_mlp)
        gd[i] = unit_back(g_last * rate_mlp, unit, inverse).astype(BF)
        copies = gd_copies(i)
        copies[0].start()
        copies[1].start()
        gd_local(i).start()

    def pass_grads(i):
        copies = gd_copies(i)
        copies[1].wait_recv()
        copies[2].start()

    stages = (norm_hidden, pass_tokens, feed, finish, pass_grads)

    def step(t, carry):
        for lag, stage in enumerate(stages):
            pl.when((t >= lag) & (t < lag + count))(functools.partial(stage, t - lag))

        @pl.when(t < 2)
        def _():
            lax.fori_loop(2 * t, 2 * t + 2, hop, 0)

        return carry

    lax.fori_loop(0, count + len(stages) - 1, step, 0)

    def close(i, carry):
        copies = gd_copies(i)
        copies[0].wait()
        copies[1].wait_send()
        copies[2].wait()
        gd_local(i).wait()
        return carry

    lax.fori_loop(0, count, close, 0)
    for i in (count - 2, count - 1):
        for copy in outs(i):
            copy.wait()


def middle(share, states, teacher, weight, mask, w_ug, w_own, rates, scales):
    rows, width = states.shape
    count = rows // CHUNK
    vmem, hbm = pl.BlockSpec(memory_space=pltpu.VMEM), pl.BlockSpec(memory_space=pl.ANY)
    dma = pltpu.SemaphoreType.DMA
    return pl.pallas_call(
        middle_kernel,
        in_specs=[hbm] + [vmem] * 8,
        out_specs=[vmem] * 8 + [hbm] * 4,
        out_shape=[
            jax.ShapeDtypeStruct((8 * w_own.shape[0], width), BF),
            jax.ShapeDtypeStruct((rows, width), BF),
            jax.ShapeDtypeStruct((rows, width), F32),
            jax.ShapeDtypeStruct((rows, width), BF),
            jax.ShapeDtypeStruct((rows, width), F32),
            jax.ShapeDtypeStruct((rows, 1), F32),
            jax.ShapeDtypeStruct((rows, 1), F32),
            jax.ShapeDtypeStruct((2, width), F32),
            jax.ShapeDtypeStruct((count, 4, CHUNK, width), BF),
            jax.ShapeDtypeStruct((count, width, 4 * CHUNK), BF),
            jax.ShapeDtypeStruct((count, width, 4 * CHUNK), BF),
            jax.ShapeDtypeStruct((count, 4 * CHUNK, 2 * width), BF),
        ],
        scratch_shapes=[
            pltpu.VMEM((count, 4, CHUNK, width), BF),
            pltpu.VMEM((2, count, CHUNK, width), BF),
            pltpu.VMEM((count, CHUNK, width), BF),
            pltpu.VMEM((count, 4, CHUNK, width), BF),
            pltpu.VMEM((count, CHUNK, width), BF),
            pltpu.VMEM((4 * CHUNK, width), BF),
            pltpu.VMEM((2, width, 4 * CHUNK), BF),
            pltpu.VMEM((2, 4 * CHUNK, 2 * width), BF),
            pltpu.VMEM((2, width, 4 * CHUNK), BF),
            dma((count,)),
            dma((2, 2, count)),
            dma((2, 2, count)),
            dma((2, count)),
            dma((2, count)),
            dma((3, count)),
            dma((3, count)),
            dma((3, count)),
            dma((3, count)),
            dma((count,)),
            dma((3, 2)),
            dma((2, 7)),
            dma((2, 7)),
        ],
        compiler_params=pltpu.CompilerParams(
            collective_id=3, has_side_effects=True, vmem_limit_bytes=60 << 20
        ),
        cost_estimate=pl.CostEstimate(flops=26 * 10**9, bytes_accessed=400 << 20, transcendentals=4 << 20),
        name="middle",
    )(share, states, teacher, weight, mask, w_ug, w_own, rates, scales)


def middle_back_kernel(gd_all, act_all, ug_all, hidden, attn_unit, states, back, attn_inv, hidden_inv, w_ug, w_d,
                       rates, scales, base, ga_all, gug_all, down_rows, sums, ff_sums,
                       part, core, x_buf, ga, gd, act, ug, gug, own_f, own_b, base_buf, dwd, column, ring_buf,
                       gd_sem, act_sem, in_sem, own_sem, core_send, core_recv, x_send, x_recv, ga_send, ga_recv,
                       ga_own, base_sem, out_sem, ring_send, ring_recv):
    sibling, across, _ = group_peers()
    dp, place = lax.axis_index("dp"), ring_place()
    right, left = {"dp": ring_dp(place + 1)}, {"dp": ring_dp(place - 1)}
    count = core.shape[1]
    width = w_d.shape[0]
    half = ring_buf.shape[2]
    rate_attn = rates[0:1]

    def rows(i):
        return pl.ds(pl.multiple_of(i * CHUNK, CHUNK), CHUNK)

    def load_gd(i):
        return pltpu.make_async_copy(gd_all.at[i], gd.at[i], gd_sem.at[i])

    def load_act(i):
        return pltpu.make_async_copy(act_all.at[i], act.at[i], act_sem.at[i])

    def load_ug(i):
        return pltpu.make_async_copy(ug_all.at[i], ug.at[i % 2], in_sem.at[i % 2])

    def store_gug(i):
        return pltpu.make_async_copy(gug.at[i % 2], gug_all.at[i], out_sem.at[i % 2])

    def own_rows(i):
        return [
            pltpu.make_async_copy(hidden.at[rows(i)], own_f.at[0], own_sem.at[0]),
            pltpu.make_async_copy(back.at[rows(i)], own_f.at[1], own_sem.at[1]),
            pltpu.make_async_copy(attn_unit.at[rows(i)], own_b.at[0], own_sem.at[2]),
            pltpu.make_async_copy(states.at[rows(i)], own_b.at[1], own_sem.at[3]),
        ]

    def core_a(i):
        return send(part.at[i % 3, 3], core.at[0, i], core_send.at[0, i], core_recv.at[0, i], sibling)

    def core_b(i):
        return send(part.at[i % 3, 1], core.at[1, i], core_send.at[1, i], core_recv.at[1, i], sibling)

    def chip(i):
        return send(part.at[i % 3, 2], x_buf.at[i], x_send.at[i], x_recv.at[i], across)

    def ga_copies(i):
        return [
            send(ga.at[i], ga_all.at[1, rows(i)], ga_send.at[0, i], ga_recv.at[0, i], sibling),
            send(ga.at[i], ga_all.at[2, rows(i)], ga_send.at[1, i], ga_recv.at[1, i], across),
            send(ga_all.at[2, rows(i)], ga_all.at[3, rows(i)], ga_send.at[2, i], ga_recv.at[2, i], sibling),
        ]

    def ga_local(i):
        return pltpu.make_async_copy(ga.at[i], ga_all.at[0, rows(i)], ga_own.at[i])

    def base_copy(i):
        return pltpu.make_async_copy(base_buf.at[i % 2], base.at[rows(i)], base_sem.at[i % 2])

    def right_half(step):
        return rows_at(ring_dp(place - 1 - step) * 2 * half, half)

    def left_half(step):
        return rows_at(ring_dp(place + 1 + step) * 2 * half + half, half)

    def ring(step):
        return [
            send(ring_buf.at[0, step], ring_buf.at[0, step + 1], ring_send.at[0, step], ring_recv.at[0, step], right),
            send(ring_buf.at[1, step], ring_buf.at[1, step + 1], ring_send.at[1, step], ring_recv.at[1, step], left),
        ]

    def hop(step, carry):
        for copy in ring(step):
            copy.wait()

        @pl.when(step < 6)
        def _():
            for side, cut in ((0, right_half(step + 1)), (1, left_half(step + 1))):
                ring_buf[side, step + 1] = (
                    ring_buf[side, step + 1].astype(F32) + dwd[cut].astype(F32)
                ).astype(BF)
            for copy in ring(step + 1):
                copy.start()

        return carry

    for copy in [load_ug(0)] + own_rows(0):
        copy.start()
    lax.fori_loop(0, count, lambda i, c: (load_gd(i).start(), c)[1], 0)
    lax.fori_loop(0, count, lambda i, c: (load_act(i).start(), c)[1], 0)
    sums[...] = jnp.zeros_like(sums)
    ff_sums[...] = jnp.zeros_like(ff_sums)
    greet([sibling, across, right, left])
    lax.fori_loop(0, count, lambda i, c: (load_gd(i).wait(), c)[1], 0)

    def feed(i):
        slot = i % 2
        load_ug(i).wait()

        @pl.when(i + 1 < count)
        def _():
            load_ug(i + 1).start()

        @pl.when(i >= 2)
        def _():
            store_gug(i - 2).wait()

        def grads(n, carry):
            g_act = nt(gd[i].reshape(4 * CHUNK, width), w_d[tile(n)])
            up_proj = ug[slot, :, tile(n)].astype(F32)
            gate_proj = ug[slot, :, tile(n, width)].astype(F32)
            scale_up, scale_gate = scales[0:1, tile(n)], scales[1:2, tile(n)]
            gated = gate_proj * scale_gate
            sigmoid = jax.nn.sigmoid(gated)
            g_upscaled = g_act * (gated * sigmoid)
            g_gated = g_act * (up_proj * scale_up) * sigmoid * (1.0 + gated * (1.0 - sigmoid))
            ff_sums[0:1, tile(n)] = ff_sums[0:1, tile(n)] + jnp.sum(g_upscaled * up_proj, axis=0, keepdims=True)
            ff_sums[1:2, tile(n)] = ff_sums[1:2, tile(n)] + jnp.sum(g_gated * gate_proj, axis=0, keepdims=True)
            gug[slot, :, tile(n)] = (g_upscaled * scale_up).astype(BF)
            gug[slot, :, tile(n, width)] = (g_gated * scale_gate).astype(BF)
            return carry

        lax.fori_loop(0, width // TILE, grads, 0)
        store_gug(i).start()

        def through(n, carry):
            value = nt(gug[slot], w_ug[tile(n)])
            part[i % 3, :, :, tile(n)] = value.astype(BF).reshape(4, CHUNK, TILE)
            return carry

        lax.fori_loop(0, width // TILE, through, 0)
        core_a(i).start()
        core_b(i).start()
        core_a(i).wait_recv()
        part[i % 3, 2] = (part[i % 3, 2].astype(F32) + core[0, i].astype(F32)).astype(BF)
        chip(i).start()

    def down_grads():
        lax.fori_loop(0, count, lambda i, c: (load_act(i).wait(), c)[1], 0)

        def outer(n, carry):
            column[...] = jnp.zeros_like(column)

            def add(k, carry):
                column[...] = column[...] + nn(act[k], gd[k, :, :, tile(n)].reshape(4 * CHUNK, TILE))
                return carry

            lax.fori_loop(0, count, add, 0)
            dwd[:, tile(n)] = column[...].astype(BF)
            return carry

        lax.fori_loop(0, width // TILE, outer, 0)
        ring_buf[0, 0] = dwd[right_half(0)]
        ring_buf[1, 0] = dwd[left_half(0)]
        for copy in ring(0):
            copy.start()

    def finish(i):
        core_b(i).wait_recv()
        chip(i).wait_recv()
        through = part[i % 3, 0].astype(F32) + core[1, i].astype(F32) + x_buf[i].astype(F32)
        core_a(i).wait_send()
        core_b(i).wait_send()
        chip(i).wait_send()
        for copy in own_rows(i):
            copy.wait()
        value, unit, own = own_f[0], own_b[0].astype(F32), own_b[1].astype(F32)
        g_pre = unit_back(own_f[1] + through, value, hidden_inv[rows(i)])

        @pl.when(i + 1 < count)
        def _():
            for copy in own_rows(i + 1):
                copy.start()

        @pl.when(i >= 2)
        def _():
            base_copy(i - 2).wait()

        base_buf[i % 2] = g_pre * (1.0 - rate_attn)
        base_copy(i).start()
        sums[0:1] = sums[0:1] + jnp.sum(g_pre * (unit - own), axis=0, keepdims=True)
        ga[i] = unit_back(g_pre * rate_attn, unit, attn_inv[rows(i)]).astype(BF)
        copies = ga_copies(i)
        copies[0].start()
        copies[1].start()
        ga_local(i).start()

    def pass_grads(i):
        copies = ga_copies(i)
        copies[1].wait_recv()
        copies[2].start()

    stages = (feed, finish, pass_grads)

    def step(t, carry):
        for lag, stage in enumerate(stages):
            pl.when((t >= lag) & (t < lag + count))(functools.partial(stage, t - lag))
        pl.when(t == 0)(down_grads)

        @pl.when((t >= 1) & (t < 4))
        def _():
            lax.fori_loop(2 * t - 2, 2 * t, hop, 0)

        return carry

    lax.fori_loop(0, count + len(stages) - 1, step, 0)
    hop(6, 0)
    own = dp * 2 * half
    down_rows[pl.ds(0, half)] = ring_buf[0, 7].astype(F32) + dwd[rows_at(own, half)].astype(F32)
    down_rows[pl.ds(half, half)] = ring_buf[1, 7].astype(F32) + dwd[rows_at(own + half, half)].astype(F32)

    def close(i, carry):
        copies = ga_copies(i)
        copies[0].wait()
        copies[1].wait_send()
        copies[2].wait()
        ga_local(i).wait()
        return carry

    lax.fori_loop(0, count, close, 0)
    for i in (count - 2, count - 1):
        base_copy(i).wait()
        store_gug(i).wait()


def middle_back(gd_all, act_all, ug_all, hidden, attn_unit, states, back, attn_inv, hidden_inv, w_ug, w_d, rates,
                scales):
    rows, width = states.shape
    count = rows // CHUNK
    piece = width // 8
    vmem, hbm = pl.BlockSpec(memory_space=pltpu.VMEM), pl.BlockSpec(memory_space=pl.ANY)
    dma = pltpu.SemaphoreType.DMA
    return pl.pallas_call(
        middle_back_kernel,
        in_specs=[hbm] * 7 + [vmem] * 6,
        out_specs=[hbm, hbm, hbm, vmem, vmem, vmem],
        out_shape=[
            jax.ShapeDtypeStruct((rows, width), F32),
            jax.ShapeDtypeStruct((4, rows, width), BF),
            jax.ShapeDtypeStruct((count, 4 * CHUNK, 2 * width), BF),
            jax.ShapeDtypeStruct((piece, width), F32),
            jax.ShapeDtypeStruct((1, width), F32),
            jax.ShapeDtypeStruct((2, width), F32),
        ],
        scratch_shapes=[
            pltpu.VMEM((3, 4, CHUNK, width), BF),
            pltpu.VMEM((2, count, CHUNK, width), BF),
            pltpu.VMEM((count, CHUNK, width), BF),
            pltpu.VMEM((count, CHUNK, width), BF),
            pltpu.VMEM((count, 4, CHUNK, width), BF),
            pltpu.VMEM((count, width, 4 * CHUNK), BF),
            pltpu.VMEM((2, 4 * CHUNK, 2 * width), BF),
            pltpu.VMEM((2, 4 * CHUNK, 2 * width), BF),
            pltpu.VMEM((2, CHUNK, width), F32),
            pltpu.VMEM((2, CHUNK, width), BF),
            pltpu.VMEM((2, CHUNK, width), F32),
            pltpu.VMEM((width, width), BF),
            pltpu.VMEM((width, TILE), F32),
            pltpu.VMEM((2, 8, piece // 2, width), BF),
            dma((count,)),
            dma((count,)),
            dma((2,)),
            dma((4,)),
            dma((2, count)),
            dma((2, count)),
            dma((count,)),
            dma((count,)),
            dma((3, count)),
            dma((3, count)),
            dma((count,)),
            dma((2,)),
            dma((2,)),
            dma((2, 7)),
            dma((2, 7)),
        ],
        compiler_params=pltpu.CompilerParams(
            collective_id=4, has_side_effects=True, vmem_limit_bytes=60 << 20
        ),
        cost_estimate=pl.CostEstimate(flops=34 * 10**9, bytes_accessed=200 << 20, transcendentals=4 << 20),
        name="middle_back",
    )(gd_all, act_all, ug_all, hidden, attn_unit, states, back, attn_inv, hidden_inv, w_ug, w_d, rates, scales)


def order_kernel(where_ref, parent_ref, out_ref):
    base, me = where_ref[0], where_ref[1]
    shape = (128, 128)
    row = lax.broadcasted_iota(jnp.int32, shape, 0)
    block = lax.broadcasted_iota(jnp.int32, (8, 128), 1)
    real = block < NB
    parent = jnp.where(real & (parent_ref[...] >= 0), parent_ref[...] - base, -1)
    up = (row == parent[0:1]).astype(F32)
    up2 = nn(up, up)
    near = up + up2
    up4 = nn(up2, up2)
    near = near + nn(near, up2)
    near = near + nn(near, up4)
    above = near + nn(nn(up4, up4), up)
    depth = jnp.broadcast_to(jnp.sum(above, axis=0, keepdims=True), (8, 128)).astype(jnp.int32)
    before = (row < lax.broadcasted_iota(jnp.int32, shape, 1)).astype(F32)
    rank = nn(((depth == TRUNK) & real).astype(F32), before)
    parent_rank = nn(rank, up).astype(jnp.int32)
    sibling = jnp.sum(nn(up.T, up) * before, axis=0, keepdims=True).astype(jnp.int32)
    leaf = TRUNK + 4 + 2 * parent_rank + sibling
    slot = jnp.where(depth < TRUNK, depth, jnp.where(depth == TRUNK, TRUNK + rank.astype(jnp.int32), leaf))
    slot = jnp.where(real, slot, 127)
    mine = jnp.where(real, jnp.bitwise_xor(block // 5, me) * 5 + block % 5, 127)
    order = nt(mine.astype(F32), (row == slot[0:1]).astype(F32))
    back = nt(slot.astype(F32), (row == mine[0:1]).astype(F32))
    which = lax.broadcasted_iota(jnp.int32, (8, 128), 0)
    out_ref[...] = jnp.where(which == 0, order, back).astype(jnp.int32)


def tree_order(where, parents):
    return pl.pallas_call(
        order_kernel,
        in_specs=[pl.BlockSpec(memory_space=pltpu.SMEM), pl.BlockSpec(memory_space=pltpu.VMEM)],
        out_specs=pl.BlockSpec(memory_space=pltpu.VMEM),
        out_shape=jax.ShapeDtypeStruct((8, 128), jnp.int32),
        name="tree_order",
    )(where, jnp.broadcast_to(jnp.pad(parents, (0, 128 - NB), constant_values=-1), (8, 128)))


def local(
    states,
    teacher,
    parent_ids,
    valid_mask,
    w_query,
    w_key,
    w_value,
    w_out,
    w_up,
    w_gate,
    w_down,
    qk_scale,
    attn_rate,
    mlp_rate,
    up_scale,
    gate_scale,
):
    both = ("dp", "fsdp")
    dps, tps = 8, 4
    rows_w = w_query.shape[0]
    cols = D // tps
    hid = FF // tps
    ff_rows = FF // (dps * tps)
    me = lax.axis_index("fsdp")
    root_width = math.sqrt(D)
    mask_f = valid_mask.astype(F32)
    group_base = lax.axis_index("dp") * NB
    order = tree_order(jnp.stack((group_base, me)).astype(jnp.int32), parent_ids)

    count = jnp.sum(valid_mask)
    first_row = jnp.arange(rows_w, dtype=jnp.int32) == 0
    small = jnp.stack(
        (
            qk_scale,
            attn_rate,
            mlp_rate,
            jnp.where(first_row, count // 128, 0).astype(BF),
            jnp.where(first_row, count % 128, 0).astype(BF),
        ),
        axis=1,
    )
    small = jnp.pad(small, ((0, 0), (0, 59)))
    qkv_send = jnp.concatenate(
        [w.reshape(rows_w, tps, cols).transpose(1, 0, 2) for w in (w_query, w_key, w_value)]
        + [jnp.broadcast_to(small[None], (tps, rows_w, 64))],
        axis=2,
    )
    extra = jnp.pad(jnp.stack((up_scale, gate_scale), axis=1), ((0, 0), (69, 57)))
    spread = [(j, tps * (j % dps) + j // dps) for j in range(dps * tps)]
    ug_send = jnp.concatenate(
        [
            w.reshape(rows_w, dps, tps, ff_rows).transpose(2, 0, 1, 3).reshape(tps, rows_w, hid)
            for w in (w_up, w_gate)
        ],
        axis=2,
    )
    tokens_t, w_t, w_o, w_ug, qkv, mixed, sums, share = forward(
        order, states, qkv_send, extra, lax.ppermute(w_out, both, spread), ug_send
    )
    small_all = w_t[3 * cols : 3 * cols + 8].astype(F32)
    rates = small_all[1:3]
    valid_count = 128.0 * jnp.sum(small_all[3]) + jnp.sum(small_all[4])
    scales = small_all[5:7] * jnp.array([[1.0], [root_width]], F32)
    scale_qk = lax.dynamic_slice_in_dim(small_all[0], me * cols, cols).reshape(cols // HEAD_DIM, HEAD_DIM, 1)

    mask_col = mask_f[:, None]
    w_d, out_states, hidden, attn_unit, back, attn_inv, hidden_inv, sums_mid, gd_all, ht_all, act_all, ug_all = middle(
        share, states, teacher, mask_col * (2.0 / valid_count), mask_col, w_ug, w_down, rates, scales
    )
    base, ga_all, gug_all, grad_down, sums_back, ff_sums = middle_back(
        gd_all, act_all, ug_all, hidden, attn_unit, states, back, attn_inv, hidden_inv, w_ug, w_d, rates, scales
    )
    loss_local = jnp.sum(sums_mid[1])
    g_rate_mlp, g_rate_attn = sums_mid[0], sums_back[0]
    grad_up_scale, grad_gate_scale = ff_sums[0], ff_sums[1] * root_width
    g_qkv, g_scale, part_out, grad_up, grad_gate = attention_back(
        order, qkv, scale_qk, sums, mixed, ga_all.reshape(NB, BLOCK, D), w_o, ht_all, gug_all
    )
    g_qkv = g_qkv.reshape(3 * cols, TOK)
    slot = jnp.arange(tps, dtype=jnp.int32) == me
    qk_rows = jnp.where(slot[:, None], g_scale.reshape(1, cols), 0.0).reshape(dps * tps, rows_w)
    ff_terms = [
        jnp.where(slot[None, :, None], term.reshape(dps, 1, ff_rows), 0.0).reshape(dps * tps, ff_rows)
        for term in (grad_up_scale, grad_gate_scale)
    ]
    vectors = jnp.concatenate(
        [g_rate_attn.reshape(dps * tps, rows_w), g_rate_mlp.reshape(dps * tps, rows_w), qk_rows]
        + ff_terms
        + [jnp.broadcast_to(loss_local, (dps * tps, 512 - 3 * rows_w - 2 * ff_rows))],
        axis=1,
    ).reshape(dps, tps, 4, 128)
    part_out = part_out.reshape(dps, rows_w, D)
    grad_states, g_query, g_key, g_value, out_back, vector_share = last_exchange(
        order, base, tokens_t, g_qkv, w_t, part_out, vectors
    )
    vector_share = vector_share.reshape(512)
    grad_out = lax.ppermute(out_back, both, [(b, a) for a, b in spread])
    cuts = (0, rows_w, 2 * rows_w, 3 * rows_w, 3 * rows_w + ff_rows, 3 * rows_w + 2 * ff_rows)
    v = [vector_share[a:b] for a, b in zip(cuts, cuts[1:])]
    return (
        out_states,
        vector_share[-1] / valid_count,
        grad_states,
        g_query,
        g_key,
        g_value,
        grad_out,
        grad_up,
        grad_gate,
        grad_down,
        v[2],
        v[0],
        v[1],
        v[3],
        v[4],
    )


def solution(mesh):
    placed = (
        P(("dp", "fsdp"), None),
        P(("dp", "fsdp"), None),
        P("dp"),
        P(("dp", "fsdp")),
        P(("dp", "fsdp"), None),
        P(("dp", "fsdp"), None),
        P(("dp", "fsdp"), None),
        P(("dp", "fsdp"), None),
        P(("dp", "fsdp"), None),
        P(("dp", "fsdp"), None),
        P(("dp", "fsdp"), None),
        P(("dp", "fsdp")),
        P(("dp", "fsdp")),
        P(("dp", "fsdp")),
        P(("dp", "fsdp")),
        P(("dp", "fsdp")),
    )
    quick = mesh.shape["fsdp"] == 4 and mesh.shape["dp"] == 8
    return jax.shard_map(
        local if quick else general,
        mesh=mesh,
        in_specs=placed,
        out_specs=(
            P(("dp", "fsdp"), None),
            P(),
            P(("dp", "fsdp"), None),
            P(("dp", "fsdp"), None),
            P(("dp", "fsdp"), None),
            P(("dp", "fsdp"), None),
            P(("dp", "fsdp"), None),
            P(("dp", "fsdp"), None),
            P(("dp", "fsdp"), None),
            P(("dp", "fsdp"), None),
            P(("dp", "fsdp")),
            P(("dp", "fsdp")),
            P(("dp", "fsdp")),
            P(("dp", "fsdp")),
            P(("dp", "fsdp")),
        ),
        check_vma=False,
    )
```

```python
import functools
import math

import jax
import jax.numpy as jnp
from jax import lax
from jax.experimental import pallas as pl
from jax.experimental.pallas import tpu as pltpu
from jax.sharding import PartitionSpec as P


D = 1280
HEADS = 20
HEAD_DIM = 64
FF = 5120
BLOCK = 128
DEPTH = 10


EPS = 1e-06


def unit_rows(vector):
    inverse = lax.rsqrt(jnp.sum(vector * vector, axis=-1, keepdims=True) + EPS)
    return (vector * inverse, inverse)


def unit_back(grad, unit, inverse):
    return (grad - unit * jnp.sum(grad * unit, axis=-1, keepdims=True)) * inverse


def project(left, right):
    return jnp.dot(left, right, preferred_element_type=jnp.float32)


def project_back(grad, weight):
    return jnp.einsum("te,de->td", grad, weight, preferred_element_type=jnp.float32)


def ancestors(local_parent):
    column = jnp.arange(local_parent.shape[0], dtype=jnp.int32)
    columns = [column]
    for depth_step in range(DEPTH - 1):
        column = jnp.where(column >= 0, local_parent[jnp.maximum(column, 0)], -1)
        columns.append(column)
    return jnp.stack(columns, axis=1)


def head_back(grad_flat, unit, inverse, scale):
    scaled = (grad_flat * scale).reshape(unit.shape)
    raw = unit_back(scaled, unit, inverse).reshape(grad_flat.shape)
    scale_grad = jnp.sum(grad_flat * unit.reshape(grad_flat.shape), axis=0)
    return (raw, scale_grad)


def general(
    states,
    teacher,
    parent_ids,
    valid_mask,
    w_query,
    w_key,
    w_value,
    w_out,
    w_up,
    w_gate,
    w_down,
    qk_scale,
    attn_rate,
    mlp_rate,
    up_scale,
    gate_scale,
):
    rows_dev = states.shape[0]
    blocks_dev = rows_dev // BLOCK
    width_rows = w_query.shape[0]
    span = DEPTH * BLOCK
    factor = math.sqrt(HEAD_DIM)
    root_width = math.sqrt(D)
    mask_f = valid_mask.astype(jnp.float32)
    qkv_local = jnp.concatenate((w_query, w_key, w_value), axis=1)
    scal_width_local = jnp.stack((qk_scale, attn_rate, mlp_rate), axis=1)
    piece_qkv = lax.all_gather(qkv_local, ("dp", "fsdp"), axis=0, tiled=True)
    piece_out = lax.all_gather(w_out, ("dp", "fsdp"), axis=0, tiled=True)
    piece_scal = lax.all_gather(scal_width_local, ("dp", "fsdp"), axis=0, tiled=True)
    lefts = states
    total = jnp.dot(lefts, piece_qkv, preferred_element_type=jnp.float32)
    scal_whole = piece_scal
    qkv_raw = total
    scal_width = scal_whole
    scale_qk = scal_width[:, 0].astype(jnp.float32)
    rate_attn = scal_width[:, 1].astype(jnp.float32)
    rate_mlp = scal_width[:, 2].astype(jnp.float32)
    query_raw = qkv_raw[:, :D]
    key_raw = qkv_raw[:, D : 2 * D]
    values = qkv_raw[:, 2 * D :].astype(jnp.bfloat16)
    query_unit, query_inv = unit_rows(query_raw.reshape(rows_dev, HEADS, HEAD_DIM))
    key_unit, key_inv = unit_rows(key_raw.reshape(rows_dev, HEADS, HEAD_DIM))
    query_n = (query_unit.reshape(rows_dev, D) * scale_qk).astype(jnp.bfloat16)
    key_n = (key_unit.reshape(rows_dev, D) * scale_qk).astype(jnp.bfloat16)
    key_group, value_group = (
        lax.all_gather(key_n, "fsdp", axis=0, tiled=True),
        lax.all_gather(values, "fsdp", axis=0, tiled=True),
    )
    group_blocks = parent_ids.shape[0]
    group_base = lax.axis_index("dp") * group_blocks
    local_parent = jnp.where(parent_ids >= 0, parent_ids - group_base, -1)
    paths_all = ancestors(local_parent)
    own_first = lax.axis_index("fsdp") * blocks_dev
    paths = lax.dynamic_slice_in_dim(paths_all, own_first, blocks_dev, 0)
    safe_paths = jnp.maximum(paths, 0)
    key_rows = key_group.reshape(group_blocks, BLOCK, D)[safe_paths].reshape(
        blocks_dev, span, HEADS, HEAD_DIM
    )
    value_rows = value_group.reshape(group_blocks, BLOCK, D)[safe_paths].reshape(
        blocks_dev, span, HEADS, HEAD_DIM
    )
    slot_of = jnp.arange(span, dtype=jnp.int32) // BLOCK
    offset = jnp.arange(span, dtype=jnp.int32) % BLOCK
    row_pos = jnp.arange(BLOCK, dtype=jnp.int32)
    causal = offset[None, :] <= row_pos[:, None]
    is_live = jnp.take(paths, slot_of, axis=1) >= 0
    allowed = jnp.where(slot_of[None, None, :] == 0, causal[None], is_live[:, None, :])[:, None]
    query_heads = query_n.reshape(blocks_dev, BLOCK, HEADS, HEAD_DIM)
    scores = factor * jnp.einsum(
        "bqhd,bkhd->bhqk", query_heads, key_rows, preferred_element_type=jnp.float32
    )
    scores = jnp.where(allowed, scores, jnp.float32(-1e30))
    row_max = jnp.max(scores, axis=-1, keepdims=True)
    powers = jnp.exp(scores - row_max)
    row_sum = jnp.sum(powers, axis=-1, keepdims=True)
    probs_b = (powers / row_sum).astype(jnp.bfloat16)
    log_total = row_max + jnp.log(row_sum)
    mixed = jnp.einsum("bhqk,bkhd->bqhd", probs_b, value_rows, preferred_element_type=jnp.float32)
    mixed = mixed.reshape(rows_dev, D).astype(jnp.bfloat16)
    inputs = states.astype(jnp.float32)
    attn = project(mixed, piece_out)
    attn_unit, attn_inv = unit_rows(attn)
    hidden, hidden_inv = unit_rows(inputs + rate_attn * (attn_unit - inputs))
    hidden_b = hidden.astype(jnp.bfloat16)
    ffn_local = jnp.concatenate((w_up, w_gate), axis=1)
    scal_hidden_local = jnp.concatenate(
        (up_scale.reshape(width_rows, 4), gate_scale.reshape(width_rows, 4)), axis=1
    )
    piece_ffn = lax.all_gather(ffn_local, ("dp", "fsdp"), axis=0, tiled=True)
    piece_scal = lax.all_gather(scal_hidden_local, ("dp", "fsdp"), axis=0, tiled=True)
    lefts = hidden_b
    total = jnp.dot(lefts, piece_ffn, preferred_element_type=jnp.float32)
    scal_whole = piece_scal
    scale_up = scal_whole[:, :4].reshape(FF).astype(jnp.float32)
    scale_gate = scal_whole[:, 4:].reshape(FF).astype(jnp.float32)
    up_proj = total[:, :FF]
    gate_proj = total[:, FF:]
    upscaled = up_proj * scale_up
    gated = gate_proj * scale_gate * root_width
    sigmoid_gate = jax.nn.sigmoid(gated)
    act = (upscaled * (gated * sigmoid_gate)).astype(jnp.bfloat16)
    lefts = act
    down = jnp.dot(
        lefts,
        lax.all_gather(w_down, ("dp", "fsdp"), axis=0, tiled=True),
        preferred_element_type=jnp.float32,
    )
    down_unit, down_inv = unit_rows(down)
    result, result_inv = unit_rows(hidden + rate_mlp * (down_unit - hidden))
    loss_local = jnp.sum(mask_f[:, None] * (result - teacher) ** 2)
    valid_count, loss_sum = lax.psum((jnp.sum(mask_f), loss_local), ("dp", "fsdp"))
    loss = loss_sum / valid_count
    g_result = 2.0 * mask_f[:, None] * (result - teacher) / valid_count
    g_last = unit_back(g_result, result, result_inv)
    g_hidden = g_last * (1.0 - rate_mlp)
    g_rate_mlp = jnp.sum(g_last * (down_unit - hidden), axis=0)
    g_down = unit_back(g_last * rate_mlp, down_unit, down_inv).astype(jnp.bfloat16)
    g_act = jnp.einsum(
        "te,fe->tf",
        g_down,
        lax.all_gather(w_down, ("dp", "fsdp"), axis=0, tiled=True),
        preferred_element_type=jnp.float32,
    )
    g_upscaled = g_act * (gated * sigmoid_gate)
    g_gated = g_act * upscaled * sigmoid_gate * (1.0 + gated * (1.0 - sigmoid_gate))
    grad_up_scale = jnp.sum(g_upscaled * up_proj, axis=0)
    grad_gate_scale = jnp.sum(g_gated * gate_proj * root_width, axis=0)
    g_up = (g_upscaled * scale_up).astype(jnp.bfloat16)
    g_gate = (g_gated * scale_gate * root_width).astype(jnp.bfloat16)
    g_both = jnp.concatenate((g_up, g_gate), axis=1)
    g_hidden = g_hidden + jnp.einsum(
        "tc,dc->td",
        g_both,
        lax.all_gather(ffn_local, ("dp", "fsdp"), axis=0, tiled=True),
        preferred_element_type=jnp.float32,
    )
    scal_terms = jnp.concatenate(
        (grad_up_scale.reshape(D, 4), grad_gate_scale.reshape(D, 4)), axis=1
    )
    lefts = hidden_b
    main = jnp.einsum("td,tc->dc", lefts, g_both, preferred_element_type=jnp.float32)
    ffn_share = lax.psum_scatter(
        jnp.concatenate((main, scal_terms), axis=1), ("dp", "fsdp"), scatter_dimension=0, tiled=True
    )
    lefts = act
    grad_down = lax.psum_scatter(
        jnp.einsum("tf,te->fe", lefts, g_down, preferred_element_type=jnp.float32),
        ("dp", "fsdp"),
        scatter_dimension=0,
        tiled=True,
    )
    g_pre = unit_back(g_hidden, hidden, hidden_inv)
    g_states = g_pre * (1.0 - rate_attn)
    g_rate_attn = jnp.sum(g_pre * (attn_unit - inputs), axis=0)
    g_attn = unit_back(g_pre * rate_attn, attn_unit, attn_inv).astype(jnp.bfloat16)
    g_mixed = project_back(g_attn, piece_out).astype(jnp.bfloat16)
    scores = factor * jnp.einsum(
        "bqhd,bkhd->bhqk", query_heads, key_rows, preferred_element_type=jnp.float32
    )
    probs = jnp.where(allowed, jnp.exp(scores - log_total), jnp.float32(0.0))
    probs_again = probs.astype(jnp.bfloat16)
    g_heads = g_mixed.reshape(blocks_dev, BLOCK, HEADS, HEAD_DIM)
    g_probs = jnp.einsum("bqhd,bkhd->bhqk", g_heads, value_rows, preferred_element_type=jnp.float32)
    delta = jnp.sum(probs * g_probs, axis=-1, keepdims=True)
    g_scores = (probs * (g_probs - delta)).astype(jnp.bfloat16)
    g_query_n = factor * jnp.einsum(
        "bhqk,bkhd->bqhd", g_scores, key_rows, preferred_element_type=jnp.float32
    )
    g_key_rows = factor * jnp.einsum(
        "bhqk,bqhd->bkhd", g_scores, query_heads, preferred_element_type=jnp.float32
    )
    g_value_rows = jnp.einsum(
        "bhqk,bqhd->bkhd", probs_again, g_heads, preferred_element_type=jnp.float32
    )
    flat_paths = safe_paths.reshape(blocks_dev * DEPTH)
    g_key_group = (
        jnp.zeros((group_blocks, BLOCK, D), jnp.float32)
        .at[flat_paths]
        .add(g_key_rows.reshape(blocks_dev * DEPTH, BLOCK, D))
    )
    g_value_group = (
        jnp.zeros((group_blocks, BLOCK, D), jnp.float32)
        .at[flat_paths]
        .add(g_value_rows.reshape(blocks_dev * DEPTH, BLOCK, D))
    )
    g_key_n, g_values = (
        lax.psum_scatter(
            g_key_group.reshape(group_blocks * BLOCK, D).astype(jnp.bfloat16),
            "fsdp",
            scatter_dimension=0,
            tiled=True,
        ).astype(jnp.float32),
        lax.psum_scatter(
            g_value_group.reshape(group_blocks * BLOCK, D).astype(jnp.bfloat16),
            "fsdp",
            scatter_dimension=0,
            tiled=True,
        ).astype(jnp.float32),
    )
    g_query_raw, scale_from_query = head_back(
        g_query_n.reshape(rows_dev, D), query_unit, query_inv, scale_qk
    )
    g_key_raw, scale_from_key = head_back(g_key_n, key_unit, key_inv, scale_qk)
    grad_qk_scale = scale_from_query + scale_from_key
    g_qkv = jnp.concatenate(
        (
            g_query_raw.astype(jnp.bfloat16),
            g_key_raw.astype(jnp.bfloat16),
            g_values.astype(jnp.bfloat16),
        ),
        axis=1,
    )
    g_states = g_states + jnp.einsum(
        "tc,dc->td",
        g_qkv,
        lax.all_gather(qkv_local, ("dp", "fsdp"), axis=0, tiled=True),
        preferred_element_type=jnp.float32,
    )
    vector_terms = jnp.stack((grad_qk_scale, g_rate_attn, g_rate_mlp), axis=1)
    lefts = states
    main = jnp.einsum("td,tc->dc", lefts, g_qkv, preferred_element_type=jnp.float32)
    outer = jnp.einsum("td,tc->dc", mixed, g_attn, preferred_element_type=jnp.float32)
    attn_share = lax.psum_scatter(
        jnp.concatenate((main, outer, vector_terms), axis=1),
        ("dp", "fsdp"),
        scatter_dimension=0,
        tiled=True,
    )
    return (
        result.astype(jnp.bfloat16),
        loss,
        g_states,
        attn_share[:, :D],
        attn_share[:, D : 2 * D],
        attn_share[:, 2 * D : 3 * D],
        attn_share[:, 3 * D : 4 * D],
        ffn_share[:, :FF],
        ffn_share[:, FF : 2 * FF],
        grad_down,
        attn_share[:, 4 * D],
        attn_share[:, 4 * D + 1],
        attn_share[:, 4 * D + 2],
        ffn_share[:, 2 * FF : 2 * FF + 4].reshape(-1),
        ffn_share[:, 2 * FF + 4 : 2 * FF + 8].reshape(-1),
    )

TRUNK = 8
NB = 20
TOK = NB * BLOCK
F32 = jnp.float32
BF = jnp.bfloat16


def head_norm(raw):
    inv = lax.rsqrt(jnp.sum(raw * raw, axis=0, keepdims=True) + EPS)
    return raw * inv, inv


def lanes_at(start, size):
    return pl.ds(pl.multiple_of(start, 128), size)


def rows_at(start, size):
    return pl.ds(pl.multiple_of(start, 16), size)


def early_chunks(visit):
    for j in range(TRUNK // 2):
        parts = [(0, 256 * j, "all")] if j else []
        visit(256 * j, parts + [(256 * j, 256, "causal")])
    trunk = TRUNK * BLOCK
    for start in (trunk, trunk + 256):
        visit(start, [(0, trunk, "all"), (start, 256, "pair")])


def late_chunks(visit):
    trunk = TRUNK * BLOCK
    for j in range(4):
        start = trunk + 4 * BLOCK + 256 * j
        visit(start, [(0, trunk, "all"), (trunk + BLOCK * j, BLOCK, "all"), (start, 256, "pair")])


def masked(kind, value):
    if kind == "all":
        return value
    key = lax.broadcasted_iota(jnp.int32, (256, 256), 0)
    query = lax.broadcasted_iota(jnp.int32, (256, 256), 1)
    keep = key <= query
    if kind == "pair":
        keep = keep & ((key < 128) == (query < 128))
    return jnp.where(keep, value, jnp.zeros_like(value))


def nn(a, b):
    return lax.dot_general(a, b, (((1,), (0,)), ((), ())), preferred_element_type=F32)


def nt(a, b):
    return lax.dot_general(a, b, (((1,), (1,)), ((), ())), preferred_element_type=F32)


def attention_back_kernel(order, qkv, scales, sums, mixed, ga_all, w_o, ht_all, gug_all,
                          g_qkv, g_scale, part_out, g_up, g_gate,
                          ga_b, ga, gm, raw, out_b, qT, q, k, kT, v, gT, g, dq, dk, dv, delta, inv,
                          gug_b, ht_r, ht_l, ring, own, hid_buf, hid_in,
                          ga_sem, gug_sem, row_sem, raw_sem, out_sem, ring_send, ring_recv, a2a_send, a2a_recv):
    me = lax.axis_index("fsdp")
    place = ring_place()
    peers = group_peers()
    right, left = {"dp": ring_dp(place + 1)}, {"dp": ring_dp(place - 1)}
    count, chunk, side = gug_b.shape[0], ring.shape[3], ring.shape[4]
    heads = g_scale.shape[0]
    rows_w = hid_buf.shape[1]

    def slices(step):
        slot = step % 2
        cut_r = rows_at(ring_dp(place - 1 - step) * chunk, chunk)
        cut_l = rows_at(ring_dp(place + 1 + step) * chunk, chunk)
        return [
            pltpu.make_async_copy(ht_all.at[:, cut_r], ht_r.at[slot], row_sem.at[0, slot]),
            pltpu.make_async_copy(ht_all.at[:, cut_l], ht_l.at[slot], row_sem.at[1, slot]),
        ]

    def raw_copy(head):
        slot = head % 2
        return pltpu.make_async_copy(
            qkv.at[:, rows_at(head * HEAD_DIM, HEAD_DIM)], raw.at[slot], raw_sem.at[slot]
        )

    def out_copy(head):
        slot = head % 2
        return pltpu.make_async_copy(
            out_b.at[slot], g_qkv.at[:, rows_at(head * HEAD_DIM, HEAD_DIM)], out_sem.at[slot]
        )

    load_ga = pltpu.make_async_copy(ga_all, ga_b, ga_sem.at[0])
    load_ga.start()
    raw_copy(0).start()
    for copy in slices(0):
        copy.start()
    loads = [pltpu.make_async_copy(gug_all.at[i], gug_b.at[i], gug_sem.at[i]) for i in range(count)]
    for copy in loads:
        copy.start()
    for copy in slices(1):
        copy.start()
    greet([*peers, right, left])
    load_ga.wait()

    def pick(i, carry):
        ga[lanes_at(i * BLOCK, BLOCK)] = ga_b[order[0, i]]
        return carry

    lax.fori_loop(0, NB, pick, 0)

    def back(n, carry):
        gm[:, tile(n)] = nt(w_o[...], ga[tile(n)]).astype(BF)
        return carry

    lax.fori_loop(0, TOK // TILE, back, 0)

    def outer(n, carry):
        part_out[:, tile(n)] = nn(mixed[...], ga[:, tile(n)]).astype(BF)
        return carry

    lax.fori_loop(0, D // TILE, outer, 0)

    def parts(step, which):
        slot = step % 2

        @pl.when(which == 0)
        def _():
            for copy in slices(step):
                copy.wait()

        own[...] = jnp.zeros_like(own)

        def add(i, carry):
            for d, rows in enumerate((ht_r, ht_l)):
                cut = lanes_at((2 * d + which) * side, side)
                own[d] = own[d] + nn(rows[slot, i], gug_b[i, :, cut])
            return carry

        lax.fori_loop(0, count, add, 0)

        @pl.when((which == 1) & (step + 2 < 8))
        def _():
            for copy in slices(step + 2):
                copy.start()

    def hop_copies(step, which):
        return [
            send(ring.at[d, which, step], ring.at[d, which, step + 1], ring_send.at[d, which, step],
                 ring_recv.at[d, which, step], peer)
            for d, peer in enumerate((right, left))
        ]

    def exchange():
        return [
            send(hid_buf.at[peer["fsdp"]], hid_in.at[me], a2a_send.at[i], a2a_recv.at[i], peer)
            for i, peer in enumerate(peers)
        ]

    def poll(index):
        step, which = index // 2, index % 2
        parts(step + 1, which)
        for copy in hop_copies(step, which):
            copy.wait()

        @pl.when(step < 6)
        def _():
            for d in range(2):
                ring[d, which, step + 1] = (ring[d, which, step + 1].astype(F32) + own[d]).astype(BF)
            for copy in hop_copies(step + 1, which):
                copy.start()

        @pl.when(step == 6)
        def _():
            for d in range(2):
                total = ring[d, which, 7].astype(F32) + own[d]
                for i in range(4):
                    hid_buf[i, :, lanes_at((2 * d + which) * side, side)] = total[
                        i * rows_w : (i + 1) * rows_w
                    ].astype(BF)

        @pl.when(index == 13)
        def _():
            for copy in exchange():
                copy.start()

    for copy in loads:
        copy.wait()

    def begin(which, carry):
        parts(0, which)
        for d in range(2):
            ring[d, which, 0] = own[d].astype(BF)
        for copy in hop_copies(0, which):
            copy.start()
        return carry

    lax.fori_loop(0, 2, begin, 0)

    def open_head(head):
        slot = head % 2
        raw_copy(head).wait()

        @pl.when(head + 1 < heads)
        def _():
            raw_copy(head + 1).start()

        @pl.when(head >= 2)
        def _():
            out_copy(head - 2).wait()

        scale = scales[head]
        mine = rows_at(head * HEAD_DIM, HEAD_DIM)

        for i in range(NB):
            here = slice(i * BLOCK, (i + 1) * BLOCK)
            q_unit, _ = head_norm(raw[slot, 0, :, here])
            k_unit, _ = head_norm(raw[slot, 1, :, here])
            q8 = (q_unit * scale).astype(BF) * BF(8.0)
            qT[:, here] = q8
            q[here, :] = q8.T
            kn = (k_unit * scale).astype(BF)
            kT[:, here] = kn
            k[here, :] = kn.T
            v[here, :] = raw[slot, 2, :, here].astype(BF).T
            gh = gm[mine, here]
            gT[:, here] = gh
            g[here, :] = gh.T
            delta[:, here] = jnp.sum(gh.astype(F32) * mixed[mine, here].astype(F32), axis=0, keepdims=True)
            inv[:, here] = sums[head, 0:1, here]
        dk[...] = jnp.zeros_like(dk)
        dv[...] = jnp.zeros_like(dv)

    def visit(start, pieces):
        span = lanes_at(start, 256)
        query, grad = qT[:, span], gT[:, span]
        query_rows, grad_rows = q[span, :], g[span, :]
        scale_row, delta_row = inv[:, span], delta[:, span]
        acc = jnp.zeros((64, 256), F32)
        for kstart, size, kind in pieces:
            keys = lanes_at(kstart, size)
            probs = masked(kind, jnp.exp(nn(k[keys, :], query)) * scale_row)
            g_probs = nn(v[keys, :], grad)
            g_scores = (probs * (g_probs - delta_row)).astype(BF)
            dv[keys, :] += nn(probs.astype(BF), grad_rows)
            dk[keys, :] += nn(g_scores, query_rows)
            acc = acc + nn(kT[:, keys], g_scores)
        dq[:, span] = acc * 8.0


    def close_head(head):
        slot = head % 2
        scale = scales[head]
        total = jnp.zeros((64, BLOCK), F32)
        for i in range(NB):
            here = slice(i * BLOCK, (i + 1) * BLOCK)
            for which, grad in ((0, dq[:, here]), (1, dk[here, :].T)):
                unit, inverse = head_norm(raw[slot, which, :, here])
                total = total + grad * unit
                scaled = grad * scale
                value = (scaled - unit * jnp.sum(scaled * unit, axis=0, keepdims=True)) * inverse
                out_b[slot, which, :, here] = value.astype(BF)
            out_b[slot, 2, :, here] = dv[here, :].T.astype(BF)
        g_scale[head] = jnp.sum(total, axis=1, keepdims=True)
        out_copy(head).start()

    def work(i, carry):
        head, segment = i // 4, i % 4
        pl.when(segment == 0)(functools.partial(open_head, head))
        pl.when(segment == 1)(functools.partial(early_chunks, visit))
        pl.when(segment == 2)(functools.partial(late_chunks, visit))
        pl.when(segment == 3)(functools.partial(close_head, head))
        pl.when(i < 14)(functools.partial(poll, i))
        return carry

    lax.fori_loop(0, 4 * heads, work, 0)
    for copy in exchange():
        copy.wait()
    hid_in[me] = hid_buf[me]
    size = g_up.shape[1] // 32
    for which, out in enumerate((g_up, g_gate)):
        for d in range(8):
            start = (8 * which + d) * size
            block = [hid_in[i, :, start : start + size].astype(F32) for i in range(4)]
            out[:, d * 4 * size : (d + 1) * 4 * size] = jnp.concatenate(block, axis=1)
    for head in (heads - 2, heads - 1):
        out_copy(head).wait()


def attention_back(order, qkv, scales, sums, mixed, ga_all, w_o, ht_all, gug_all):
    heads = scales.shape[0]
    count, tokens, hidden_width = gug_all.shape
    chunk = ht_all.shape[1] // 8
    side = hidden_width // 4
    rows_w = chunk // 4
    vmem, hbm = pl.BlockSpec(memory_space=pltpu.VMEM), pl.BlockSpec(memory_space=pl.ANY)
    smem = pl.BlockSpec(memory_space=pltpu.SMEM)
    dma = pltpu.SemaphoreType.DMA
    return pl.pallas_call(
        attention_back_kernel,
        in_specs=[smem, hbm, vmem, vmem, vmem, hbm, vmem, hbm, hbm],
        out_specs=[hbm, vmem, vmem, vmem, vmem],
        out_shape=[
            jax.ShapeDtypeStruct(qkv.shape, BF),
            jax.ShapeDtypeStruct(scales.shape, F32),
            jax.ShapeDtypeStruct(w_o.shape, BF),
            jax.ShapeDtypeStruct((rows_w, 2 * hidden_width), F32),
            jax.ShapeDtypeStruct((rows_w, 2 * hidden_width), F32),
        ],
        scratch_shapes=[
            pltpu.VMEM(ga_all.shape, BF),
            pltpu.VMEM((TOK, w_o.shape[1]), BF),
            pltpu.VMEM(mixed.shape, BF),
            pltpu.VMEM((2, 3, HEAD_DIM, TOK), F32),
            pltpu.VMEM((2, 3, HEAD_DIM, TOK), BF),
            pltpu.VMEM((HEAD_DIM, TOK), BF),
            pltpu.VMEM((TOK, HEAD_DIM), BF),
            pltpu.VMEM((TOK, HEAD_DIM), BF),
            pltpu.VMEM((HEAD_DIM, TOK), BF),
            pltpu.VMEM((TOK, HEAD_DIM), BF),
            pltpu.VMEM((HEAD_DIM, TOK), BF),
            pltpu.VMEM((TOK, HEAD_DIM), BF),
            pltpu.VMEM((HEAD_DIM, TOK), F32),
            pltpu.VMEM((TOK, HEAD_DIM), F32),
            pltpu.VMEM((TOK, HEAD_DIM), F32),
            pltpu.VMEM((1, TOK), F32),
            pltpu.VMEM((1, TOK), F32),
            pltpu.VMEM(gug_all.shape, BF),
            pltpu.VMEM((2, count, chunk, tokens), BF),
            pltpu.VMEM((2, count, chunk, tokens), BF),
            pltpu.VMEM((2, 2, 8, chunk, side), BF),
            pltpu.VMEM((2, chunk, side), F32),
            pltpu.VMEM((4, rows_w, hidden_width), BF),
            pltpu.VMEM((4, rows_w, hidden_width), BF),
            dma((1,)),
            dma((count,)),
            dma((2, 2)),
            dma((2,)),
            dma((2,)),
            dma((2, 2, 7)),
            dma((2, 2, 7)),
            dma((3,)),
            dma((3,)),
        ],
        compiler_params=pltpu.CompilerParams(
            collective_id=5, has_side_effects=True, vmem_limit_bytes=62 << 20
        ),
        name="attention_back",
        cost_estimate=pl.CostEstimate(flops=40 * 10**9, bytes_accessed=60 << 20, transcendentals=14 << 20),
    )(order, qkv, scales, sums, mixed, ga_all, w_o, ht_all, gug_all)


MESH = pl.DeviceIdType.MESH


def ring_place():
    dp = lax.axis_index("dp")
    z, y = dp // 2, dp % 2
    return z + y * (7 - 2 * z)


def ring_dp(place):
    place = (place + 16) % 8
    y = place // 4
    return 2 * (place + y * (7 - 2 * place)) + y


def greet(peers):
    barrier = pltpu.get_barrier_semaphore()
    for peer in peers:
        pl.semaphore_signal(barrier, inc=1, device_id=peer, device_id_type=MESH)
    pl.semaphore_wait(barrier, len(peers))


def group_peers():
    me = lax.axis_index("fsdp")
    core = 1 - 2 * (me % 2)
    chip = 2 - 4 * (me // 2)
    return {"fsdp": me + core}, {"fsdp": me + chip}, {"fsdp": me + core + chip}


def send(src, dst, send_sem, recv_sem, peer):
    return pltpu.make_async_remote_copy(
        src_ref=src, dst_ref=dst, send_sem=send_sem, recv_sem=recv_sem, device_id=peer, device_id_type=MESH
    )


EARLY_HOPS = 5


def hidden_ring(ref, sends, recvs, step, base=0):
    place = ring_place()
    right, left = {"dp": ring_dp(place + 1)}, {"dp": ring_dp(place - 1)}
    chunk = ref.shape[0] // 8
    to_right, to_left = ring_dp(place - step) * chunk, ring_dp(place + step) * chunk
    first, size = 48, chunk // 2
    cuts = ((to_right, first, right), (to_left + size, first, left),
            (to_right + first, size - first, right), (to_left + size + first, size - first, left))
    return [
        send(ref.at[rows_at(start, rows)], ref.at[rows_at(start, rows)], sends.at[i, step - base],
             recvs.at[i, step - base], peer)
        for i, (start, rows, peer) in enumerate(cuts)
    ]


def forward_kernel(order, states, w_query, w_key, w_value, small, extra, out_piece, w_up, w_gate,
                   tokens_t, w_t, w_o, w_ug, qkv, mixed, sums, share,
                   qkv_send, ug_send, land, weights, tok, turned, tok_t, out_w, ug_land, ug_own, raw, qs, ks, vs, blocks, stage,
                   tok_send, tok_recv, a2a_send, a2a_recv, ring_send, ring_recv, ug_s, ug_r, local_sem, raw_sem,
                   stage_sem):
    me, dp = lax.axis_index("fsdp"), lax.axis_index("dp")
    place = ring_place()
    sibling, across, corner = group_peers()
    right, left = {"dp": ring_dp(place + 1)}, {"dp": ring_dp(place - 1)}
    rows, width = states.shape
    piece = land.shape[1]
    chunk = 4 * piece
    half = chunk // 2
    cols = mixed.shape[0]
    heads = cols // HEAD_DIM
    own = pltpu.make_async_copy(states, tok.at[pl.ds(0, rows)], local_sem.at[0])
    own.start()
    for i in range(4):
        cut = slice(i * cols, (i + 1) * cols)
        block = [w[:, cut].astype(F32) for w in (w_query, w_key, w_value)] + [small[...].astype(F32)]
        qkv_send[i] = jnp.concatenate(block, axis=1).astype(BF)
    greet([sibling, across, corner, right, left])

    exchange, ug_exchange = [], []
    for i, peer in enumerate((sibling, across, corner)):
        copy = send(qkv_send.at[peer["fsdp"]], land.at[me], a2a_send.at[i], a2a_recv.at[i], peer)
        copy.start()
        exchange.append(copy)
    far = []
    for i in range(2):
        part = pl.ds(i * (rows // 2), rows // 2)
        here = pl.ds(2 * rows + i * (rows // 2), rows // 2)
        copy = send(states.at[part], tok.at[here], tok_send.at[i], tok_recv.at[i], across)
        copy.start()
        far.append(copy)
    near = send(states, tok.at[pl.ds(rows, rows)], tok_send.at[2], tok_recv.at[2], sibling)
    near.start()
    size = w_up.shape[1] // 32
    for i in range(4):
        for which, w in enumerate((w_up, w_gate)):
            for half_d in range(2):
                block = [
                    w[:, (4 * d + i) * size : (4 * d + i + 1) * size].astype(F32)
                    for d in range(4 * half_d, 4 * half_d + 4)
                ]
                start = (8 * which + 4 * half_d) * size
                ug_send[i, :, start : start + 4 * size] = jnp.concatenate(block, axis=1).astype(BF)
    land[me] = qkv_send[me]
    ug_land[me] = ug_send[me]
    out_w[dp] = out_piece[...]
    vs[HEAD_DIM:, :] = jnp.ones((vs.shape[0] - HEAD_DIM, TOK), BF)
    for copy in exchange:
        copy.wait()
    weights[rows_at(dp * chunk, chunk)] = jnp.concatenate([land[i].astype(F32) for i in range(4)], axis=0).astype(BF)
    last = pl.ds(weights.shape[1] - 128, 128)
    weights[rows_at(dp * chunk, chunk), last] = weights[rows_at(dp * chunk, chunk), last] + extra[...]

    def ring_copies(step):
        to_right, to_left = ring_dp(place - step), ring_dp(place + step)
        first, second = rows_at(to_right * chunk, half), rows_at(to_left * chunk + half, half)
        lanes_r, lanes_l = pl.ds(0, width // 2), pl.ds(width // 2, width // 2)
        return [
            send(ref, ref, ring_send.at[i, step], ring_recv.at[i, step], peer)
            for i, (ref, peer) in enumerate(
                (
                    (weights.at[first], right),
                    (weights.at[second], left),
                    (out_w.at[to_right, :, lanes_r], right),
                    (out_w.at[to_left, :, lanes_l], left),
                )
            )
        ]

    def hop(step, carry):
        for copy, later in zip(ring_copies(step), ring_copies(step + 1)):
            copy.wait()
            pl.when(step < 6)(later.start)
        return carry

    def ug_hop(step):
        for copy, later in zip(hidden_ring(w_ug, ug_s, ug_r, step), hidden_ring(w_ug, ug_s, ug_r, step + 1)):
            copy.wait()
            pl.when(step < EARLY_HOPS - 1)(later.start)

    for copy in ring_copies(0):
        copy.start()

    def turn(i, carry):
        turned[i] = tok[lanes_at(i * BLOCK, BLOCK)].T
        return carry

    lax.fori_loop(0, 1, hop, 0)
    near.wait()
    own.wait()
    lax.fori_loop(0, 4, turn, 0)
    lax.fori_loop(1, 2, hop, 0)
    lax.fori_loop(4, 7, turn, 0)
    lax.fori_loop(2, 3, hop, 0)
    lax.fori_loop(7, 10, turn, 0)
    lax.fori_loop(3, 5, hop, 0)
    passed = []
    for i in range(2):
        far[i].wait()
        here = pl.ds(2 * rows + i * (rows // 2), rows // 2)
        there = pl.ds(3 * rows + i * (rows // 2), rows // 2)
        copy = send(tok.at[here], tok.at[there], tok_send.at[3 + i], tok_recv.at[3 + i], sibling)
        copy.start()
        passed.append(copy)
    for i, peer in enumerate((sibling, across, corner)):
        copy = send(ug_send.at[peer["fsdp"]], ug_land.at[me], a2a_send.at[3 + i], a2a_recv.at[3 + i], peer)
        copy.start()
        ug_exchange.append(copy)
    lax.fori_loop(5, 6, hop, 0)
    lax.fori_loop(10, 15, turn, 0)
    lax.fori_loop(6, 7, hop, 0)
    for copy in passed:
        copy.wait()

    lax.fori_loop(15, NB, turn, 0)

    def arrange(i, carry):
        tok_t[:, lanes_at(i * BLOCK, BLOCK)] = turned[order[0, i]]
        return carry

    lax.fori_loop(0, NB, arrange, 0)
    keep = pltpu.make_async_copy(tok_t, tokens_t, local_sem.at[2])
    keep.start()

    def turn_weights(i, carry):
        w_t[:, lanes_at(i * BLOCK, BLOCK)] = weights[rows_at(i * BLOCK, BLOCK)].T
        return carry

    lax.fori_loop(0, width // BLOCK, turn_weights, 0)
    for copy in ug_exchange:
        copy.wait()
    ug_own[...] = jnp.concatenate([ug_land[i].astype(F32) for i in range(4)], axis=0).astype(BF)
    ug_store = pltpu.make_async_copy(ug_own, w_ug.at[rows_at(dp * chunk, chunk)], local_sem.at[1])
    ug_store.start()
    ug_store.wait()
    for copy in hidden_ring(w_ug, ug_s, ug_r, 0):
        copy.start()
    w_o[...] = jnp.concatenate([out_w[i].astype(F32) for i in range(8)], axis=0).astype(BF)

    def raw_copies(head):
        slot = head % 2
        return [
            pltpu.make_async_copy(
                raw.at[slot, pl.ds(which * HEAD_DIM, HEAD_DIM)],
                qkv.at[which, rows_at(head * HEAD_DIM, HEAD_DIM)],
                raw_sem.at[slot, which],
            )
            for which in range(3)
        ]

    def attend(head, carry):
        slot = head % 2

        @pl.when(head >= 2)
        def _():
            for copy in raw_copies(head - 2):
                copy.wait()

        left_rows = jnp.concatenate(
            [w_t[rows_at(which * cols + head * HEAD_DIM, HEAD_DIM)] for which in range(3)], axis=0
        )

        def project_tile(n, carry):
            raw[slot, :, tile(n)] = nn(left_rows, tok_t[:, tile(n)])
            return carry

        lax.fori_loop(0, TOK // TILE, project_tile, 0, unroll=2)
        for copy in raw_copies(head):
            copy.start()
        scale = weights[rows_at(me * cols + head * HEAD_DIM, HEAD_DIM), last][:, HEAD_DIM : HEAD_DIM + 1].astype(F32)

        def prepare(i, carry):
            here = lanes_at(i * BLOCK, BLOCK)
            q_unit, _ = head_norm(raw[slot, pl.ds(0, HEAD_DIM), here])
            k_unit, _ = head_norm(raw[slot, pl.ds(HEAD_DIM, HEAD_DIM), here])
            qs[:, here] = (q_unit * scale).astype(BF) * BF(8.0)
            ks[here, :] = (k_unit * scale).astype(BF).T
            vs[0:HEAD_DIM, here] = raw[slot, pl.ds(2 * HEAD_DIM, HEAD_DIM), here].astype(BF)
            return carry

        lax.fori_loop(0, NB, prepare, 0, unroll=NB)

        def visit(start, parts):
            span = lanes_at(start, 256)
            query = qs[:, span]
            acc = jnp.zeros((vs.shape[0], 256), F32)
            for kstart, count, kind in parts:
                keys = lanes_at(kstart, count)
                powers = masked(kind, jnp.exp(nn(ks[keys, :], query))).astype(BF)
                acc = acc + nn(vs[:, keys], powers)
            total = 1.0 / acc[HEAD_DIM : HEAD_DIM + 1, :]
            mixed[rows_at(head * HEAD_DIM, HEAD_DIM), span] = (acc[0:HEAD_DIM, :] * total).astype(BF)
            sums[head, :, span] = jnp.broadcast_to(total, (8, 256))

        early_chunks(visit)
        late_chunks(visit)

        @pl.when(head % 2 == 1)
        def _():
            ug_hop(head // 2)

        return carry

    lax.fori_loop(0, heads, attend, 0)
    ug_hop(heads // 2)

    def share_copy(b):
        slot = b % 2
        return pltpu.make_async_copy(
            stage.at[slot], share.at[b // 5, lanes_at((b % 5) * BLOCK, BLOCK)], stage_sem.at[slot]
        )

    def split(i, carry):
        blocks[i] = mixed[:, lanes_at(i * BLOCK, BLOCK)]
        return carry

    lax.fori_loop(0, NB, split, 0)

    def out_project(b, carry):
        @pl.when(b >= 2)
        def _():
            share_copy(b - 2).wait()

        stage[b % 2] = nn(blocks[order[1, b]].T, w_o[...]).astype(BF)
        share_copy(b).start()
        return carry

    lax.fori_loop(0, NB // 2, out_project, 0, unroll=2)
    ug_hop(heads // 2 + 1)
    lax.fori_loop(NB // 2, NB, out_project, 0, unroll=2)
    lax.fori_loop(heads // 2 + 2, EARLY_HOPS, lambda step, c: (ug_hop(step), c)[1], 0)
    keep.wait()
    for b in (NB - 2, NB - 1):
        share_copy(b).wait()
    for head in (heads - 2, heads - 1):
        for copy in raw_copies(head):
            copy.wait()


def forward(order, states, w_query, w_key, w_value, small, extra, out_piece, w_up, w_gate):
    tps, rows_w = 4, w_query.shape[0]
    tokens, width = states.shape
    packed = 3 * width // tps + small.shape[1]
    hidden_width = 2 * w_up.shape[1] // tps
    cols = 8 * rows_w
    vmem, hbm = pl.BlockSpec(memory_space=pltpu.VMEM), pl.BlockSpec(memory_space=pl.ANY)
    smem = pl.BlockSpec(memory_space=pltpu.SMEM)
    dma = pltpu.SemaphoreType.DMA
    return pl.pallas_call(
        forward_kernel,
        in_specs=[smem, hbm] + [vmem] * 8,
        out_specs=[hbm, vmem, vmem, hbm, hbm, vmem, vmem, hbm],
        out_shape=[
            jax.ShapeDtypeStruct((width, TOK), BF),
            jax.ShapeDtypeStruct((packed, width), BF),
            jax.ShapeDtypeStruct((cols, width), BF),
            jax.ShapeDtypeStruct((width, hidden_width), BF),
            jax.ShapeDtypeStruct((3, cols, TOK), F32),
            jax.ShapeDtypeStruct((cols, TOK), BF),
            jax.ShapeDtypeStruct((cols // HEAD_DIM, 8, TOK), F32),
            jax.ShapeDtypeStruct((tps, tokens, width), BF),
        ],
        scratch_shapes=[
            pltpu.VMEM((tps, rows_w, packed), BF),
            pltpu.VMEM((tps, rows_w, hidden_width), BF),
            pltpu.VMEM((tps, rows_w, packed), BF),
            pltpu.VMEM((width, packed), BF),
            pltpu.VMEM((TOK, width), BF),
            pltpu.VMEM((NB, width, BLOCK), BF),
            pltpu.VMEM((width, TOK), BF),
            pltpu.VMEM((8, rows_w, width), BF),
            pltpu.VMEM((tps, rows_w, hidden_width), BF),
            pltpu.VMEM((tps * rows_w, hidden_width), BF),
            pltpu.VMEM((2, 3 * HEAD_DIM, TOK), F32),
            pltpu.VMEM((HEAD_DIM, TOK), BF),
            pltpu.VMEM((TOK, HEAD_DIM), BF),
            pltpu.VMEM((HEAD_DIM + 16, TOK), BF),
            pltpu.VMEM((NB, cols, BLOCK), BF),
            pltpu.VMEM((2, BLOCK, width), BF),
            dma((5,)),
            dma((5,)),
            dma((6,)),
            dma((6,)),
            dma((4, 7)),
            dma((4, 7)),
            dma((4, EARLY_HOPS)),
            dma((4, EARLY_HOPS)),
            dma((3,)),
            dma((2, 3)),
            dma((2,)),
        ],
        compiler_params=pltpu.CompilerParams(
            collective_id=1, has_side_effects=True, vmem_limit_bytes=56 << 20
        ),
        cost_estimate=pl.CostEstimate(flops=12 * 10**9, bytes_accessed=200 << 20, transcendentals=14 << 20),
        name="forward",
    )(order, states, w_query, w_key, w_value, small, extra, out_piece, w_up, w_gate)


def last_kernel(order, base, tokens_t, g_qkv, w_t, part_out, vectors,
                g_states, g_query, g_key, g_value, out_rows, vec_own,
                gq_b, blocks, tok_r, tok_l, share, turned, core_buf, x_buf, base_b, gs_b,
                ring_r, ring_l, ring_o, ring_v, next_r, next_l, row_buf, row_in, vec_part, vec_in,
                in_sem, row_sem, base_sem, core_send, core_recv, x_send, x_recv,
                ring_send, ring_recv, a2a_send, a2a_recv):
    me, dp = lax.axis_index("fsdp"), lax.axis_index("dp")
    place = ring_place()
    sibling, across, corner = group_peers()
    right, left = {"dp": ring_dp(place + 1)}, {"dp": ring_dp(place - 1)}
    chunk, side = ring_r.shape[1], ring_r.shape[2]
    rows = share.shape[1]
    quarter = rows // 4
    width = w_t.shape[1]
    heads_width = gq_b.shape[0]
    rows_w = row_buf.shape[1]

    def slices(step):
        slot = step % 2
        cut_r = rows_at(ring_dp(place - 1 - step) * chunk, chunk)
        cut_l = rows_at(ring_dp(place + 1 + step) * chunk, chunk)
        return [
            pltpu.make_async_copy(tokens_t.at[cut_r], tok_r.at[slot], row_sem.at[0, slot]),
            pltpu.make_async_copy(tokens_t.at[cut_l], tok_l.at[slot], row_sem.at[1, slot]),
        ]

    def base_copy(i):
        return pltpu.make_async_copy(base.at[pl.ds(i * quarter, quarter)], base_b.at[i % 2], base_sem.at[0, i % 2])

    def gs_copy(i):
        return pltpu.make_async_copy(gs_b.at[i % 2], g_states.at[pl.ds(i * quarter, quarter)], base_sem.at[1, i % 2])

    load_q = pltpu.make_async_copy(g_qkv, gq_b, in_sem.at[0])
    load_q.start()
    for step in (0, 1):
        for copy in slices(step):
            copy.start()
    greet([sibling, across, corner, right, left])

    def parts(step):
        slot = step % 2
        for copy in slices(step):
            copy.wait()
        next_r[...] = nt(tok_r[slot], gq_b[pl.ds(0, side)])
        next_l[...] = nt(tok_l[slot], gq_b[pl.ds(side, heads_width - side)])

        @pl.when(step + 2 < 8)
        def _():
            for copy in slices(step + 2):
                copy.start()

    def hop_copies(step):
        return [
            send(ring.at[step], ring.at[step + 1], ring_send.at[i, step], ring_recv.at[i, step], peer)
            for i, (ring, peer) in enumerate(((ring_r, right), (ring_l, left), (ring_o, left), (ring_v, right)))
        ]

    def through(r, slot):
        for i in range(rows // BLOCK):
            turned[i * BLOCK : (i + 1) * BLOCK] = blocks[order[1, r * (rows // BLOCK) + i]].T

        def one(n, carry):
            share[slot, :, tile(n)] = nn(turned[...], w_t[pl.ds(0, heads_width), tile(n)]).astype(BF)
            return carry

        lax.fori_loop(0, width // TILE, one, 0)

    core = [
        send(share.at[0], core_buf.at[0], core_send.at[0], core_recv.at[0], sibling),
        send(share.at[2], core_buf.at[1], core_send.at[1], core_recv.at[1], sibling),
    ]
    far = [
        send(share.at[1, pl.ds(i * quarter, quarter)], x_buf.at[pl.ds(i * quarter, quarter)], x_send.at[i],
             x_recv.at[i], across)
        for i in range(4)
    ]
    load_q.wait()

    def split(i, carry):
        blocks[i] = gq_b[:, lanes_at(i * BLOCK, BLOCK)]
        return carry

    def hop(step, carry):
        parts(step)

        @pl.when(step == 0)
        def _():
            ring_r[0] = next_r[...].astype(BF)
            ring_l[0] = next_l[...].astype(BF)
            ring_o[0] = part_out[ring_dp(place + 1)]
            ring_v[0] = vectors[ring_dp(place - 1)]

        @pl.when(step > 0)
        def _():
            before, now = hop_copies(step - 1), hop_copies(step)
            before[0].wait()
            ring_r[step] = (ring_r[step].astype(F32) + next_r[...]).astype(BF)
            now[0].start()
            before[1].wait()
            ring_l[step] = (ring_l[step].astype(F32) + next_l[...]).astype(BF)
            now[1].start()
            before[2].wait()
            ring_o[step] = (ring_o[step].astype(F32) + part_out[ring_dp(place + 1 + step)].astype(F32)).astype(BF)
            now[2].start()
            before[3].wait()
            ring_v[step] = ring_v[step] + vectors[ring_dp(place - 1 - step)]
            now[3].start()

        @pl.when(step == 0)
        def _():
            for copy in hop_copies(0):
                copy.start()

        @pl.when(step == 0)
        def _():
            lax.fori_loop(0, NB, split, 0)

        pl.when(step < 4)(functools.partial(through, 3 - step, step % 3))

        @pl.when(step == 0)
        def _():
            core[0].start()

        @pl.when(step == 1)
        def _():
            core[0].wait()
            for i in range(4):
                span = pl.ds(i * quarter, quarter)
                share[1, span] = (share[1, span].astype(F32) + core_buf[0, span].astype(F32)).astype(BF)
                far[i].start()

        @pl.when(step == 2)
        def _():
            core[1].start()

        return carry

    lax.fori_loop(0, 7, hop, 0)
    base_copy(0).start()
    base_copy(1).start()
    parts(7)
    for copy in hop_copies(6):
        copy.wait()
    total = jnp.concatenate((ring_r[7].astype(F32) + next_r[...], ring_l[7].astype(F32) + next_l[...]), axis=1)
    for i in range(4):
        row_buf[i] = total[i * rows_w : (i + 1) * rows_w].astype(BF)
    vec_part[...] = ring_v[7] + vectors[dp]
    exchange = []
    for i, peer in enumerate((sibling, across, corner)):
        to = peer["fsdp"]
        copies = [
            send(row_buf.at[to], row_in.at[me], a2a_send.at[i], a2a_recv.at[i], peer),
            send(vec_part.at[to], vec_in.at[me], a2a_send.at[3 + i], a2a_recv.at[3 + i], peer),
        ]
        for copy in copies:
            copy.start()
        exchange += copies
    row_in[me] = row_buf[me]
    vec_in[me] = vec_part[me]
    out_rows[...] = ring_o[7].astype(F32) + part_out[dp].astype(F32)
    core[1].wait()
    for i in range(4):
        span = pl.ds(i * quarter, quarter)
        far[i].wait()
        base_copy(i).wait()
        if i >= 2:
            gs_copy(i - 2).wait()
        gs_b[i % 2] = base_b[i % 2] + (
            share[0, span].astype(F32) + core_buf[1, span].astype(F32) + x_buf[span].astype(F32)
        )
        gs_copy(i).start()
        if i < 2:
            base_copy(i + 2).start()
    for copy in exchange:
        copy.wait()
    vec_own[...] = vec_in[0] + vec_in[1] + vec_in[2] + vec_in[3]
    cols = heads_width // 3
    for which, out in enumerate((g_query, g_key, g_value)):
        out[...] = jnp.concatenate(
            [row_in[i, :, which * cols : (which + 1) * cols].astype(F32) for i in range(4)], axis=1
        )
    for i in (2, 3):
        gs_copy(i).wait()


def last_exchange(order, base, tokens_t, g_qkv, w_t, part_out, vectors):
    rows, width = base.shape
    heads_width = g_qkv.shape[0]
    rows_w = part_out.shape[1]
    chunk = 4 * rows_w
    side = 2 * heads_width // 3
    vmem, hbm = pl.BlockSpec(memory_space=pltpu.VMEM), pl.BlockSpec(memory_space=pl.ANY)
    dma = pltpu.SemaphoreType.DMA
    return pl.pallas_call(
        last_kernel,
        in_specs=[pl.BlockSpec(memory_space=pltpu.SMEM), hbm, hbm, hbm, vmem, vmem, vmem],
        out_specs=[hbm] + [vmem] * 5,
        out_shape=[jax.ShapeDtypeStruct((rows, width), F32)]
        + [jax.ShapeDtypeStruct((rows_w, width), F32)] * 4
        + [jax.ShapeDtypeStruct(vectors.shape[2:], F32)],
        scratch_shapes=[
            pltpu.VMEM(g_qkv.shape, BF),
            pltpu.VMEM((NB, heads_width, BLOCK), BF),
            pltpu.VMEM((2, chunk, tokens_t.shape[1]), BF),
            pltpu.VMEM((2, chunk, tokens_t.shape[1]), BF),
            pltpu.VMEM((3, rows, width), BF),
            pltpu.VMEM((rows, heads_width), BF),
            pltpu.VMEM((2, rows, width), BF),
            pltpu.VMEM((rows, width), BF),
            pltpu.VMEM((2, rows // 4, width), F32),
            pltpu.VMEM((2, rows // 4, width), F32),
            pltpu.VMEM((8, chunk, side), BF),
            pltpu.VMEM((8, chunk, heads_width - side), BF),
            pltpu.VMEM((8, rows_w, width), BF),
            pltpu.VMEM(vectors.shape, F32),
            pltpu.VMEM((chunk, side), F32),
            pltpu.VMEM((chunk, heads_width - side), F32),
            pltpu.VMEM((4, rows_w, heads_width), BF),
            pltpu.VMEM((4, rows_w, heads_width), BF),
            pltpu.VMEM(vectors.shape[1:], F32),
            pltpu.VMEM(vectors.shape[1:], F32),
            dma((1,)),
            dma((2, 2)),
            dma((2, 2)),
            dma((2,)),
            dma((2,)),
            dma((4,)),
            dma((4,)),
            dma((4, 7)),
            dma((4, 7)),
            dma((6,)),
            dma((6,)),
        ],
        compiler_params=pltpu.CompilerParams(
            collective_id=2, has_side_effects=True, vmem_limit_bytes=48 << 20
        ),
        cost_estimate=pl.CostEstimate(flops=13 * 10**9, bytes_accessed=100 << 20, transcendentals=0),
        name="last_exchange",
    )(order, base, tokens_t, g_qkv, w_t, part_out, vectors)


CHUNK = 128
TILE = 256
LAG = 3


def tile(index, base=0):
    return pl.ds(pl.multiple_of(base + index * TILE, TILE), TILE)


def nt(a, b):
    return lax.dot_general(a, b, (((1,), (1,)), ((), ())), preferred_element_type=F32)


def middle_kernel(share, states, teacher, weight, mask, w_in, w_own, rates, scales,
                  w_ug, w_d, out_states, hidden, attn_unit, back, attn_inv, hidden_inv, sums, gd_all, ht_all, act_all, ug_all,
                  part, core, x_buf, tok, gd, act, act_t, ug, ht,
                  ld_sem, core_send, core_recv, x_send, x_recv, tok_send, tok_recv, gd_send, gd_recv, gd_own,
                  out_sem, ring_send, ring_recv, ug_s, ug_r, ug_sem):
    sibling, across, _ = group_peers()
    dp, place = lax.axis_index("dp"), ring_place()
    right, left = {"dp": ring_dp(place + 1)}, {"dp": ring_dp(place - 1)}
    piece = w_own.shape[0]
    count = part.shape[0]
    width = hidden.shape[1]
    rate_attn, rate_mlp = rates[0:1], rates[1:2]

    def rows(i):
        return pl.ds(pl.multiple_of(i * CHUNK, CHUNK), CHUNK)

    def load(i):
        return pltpu.make_async_copy(share.at[:, rows(i)], part.at[i], ld_sem.at[i])

    def core_a(stage, i):
        return send(part.at[i, 3], core.at[0, i], core_send.at[stage, 0, i], core_recv.at[stage, 0, i], sibling)

    def core_b(stage, i):
        return send(part.at[i, 1], core.at[1, i], core_send.at[stage, 1, i], core_recv.at[stage, 1, i], sibling)

    def chip(stage, i):
        return send(part.at[i, 2], x_buf.at[i], x_send.at[stage, i], x_recv.at[stage, i], across)

    def spread(buf, own, sems, recvs, i):
        return [
            send(own, buf.at[i, 1], sems.at[0, i], recvs.at[0, i], sibling),
            send(own, buf.at[i, 2], sems.at[1, i], recvs.at[1, i], across),
            send(buf.at[i, 2], buf.at[i, 3], sems.at[2, i], recvs.at[2, i], sibling),
        ]

    def tok_copies(i):
        return spread(tok, tok.at[i, 0], tok_send, tok_recv, i)

    def gd_copies(i):
        return spread(gd_all, gd.at[i], gd_send, gd_recv, i)

    def gd_local(i):
        return pltpu.make_async_copy(gd.at[i], gd_all.at[i, 0], gd_own.at[i])

    def outs(i):
        slot = i % 2
        return [
            pltpu.make_async_copy(ht.at[slot], ht_all.at[i], out_sem.at[0, slot]),
            pltpu.make_async_copy(act_t.at[slot], act_all.at[i], out_sem.at[1, slot]),
            pltpu.make_async_copy(ug.at[slot], ug_all.at[i], out_sem.at[2, slot]),
        ]

    def hop(step):
        late = hidden_ring(w_d, ring_send, ring_recv, step + 1)
        for copy, later in zip(hidden_ring(w_d, ring_send, ring_recv, step), late):
            copy.wait()
            pl.when(step < 6)(later.start)

    def ug_hop(step):
        late = hidden_ring(w_ug, ug_s, ug_r, step + 1, EARLY_HOPS)
        for copy, later in zip(hidden_ring(w_ug, ug_s, ug_r, step, EARLY_HOPS), late):
            copy.wait()
            pl.when(step < 6)(later.start)

    def forward_far(stage, i):
        core_a(stage, i).wait_recv()
        part[i, 2] = (part[i, 2].astype(F32) + core[0, i].astype(F32)).astype(BF)
        chip(stage, i).start()

    def reduced(stage, i):
        core_b(stage, i).wait_recv()
        chip(stage, i).wait_recv()
        total = part[i, 0].astype(F32) + core[1, i].astype(F32) + x_buf[i].astype(F32)
        core_a(stage, i).wait_send()
        core_b(stage, i).wait_send()
        chip(stage, i).wait_send()
        return total

    sums[...] = jnp.zeros_like(sums)
    lax.fori_loop(0, count, lambda i, c: (load(i).start(), c)[1], 0)
    w_d[rows_at(dp * piece, piece)] = w_own[...]
    chunk = w_ug.shape[0] // 8

    def load_w(i):
        cuts = rows_at(ring_dp(place - i) * chunk, chunk // 2), rows_at(
            ring_dp(place + i) * chunk + chunk // 2, chunk // 2
        )
        return [pltpu.make_async_copy(w_in.at[cut], w_ug.at[cut], ug_sem.at[d, i]) for d, cut in enumerate(cuts)]

    def start_w(i, carry):
        for copy in load_w(i):
            copy.start()
        return carry

    def wait_w(i, carry):
        for copy in load_w(i):
            copy.wait()
        return carry

    lax.fori_loop(0, EARLY_HOPS + 1, start_w, 0)
    greet([sibling, across, right, left])
    for copy in hidden_ring(w_d, ring_send, ring_recv, 0):
        copy.start()

    def open_core(i, carry):
        load(i).wait()
        core_a(0, i).start()
        core_b(0, i).start()
        return carry

    lax.fori_loop(0, count, open_core, 0)
    lax.fori_loop(0, EARLY_HOPS + 1, wait_w, 0)
    for copy in hidden_ring(w_ug, ug_s, ug_r, EARLY_HOPS, EARLY_HOPS):
        copy.start()
    lax.fori_loop(0, count, lambda i, c: (forward_far(0, i), c)[1], 0)

    def norm_hidden(i):
        unit, inverse = unit_rows(reduced(0, i))
        own = states[rows(i)].astype(F32)
        value, value_inv = unit_rows(own + rate_attn * (unit - own))
        hidden[rows(i)] = value
        attn_unit[rows(i)] = unit.astype(BF)
        attn_inv[rows(i)] = inverse
        hidden_inv[rows(i)] = value_inv
        tok[i, 0] = value.astype(BF)
        copies = tok_copies(i)
        copies[0].start()
        copies[1].start()

    def pass_tokens(i):
        copies = tok_copies(i)
        copies[1].wait_recv()
        copies[2].start()

    def feed(i):
        copies = tok_copies(i)
        copies[0].wait()
        copies[1].wait_send()
        copies[2].wait()
        slot = i % 2

        @pl.when(i >= 2)
        def _():
            for copy in outs(i - 2):
                copy.wait()

        def up(n, carry):
            here = tok[i].reshape(4 * CHUNK, width)
            up_proj = nn(here, w_ug[:, tile(n)])
            gate_proj = nn(here, w_ug[:, tile(n, width)])
            gated = gate_proj * scales[1:2, tile(n)]
            value = up_proj * scales[0:1, tile(n)] * (gated * jax.nn.sigmoid(gated))
            act[:, tile(n)] = value.astype(BF)
            act_t[slot, tile(n)] = value.astype(BF).T
            ug[slot, :, tile(n)] = up_proj.astype(BF)
            ug[slot, :, tile(n, width)] = gate_proj.astype(BF)
            return carry

        lax.fori_loop(0, width // TILE, up, 0)

        def down(n, carry):
            value = nn(act[...], w_d[:, tile(n)])
            part[i, :, :, tile(n)] = value.astype(BF).reshape(4, CHUNK, TILE)
            ht[slot, tile(n)] = tok[i, :, :, tile(n)].reshape(4 * CHUNK, TILE).T
            return carry

        lax.fori_loop(0, width // TILE, down, 0)
        core_a(1, i).start()
        core_b(1, i).start()
        for copy in outs(i):
            copy.start()
        forward_far(1, i)

    def finish(i):
        unit, inverse = unit_rows(reduced(1, i))
        own = hidden[rows(i)]
        result, result_inv = unit_rows(own + rate_mlp * (unit - own))
        out_states[rows(i)] = result.astype(BF)
        diff = result - teacher[rows(i)]
        sums[1:2] = sums[1:2] + jnp.sum(mask[rows(i)] * (diff * diff), axis=0, keepdims=True)
        g_last = unit_back(weight[rows(i)] * diff, result, result_inv)
        sums[0:1] = sums[0:1] + jnp.sum(g_last * (unit - own), axis=0, keepdims=True)
        back[rows(i)] = g_last * (1.0 - rate_mlp)
        gd[i] = unit_back(g_last * rate_mlp, unit, inverse).astype(BF)
        copies = gd_copies(i)
        copies[0].start()
        copies[1].start()
        gd_local(i).start()

    def pass_grads(i):
        copies = gd_copies(i)
        copies[1].wait_recv()
        copies[2].start()

    stages = ((0, norm_hidden), (1, pass_tokens), (LAG, feed), (LAG + 1, finish), (LAG + 2, pass_grads))

    def step(t, carry):
        for lag, stage in stages:
            if lag == LAG:
                pl.when(t < 7 - EARLY_HOPS)(lambda: ug_hop(EARLY_HOPS + t))
                pl.when(t < 3)(lambda: hop(2 * t + 1))
                pl.when(t == 2)(lambda: hop(6))
            pl.when((t >= lag) & (t < lag + count))(functools.partial(stage, t - lag))
            if lag == 0:
                pl.when(t < 3)(lambda: hop(2 * t))
        return carry

    lax.fori_loop(0, count + LAG + 2, step, 0)

    def close(i, carry):
        copies = gd_copies(i)
        copies[0].wait()
        copies[1].wait_send()
        copies[2].wait()
        gd_local(i).wait()
        return carry

    lax.fori_loop(0, count, close, 0)
    for i in (count - 2, count - 1):
        for copy in outs(i):
            copy.wait()


def middle(share, states, teacher, weight, mask, w_ug, w_own, rates, scales):
    rows, width = states.shape
    count = rows // CHUNK
    vmem, hbm = pl.BlockSpec(memory_space=pltpu.VMEM), pl.BlockSpec(memory_space=pl.ANY)
    dma = pltpu.SemaphoreType.DMA
    return pl.pallas_call(
        middle_kernel,
        in_specs=[hbm] + [vmem] * 4 + [hbm] + [vmem] * 3,
        out_specs=[vmem] * 9 + [hbm] * 4,
        out_shape=[
            jax.ShapeDtypeStruct(w_ug.shape, BF),
            jax.ShapeDtypeStruct((8 * w_own.shape[0], width), BF),
            jax.ShapeDtypeStruct((rows, width), BF),
            jax.ShapeDtypeStruct((rows, width), F32),
            jax.ShapeDtypeStruct((rows, width), BF),
            jax.ShapeDtypeStruct((rows, width), F32),
            jax.ShapeDtypeStruct((rows, 1), F32),
            jax.ShapeDtypeStruct((rows, 1), F32),
            jax.ShapeDtypeStruct((2, width), F32),
            jax.ShapeDtypeStruct((count, 4, CHUNK, width), BF),
            jax.ShapeDtypeStruct((count, width, 4 * CHUNK), BF),
            jax.ShapeDtypeStruct((count, width, 4 * CHUNK), BF),
            jax.ShapeDtypeStruct((count, 4 * CHUNK, 2 * width), BF),
        ],
        scratch_shapes=[
            pltpu.VMEM((count, 4, CHUNK, width), BF),
            pltpu.VMEM((2, count, CHUNK, width), BF),
            pltpu.VMEM((count, CHUNK, width), BF),
            pltpu.VMEM((count, 4, CHUNK, width), BF),
            pltpu.VMEM((count, CHUNK, width), BF),
            pltpu.VMEM((4 * CHUNK, width), BF),
            pltpu.VMEM((2, width, 4 * CHUNK), BF),
            pltpu.VMEM((2, 4 * CHUNK, 2 * width), BF),
            pltpu.VMEM((2, width, 4 * CHUNK), BF),
            dma((count,)),
            dma((2, 2, count)),
            dma((2, 2, count)),
            dma((2, count)),
            dma((2, count)),
            dma((3, count)),
            dma((3, count)),
            dma((3, count)),
            dma((3, count)),
            dma((count,)),
            dma((3, 2)),
            dma((4, 7)),
            dma((4, 7)),
            dma((4, 7 - EARLY_HOPS)),
            dma((4, 7 - EARLY_HOPS)),
            dma((2, EARLY_HOPS + 1)),
        ],
        compiler_params=pltpu.CompilerParams(
            collective_id=3, has_side_effects=True, vmem_limit_bytes=60 << 20
        ),
        cost_estimate=pl.CostEstimate(flops=26 * 10**9, bytes_accessed=400 << 20, transcendentals=4 << 20),
        name="middle",
    )(share, states, teacher, weight, mask, w_ug, w_own, rates, scales)


def middle_back_kernel(gd_all, act_all, ug_all, hidden, attn_unit, states, back, attn_inv, hidden_inv, w_ug, w_d,
                       rates, scales, base, ga_all, gug_all, down_rows, sums, ff_sums,
                       w_ug_b, w_d_b, part, core, x_buf, ga, gd, act, ug, gug, own_f, own_b, base_buf, dwd, column, ring_buf,
                       gd_sem, act_sem, in_sem, own_sem, core_send, core_recv, x_send, x_recv, ga_send, ga_recv,
                       ga_own, base_sem, out_sem, w_sem, ring_send, ring_recv):
    sibling, across, _ = group_peers()
    dp, place = lax.axis_index("dp"), ring_place()
    right, left = {"dp": ring_dp(place + 1)}, {"dp": ring_dp(place - 1)}
    count = core.shape[1]
    width = w_d.shape[0]
    load_d = pltpu.make_async_copy(w_d, w_d_b, w_sem.at[0])
    load_u = pltpu.make_async_copy(w_ug, w_ug_b, w_sem.at[1])
    load_d.start()
    half = ring_buf.shape[2]
    rate_attn = rates[0:1]

    def rows(i):
        return pl.ds(pl.multiple_of(i * CHUNK, CHUNK), CHUNK)

    def load_gd(i):
        return pltpu.make_async_copy(gd_all.at[i], gd.at[i], gd_sem.at[i])

    def load_act(i):
        return pltpu.make_async_copy(act_all.at[i], act.at[i], act_sem.at[i])

    def load_ug(i):
        return pltpu.make_async_copy(ug_all.at[i], ug.at[i % 2], in_sem.at[i % 2])

    def store_gug(i):
        return pltpu.make_async_copy(gug.at[i % 2], gug_all.at[i], out_sem.at[i % 2])

    def own_rows(i):
        return [
            pltpu.make_async_copy(hidden.at[rows(i)], own_f.at[0], own_sem.at[0]),
            pltpu.make_async_copy(back.at[rows(i)], own_f.at[1], own_sem.at[1]),
            pltpu.make_async_copy(attn_unit.at[rows(i)], own_b.at[0], own_sem.at[2]),
            pltpu.make_async_copy(states.at[rows(i)], own_b.at[1], own_sem.at[3]),
        ]

    def core_a(i):
        return send(part.at[i % 3, 3], core.at[0, i], core_send.at[0, i], core_recv.at[0, i], sibling)

    def core_b(i):
        return send(part.at[i % 3, 1], core.at[1, i], core_send.at[1, i], core_recv.at[1, i], sibling)

    def chip(i):
        return send(part.at[i % 3, 2], x_buf.at[i], x_send.at[i], x_recv.at[i], across)

    def ga_copies(i):
        return [
            send(ga.at[i], ga_all.at[1, rows(i)], ga_send.at[0, i], ga_recv.at[0, i], sibling),
            send(ga.at[i], ga_all.at[2, rows(i)], ga_send.at[1, i], ga_recv.at[1, i], across),
            send(ga_all.at[2, rows(i)], ga_all.at[3, rows(i)], ga_send.at[2, i], ga_recv.at[2, i], sibling),
        ]

    def ga_local(i):
        return pltpu.make_async_copy(ga.at[i], ga_all.at[0, rows(i)], ga_own.at[i])

    def base_copy(i):
        return pltpu.make_async_copy(base_buf.at[i % 2], base.at[rows(i)], base_sem.at[i % 2])

    def right_half(step):
        return rows_at(ring_dp(place - 1 - step) * 2 * half, half)

    def left_half(step):
        return rows_at(ring_dp(place + 1 + step) * 2 * half + half, half)

    def ring(step):
        return [
            send(ring_buf.at[0, step], ring_buf.at[0, step + 1], ring_send.at[0, step], ring_recv.at[0, step], right),
            send(ring_buf.at[1, step], ring_buf.at[1, step + 1], ring_send.at[1, step], ring_recv.at[1, step], left),
        ]

    def hop(step, carry):
        for copy in ring(step):
            copy.wait()

        @pl.when(step < 6)
        def _():
            for side, cut in ((0, right_half(step + 1)), (1, left_half(step + 1))):
                ring_buf[side, step + 1] = (
                    ring_buf[side, step + 1].astype(F32) + dwd[cut].astype(F32)
                ).astype(BF)
            for copy in ring(step + 1):
                copy.start()

        return carry

    for copy in [load_ug(0)] + own_rows(0):
        copy.start()
    lax.fori_loop(0, count, lambda i, c: (load_gd(i).start(), c)[1], 0)
    load_u.start()
    lax.fori_loop(0, count, lambda i, c: (load_act(i).start(), c)[1], 0)
    sums[...] = jnp.zeros_like(sums)
    ff_sums[...] = jnp.zeros_like(ff_sums)
    greet([sibling, across, right, left])
    lax.fori_loop(0, count, lambda i, c: (load_gd(i).wait(), c)[1], 0)
    load_d.wait()

    def feed(i):
        slot = i % 2
        load_ug(i).wait()

        @pl.when(i + 1 < count)
        def _():
            load_ug(i + 1).start()

        @pl.when(i >= 2)
        def _():
            store_gug(i - 2).wait()

        def grads(n, carry):
            g_act = nt(gd[i].reshape(4 * CHUNK, width), w_d_b[tile(n)])
            up_proj = ug[slot, :, tile(n)].astype(F32)
            gate_proj = ug[slot, :, tile(n, width)].astype(F32)
            scale_up, scale_gate = scales[0:1, tile(n)], scales[1:2, tile(n)]
            gated = gate_proj * scale_gate
            sigmoid = jax.nn.sigmoid(gated)
            g_upscaled = g_act * (gated * sigmoid)
            g_gated = g_act * (up_proj * scale_up) * sigmoid * (1.0 + gated * (1.0 - sigmoid))
            ff_sums[0:1, tile(n)] = ff_sums[0:1, tile(n)] + jnp.sum(g_upscaled * up_proj, axis=0, keepdims=True)
            ff_sums[1:2, tile(n)] = ff_sums[1:2, tile(n)] + jnp.sum(g_gated * gate_proj, axis=0, keepdims=True)
            gug[slot, :, tile(n)] = (g_upscaled * scale_up).astype(BF)
            gug[slot, :, tile(n, width)] = (g_gated * scale_gate).astype(BF)
            return carry

        lax.fori_loop(0, width // TILE, grads, 0)
        store_gug(i).start()
        pl.when(i == 0)(load_u.wait)

        def through(n, carry):
            value = nt(gug[slot], w_ug_b[tile(n)])
            part[i % 3, :, :, tile(n)] = value.astype(BF).reshape(4, CHUNK, TILE)
            return carry

        lax.fori_loop(0, width // TILE, through, 0)
        core_a(i).start()
        core_b(i).start()
        core_a(i).wait_recv()
        part[i % 3, 2] = (part[i % 3, 2].astype(F32) + core[0, i].astype(F32)).astype(BF)
        chip(i).start()

    def down_grads():
        lax.fori_loop(0, count, lambda i, c: (load_act(i).wait(), c)[1], 0)

        def outer(n, carry):
            column[...] = jnp.zeros_like(column)

            def add(k, carry):
                column[...] = column[...] + nn(act[k], gd[k, :, :, tile(n)].reshape(4 * CHUNK, TILE))
                return carry

            lax.fori_loop(0, count, add, 0)
            dwd[:, tile(n)] = column[...].astype(BF)
            return carry

        lax.fori_loop(0, width // TILE, outer, 0)
        ring_buf[0, 0] = dwd[right_half(0)]
        ring_buf[1, 0] = dwd[left_half(0)]
        for copy in ring(0):
            copy.start()

    def finish(i):
        core_b(i).wait_recv()
        chip(i).wait_recv()
        through = part[i % 3, 0].astype(F32) + core[1, i].astype(F32) + x_buf[i].astype(F32)
        core_a(i).wait_send()
        core_b(i).wait_send()
        chip(i).wait_send()
        for copy in own_rows(i):
            copy.wait()
        value, unit, own = own_f[0], own_b[0].astype(F32), own_b[1].astype(F32)
        g_pre = unit_back(own_f[1] + through, value, hidden_inv[rows(i)])

        @pl.when(i + 1 < count)
        def _():
            for copy in own_rows(i + 1):
                copy.start()

        @pl.when(i >= 2)
        def _():
            base_copy(i - 2).wait()

        base_buf[i % 2] = g_pre * (1.0 - rate_attn)
        base_copy(i).start()
        sums[0:1] = sums[0:1] + jnp.sum(g_pre * (unit - own), axis=0, keepdims=True)
        ga[i] = unit_back(g_pre * rate_attn, unit, attn_inv[rows(i)]).astype(BF)
        copies = ga_copies(i)
        copies[0].start()
        copies[1].start()
        ga_local(i).start()

    def pass_grads(i):
        copies = ga_copies(i)
        copies[1].wait_recv()
        copies[2].start()

    stages = (feed, finish, pass_grads)

    def step(t, carry):
        for lag, stage in enumerate(stages):
            pl.when((t >= lag) & (t < lag + count))(functools.partial(stage, t - lag))
        pl.when(t == 0)(down_grads)

        @pl.when((t >= 1) & (t < 4))
        def _():
            lax.fori_loop(2 * t - 2, 2 * t, hop, 0)

        return carry

    lax.fori_loop(0, count + len(stages) - 1, step, 0)
    hop(6, 0)
    own = dp * 2 * half
    down_rows[pl.ds(0, half)] = ring_buf[0, 7].astype(F32) + dwd[rows_at(own, half)].astype(F32)
    down_rows[pl.ds(half, half)] = ring_buf[1, 7].astype(F32) + dwd[rows_at(own + half, half)].astype(F32)

    def close(i, carry):
        copies = ga_copies(i)
        copies[0].wait()
        copies[1].wait_send()
        copies[2].wait()
        ga_local(i).wait()
        return carry

    lax.fori_loop(0, count, close, 0)
    for i in (count - 2, count - 1):
        base_copy(i).wait()
        store_gug(i).wait()


def middle_back(gd_all, act_all, ug_all, hidden, attn_unit, states, back, attn_inv, hidden_inv, w_ug, w_d, rates,
                scales):
    rows, width = states.shape
    count = rows // CHUNK
    piece = width // 8
    vmem, hbm = pl.BlockSpec(memory_space=pltpu.VMEM), pl.BlockSpec(memory_space=pl.ANY)
    dma = pltpu.SemaphoreType.DMA
    return pl.pallas_call(
        middle_back_kernel,
        in_specs=[hbm] * 7 + [vmem] * 2 + [hbm] * 2 + [vmem] * 2,
        out_specs=[hbm, hbm, hbm, vmem, vmem, vmem],
        out_shape=[
            jax.ShapeDtypeStruct((rows, width), F32),
            jax.ShapeDtypeStruct((4, rows, width), BF),
            jax.ShapeDtypeStruct((count, 4 * CHUNK, 2 * width), BF),
            jax.ShapeDtypeStruct((piece, width), F32),
            jax.ShapeDtypeStruct((1, width), F32),
            jax.ShapeDtypeStruct((2, width), F32),
        ],
        scratch_shapes=[
            pltpu.VMEM(w_ug.shape, BF),
            pltpu.VMEM(w_d.shape, BF),
            pltpu.VMEM((3, 4, CHUNK, width), BF),
            pltpu.VMEM((2, count, CHUNK, width), BF),
            pltpu.VMEM((count, CHUNK, width), BF),
            pltpu.VMEM((count, CHUNK, width), BF),
            pltpu.VMEM((count, 4, CHUNK, width), BF),
            pltpu.VMEM((count, width, 4 * CHUNK), BF),
            pltpu.VMEM((2, 4 * CHUNK, 2 * width), BF),
            pltpu.VMEM((2, 4 * CHUNK, 2 * width), BF),
            pltpu.VMEM((2, CHUNK, width), F32),
            pltpu.VMEM((2, CHUNK, width), BF),
            pltpu.VMEM((2, CHUNK, width), F32),
            pltpu.VMEM((width, width), BF),
            pltpu.VMEM((width, TILE), F32),
            pltpu.VMEM((2, 8, piece // 2, width), BF),
            dma((count,)),
            dma((count,)),
            dma((2,)),
            dma((4,)),
            dma((2, count)),
            dma((2, count)),
            dma((count,)),
            dma((count,)),
            dma((3, count)),
            dma((3, count)),
            dma((count,)),
            dma((2,)),
            dma((2,)),
            dma((2,)),
            dma((2, 7)),
            dma((2, 7)),
        ],
        compiler_params=pltpu.CompilerParams(
            collective_id=4, has_side_effects=True, vmem_limit_bytes=60 << 20
        ),
        cost_estimate=pl.CostEstimate(flops=34 * 10**9, bytes_accessed=200 << 20, transcendentals=4 << 20),
        name="middle_back",
    )(gd_all, act_all, ug_all, hidden, attn_unit, states, back, attn_inv, hidden_inv, w_ug, w_d, rates, scales)


def order_kernel(where_ref, parent_ref, out_ref):
    base, me = where_ref[0], where_ref[1]
    shape = (128, 128)
    row = lax.broadcasted_iota(jnp.int32, shape, 0)
    block = lax.broadcasted_iota(jnp.int32, (8, 128), 1)
    real = block < NB
    parent = jnp.where(real & (parent_ref[...] >= 0), parent_ref[...] - base, -1)
    up = (row == parent[0:1]).astype(F32)
    up2 = nn(up, up)
    near = up + up2
    up4 = nn(up2, up2)
    near = near + nn(near, up2)
    near = near + nn(near, up4)
    above = near + nn(nn(up4, up4), up)
    depth = jnp.broadcast_to(jnp.sum(above, axis=0, keepdims=True), (8, 128)).astype(jnp.int32)
    before = (row < lax.broadcasted_iota(jnp.int32, shape, 1)).astype(F32)
    rank = nn(((depth == TRUNK) & real).astype(F32), before)
    parent_rank = nn(rank, up).astype(jnp.int32)
    sibling = jnp.sum(nn(up.T, up) * before, axis=0, keepdims=True).astype(jnp.int32)
    leaf = TRUNK + 4 + 2 * parent_rank + sibling
    slot = jnp.where(depth < TRUNK, depth, jnp.where(depth == TRUNK, TRUNK + rank.astype(jnp.int32), leaf))
    slot = jnp.where(real, slot, 127)
    mine = jnp.where(real, jnp.bitwise_xor(block // 5, me) * 5 + block % 5, 127)
    order = nt(mine.astype(F32), (row == slot[0:1]).astype(F32))
    back = nt(slot.astype(F32), (row == mine[0:1]).astype(F32))
    which = lax.broadcasted_iota(jnp.int32, (8, 128), 0)
    out_ref[...] = jnp.where(which == 0, order, back).astype(jnp.int32)


def tree_order(where, parents):
    return pl.pallas_call(
        order_kernel,
        in_specs=[pl.BlockSpec(memory_space=pltpu.SMEM), pl.BlockSpec(memory_space=pltpu.VMEM)],
        out_specs=pl.BlockSpec(memory_space=pltpu.VMEM),
        out_shape=jax.ShapeDtypeStruct((8, 128), jnp.int32),
        name="tree_order",
    )(where, jnp.broadcast_to(jnp.pad(parents, (0, 128 - NB), constant_values=-1), (8, 128)))


def local(
    states,
    teacher,
    parent_ids,
    valid_mask,
    w_query,
    w_key,
    w_value,
    w_out,
    w_up,
    w_gate,
    w_down,
    qk_scale,
    attn_rate,
    mlp_rate,
    up_scale,
    gate_scale,
):
    both = ("dp", "fsdp")
    dps, tps = 8, 4
    rows_w = w_query.shape[0]
    cols = D // tps
    hid = FF // tps
    ff_rows = FF // (dps * tps)
    me = lax.axis_index("fsdp")
    root_width = math.sqrt(D)
    mask_f = valid_mask.astype(F32)
    group_base = lax.axis_index("dp") * NB
    order = tree_order(jnp.stack((group_base, me)).astype(jnp.int32), parent_ids)

    count = jnp.sum(valid_mask)
    first_row = jnp.arange(rows_w, dtype=jnp.int32) == 0
    small = jnp.stack(
        (
            qk_scale,
            attn_rate,
            mlp_rate,
            jnp.where(first_row, count // 128, 0).astype(BF),
            jnp.where(first_row, count % 128, 0).astype(BF),
        ),
        axis=1,
    )
    small = jnp.pad(small, ((0, 0), (0, 59)))
    extra = jnp.pad(jnp.stack((up_scale, gate_scale), axis=1), ((0, 0), (69, 57)))
    spread = [(j, tps * (j % dps) + j // dps) for j in range(dps * tps)]
    tokens_t, w_t, w_o, w_ug, qkv, mixed, sums, share = forward(
        order, states, w_query, w_key, w_value, small, extra, lax.ppermute(w_out, both, spread), w_up, w_gate
    )
    small_all = w_t[3 * cols : 3 * cols + 8].astype(F32)
    rates = small_all[1:3]
    valid_count = 128.0 * jnp.sum(small_all[3]) + jnp.sum(small_all[4])
    scales = small_all[5:7] * jnp.array([[1.0], [root_width]], F32)
    scale_qk = lax.dynamic_slice_in_dim(small_all[0], me * cols, cols).reshape(cols // HEAD_DIM, HEAD_DIM, 1)

    mask_col = mask_f[:, None]
    w_ug, w_d, out_states, hidden, attn_unit, back, attn_inv, hidden_inv, sums_mid, gd_all, ht_all, act_all, ug_all = middle(
        share, states, teacher, mask_col * (2.0 / valid_count), mask_col, w_ug, w_down, rates, scales
    )
    base, ga_all, gug_all, grad_down, sums_back, ff_sums = middle_back(
        gd_all, act_all, ug_all, hidden, attn_unit, states, back, attn_inv, hidden_inv, w_ug, w_d, rates, scales
    )
    loss_local = jnp.sum(sums_mid[1])
    g_rate_mlp, g_rate_attn = sums_mid[0], sums_back[0]
    grad_up_scale, grad_gate_scale = ff_sums[0], ff_sums[1] * root_width
    g_qkv, g_scale, part_out, grad_up, grad_gate = attention_back(
        order, qkv, scale_qk, sums, mixed, ga_all.reshape(NB, BLOCK, D), w_o, ht_all, gug_all
    )
    g_qkv = g_qkv.reshape(3 * cols, TOK)
    slot = jnp.arange(tps, dtype=jnp.int32) == me
    qk_rows = jnp.where(slot[:, None], g_scale.reshape(1, cols), 0.0).reshape(dps * tps, rows_w)
    ff_terms = [
        jnp.where(slot[None, :, None], term.reshape(dps, 1, ff_rows), 0.0).reshape(dps * tps, ff_rows)
        for term in (grad_up_scale, grad_gate_scale)
    ]
    vectors = jnp.concatenate(
        [g_rate_attn.reshape(dps * tps, rows_w), g_rate_mlp.reshape(dps * tps, rows_w), qk_rows]
        + ff_terms
        + [jnp.broadcast_to(loss_local, (dps * tps, 512 - 3 * rows_w - 2 * ff_rows))],
        axis=1,
    ).reshape(dps, tps, 4, 128)
    part_out = part_out.reshape(dps, rows_w, D)
    grad_states, g_query, g_key, g_value, out_back, vector_share = last_exchange(
        order, base, tokens_t, g_qkv, w_t, part_out, vectors
    )
    vector_share = vector_share.reshape(512)
    grad_out = lax.ppermute(out_back, both, [(b, a) for a, b in spread])
    cuts = (0, rows_w, 2 * rows_w, 3 * rows_w, 3 * rows_w + ff_rows, 3 * rows_w + 2 * ff_rows)
    v = [vector_share[a:b] for a, b in zip(cuts, cuts[1:])]
    return (
        out_states,
        vector_share[-1] / valid_count,
        grad_states,
        g_query,
        g_key,
        g_value,
        grad_out,
        grad_up,
        grad_gate,
        grad_down,
        v[2],
        v[0],
        v[1],
        v[3],
        v[4],
    )


def solution(mesh):
    placed = (
        P(("dp", "fsdp"), None),
        P(("dp", "fsdp"), None),
        P("dp"),
        P(("dp", "fsdp")),
        P(("dp", "fsdp"), None),
        P(("dp", "fsdp"), None),
        P(("dp", "fsdp"), None),
        P(("dp", "fsdp"), None),
        P(("dp", "fsdp"), None),
        P(("dp", "fsdp"), None),
        P(("dp", "fsdp"), None),
        P(("dp", "fsdp")),
        P(("dp", "fsdp")),
        P(("dp", "fsdp")),
        P(("dp", "fsdp")),
        P(("dp", "fsdp")),
    )
    quick = mesh.shape["fsdp"] == 4 and mesh.shape["dp"] == 8
    return jax.shard_map(
        local if quick else general,
        mesh=mesh,
        in_specs=placed,
        out_specs=(
            P(("dp", "fsdp"), None),
            P(),
            P(("dp", "fsdp"), None),
            P(("dp", "fsdp"), None),
            P(("dp", "fsdp"), None),
            P(("dp", "fsdp"), None),
            P(("dp", "fsdp"), None),
            P(("dp", "fsdp"), None),
            P(("dp", "fsdp"), None),
            P(("dp", "fsdp"), None),
            P(("dp", "fsdp")),
            P(("dp", "fsdp")),
            P(("dp", "fsdp")),
            P(("dp", "fsdp")),
            P(("dp", "fsdp")),
        ),
        check_vma=False,
    )
```

```python
import functools
import math

import jax
import jax.numpy as jnp
from jax import lax
from jax.experimental import pallas as pl
from jax.experimental.pallas import tpu as pltpu
from jax.sharding import PartitionSpec as P


D = 1280
HEADS = 20
HEAD_DIM = 64
FF = 5120
BLOCK = 128
DEPTH = 10


EPS = 1e-06


def unit_rows(vector):
    inverse = lax.rsqrt(jnp.sum(vector * vector, axis=-1, keepdims=True) + EPS)
    return (vector * inverse, inverse)


def unit_back(grad, unit, inverse):
    return (grad - unit * jnp.sum(grad * unit, axis=-1, keepdims=True)) * inverse


def project(left, right):
    return jnp.dot(left, right, preferred_element_type=jnp.float32)


def project_back(grad, weight):
    return jnp.einsum("te,de->td", grad, weight, preferred_element_type=jnp.float32)


def ancestors(local_parent):
    column = jnp.arange(local_parent.shape[0], dtype=jnp.int32)
    columns = [column]
    for depth_step in range(DEPTH - 1):
        column = jnp.where(column >= 0, local_parent[jnp.maximum(column, 0)], -1)
        columns.append(column)
    return jnp.stack(columns, axis=1)


def head_back(grad_flat, unit, inverse, scale):
    scaled = (grad_flat * scale).reshape(unit.shape)
    raw = unit_back(scaled, unit, inverse).reshape(grad_flat.shape)
    scale_grad = jnp.sum(grad_flat * unit.reshape(grad_flat.shape), axis=0)
    return (raw, scale_grad)


def general(
    states,
    teacher,
    parent_ids,
    valid_mask,
    w_query,
    w_key,
    w_value,
    w_out,
    w_up,
    w_gate,
    w_down,
    qk_scale,
    attn_rate,
    mlp_rate,
    up_scale,
    gate_scale,
):
    rows_dev = states.shape[0]
    blocks_dev = rows_dev // BLOCK
    width_rows = w_query.shape[0]
    span = DEPTH * BLOCK
    factor = math.sqrt(HEAD_DIM)
    root_width = math.sqrt(D)
    mask_f = valid_mask.astype(jnp.float32)
    qkv_local = jnp.concatenate((w_query, w_key, w_value), axis=1)
    scal_width_local = jnp.stack((qk_scale, attn_rate, mlp_rate), axis=1)
    piece_qkv = lax.all_gather(qkv_local, ("dp", "fsdp"), axis=0, tiled=True)
    piece_out = lax.all_gather(w_out, ("dp", "fsdp"), axis=0, tiled=True)
    piece_scal = lax.all_gather(scal_width_local, ("dp", "fsdp"), axis=0, tiled=True)
    lefts = states
    total = jnp.dot(lefts, piece_qkv, preferred_element_type=jnp.float32)
    scal_whole = piece_scal
    qkv_raw = total
    scal_width = scal_whole
    scale_qk = scal_width[:, 0].astype(jnp.float32)
    rate_attn = scal_width[:, 1].astype(jnp.float32)
    rate_mlp = scal_width[:, 2].astype(jnp.float32)
    query_raw = qkv_raw[:, :D]
    key_raw = qkv_raw[:, D : 2 * D]
    values = qkv_raw[:, 2 * D :].astype(jnp.bfloat16)
    query_unit, query_inv = unit_rows(query_raw.reshape(rows_dev, HEADS, HEAD_DIM))
    key_unit, key_inv = unit_rows(key_raw.reshape(rows_dev, HEADS, HEAD_DIM))
    query_n = (query_unit.reshape(rows_dev, D) * scale_qk).astype(jnp.bfloat16)
    key_n = (key_unit.reshape(rows_dev, D) * scale_qk).astype(jnp.bfloat16)
    key_group, value_group = (
        lax.all_gather(key_n, "fsdp", axis=0, tiled=True),
        lax.all_gather(values, "fsdp", axis=0, tiled=True),
    )
    group_blocks = parent_ids.shape[0]
    group_base = lax.axis_index("dp") * group_blocks
    local_parent = jnp.where(parent_ids >= 0, parent_ids - group_base, -1)
    paths_all = ancestors(local_parent)
    own_first = lax.axis_index("fsdp") * blocks_dev
    paths = lax.dynamic_slice_in_dim(paths_all, own_first, blocks_dev, 0)
    safe_paths = jnp.maximum(paths, 0)
    key_rows = key_group.reshape(group_blocks, BLOCK, D)[safe_paths].reshape(
        blocks_dev, span, HEADS, HEAD_DIM
    )
    value_rows = value_group.reshape(group_blocks, BLOCK, D)[safe_paths].reshape(
        blocks_dev, span, HEADS, HEAD_DIM
    )
    slot_of = jnp.arange(span, dtype=jnp.int32) // BLOCK
    offset = jnp.arange(span, dtype=jnp.int32) % BLOCK
    row_pos = jnp.arange(BLOCK, dtype=jnp.int32)
    causal = offset[None, :] <= row_pos[:, None]
    is_live = jnp.take(paths, slot_of, axis=1) >= 0
    allowed = jnp.where(slot_of[None, None, :] == 0, causal[None], is_live[:, None, :])[:, None]
    query_heads = query_n.reshape(blocks_dev, BLOCK, HEADS, HEAD_DIM)
    scores = factor * jnp.einsum(
        "bqhd,bkhd->bhqk", query_heads, key_rows, preferred_element_type=jnp.float32
    )
    scores = jnp.where(allowed, scores, jnp.float32(-1e30))
    row_max = jnp.max(scores, axis=-1, keepdims=True)
    powers = jnp.exp(scores - row_max)
    row_sum = jnp.sum(powers, axis=-1, keepdims=True)
    probs_b = (powers / row_sum).astype(jnp.bfloat16)
    log_total = row_max + jnp.log(row_sum)
    mixed = jnp.einsum("bhqk,bkhd->bqhd", probs_b, value_rows, preferred_element_type=jnp.float32)
    mixed = mixed.reshape(rows_dev, D).astype(jnp.bfloat16)
    inputs = states.astype(jnp.float32)
    attn = project(mixed, piece_out)
    attn_unit, attn_inv = unit_rows(attn)
    hidden, hidden_inv = unit_rows(inputs + rate_attn * (attn_unit - inputs))
    hidden_b = hidden.astype(jnp.bfloat16)
    ffn_local = jnp.concatenate((w_up, w_gate), axis=1)
    scal_hidden_local = jnp.concatenate(
        (up_scale.reshape(width_rows, 4), gate_scale.reshape(width_rows, 4)), axis=1
    )
    piece_ffn = lax.all_gather(ffn_local, ("dp", "fsdp"), axis=0, tiled=True)
    piece_scal = lax.all_gather(scal_hidden_local, ("dp", "fsdp"), axis=0, tiled=True)
    lefts = hidden_b
    total = jnp.dot(lefts, piece_ffn, preferred_element_type=jnp.float32)
    scal_whole = piece_scal
    scale_up = scal_whole[:, :4].reshape(FF).astype(jnp.float32)
    scale_gate = scal_whole[:, 4:].reshape(FF).astype(jnp.float32)
    up_proj = total[:, :FF]
    gate_proj = total[:, FF:]
    upscaled = up_proj * scale_up
    gated = gate_proj * scale_gate * root_width
    sigmoid_gate = jax.nn.sigmoid(gated)
    act = (upscaled * (gated * sigmoid_gate)).astype(jnp.bfloat16)
    lefts = act
    down = jnp.dot(
        lefts,
        lax.all_gather(w_down, ("dp", "fsdp"), axis=0, tiled=True),
        preferred_element_type=jnp.float32,
    )
    down_unit, down_inv = unit_rows(down)
    result, result_inv = unit_rows(hidden + rate_mlp * (down_unit - hidden))
    loss_local = jnp.sum(mask_f[:, None] * (result - teacher) ** 2)
    valid_count, loss_sum = lax.psum((jnp.sum(mask_f), loss_local), ("dp", "fsdp"))
    loss = loss_sum / valid_count
    g_result = 2.0 * mask_f[:, None] * (result - teacher) / valid_count
    g_last = unit_back(g_result, result, result_inv)
    g_hidden = g_last * (1.0 - rate_mlp)
    g_rate_mlp = jnp.sum(g_last * (down_unit - hidden), axis=0)
    g_down = unit_back(g_last * rate_mlp, down_unit, down_inv).astype(jnp.bfloat16)
    g_act = jnp.einsum(
        "te,fe->tf",
        g_down,
        lax.all_gather(w_down, ("dp", "fsdp"), axis=0, tiled=True),
        preferred_element_type=jnp.float32,
    )
    g_upscaled = g_act * (gated * sigmoid_gate)
    g_gated = g_act * upscaled * sigmoid_gate * (1.0 + gated * (1.0 - sigmoid_gate))
    grad_up_scale = jnp.sum(g_upscaled * up_proj, axis=0)
    grad_gate_scale = jnp.sum(g_gated * gate_proj * root_width, axis=0)
    g_up = (g_upscaled * scale_up).astype(jnp.bfloat16)
    g_gate = (g_gated * scale_gate * root_width).astype(jnp.bfloat16)
    g_both = jnp.concatenate((g_up, g_gate), axis=1)
    g_hidden = g_hidden + jnp.einsum(
        "tc,dc->td",
        g_both,
        lax.all_gather(ffn_local, ("dp", "fsdp"), axis=0, tiled=True),
        preferred_element_type=jnp.float32,
    )
    scal_terms = jnp.concatenate(
        (grad_up_scale.reshape(D, 4), grad_gate_scale.reshape(D, 4)), axis=1
    )
    lefts = hidden_b
    main = jnp.einsum("td,tc->dc", lefts, g_both, preferred_element_type=jnp.float32)
    ffn_share = lax.psum_scatter(
        jnp.concatenate((main, scal_terms), axis=1), ("dp", "fsdp"), scatter_dimension=0, tiled=True
    )
    lefts = act
    grad_down = lax.psum_scatter(
        jnp.einsum("tf,te->fe", lefts, g_down, preferred_element_type=jnp.float32),
        ("dp", "fsdp"),
        scatter_dimension=0,
        tiled=True,
    )
    g_pre = unit_back(g_hidden, hidden, hidden_inv)
    g_states = g_pre * (1.0 - rate_attn)
    g_rate_attn = jnp.sum(g_pre * (attn_unit - inputs), axis=0)
    g_attn = unit_back(g_pre * rate_attn, attn_unit, attn_inv).astype(jnp.bfloat16)
    g_mixed = project_back(g_attn, piece_out).astype(jnp.bfloat16)
    scores = factor * jnp.einsum(
        "bqhd,bkhd->bhqk", query_heads, key_rows, preferred_element_type=jnp.float32
    )
    probs = jnp.where(allowed, jnp.exp(scores - log_total), jnp.float32(0.0))
    probs_again = probs.astype(jnp.bfloat16)
    g_heads = g_mixed.reshape(blocks_dev, BLOCK, HEADS, HEAD_DIM)
    g_probs = jnp.einsum("bqhd,bkhd->bhqk", g_heads, value_rows, preferred_element_type=jnp.float32)
    delta = jnp.sum(probs * g_probs, axis=-1, keepdims=True)
    g_scores = (probs * (g_probs - delta)).astype(jnp.bfloat16)
    g_query_n = factor * jnp.einsum(
        "bhqk,bkhd->bqhd", g_scores, key_rows, preferred_element_type=jnp.float32
    )
    g_key_rows = factor * jnp.einsum(
        "bhqk,bqhd->bkhd", g_scores, query_heads, preferred_element_type=jnp.float32
    )
    g_value_rows = jnp.einsum(
        "bhqk,bqhd->bkhd", probs_again, g_heads, preferred_element_type=jnp.float32
    )
    flat_paths = safe_paths.reshape(blocks_dev * DEPTH)
    g_key_group = (
        jnp.zeros((group_blocks, BLOCK, D), jnp.float32)
        .at[flat_paths]
        .add(g_key_rows.reshape(blocks_dev * DEPTH, BLOCK, D))
    )
    g_value_group = (
        jnp.zeros((group_blocks, BLOCK, D), jnp.float32)
        .at[flat_paths]
        .add(g_value_rows.reshape(blocks_dev * DEPTH, BLOCK, D))
    )
    g_key_n, g_values = (
        lax.psum_scatter(
            g_key_group.reshape(group_blocks * BLOCK, D).astype(jnp.bfloat16),
            "fsdp",
            scatter_dimension=0,
            tiled=True,
        ).astype(jnp.float32),
        lax.psum_scatter(
            g_value_group.reshape(group_blocks * BLOCK, D).astype(jnp.bfloat16),
            "fsdp",
            scatter_dimension=0,
            tiled=True,
        ).astype(jnp.float32),
    )
    g_query_raw, scale_from_query = head_back(
        g_query_n.reshape(rows_dev, D), query_unit, query_inv, scale_qk
    )
    g_key_raw, scale_from_key = head_back(g_key_n, key_unit, key_inv, scale_qk)
    grad_qk_scale = scale_from_query + scale_from_key
    g_qkv = jnp.concatenate(
        (
            g_query_raw.astype(jnp.bfloat16),
            g_key_raw.astype(jnp.bfloat16),
            g_values.astype(jnp.bfloat16),
        ),
        axis=1,
    )
    g_states = g_states + jnp.einsum(
        "tc,dc->td",
        g_qkv,
        lax.all_gather(qkv_local, ("dp", "fsdp"), axis=0, tiled=True),
        preferred_element_type=jnp.float32,
    )
    vector_terms = jnp.stack((grad_qk_scale, g_rate_attn, g_rate_mlp), axis=1)
    lefts = states
    main = jnp.einsum("td,tc->dc", lefts, g_qkv, preferred_element_type=jnp.float32)
    outer = jnp.einsum("td,tc->dc", mixed, g_attn, preferred_element_type=jnp.float32)
    attn_share = lax.psum_scatter(
        jnp.concatenate((main, outer, vector_terms), axis=1),
        ("dp", "fsdp"),
        scatter_dimension=0,
        tiled=True,
    )
    return (
        result.astype(jnp.bfloat16),
        loss,
        g_states,
        attn_share[:, :D],
        attn_share[:, D : 2 * D],
        attn_share[:, 2 * D : 3 * D],
        attn_share[:, 3 * D : 4 * D],
        ffn_share[:, :FF],
        ffn_share[:, FF : 2 * FF],
        grad_down,
        attn_share[:, 4 * D],
        attn_share[:, 4 * D + 1],
        attn_share[:, 4 * D + 2],
        ffn_share[:, 2 * FF : 2 * FF + 4].reshape(-1),
        ffn_share[:, 2 * FF + 4 : 2 * FF + 8].reshape(-1),
    )

TRUNK = 8
NB = 20
TOK = NB * BLOCK
F32 = jnp.float32
BF = jnp.bfloat16


def head_norm(raw):
    inv = lax.rsqrt(jnp.sum(raw * raw, axis=0, keepdims=True) + EPS)
    return raw * inv, inv


def lanes_at(start, size):
    return pl.ds(pl.multiple_of(start, 128), size)


def rows_at(start, size):
    return pl.ds(pl.multiple_of(start, 16), size)


def early_chunks(visit):
    for j in range(TRUNK // 2):
        parts = [(0, 256 * j, "all")] if j else []
        visit(256 * j, parts + [(256 * j, 256, "causal")])
    trunk = TRUNK * BLOCK
    for start in (trunk, trunk + 256):
        visit(start, [(0, trunk, "all"), (start, 256, "pair")])


def late_chunks(visit):
    trunk = TRUNK * BLOCK
    for j in range(4):
        start = trunk + 4 * BLOCK + 256 * j
        visit(start, [(0, trunk, "all"), (trunk + BLOCK * j, BLOCK, "all"), (start, 256, "pair")])


def masked(kind, value):
    if kind == "all":
        return value
    key = lax.broadcasted_iota(jnp.int32, (256, 256), 0)
    query = lax.broadcasted_iota(jnp.int32, (256, 256), 1)
    keep = key <= query
    if kind == "pair":
        keep = keep & ((key < 128) == (query < 128))
    return jnp.where(keep, value, jnp.zeros_like(value))


def nn(a, b):
    return lax.dot_general(a, b, (((1,), (0,)), ((), ())), preferred_element_type=F32)


def nt(a, b):
    return lax.dot_general(a, b, (((1,), (1,)), ((), ())), preferred_element_type=F32)


def attention_back_kernel(order, qkv, scales, sums, mixed, ga_all, w_o, ht_all, gug_all,
                          g_qkv, g_scale, part_out, g_up, g_gate,
                          w_b, ga_b, ga, gm, raw, out_b, qT, q, k, kT, v, gT, g, dq, dk, dv, delta, inv,
                          gug_b, ht_r, ht_l, ring, own, hid_buf, hid_in,
                          ga_sem, gug_sem, row_sem, raw_sem, out_sem, ring_send, ring_recv, a2a_send, a2a_recv):
    me = lax.axis_index("fsdp")
    place = ring_place()
    peers = group_peers()
    right, left = {"dp": ring_dp(place + 1)}, {"dp": ring_dp(place - 1)}
    count, chunk, side = gug_b.shape[0], ring.shape[3], ring.shape[4]
    heads = g_scale.shape[0]
    rows_w = hid_buf.shape[1]

    def slices(step):
        slot = step % 2
        cut_r = rows_at(ring_dp(place - 1 - step) * chunk, chunk)
        cut_l = rows_at(ring_dp(place + 1 + step) * chunk, chunk)
        return [
            pltpu.make_async_copy(ht_all.at[:, cut_r], ht_r.at[slot], row_sem.at[0, slot]),
            pltpu.make_async_copy(ht_all.at[:, cut_l], ht_l.at[slot], row_sem.at[1, slot]),
        ]

    def raw_copy(head):
        slot = head % 2
        return pltpu.make_async_copy(
            qkv.at[:, rows_at(head * HEAD_DIM, HEAD_DIM)], raw.at[slot], raw_sem.at[slot]
        )

    def out_copy(head):
        slot = head % 2
        return pltpu.make_async_copy(
            out_b.at[slot], g_qkv.at[:, rows_at(head * HEAD_DIM, HEAD_DIM)], out_sem.at[slot]
        )

    load_ga = pltpu.make_async_copy(ga_all, ga_b, ga_sem.at[0])
    load_ga.start()
    load_w = pltpu.make_async_copy(w_o.at[0], w_b, ga_sem.at[1])
    load_w.start()
    raw_copy(0).start()
    for copy in slices(0):
        copy.start()
    loads = [pltpu.make_async_copy(gug_all.at[i], gug_b.at[i], gug_sem.at[i]) for i in range(count)]
    for copy in loads:
        copy.start()
    for copy in slices(1):
        copy.start()
    greet([*peers, right, left])
    load_ga.wait()
    load_w.wait()

    def pick(i, carry):
        ga[lanes_at(i * BLOCK, BLOCK)] = ga_b[order[0, i]]
        return carry

    lax.fori_loop(0, NB, pick, 0)

    def back(n, carry):
        gm[:, tile(n)] = nt(w_b[...], ga[tile(n)]).astype(BF)
        return carry

    lax.fori_loop(0, TOK // TILE, back, 0)

    def outer(n, carry):
        part_out[:, tile(n)] = nn(mixed[...], ga[:, tile(n)]).astype(BF)
        return carry

    lax.fori_loop(0, D // TILE, outer, 0)

    def parts(step, which):
        slot = step % 2

        @pl.when(which == 0)
        def _():
            for copy in slices(step):
                copy.wait()

        own[...] = jnp.zeros_like(own)

        def add(i, carry):
            for d, rows in enumerate((ht_r, ht_l)):
                cut = lanes_at((2 * d + which) * side, side)
                own[d] = own[d] + nn(rows[slot, i], gug_b[i, :, cut])
            return carry

        lax.fori_loop(0, count, add, 0)

        @pl.when((which == 1) & (step + 2 < 8))
        def _():
            for copy in slices(step + 2):
                copy.start()

    def hop_copies(step, which):
        return [
            send(ring.at[d, which, step], ring.at[d, which, step + 1], ring_send.at[d, which, step],
                 ring_recv.at[d, which, step], peer)
            for d, peer in enumerate((right, left))
        ]

    def exchange():
        return [
            send(hid_buf.at[peer["fsdp"]], hid_in.at[me], a2a_send.at[i], a2a_recv.at[i], peer)
            for i, peer in enumerate(peers)
        ]

    def poll(index):
        step, which = index // 2, index % 2
        parts(step + 1, which)
        for copy in hop_copies(step, which):
            copy.wait()

        @pl.when(step < 6)
        def _():
            for d in range(2):
                ring[d, which, step + 1] = (ring[d, which, step + 1].astype(F32) + own[d]).astype(BF)
            for copy in hop_copies(step + 1, which):
                copy.start()

        @pl.when(step == 6)
        def _():
            for d in range(2):
                total = ring[d, which, 7].astype(F32) + own[d]
                for i in range(4):
                    hid_buf[i, :, lanes_at((2 * d + which) * side, side)] = total[
                        i * rows_w : (i + 1) * rows_w
                    ].astype(BF)

        @pl.when(index == 13)
        def _():
            for copy in exchange():
                copy.start()

    for copy in loads:
        copy.wait()

    def begin(which, carry):
        parts(0, which)
        for d in range(2):
            ring[d, which, 0] = own[d].astype(BF)
        for copy in hop_copies(0, which):
            copy.start()
        return carry

    lax.fori_loop(0, 2, begin, 0)

    def open_head(head):
        slot = head % 2
        raw_copy(head).wait()

        @pl.when(head + 1 < heads)
        def _():
            raw_copy(head + 1).start()

        @pl.when(head >= 2)
        def _():
            out_copy(head - 2).wait()

        scale = scales[head]
        mine = rows_at(head * HEAD_DIM, HEAD_DIM)

        for i in range(NB):
            here = slice(i * BLOCK, (i + 1) * BLOCK)
            q_unit, _ = head_norm(raw[slot, 0, :, here])
            k_unit, _ = head_norm(raw[slot, 1, :, here])
            q8 = (q_unit * scale).astype(BF) * BF(8.0)
            qT[:, here] = q8
            q[here, :] = q8.T
            kn = (k_unit * scale).astype(BF)
            kT[:, here] = kn
            k[here, :] = kn.T
            v[here, :] = raw[slot, 2, :, here].astype(BF).T
            gh = gm[mine, here]
            gT[:, here] = gh
            g[here, :] = gh.T
            delta[:, here] = jnp.sum(gh.astype(F32) * mixed[mine, here].astype(F32), axis=0, keepdims=True)
            inv[:, here] = sums[head, 0:1, here]
        dk[...] = jnp.zeros_like(dk)
        dv[...] = jnp.zeros_like(dv)

    def visit(start, pieces):
        span = lanes_at(start, 256)
        query, grad = qT[:, span], gT[:, span]
        query_rows, grad_rows = q[span, :], g[span, :]
        scale_row, delta_row = inv[:, span], delta[:, span]
        acc = jnp.zeros((64, 256), F32)
        for kstart, size, kind in pieces:
            keys = lanes_at(kstart, size)
            probs = masked(kind, jnp.exp(nn(k[keys, :], query)) * scale_row)
            g_probs = nn(v[keys, :], grad)
            g_scores = (probs * (g_probs - delta_row)).astype(BF)
            dv[keys, :] += nn(probs.astype(BF), grad_rows)
            dk[keys, :] += nn(g_scores, query_rows)
            acc = acc + nn(kT[:, keys], g_scores)
        dq[:, span] = acc * 8.0


    def close_head(head):
        slot = head % 2
        scale = scales[head]
        total = jnp.zeros((64, BLOCK), F32)
        for i in range(NB):
            here = slice(i * BLOCK, (i + 1) * BLOCK)
            for which, grad in ((0, dq[:, here]), (1, dk[here, :].T)):
                unit, inverse = head_norm(raw[slot, which, :, here])
                total = total + grad * unit
                scaled = grad * scale
                value = (scaled - unit * jnp.sum(scaled * unit, axis=0, keepdims=True)) * inverse
                out_b[slot, which, :, here] = value.astype(BF)
            out_b[slot, 2, :, here] = dv[here, :].T.astype(BF)
        g_scale[head] = jnp.sum(total, axis=1, keepdims=True)
        out_copy(head).start()

    def work(i, carry):
        head, segment = i // 4, i % 4
        pl.when(segment == 0)(functools.partial(open_head, head))
        pl.when(segment == 1)(functools.partial(early_chunks, visit))
        pl.when(segment == 2)(functools.partial(late_chunks, visit))
        pl.when(segment == 3)(functools.partial(close_head, head))
        pl.when(i < 14)(functools.partial(poll, i))
        return carry

    lax.fori_loop(0, 4 * heads, work, 0)
    for copy in exchange():
        copy.wait()
    hid_in[me] = hid_buf[me]
    size = g_up.shape[1] // 32
    for which, out in enumerate((g_up, g_gate)):
        for d in range(8):
            start = (8 * which + d) * size
            block = [hid_in[i, :, start : start + size].astype(F32) for i in range(4)]
            out[:, d * 4 * size : (d + 1) * 4 * size] = jnp.concatenate(block, axis=1)
    for head in (heads - 2, heads - 1):
        out_copy(head).wait()


def attention_back(order, qkv, scales, sums, mixed, ga_all, w_o, ht_all, gug_all):
    heads = scales.shape[0]
    count, tokens, hidden_width = gug_all.shape
    chunk = ht_all.shape[1] // 8
    side = hidden_width // 4
    rows_w = chunk // 4
    vmem, hbm = pl.BlockSpec(memory_space=pltpu.VMEM), pl.BlockSpec(memory_space=pl.ANY)
    smem = pl.BlockSpec(memory_space=pltpu.SMEM)
    dma = pltpu.SemaphoreType.DMA
    return pl.pallas_call(
        attention_back_kernel,
        in_specs=[smem, hbm, vmem, vmem, vmem, hbm, hbm, hbm, hbm],
        out_specs=[hbm, vmem, vmem, vmem, vmem],
        out_shape=[
            jax.ShapeDtypeStruct(qkv.shape, BF),
            jax.ShapeDtypeStruct(scales.shape, F32),
            jax.ShapeDtypeStruct(w_o.shape[1:], BF),
            jax.ShapeDtypeStruct((rows_w, 2 * hidden_width), F32),
            jax.ShapeDtypeStruct((rows_w, 2 * hidden_width), F32),
        ],
        scratch_shapes=[
            pltpu.VMEM(w_o.shape[1:], BF),
            pltpu.VMEM(ga_all.shape, BF),
            pltpu.VMEM((TOK, w_o.shape[2]), BF),
            pltpu.VMEM(mixed.shape, BF),
            pltpu.VMEM((2, 3, HEAD_DIM, TOK), F32),
            pltpu.VMEM((2, 3, HEAD_DIM, TOK), BF),
            pltpu.VMEM((HEAD_DIM, TOK), BF),
            pltpu.VMEM((TOK, HEAD_DIM), BF),
            pltpu.VMEM((TOK, HEAD_DIM), BF),
            pltpu.VMEM((HEAD_DIM, TOK), BF),
            pltpu.VMEM((TOK, HEAD_DIM), BF),
            pltpu.VMEM((HEAD_DIM, TOK), BF),
            pltpu.VMEM((TOK, HEAD_DIM), BF),
            pltpu.VMEM((HEAD_DIM, TOK), F32),
            pltpu.VMEM((TOK, HEAD_DIM), F32),
            pltpu.VMEM((TOK, HEAD_DIM), F32),
            pltpu.VMEM((1, TOK), F32),
            pltpu.VMEM((1, TOK), F32),
            pltpu.VMEM(gug_all.shape, BF),
            pltpu.VMEM((2, count, chunk, tokens), BF),
            pltpu.VMEM((2, count, chunk, tokens), BF),
            pltpu.VMEM((2, 2, 8, chunk, side), BF),
            pltpu.VMEM((2, chunk, side), F32),
            pltpu.VMEM((4, rows_w, hidden_width), BF),
            pltpu.VMEM((4, rows_w, hidden_width), BF),
            dma((2,)),
            dma((count,)),
            dma((2, 2)),
            dma((2,)),
            dma((2,)),
            dma((2, 2, 7)),
            dma((2, 2, 7)),
            dma((3,)),
            dma((3,)),
        ],
        compiler_params=pltpu.CompilerParams(
            collective_id=5, has_side_effects=True, vmem_limit_bytes=62 << 20
        ),
        name="attention_back",
        cost_estimate=pl.CostEstimate(flops=40 * 10**9, bytes_accessed=60 << 20, transcendentals=14 << 20),
    )(order, qkv, scales, sums, mixed, ga_all, w_o, ht_all, gug_all)


MESH = pl.DeviceIdType.MESH


def ring_place():
    dp = lax.axis_index("dp")
    z, y = dp // 2, dp % 2
    return z + y * (7 - 2 * z)


def ring_dp(place):
    place = (place + 16) % 8
    y = place // 4
    return 2 * (place + y * (7 - 2 * place)) + y


def greet(peers):
    barrier = pltpu.get_barrier_semaphore()
    for peer in peers:
        pl.semaphore_signal(barrier, inc=1, device_id=peer, device_id_type=MESH)
    pl.semaphore_wait(barrier, len(peers))


def group_peers():
    me = lax.axis_index("fsdp")
    core = 1 - 2 * (me % 2)
    chip = 2 - 4 * (me // 2)
    return {"fsdp": me + core}, {"fsdp": me + chip}, {"fsdp": me + core + chip}


def send(src, dst, send_sem, recv_sem, peer):
    return pltpu.make_async_remote_copy(
        src_ref=src, dst_ref=dst, send_sem=send_sem, recv_sem=recv_sem, device_id=peer, device_id_type=MESH
    )


EARLY_HOPS = 4


def hidden_ring(ref, sends, recvs, step, base=0):
    place = ring_place()
    right, left = {"dp": ring_dp(place + 1)}, {"dp": ring_dp(place - 1)}
    chunk = ref.shape[0] // 8
    to_right, to_left = ring_dp(place - step) * chunk, ring_dp(place + step) * chunk
    first, size = 48, chunk // 2
    cuts = ((to_right, first, right), (to_left + size, first, left),
            (to_right + first, size - first, right), (to_left + size + first, size - first, left))
    return [
        send(ref.at[rows_at(start, rows)], ref.at[rows_at(start, rows)], sends.at[i, step - base],
             recvs.at[i, step - base], peer)
        for i, (start, rows, peer) in enumerate(cuts)
    ]


def forward_kernel(order, states, w_query, w_key, w_value, small, extra, out_piece, w_up, w_gate,
                   tokens_t, w_t, w_o, w_ug, qkv, mixed, sums, mixed_n,
                   qkv_send, ug_send, land, weights, tok, turned, tok_t, out_w, ug_land, ug_own, raw, qs, ks, vs, blocks, natural,
                   tok_send, tok_recv, a2a_send, a2a_recv, ring_send, ring_recv, ug_s, ug_r, local_sem, raw_sem,
                   w_send, w_recv):
    me, dp = lax.axis_index("fsdp"), lax.axis_index("dp")
    place = ring_place()
    sibling, across, corner = group_peers()
    right, left = {"dp": ring_dp(place + 1)}, {"dp": ring_dp(place - 1)}
    rows, width = states.shape
    piece = land.shape[1]
    chunk = 4 * piece
    half = chunk // 2
    cols = mixed.shape[0]
    heads = cols // HEAD_DIM
    own = pltpu.make_async_copy(states, tok.at[pl.ds(0, rows)], local_sem.at[0])
    own.start()
    for i in range(4):
        cut = slice(i * cols, (i + 1) * cols)
        block = [w[:, cut].astype(F32) for w in (w_query, w_key, w_value)] + [small[...].astype(F32)]
        qkv_send[i] = jnp.concatenate(block, axis=1).astype(BF)
    greet([sibling, across, corner, right, left])

    exchange, ug_exchange = [], []
    for i, peer in enumerate((sibling, across, corner)):
        copy = send(qkv_send.at[peer["fsdp"]], land.at[me], a2a_send.at[i], a2a_recv.at[i], peer)
        copy.start()
        exchange.append(copy)
    far = []
    for i in range(2):
        part = pl.ds(i * (rows // 2), rows // 2)
        here = pl.ds(2 * rows + i * (rows // 2), rows // 2)
        copy = send(states.at[part], tok.at[here], tok_send.at[i], tok_recv.at[i], across)
        copy.start()
        far.append(copy)
    near = send(states, tok.at[pl.ds(rows, rows)], tok_send.at[2], tok_recv.at[2], sibling)
    near.start()
    size = w_up.shape[1] // 32
    for i in range(4):
        for which, w in enumerate((w_up, w_gate)):
            for half_d in range(2):
                block = [
                    w[:, (4 * d + i) * size : (4 * d + i + 1) * size].astype(F32)
                    for d in range(4 * half_d, 4 * half_d + 4)
                ]
                start = (8 * which + 4 * half_d) * size
                ug_send[i, :, start : start + 4 * size] = jnp.concatenate(block, axis=1).astype(BF)
    land[me] = qkv_send[me]
    ug_land[me] = ug_send[me]
    out_w[dp] = out_piece[...]
    vs[HEAD_DIM:, :] = jnp.ones((vs.shape[0] - HEAD_DIM, TOK), BF)
    for copy in exchange:
        copy.wait()
    weights[rows_at(dp * chunk, chunk)] = jnp.concatenate([land[i].astype(F32) for i in range(4)], axis=0).astype(BF)
    last = pl.ds(weights.shape[1] - 128, 128)
    weights[rows_at(dp * chunk, chunk), last] = weights[rows_at(dp * chunk, chunk), last] + extra[...]

    def ring_copies(step):
        to_right, to_left = ring_dp(place - step), ring_dp(place + step)
        first, second = rows_at(to_right * chunk, half), rows_at(to_left * chunk + half, half)
        lanes_r, lanes_l = pl.ds(0, width // 2), pl.ds(width // 2, width // 2)
        return [
            send(ref, ref, ring_send.at[i, step], ring_recv.at[i, step], peer)
            for i, (ref, peer) in enumerate(
                (
                    (weights.at[first], right),
                    (weights.at[second], left),
                    (out_w.at[to_right, :, lanes_r], right),
                    (out_w.at[to_left, :, lanes_l], left),
                )
            )
        ]

    def hop(step, carry):
        for copy, later in zip(ring_copies(step), ring_copies(step + 1)):
            copy.wait()
            pl.when(step < 6)(later.start)
        return carry

    def ug_hop(step):
        for copy, later in zip(hidden_ring(w_ug, ug_s, ug_r, step), hidden_ring(w_ug, ug_s, ug_r, step + 1)):
            copy.wait()
            pl.when(step < EARLY_HOPS - 1)(later.start)

    for copy in ring_copies(0):
        copy.start()

    def turn(i, carry):
        turned[i] = tok[lanes_at(i * BLOCK, BLOCK)].T
        return carry

    lax.fori_loop(0, 1, hop, 0)
    near.wait()
    own.wait()
    lax.fori_loop(0, 4, turn, 0)
    lax.fori_loop(1, 2, hop, 0)
    lax.fori_loop(4, 7, turn, 0)
    lax.fori_loop(2, 3, hop, 0)
    lax.fori_loop(7, 10, turn, 0)
    lax.fori_loop(3, 5, hop, 0)
    passed = []
    for i in range(2):
        far[i].wait()
        here = pl.ds(2 * rows + i * (rows // 2), rows // 2)
        there = pl.ds(3 * rows + i * (rows // 2), rows // 2)
        copy = send(tok.at[here], tok.at[there], tok_send.at[3 + i], tok_recv.at[3 + i], sibling)
        copy.start()
        passed.append(copy)
    for i, peer in enumerate((sibling, across, corner)):
        copy = send(ug_send.at[peer["fsdp"]], ug_land.at[me], a2a_send.at[3 + i], a2a_recv.at[3 + i], peer)
        copy.start()
        ug_exchange.append(copy)
    lax.fori_loop(5, 6, hop, 0)
    lax.fori_loop(10, 15, turn, 0)
    lax.fori_loop(6, 7, hop, 0)
    for copy in passed:
        copy.wait()

    lax.fori_loop(15, NB, turn, 0)

    def arrange(i, carry):
        tok_t[:, lanes_at(i * BLOCK, BLOCK)] = turned[order[0, i]]
        return carry

    lax.fori_loop(0, NB, arrange, 0)
    keep = pltpu.make_async_copy(tok_t, tokens_t, local_sem.at[2])
    keep.start()

    def turn_weights(i, carry):
        w_t[:, lanes_at(i * BLOCK, BLOCK)] = weights[rows_at(i * BLOCK, BLOCK)].T
        return carry

    lax.fori_loop(0, width // BLOCK, turn_weights, 0)
    for copy in ug_exchange:
        copy.wait()
    ug_own[...] = jnp.concatenate([ug_land[i].astype(F32) for i in range(4)], axis=0).astype(BF)
    ug_store = pltpu.make_async_copy(ug_own, w_ug.at[rows_at(dp * chunk, chunk)], local_sem.at[1])
    ug_store.start()
    ug_store.wait()
    for copy in hidden_ring(w_ug, ug_s, ug_r, 0):
        copy.start()
    w_o[0] = jnp.concatenate([out_w[i].astype(F32) for i in range(8)], axis=0).astype(BF)
    w_copies = [
        send(w_o.at[0], w_o.at[i + 1], w_send.at[i], w_recv.at[i], peer)
        for i, peer in enumerate((sibling, across, corner))
    ]
    for copy in w_copies:
        copy.start()

    def raw_copies(head):
        slot = head % 2
        return [
            pltpu.make_async_copy(
                raw.at[slot, pl.ds(which * HEAD_DIM, HEAD_DIM)],
                qkv.at[which, rows_at(head * HEAD_DIM, HEAD_DIM)],
                raw_sem.at[slot, which],
            )
            for which in range(3)
        ]

    def attend(head, carry):
        slot = head % 2

        @pl.when(head >= 2)
        def _():
            for copy in raw_copies(head - 2):
                copy.wait()

        left_rows = jnp.concatenate(
            [w_t[rows_at(which * cols + head * HEAD_DIM, HEAD_DIM)] for which in range(3)], axis=0
        )

        def project_tile(n, carry):
            raw[slot, :, tile(n)] = nn(left_rows, tok_t[:, tile(n)])
            return carry

        lax.fori_loop(0, TOK // TILE, project_tile, 0, unroll=2)
        for copy in raw_copies(head):
            copy.start()
        scale = weights[rows_at(me * cols + head * HEAD_DIM, HEAD_DIM), last][:, HEAD_DIM : HEAD_DIM + 1].astype(F32)

        def prepare(i, carry):
            here = lanes_at(i * BLOCK, BLOCK)
            q_unit, _ = head_norm(raw[slot, pl.ds(0, HEAD_DIM), here])
            k_unit, _ = head_norm(raw[slot, pl.ds(HEAD_DIM, HEAD_DIM), here])
            qs[:, here] = (q_unit * scale).astype(BF) * BF(8.0)
            ks[here, :] = (k_unit * scale).astype(BF).T
            vs[0:HEAD_DIM, here] = raw[slot, pl.ds(2 * HEAD_DIM, HEAD_DIM), here].astype(BF)
            return carry

        lax.fori_loop(0, NB, prepare, 0, unroll=NB)

        def visit(start, parts):
            span = lanes_at(start, 256)
            query = qs[:, span]
            acc = jnp.zeros((vs.shape[0], 256), F32)
            for kstart, count, kind in parts:
                keys = lanes_at(kstart, count)
                powers = masked(kind, jnp.exp(nn(ks[keys, :], query))).astype(BF)
                acc = acc + nn(vs[:, keys], powers)
            total = 1.0 / acc[HEAD_DIM : HEAD_DIM + 1, :]
            mixed[rows_at(head * HEAD_DIM, HEAD_DIM), span] = (acc[0:HEAD_DIM, :] * total).astype(BF)
            sums[head, :, span] = jnp.broadcast_to(total, (8, 256))

        early_chunks(visit)
        late_chunks(visit)

        @pl.when(head % 2 == 1)
        def _():
            ug_hop(head // 2)

        return carry

    lax.fori_loop(0, heads, attend, 0)
    ug_hop(heads // 2)

    def split(i, carry):
        blocks[i] = mixed[:, lanes_at(i * BLOCK, BLOCK)]
        return carry

    def arrange_back(i, carry):
        natural[i] = blocks[order[1, i]]
        return carry

    lax.fori_loop(0, NB, split, 0)
    lax.fori_loop(0, NB, arrange_back, 0)
    keep_mixed = pltpu.make_async_copy(natural, mixed_n, local_sem.at[3])
    keep_mixed.start()
    ug_hop(heads // 2 + 1)
    lax.fori_loop(heads // 2 + 2, EARLY_HOPS, lambda step, c: (ug_hop(step), c)[1], 0)
    keep.wait()
    keep_mixed.wait()
    for copy in w_copies:
        copy.wait()
    for head in (heads - 2, heads - 1):
        for copy in raw_copies(head):
            copy.wait()


def forward(order, states, w_query, w_key, w_value, small, extra, out_piece, w_up, w_gate):
    tps, rows_w = 4, w_query.shape[0]
    tokens, width = states.shape
    packed = 3 * width // tps + small.shape[1]
    hidden_width = 2 * w_up.shape[1] // tps
    cols = 8 * rows_w
    vmem, hbm = pl.BlockSpec(memory_space=pltpu.VMEM), pl.BlockSpec(memory_space=pl.ANY)
    smem = pl.BlockSpec(memory_space=pltpu.SMEM)
    dma = pltpu.SemaphoreType.DMA
    return pl.pallas_call(
        forward_kernel,
        in_specs=[smem, hbm] + [vmem] * 8,
        out_specs=[hbm, vmem, vmem, hbm, hbm, vmem, vmem, hbm],
        out_shape=[
            jax.ShapeDtypeStruct((width, TOK), BF),
            jax.ShapeDtypeStruct((packed, width), BF),
            jax.ShapeDtypeStruct((tps, cols, width), BF),
            jax.ShapeDtypeStruct((width, hidden_width), BF),
            jax.ShapeDtypeStruct((3, cols, TOK), F32),
            jax.ShapeDtypeStruct((cols, TOK), BF),
            jax.ShapeDtypeStruct((cols // HEAD_DIM, 8, TOK), F32),
            jax.ShapeDtypeStruct((NB, cols, BLOCK), BF),
        ],
        scratch_shapes=[
            pltpu.VMEM((tps, rows_w, packed), BF),
            pltpu.VMEM((tps, rows_w, hidden_width), BF),
            pltpu.VMEM((tps, rows_w, packed), BF),
            pltpu.VMEM((width, packed), BF),
            pltpu.VMEM((TOK, width), BF),
            pltpu.VMEM((NB, width, BLOCK), BF),
            pltpu.VMEM((width, TOK), BF),
            pltpu.VMEM((8, rows_w, width), BF),
            pltpu.VMEM((tps, rows_w, hidden_width), BF),
            pltpu.VMEM((tps * rows_w, hidden_width), BF),
            pltpu.VMEM((2, 3 * HEAD_DIM, TOK), F32),
            pltpu.VMEM((HEAD_DIM, TOK), BF),
            pltpu.VMEM((TOK, HEAD_DIM), BF),
            pltpu.VMEM((HEAD_DIM + 16, TOK), BF),
            pltpu.VMEM((NB, cols, BLOCK), BF),
            pltpu.VMEM((NB, cols, BLOCK), BF),
            dma((5,)),
            dma((5,)),
            dma((6,)),
            dma((6,)),
            dma((4, 7)),
            dma((4, 7)),
            dma((4, EARLY_HOPS)),
            dma((4, EARLY_HOPS)),
            dma((4,)),
            dma((2, 3)),
            dma((3,)),
            dma((3,)),
        ],
        compiler_params=pltpu.CompilerParams(
            collective_id=1, has_side_effects=True, vmem_limit_bytes=56 << 20
        ),
        cost_estimate=pl.CostEstimate(flops=12 * 10**9, bytes_accessed=200 << 20, transcendentals=14 << 20),
        name="forward",
    )(order, states, w_query, w_key, w_value, small, extra, out_piece, w_up, w_gate)


def last_kernel(order, base, tokens_t, g_qkv, w_t, part_out, vectors,
                g_states, g_query, g_key, g_value, out_rows, vec_own,
                gq_b, blocks, tok_r, tok_l, share, turned, core_buf, x_buf, base_b, gs_b,
                ring_r, ring_l, ring_o, ring_v, next_r, next_l, row_buf, row_in, vec_part, vec_in,
                in_sem, row_sem, base_sem, core_send, core_recv, x_send, x_recv,
                ring_send, ring_recv, a2a_send, a2a_recv):
    me, dp = lax.axis_index("fsdp"), lax.axis_index("dp")
    place = ring_place()
    sibling, across, corner = group_peers()
    right, left = {"dp": ring_dp(place + 1)}, {"dp": ring_dp(place - 1)}
    chunk, side = ring_r.shape[1], ring_r.shape[2]
    rows = share.shape[1]
    quarter = rows // 4
    width = w_t.shape[1]
    heads_width = gq_b.shape[0]
    rows_w = row_buf.shape[1]

    def slices(step):
        slot = step % 2
        cut_r = rows_at(ring_dp(place - 1 - step) * chunk, chunk)
        cut_l = rows_at(ring_dp(place + 1 + step) * chunk, chunk)
        return [
            pltpu.make_async_copy(tokens_t.at[cut_r], tok_r.at[slot], row_sem.at[0, slot]),
            pltpu.make_async_copy(tokens_t.at[cut_l], tok_l.at[slot], row_sem.at[1, slot]),
        ]

    def base_copy(i):
        return pltpu.make_async_copy(base.at[pl.ds(i * quarter, quarter)], base_b.at[i % 2], base_sem.at[0, i % 2])

    def gs_copy(i):
        return pltpu.make_async_copy(gs_b.at[i % 2], g_states.at[pl.ds(i * quarter, quarter)], base_sem.at[1, i % 2])

    load_q = pltpu.make_async_copy(g_qkv, gq_b, in_sem.at[0])
    load_q.start()
    for step in (0, 1):
        for copy in slices(step):
            copy.start()
    greet([sibling, across, corner, right, left])

    def parts(step):
        slot = step % 2
        for copy in slices(step):
            copy.wait()
        next_r[...] = nt(tok_r[slot], gq_b[pl.ds(0, side)])
        next_l[...] = nt(tok_l[slot], gq_b[pl.ds(side, heads_width - side)])

        @pl.when(step + 2 < 8)
        def _():
            for copy in slices(step + 2):
                copy.start()

    def hop_copies(step):
        return [
            send(ring.at[step], ring.at[step + 1], ring_send.at[i, step], ring_recv.at[i, step], peer)
            for i, (ring, peer) in enumerate(((ring_r, right), (ring_l, left), (ring_o, left), (ring_v, right)))
        ]

    def through(r, slot):
        for i in range(rows // BLOCK):
            turned[i * BLOCK : (i + 1) * BLOCK] = blocks[order[1, r * (rows // BLOCK) + i]].T

        def one(n, carry):
            share[slot, :, tile(n)] = nn(turned[...], w_t[pl.ds(0, heads_width), tile(n)]).astype(BF)
            return carry

        lax.fori_loop(0, width // TILE, one, 0)

    core = [
        send(share.at[0], core_buf.at[0], core_send.at[0], core_recv.at[0], sibling),
        send(share.at[2], core_buf.at[1], core_send.at[1], core_recv.at[1], sibling),
    ]
    far = [
        send(share.at[1, pl.ds(i * quarter, quarter)], x_buf.at[pl.ds(i * quarter, quarter)], x_send.at[i],
             x_recv.at[i], across)
        for i in range(4)
    ]
    load_q.wait()

    def split(i, carry):
        blocks[i] = gq_b[:, lanes_at(i * BLOCK, BLOCK)]
        return carry

    def hop(step, carry):
        parts(step)

        @pl.when(step == 0)
        def _():
            ring_r[0] = next_r[...].astype(BF)
            ring_l[0] = next_l[...].astype(BF)
            ring_o[0] = part_out[ring_dp(place + 1)]
            ring_v[0] = vectors[ring_dp(place - 1)]

        @pl.when(step > 0)
        def _():
            before, now = hop_copies(step - 1), hop_copies(step)
            before[0].wait()
            ring_r[step] = (ring_r[step].astype(F32) + next_r[...]).astype(BF)
            now[0].start()
            before[1].wait()
            ring_l[step] = (ring_l[step].astype(F32) + next_l[...]).astype(BF)
            now[1].start()
            before[2].wait()
            ring_o[step] = (ring_o[step].astype(F32) + part_out[ring_dp(place + 1 + step)].astype(F32)).astype(BF)
            now[2].start()
            before[3].wait()
            ring_v[step] = ring_v[step] + vectors[ring_dp(place - 1 - step)]
            now[3].start()

        @pl.when(step == 0)
        def _():
            for copy in hop_copies(0):
                copy.start()

        @pl.when(step < 4)
        def _():
            @pl.when(step == 0)
            def _():
                lax.fori_loop(0, NB, split, 0)
                through(3, 0)
                core[0].start()

            @pl.when(step < 3)
            def _():
                through(2 - step, (step + 1) % 3)

            @pl.when(step == 0)
            def _():
                core[0].wait()
                for i in range(4):
                    span = pl.ds(i * quarter, quarter)
                    share[1, span] = (share[1, span].astype(F32) + core_buf[0, span].astype(F32)).astype(BF)
                    far[i].start()

            @pl.when(step == 1)
            def _():
                core[1].start()

        return carry

    lax.fori_loop(0, 7, hop, 0)
    base_copy(0).start()
    base_copy(1).start()
    parts(7)
    for copy in hop_copies(6):
        copy.wait()
    total = jnp.concatenate((ring_r[7].astype(F32) + next_r[...], ring_l[7].astype(F32) + next_l[...]), axis=1)
    for i in range(4):
        row_buf[i] = total[i * rows_w : (i + 1) * rows_w].astype(BF)
    vec_part[...] = ring_v[7] + vectors[dp]
    exchange = []
    for i, peer in enumerate((sibling, across, corner)):
        to = peer["fsdp"]
        copies = [
            send(row_buf.at[to], row_in.at[me], a2a_send.at[i], a2a_recv.at[i], peer),
            send(vec_part.at[to], vec_in.at[me], a2a_send.at[3 + i], a2a_recv.at[3 + i], peer),
        ]
        for copy in copies:
            copy.start()
        exchange += copies
    row_in[me] = row_buf[me]
    vec_in[me] = vec_part[me]
    out_rows[...] = ring_o[7].astype(F32) + part_out[dp].astype(F32)
    core[1].wait()
    for i in range(4):
        span = pl.ds(i * quarter, quarter)
        far[i].wait()
        base_copy(i).wait()
        if i >= 2:
            gs_copy(i - 2).wait()
        gs_b[i % 2] = base_b[i % 2] + (
            share[0, span].astype(F32) + core_buf[1, span].astype(F32) + x_buf[span].astype(F32)
        )
        gs_copy(i).start()
        if i < 2:
            base_copy(i + 2).start()
    for copy in exchange:
        copy.wait()
    vec_own[...] = vec_in[0] + vec_in[1] + vec_in[2] + vec_in[3]
    cols = heads_width // 3
    for which, out in enumerate((g_query, g_key, g_value)):
        out[...] = jnp.concatenate(
            [row_in[i, :, which * cols : (which + 1) * cols].astype(F32) for i in range(4)], axis=1
        )
    for i in (2, 3):
        gs_copy(i).wait()


def last_exchange(order, base, tokens_t, g_qkv, w_t, part_out, vectors):
    rows, width = base.shape
    heads_width = g_qkv.shape[0]
    rows_w = part_out.shape[1]
    chunk = 4 * rows_w
    side = 2 * heads_width // 3
    vmem, hbm = pl.BlockSpec(memory_space=pltpu.VMEM), pl.BlockSpec(memory_space=pl.ANY)
    dma = pltpu.SemaphoreType.DMA
    return pl.pallas_call(
        last_kernel,
        in_specs=[pl.BlockSpec(memory_space=pltpu.SMEM), hbm, hbm, hbm, vmem, vmem, vmem],
        out_specs=[hbm] + [vmem] * 5,
        out_shape=[jax.ShapeDtypeStruct((rows, width), F32)]
        + [jax.ShapeDtypeStruct((rows_w, width), F32)] * 4
        + [jax.ShapeDtypeStruct(vectors.shape[2:], F32)],
        scratch_shapes=[
            pltpu.VMEM(g_qkv.shape, BF),
            pltpu.VMEM((NB, heads_width, BLOCK), BF),
            pltpu.VMEM((2, chunk, tokens_t.shape[1]), BF),
            pltpu.VMEM((2, chunk, tokens_t.shape[1]), BF),
            pltpu.VMEM((3, rows, width), BF),
            pltpu.VMEM((rows, heads_width), BF),
            pltpu.VMEM((2, rows, width), BF),
            pltpu.VMEM((rows, width), BF),
            pltpu.VMEM((2, rows // 4, width), F32),
            pltpu.VMEM((2, rows // 4, width), F32),
            pltpu.VMEM((8, chunk, side), BF),
            pltpu.VMEM((8, chunk, heads_width - side), BF),
            pltpu.VMEM((8, rows_w, width), BF),
            pltpu.VMEM(vectors.shape, F32),
            pltpu.VMEM((chunk, side), F32),
            pltpu.VMEM((chunk, heads_width - side), F32),
            pltpu.VMEM((4, rows_w, heads_width), BF),
            pltpu.VMEM((4, rows_w, heads_width), BF),
            pltpu.VMEM(vectors.shape[1:], F32),
            pltpu.VMEM(vectors.shape[1:], F32),
            dma((1,)),
            dma((2, 2)),
            dma((2, 2)),
            dma((2,)),
            dma((2,)),
            dma((4,)),
            dma((4,)),
            dma((4, 7)),
            dma((4, 7)),
            dma((6,)),
            dma((6,)),
        ],
        compiler_params=pltpu.CompilerParams(
            collective_id=2, has_side_effects=True, vmem_limit_bytes=48 << 20
        ),
        cost_estimate=pl.CostEstimate(flops=13 * 10**9, bytes_accessed=100 << 20, transcendentals=0),
        name="last_exchange",
    )(order, base, tokens_t, g_qkv, w_t, part_out, vectors)


CHUNK = 128
TILE = 256
LAG = 3


def tile(index, base=0):
    return pl.ds(pl.multiple_of(base + index * TILE, TILE), TILE)


def nt(a, b):
    return lax.dot_general(a, b, (((1,), (1,)), ((), ())), preferred_element_type=F32)


def middle_kernel(mixed_n, states, teacher, weight, mask, w_in, w_own, w_o, rates, scales,
                  w_ug_out, w_d_out, hidden_out, back_out, out_states, attn_unit, attn_inv, hidden_inv, sums, gd_all,
                  ht_all, act_all, ug_all, w_ug, w_d, hidden, back, mx, part, core, x_buf, tok, gd, act, act_t, ug, ht,
                  mx_send, mx_recv, mx_own, keep_sem, core_send, core_recv, x_send, x_recv, tok_send, tok_recv, gd_send, gd_recv, gd_own,
                  out_sem, ring_send, ring_recv, ug_s, ug_r, ug_sem):
    sibling, across, corner = group_peers()
    dp, place = lax.axis_index("dp"), ring_place()
    right, left = {"dp": ring_dp(place + 1)}, {"dp": ring_dp(place - 1)}
    piece = w_own.shape[0]
    count = x_buf.shape[0]
    width = hidden.shape[1]
    rate_attn, rate_mlp = rates[0:1], rates[1:2]

    def rows(i):
        return pl.ds(pl.multiple_of(i * CHUNK, CHUNK), CHUNK)

    def mx_copies(i):
        return [
            send(mixed_n.at[(r + 1) * count + i], mx.at[i, r + 1], mx_send.at[r, i], mx_recv.at[r, i], peer)
            for r, peer in enumerate((sibling, across, corner))
        ]

    def mx_local(i):
        return pltpu.make_async_copy(mixed_n.at[i], mx.at[i, 0], mx_own.at[i])

    def keep_rows(i):
        return [
            pltpu.make_async_copy(hidden.at[rows(i)], hidden_out.at[rows(i)], keep_sem.at[0, i]),
            pltpu.make_async_copy(back.at[rows(i)], back_out.at[rows(i)], keep_sem.at[1, i]),
        ]

    keep_w = [
        pltpu.make_async_copy(w_ug, w_ug_out, keep_sem.at[2, 0]),
        pltpu.make_async_copy(w_d, w_d_out, keep_sem.at[2, 1]),
    ]

    def core_a(stage, i):
        return send(part.at[i % 3, 3], core.at[0, i], core_send.at[stage, 0, i], core_recv.at[stage, 0, i], sibling)

    def core_b(stage, i):
        return send(part.at[i % 3, 1], core.at[1, i], core_send.at[stage, 1, i], core_recv.at[stage, 1, i], sibling)

    def chip(stage, i):
        return send(part.at[i % 3, 2], x_buf.at[i], x_send.at[stage, i], x_recv.at[stage, i], across)

    def spread(buf, own, sems, recvs, i):
        return [
            send(own, buf.at[i, 1], sems.at[0, i], recvs.at[0, i], sibling),
            send(own, buf.at[i, 2], sems.at[1, i], recvs.at[1, i], across),
            send(buf.at[i, 2], buf.at[i, 3], sems.at[2, i], recvs.at[2, i], sibling),
        ]

    def tok_copies(i):
        return spread(tok, tok.at[i, 0], tok_send, tok_recv, i)

    def gd_copies(i):
        return spread(gd_all, gd.at[i], gd_send, gd_recv, i)

    def gd_local(i):
        return pltpu.make_async_copy(gd.at[i], gd_all.at[i, 0], gd_own.at[i])

    def outs(i):
        slot = i % 2
        return [
            pltpu.make_async_copy(ht.at[slot], ht_all.at[i], out_sem.at[0, slot]),
            pltpu.make_async_copy(act_t.at[slot], act_all.at[i], out_sem.at[1, slot]),
            pltpu.make_async_copy(ug.at[slot], ug_all.at[i], out_sem.at[2, slot]),
        ]

    def hop(step):
        late = hidden_ring(w_d, ring_send, ring_recv, step + 1)
        for copy, later in zip(hidden_ring(w_d, ring_send, ring_recv, step), late):
            copy.wait()
            pl.when(step < 6)(later.start)

    def ug_hop(step):
        late = hidden_ring(w_ug, ug_s, ug_r, step + 1, EARLY_HOPS)
        for copy, later in zip(hidden_ring(w_ug, ug_s, ug_r, step, EARLY_HOPS), late):
            copy.wait()
            pl.when(step < 6)(later.start)

    def forward_far(stage, i):
        core_a(stage, i).wait_recv()
        part[i % 3, 2] = (part[i % 3, 2].astype(F32) + core[0, i].astype(F32)).astype(BF)
        chip(stage, i).start()

    def reduced(stage, i):
        core_b(stage, i).wait_recv()
        chip(stage, i).wait_recv()
        total = part[i % 3, 0].astype(F32) + core[1, i].astype(F32) + x_buf[i].astype(F32)
        core_a(stage, i).wait_send()
        core_b(stage, i).wait_send()
        chip(stage, i).wait_send()
        return total

    sums[...] = jnp.zeros_like(sums)
    w_d[rows_at(dp * piece, piece)] = w_own[...]
    chunk = w_ug.shape[0] // 8

    def load_w(i):
        cuts = rows_at(ring_dp(place - i) * chunk, chunk // 2), rows_at(
            ring_dp(place + i) * chunk + chunk // 2, chunk // 2
        )
        return [pltpu.make_async_copy(w_in.at[cut], w_ug.at[cut], ug_sem.at[d, i]) for d, cut in enumerate(cuts)]

    def start_w(i, carry):
        for copy in load_w(i):
            copy.start()
        return carry

    def wait_w(i, carry):
        for copy in load_w(i):
            copy.wait()
        return carry

    lax.fori_loop(0, EARLY_HOPS + 1, start_w, 0)
    greet([sibling, across, corner, right, left])
    for copy in hidden_ring(w_d, ring_send, ring_recv, 0):
        copy.start()

    def open_mixed(i, carry):
        mx_local(i).start()
        for copy in mx_copies(i):
            copy.start()
        return carry

    lax.fori_loop(0, count, open_mixed, 0)
    lax.fori_loop(0, EARLY_HOPS + 1, wait_w, 0)
    for copy in hidden_ring(w_ug, ug_s, ug_r, EARLY_HOPS, EARLY_HOPS):
        copy.start()

    def norm_hidden(i):
        mx_local(i).wait()
        for copy in mx_copies(i):
            copy.wait()
        attn = nn(mx[i, 0].T, w_o[0])
        for r in range(1, 4):
            attn = attn + nn(mx[i, r].T, w_o[r])
        unit, inverse = unit_rows(attn)
        own = states[rows(i)].astype(F32)
        value, value_inv = unit_rows(own + rate_attn * (unit - own))
        hidden[rows(i)] = value
        attn_unit[rows(i)] = unit.astype(BF)
        attn_inv[rows(i)] = inverse
        hidden_inv[rows(i)] = value_inv
        tok[i, 0] = value.astype(BF)
        copies = tok_copies(i)
        copies[0].start()
        copies[1].start()

    def pass_tokens(i):
        copies = tok_copies(i)
        copies[1].wait_recv()
        copies[2].start()

    def feed(i):
        copies = tok_copies(i)
        copies[0].wait()
        copies[1].wait_send()
        copies[2].wait()
        slot = i % 2

        @pl.when(i >= 2)
        def _():
            for copy in outs(i - 2):
                copy.wait()

        def up(n, carry):
            here = tok[i].reshape(4 * CHUNK, width)
            up_proj = nn(here, w_ug[:, tile(n)])
            gate_proj = nn(here, w_ug[:, tile(n, width)])
            gated = gate_proj * scales[1:2, tile(n)]
            value = up_proj * scales[0:1, tile(n)] * (gated * jax.nn.sigmoid(gated))
            act[:, tile(n)] = value.astype(BF)
            act_t[slot, tile(n)] = value.astype(BF).T
            ug[slot, :, tile(n)] = up_proj.astype(BF)
            ug[slot, :, tile(n, width)] = gate_proj.astype(BF)
            return carry

        lax.fori_loop(0, width // TILE, up, 0)

        def down(n, carry):
            value = nn(act[...], w_d[:, tile(n)])
            part[i % 3, :, :, tile(n)] = value.astype(BF).reshape(4, CHUNK, TILE)
            ht[slot, tile(n)] = tok[i, :, :, tile(n)].reshape(4 * CHUNK, TILE).T
            return carry

        lax.fori_loop(0, width // TILE, down, 0)
        core_a(0, i).start()
        core_b(0, i).start()
        for copy in outs(i):
            copy.start()
        forward_far(0, i)

    def finish(i):
        unit, inverse = unit_rows(reduced(0, i))
        own = hidden[rows(i)]
        result, result_inv = unit_rows(own + rate_mlp * (unit - own))
        out_states[rows(i)] = result.astype(BF)
        diff = result - teacher[rows(i)]
        sums[1:2] = sums[1:2] + jnp.sum(mask[rows(i)] * (diff * diff), axis=0, keepdims=True)
        g_last = unit_back(weight[rows(i)] * diff, result, result_inv)
        sums[0:1] = sums[0:1] + jnp.sum(g_last * (unit - own), axis=0, keepdims=True)
        back[rows(i)] = g_last * (1.0 - rate_mlp)
        gd[i] = unit_back(g_last * rate_mlp, unit, inverse).astype(BF)
        copies = gd_copies(i)
        copies[0].start()
        copies[1].start()
        gd_local(i).start()
        for copy in keep_rows(i):
            copy.start()

    def pass_grads(i):
        copies = gd_copies(i)
        copies[1].wait_recv()
        copies[2].start()

    stages = ((0, norm_hidden), (1, pass_tokens), (LAG, feed), (LAG + 1, finish), (LAG + 2, pass_grads))

    def step(t, carry):
        for lag, stage in stages:
            if lag == LAG:
                pl.when(t < 7 - EARLY_HOPS)(lambda: ug_hop(EARLY_HOPS + t))
                pl.when(t < 3)(lambda: hop(2 * t + 1))
                pl.when(t == 2)(lambda: hop(6))

                @pl.when(t == 2)
                def _():
                    for copy in keep_w:
                        copy.start()

            pl.when((t >= lag) & (t < lag + count))(functools.partial(stage, t - lag))
            if lag == 0:
                pl.when(t < 3)(lambda: hop(2 * t))
        return carry

    lax.fori_loop(0, count + LAG + 2, step, 0)

    def close(i, carry):
        copies = gd_copies(i)
        copies[0].wait()
        copies[1].wait_send()
        copies[2].wait()
        gd_local(i).wait()
        for copy in keep_rows(i):
            copy.wait()
        return carry

    lax.fori_loop(0, count, close, 0)
    for i in (count - 2, count - 1):
        for copy in outs(i):
            copy.wait()
    for copy in keep_w:
        copy.wait()


def middle(mixed_n, states, teacher, weight, mask, w_ug, w_own, w_o, rates, scales):
    rows, width = states.shape
    count = rows // CHUNK
    vmem, hbm = pl.BlockSpec(memory_space=pltpu.VMEM), pl.BlockSpec(memory_space=pl.ANY)
    dma = pltpu.SemaphoreType.DMA
    return pl.pallas_call(
        middle_kernel,
        in_specs=[hbm] + [vmem] * 4 + [hbm] + [vmem] * 4,
        out_specs=[hbm] * 4 + [vmem] * 5 + [hbm] * 4,
        out_shape=[
            jax.ShapeDtypeStruct(w_ug.shape, BF),
            jax.ShapeDtypeStruct((8 * w_own.shape[0], width), BF),
            jax.ShapeDtypeStruct((rows, width), F32),
            jax.ShapeDtypeStruct((rows, width), F32),
            jax.ShapeDtypeStruct((rows, width), BF),
            jax.ShapeDtypeStruct((rows, width), BF),
            jax.ShapeDtypeStruct((rows, 1), F32),
            jax.ShapeDtypeStruct((rows, 1), F32),
            jax.ShapeDtypeStruct((2, width), F32),
            jax.ShapeDtypeStruct((count, 4, CHUNK, width), BF),
            jax.ShapeDtypeStruct((count, width, 4 * CHUNK), BF),
            jax.ShapeDtypeStruct((count, width, 4 * CHUNK), BF),
            jax.ShapeDtypeStruct((count, 4 * CHUNK, 2 * width), BF),
        ],
        scratch_shapes=[
            pltpu.VMEM(w_ug.shape, BF),
            pltpu.VMEM((8 * w_own.shape[0], width), BF),
            pltpu.VMEM((rows, width), F32),
            pltpu.VMEM((rows, width), F32),
            pltpu.VMEM((count, 4) + mixed_n.shape[1:], BF),
            pltpu.VMEM((3, 4, CHUNK, width), BF),
            pltpu.VMEM((2, count, CHUNK, width), BF),
            pltpu.VMEM((count, CHUNK, width), BF),
            pltpu.VMEM((count, 4, CHUNK, width), BF),
            pltpu.VMEM((count, CHUNK, width), BF),
            pltpu.VMEM((4 * CHUNK, width), BF),
            pltpu.VMEM((2, width, 4 * CHUNK), BF),
            pltpu.VMEM((2, 4 * CHUNK, 2 * width), BF),
            pltpu.VMEM((2, width, 4 * CHUNK), BF),
            dma((3, count)),
            dma((3, count)),
            dma((count,)),
            dma((3, count)),
            dma((1, 2, count)),
            dma((1, 2, count)),
            dma((1, count)),
            dma((1, count)),
            dma((3, count)),
            dma((3, count)),
            dma((3, count)),
            dma((3, count)),
            dma((count,)),
            dma((3, 2)),
            dma((4, 7)),
            dma((4, 7)),
            dma((4, 7 - EARLY_HOPS)),
            dma((4, 7 - EARLY_HOPS)),
            dma((2, EARLY_HOPS + 1)),
        ],
        compiler_params=pltpu.CompilerParams(
            collective_id=3, has_side_effects=True, vmem_limit_bytes=62 << 20
        ),
        cost_estimate=pl.CostEstimate(flops=26 * 10**9, bytes_accessed=400 << 20, transcendentals=4 << 20),
        name="middle",
    )(mixed_n, states, teacher, weight, mask, w_ug, w_own, w_o, rates, scales)


def middle_back_kernel(gd_all, act_all, ug_all, hidden, attn_unit, states, back, attn_inv, hidden_inv, w_ug, w_d,
                       rates, scales, base, ga_all, gug_all, down_rows, sums, ff_sums,
                       w_ug_b, w_d_b, part, core, x_buf, ga, gd, act, ug, gug, own_f, own_b, base_buf, dwd, column, ring_buf,
                       gd_sem, act_sem, in_sem, own_sem, core_send, core_recv, x_send, x_recv, ga_send, ga_recv,
                       ga_own, base_sem, out_sem, w_sem, ring_send, ring_recv):
    sibling, across, _ = group_peers()
    dp, place = lax.axis_index("dp"), ring_place()
    right, left = {"dp": ring_dp(place + 1)}, {"dp": ring_dp(place - 1)}
    count = core.shape[1]
    width = w_d.shape[0]
    load_d = pltpu.make_async_copy(w_d, w_d_b, w_sem.at[0])
    load_u = pltpu.make_async_copy(w_ug, w_ug_b, w_sem.at[1])
    load_d.start()
    half = ring_buf.shape[2]
    rate_attn = rates[0:1]

    def rows(i):
        return pl.ds(pl.multiple_of(i * CHUNK, CHUNK), CHUNK)

    def load_gd(i):
        return pltpu.make_async_copy(gd_all.at[i], gd.at[i], gd_sem.at[i])

    def load_act(i):
        return pltpu.make_async_copy(act_all.at[i], act.at[i], act_sem.at[i])

    def load_ug(i):
        return pltpu.make_async_copy(ug_all.at[i], ug.at[i % 2], in_sem.at[i % 2])

    def store_gug(i):
        return pltpu.make_async_copy(gug.at[i % 2], gug_all.at[i], out_sem.at[i % 2])

    def own_rows(i):
        return [
            pltpu.make_async_copy(hidden.at[rows(i)], own_f.at[0], own_sem.at[0]),
            pltpu.make_async_copy(back.at[rows(i)], own_f.at[1], own_sem.at[1]),
            pltpu.make_async_copy(attn_unit.at[rows(i)], own_b.at[0], own_sem.at[2]),
            pltpu.make_async_copy(states.at[rows(i)], own_b.at[1], own_sem.at[3]),
        ]

    def core_a(i):
        return send(part.at[i % 3, 3], core.at[0, i], core_send.at[0, i], core_recv.at[0, i], sibling)

    def core_b(i):
        return send(part.at[i % 3, 1], core.at[1, i], core_send.at[1, i], core_recv.at[1, i], sibling)

    def chip(i):
        return send(part.at[i % 3, 2], x_buf.at[i], x_send.at[i], x_recv.at[i], across)

    def ga_copies(i):
        return [
            send(ga.at[i], ga_all.at[1, rows(i)], ga_send.at[0, i], ga_recv.at[0, i], sibling),
            send(ga.at[i], ga_all.at[2, rows(i)], ga_send.at[1, i], ga_recv.at[1, i], across),
            send(ga_all.at[2, rows(i)], ga_all.at[3, rows(i)], ga_send.at[2, i], ga_recv.at[2, i], sibling),
        ]

    def ga_local(i):
        return pltpu.make_async_copy(ga.at[i], ga_all.at[0, rows(i)], ga_own.at[i])

    def base_copy(i):
        return pltpu.make_async_copy(base_buf.at[i % 2], base.at[rows(i)], base_sem.at[i % 2])

    def right_half(step):
        return rows_at(ring_dp(place - 1 - step) * 2 * half, half)

    def left_half(step):
        return rows_at(ring_dp(place + 1 + step) * 2 * half + half, half)

    def ring(step):
        return [
            send(ring_buf.at[0, step], ring_buf.at[0, step + 1], ring_send.at[0, step], ring_recv.at[0, step], right),
            send(ring_buf.at[1, step], ring_buf.at[1, step + 1], ring_send.at[1, step], ring_recv.at[1, step], left),
        ]

    def hop(step, carry):
        for copy in ring(step):
            copy.wait()

        @pl.when(step < 6)
        def _():
            for side, cut in ((0, right_half(step + 1)), (1, left_half(step + 1))):
                ring_buf[side, step + 1] = (
                    ring_buf[side, step + 1].astype(F32) + dwd[cut].astype(F32)
                ).astype(BF)
            for copy in ring(step + 1):
                copy.start()

        return carry

    for copy in [load_ug(0)] + own_rows(0):
        copy.start()
    lax.fori_loop(0, count, lambda i, c: (load_gd(i).start(), c)[1], 0)
    load_u.start()
    lax.fori_loop(0, count, lambda i, c: (load_act(i).start(), c)[1], 0)
    sums[...] = jnp.zeros_like(sums)
    ff_sums[...] = jnp.zeros_like(ff_sums)
    greet([sibling, across, right, left])
    lax.fori_loop(0, count, lambda i, c: (load_gd(i).wait(), c)[1], 0)
    load_d.wait()

    def feed(i):
        slot = i % 2
        load_ug(i).wait()

        @pl.when(i + 1 < count)
        def _():
            load_ug(i + 1).start()

        @pl.when(i >= 2)
        def _():
            store_gug(i - 2).wait()

        def grads(n, carry):
            g_act = nt(gd[i].reshape(4 * CHUNK, width), w_d_b[tile(n)])
            up_proj = ug[slot, :, tile(n)].astype(F32)
            gate_proj = ug[slot, :, tile(n, width)].astype(F32)
            scale_up, scale_gate = scales[0:1, tile(n)], scales[1:2, tile(n)]
            gated = gate_proj * scale_gate
            sigmoid = jax.nn.sigmoid(gated)
            g_upscaled = g_act * (gated * sigmoid)
            g_gated = g_act * (up_proj * scale_up) * sigmoid * (1.0 + gated * (1.0 - sigmoid))
            ff_sums[0:1, tile(n)] = ff_sums[0:1, tile(n)] + jnp.sum(g_upscaled * up_proj, axis=0, keepdims=True)
            ff_sums[1:2, tile(n)] = ff_sums[1:2, tile(n)] + jnp.sum(g_gated * gate_proj, axis=0, keepdims=True)
            gug[slot, :, tile(n)] = (g_upscaled * scale_up).astype(BF)
            gug[slot, :, tile(n, width)] = (g_gated * scale_gate).astype(BF)
            return carry

        lax.fori_loop(0, width // TILE, grads, 0)
        store_gug(i).start()
        pl.when(i == 0)(load_u.wait)

        def through(n, carry):
            value = nt(gug[slot], w_ug_b[tile(n)])
            part[i % 3, :, :, tile(n)] = value.astype(BF).reshape(4, CHUNK, TILE)
            return carry

        lax.fori_loop(0, width // TILE, through, 0)
        core_a(i).start()
        core_b(i).start()
        core_a(i).wait_recv()
        part[i % 3, 2] = (part[i % 3, 2].astype(F32) + core[0, i].astype(F32)).astype(BF)
        chip(i).start()

    def down_grads():
        lax.fori_loop(0, count, lambda i, c: (load_act(i).wait(), c)[1], 0)

        def outer(n, carry):
            column[...] = jnp.zeros_like(column)

            def add(k, carry):
                column[...] = column[...] + nn(act[k], gd[k, :, :, tile(n)].reshape(4 * CHUNK, TILE))
                return carry

            lax.fori_loop(0, count, add, 0)
            dwd[:, tile(n)] = column[...].astype(BF)
            return carry

        lax.fori_loop(0, width // TILE, outer, 0)
        ring_buf[0, 0] = dwd[right_half(0)]
        ring_buf[1, 0] = dwd[left_half(0)]
        for copy in ring(0):
            copy.start()

    def finish(i):
        core_b(i).wait_recv()
        chip(i).wait_recv()
        through = part[i % 3, 0].astype(F32) + core[1, i].astype(F32) + x_buf[i].astype(F32)
        core_a(i).wait_send()
        core_b(i).wait_send()
        chip(i).wait_send()
        for copy in own_rows(i):
            copy.wait()
        value, unit, own = own_f[0], own_b[0].astype(F32), own_b[1].astype(F32)
        g_pre = unit_back(own_f[1] + through, value, hidden_inv[rows(i)])

        @pl.when(i + 1 < count)
        def _():
            for copy in own_rows(i + 1):
                copy.start()

        @pl.when(i >= 2)
        def _():
            base_copy(i - 2).wait()

        base_buf[i % 2] = g_pre * (1.0 - rate_attn)
        base_copy(i).start()
        sums[0:1] = sums[0:1] + jnp.sum(g_pre * (unit - own), axis=0, keepdims=True)
        ga[i] = unit_back(g_pre * rate_attn, unit, attn_inv[rows(i)]).astype(BF)
        copies = ga_copies(i)
        copies[0].start()
        copies[1].start()
        ga_local(i).start()

    def pass_grads(i):
        copies = ga_copies(i)
        copies[1].wait_recv()
        copies[2].start()

    stages = (feed, finish, pass_grads)

    def step(t, carry):
        for lag, stage in enumerate(stages):
            pl.when((t >= lag) & (t < lag + count))(functools.partial(stage, t - lag))
        pl.when(t == 0)(down_grads)

        @pl.when((t >= 1) & (t < 4))
        def _():
            lax.fori_loop(2 * t - 2, 2 * t, hop, 0)

        return carry

    lax.fori_loop(0, count + len(stages) - 1, step, 0)
    hop(6, 0)
    own = dp * 2 * half
    down_rows[pl.ds(0, half)] = ring_buf[0, 7].astype(F32) + dwd[rows_at(own, half)].astype(F32)
    down_rows[pl.ds(half, half)] = ring_buf[1, 7].astype(F32) + dwd[rows_at(own + half, half)].astype(F32)

    def close(i, carry):
        copies = ga_copies(i)
        copies[0].wait()
        copies[1].wait_send()
        copies[2].wait()
        ga_local(i).wait()
        return carry

    lax.fori_loop(0, count, close, 0)
    for i in (count - 2, count - 1):
        base_copy(i).wait()
        store_gug(i).wait()


def middle_back(gd_all, act_all, ug_all, hidden, attn_unit, states, back, attn_inv, hidden_inv, w_ug, w_d, rates,
                scales):
    rows, width = states.shape
    count = rows // CHUNK
    piece = width // 8
    vmem, hbm = pl.BlockSpec(memory_space=pltpu.VMEM), pl.BlockSpec(memory_space=pl.ANY)
    dma = pltpu.SemaphoreType.DMA
    return pl.pallas_call(
        middle_back_kernel,
        in_specs=[hbm] * 7 + [vmem] * 2 + [hbm] * 2 + [vmem] * 2,
        out_specs=[hbm, hbm, hbm, vmem, vmem, vmem],
        out_shape=[
            jax.ShapeDtypeStruct((rows, width), F32),
            jax.ShapeDtypeStruct((4, rows, width), BF),
            jax.ShapeDtypeStruct((count, 4 * CHUNK, 2 * width), BF),
            jax.ShapeDtypeStruct((piece, width), F32),
            jax.ShapeDtypeStruct((1, width), F32),
            jax.ShapeDtypeStruct((2, width), F32),
        ],
        scratch_shapes=[
            pltpu.VMEM(w_ug.shape, BF),
            pltpu.VMEM(w_d.shape, BF),
            pltpu.VMEM((3, 4, CHUNK, width), BF),
            pltpu.VMEM((2, count, CHUNK, width), BF),
            pltpu.VMEM((count, CHUNK, width), BF),
            pltpu.VMEM((count, CHUNK, width), BF),
            pltpu.VMEM((count, 4, CHUNK, width), BF),
            pltpu.VMEM((count, width, 4 * CHUNK), BF),
            pltpu.VMEM((2, 4 * CHUNK, 2 * width), BF),
            pltpu.VMEM((2, 4 * CHUNK, 2 * width), BF),
            pltpu.VMEM((2, CHUNK, width), F32),
            pltpu.VMEM((2, CHUNK, width), BF),
            pltpu.VMEM((2, CHUNK, width), F32),
            pltpu.VMEM((width, width), BF),
            pltpu.VMEM((width, TILE), F32),
            pltpu.VMEM((2, 8, piece // 2, width), BF),
            dma((count,)),
            dma((count,)),
            dma((2,)),
            dma((4,)),
            dma((2, count)),
            dma((2, count)),
            dma((count,)),
            dma((count,)),
            dma((3, count)),
            dma((3, count)),
            dma((count,)),
            dma((2,)),
            dma((2,)),
            dma((2,)),
            dma((2, 7)),
            dma((2, 7)),
        ],
        compiler_params=pltpu.CompilerParams(
            collective_id=4, has_side_effects=True, vmem_limit_bytes=60 << 20
        ),
        cost_estimate=pl.CostEstimate(flops=34 * 10**9, bytes_accessed=200 << 20, transcendentals=4 << 20),
        name="middle_back",
    )(gd_all, act_all, ug_all, hidden, attn_unit, states, back, attn_inv, hidden_inv, w_ug, w_d, rates, scales)


def order_kernel(where_ref, parent_ref, out_ref):
    base, me = where_ref[0], where_ref[1]
    shape = (128, 128)
    row = lax.broadcasted_iota(jnp.int32, shape, 0)
    block = lax.broadcasted_iota(jnp.int32, (8, 128), 1)
    real = block < NB
    parent = jnp.where(real & (parent_ref[...] >= 0), parent_ref[...] - base, -1)
    up = (row == parent[0:1]).astype(F32)
    up2 = nn(up, up)
    near = up + up2
    up4 = nn(up2, up2)
    near = near + nn(near, up2)
    near = near + nn(near, up4)
    above = near + nn(nn(up4, up4), up)
    depth = jnp.broadcast_to(jnp.sum(above, axis=0, keepdims=True), (8, 128)).astype(jnp.int32)
    before = (row < lax.broadcasted_iota(jnp.int32, shape, 1)).astype(F32)
    rank = nn(((depth == TRUNK) & real).astype(F32), before)
    parent_rank = nn(rank, up).astype(jnp.int32)
    sibling = jnp.sum(nn(up.T, up) * before, axis=0, keepdims=True).astype(jnp.int32)
    leaf = TRUNK + 4 + 2 * parent_rank + sibling
    slot = jnp.where(depth < TRUNK, depth, jnp.where(depth == TRUNK, TRUNK + rank.astype(jnp.int32), leaf))
    slot = jnp.where(real, slot, 127)
    mine = jnp.where(real, jnp.bitwise_xor(block // 5, me) * 5 + block % 5, 127)
    order = nt(mine.astype(F32), (row == slot[0:1]).astype(F32))
    back = nt(slot.astype(F32), (row == mine[0:1]).astype(F32))
    which = lax.broadcasted_iota(jnp.int32, (8, 128), 0)
    out_ref[...] = jnp.where(which == 0, order, back).astype(jnp.int32)


def tree_order(where, parents):
    return pl.pallas_call(
        order_kernel,
        in_specs=[pl.BlockSpec(memory_space=pltpu.SMEM), pl.BlockSpec(memory_space=pltpu.VMEM)],
        out_specs=pl.BlockSpec(memory_space=pltpu.VMEM),
        out_shape=jax.ShapeDtypeStruct((8, 128), jnp.int32),
        name="tree_order",
    )(where, jnp.broadcast_to(jnp.pad(parents, (0, 128 - NB), constant_values=-1), (8, 128)))


def local(
    states,
    teacher,
    parent_ids,
    valid_mask,
    w_query,
    w_key,
    w_value,
    w_out,
    w_up,
    w_gate,
    w_down,
    qk_scale,
    attn_rate,
    mlp_rate,
    up_scale,
    gate_scale,
):
    both = ("dp", "fsdp")
    dps, tps = 8, 4
    rows_w = w_query.shape[0]
    cols = D // tps
    hid = FF // tps
    ff_rows = FF // (dps * tps)
    me = lax.axis_index("fsdp")
    root_width = math.sqrt(D)
    mask_f = valid_mask.astype(F32)
    group_base = lax.axis_index("dp") * NB
    order = tree_order(jnp.stack((group_base, me)).astype(jnp.int32), parent_ids)

    count = jnp.sum(valid_mask)
    first_row = jnp.arange(rows_w, dtype=jnp.int32) == 0
    small = jnp.stack(
        (
            qk_scale,
            attn_rate,
            mlp_rate,
            jnp.where(first_row, count // 128, 0).astype(BF),
            jnp.where(first_row, count % 128, 0).astype(BF),
        ),
        axis=1,
    )
    small = jnp.pad(small, ((0, 0), (0, 59)))
    extra = jnp.pad(jnp.stack((up_scale, gate_scale), axis=1), ((0, 0), (69, 57)))
    spread = [(j, tps * (j % dps) + j // dps) for j in range(dps * tps)]
    tokens_t, w_t, w_o, w_ug, qkv, mixed, sums, mixed_n = forward(
        order, states, w_query, w_key, w_value, small, extra, lax.ppermute(w_out, both, spread), w_up, w_gate
    )
    small_all = w_t[3 * cols : 3 * cols + 8].astype(F32)
    rates = small_all[1:3]
    valid_count = 128.0 * jnp.sum(small_all[3]) + jnp.sum(small_all[4])
    scales = small_all[5:7] * jnp.array([[1.0], [root_width]], F32)
    scale_qk = lax.dynamic_slice_in_dim(small_all[0], me * cols, cols).reshape(cols // HEAD_DIM, HEAD_DIM, 1)

    mask_col = mask_f[:, None]
    w_ug, w_d, hidden, back, out_states, attn_unit, attn_inv, hidden_inv, sums_mid, gd_all, ht_all, act_all, ug_all = middle(
        mixed_n, states, teacher, mask_col * (2.0 / valid_count), mask_col, w_ug, w_down, w_o, rates, scales
    )
    base, ga_all, gug_all, grad_down, sums_back, ff_sums = middle_back(
        gd_all, act_all, ug_all, hidden, attn_unit, states, back, attn_inv, hidden_inv, w_ug, w_d, rates, scales
    )
    loss_local = jnp.sum(sums_mid[1])
    g_rate_mlp, g_rate_attn = sums_mid[0], sums_back[0]
    grad_up_scale, grad_gate_scale = ff_sums[0], ff_sums[1] * root_width
    g_qkv, g_scale, part_out, grad_up, grad_gate = attention_back(
        order, qkv, scale_qk, sums, mixed, ga_all.reshape(NB, BLOCK, D), w_o, ht_all, gug_all
    )
    g_qkv = g_qkv.reshape(3 * cols, TOK)
    slot = jnp.arange(tps, dtype=jnp.int32) == me
    qk_rows = jnp.where(slot[:, None], g_scale.reshape(1, cols), 0.0).reshape(dps * tps, rows_w)
    ff_terms = [
        jnp.where(slot[None, :, None], term.reshape(dps, 1, ff_rows), 0.0).reshape(dps * tps, ff_rows)
        for term in (grad_up_scale, grad_gate_scale)
    ]
    vectors = jnp.concatenate(
        [g_rate_attn.reshape(dps * tps, rows_w), g_rate_mlp.reshape(dps * tps, rows_w), qk_rows]
        + ff_terms
        + [jnp.broadcast_to(loss_local, (dps * tps, 512 - 3 * rows_w - 2 * ff_rows))],
        axis=1,
    ).reshape(dps, tps, 4, 128)
    part_out = part_out.reshape(dps, rows_w, D)
    grad_states, g_query, g_key, g_value, out_back, vector_share = last_exchange(
        order, base, tokens_t, g_qkv, w_t, part_out, vectors
    )
    vector_share = vector_share.reshape(512)
    grad_out = lax.ppermute(out_back, both, [(b, a) for a, b in spread])
    cuts = (0, rows_w, 2 * rows_w, 3 * rows_w, 3 * rows_w + ff_rows, 3 * rows_w + 2 * ff_rows)
    v = [vector_share[a:b] for a, b in zip(cuts, cuts[1:])]
    return (
        out_states,
        vector_share[-1] / valid_count,
        grad_states,
        g_query,
        g_key,
        g_value,
        grad_out,
        grad_up,
        grad_gate,
        grad_down,
        v[2],
        v[0],
        v[1],
        v[3],
        v[4],
    )


def solution(mesh):
    placed = (
        P(("dp", "fsdp"), None),
        P(("dp", "fsdp"), None),
        P("dp"),
        P(("dp", "fsdp")),
        P(("dp", "fsdp"), None),
        P(("dp", "fsdp"), None),
        P(("dp", "fsdp"), None),
        P(("dp", "fsdp"), None),
        P(("dp", "fsdp"), None),
        P(("dp", "fsdp"), None),
        P(("dp", "fsdp"), None),
        P(("dp", "fsdp")),
        P(("dp", "fsdp")),
        P(("dp", "fsdp")),
        P(("dp", "fsdp")),
        P(("dp", "fsdp")),
    )
    quick = mesh.shape["fsdp"] == 4 and mesh.shape["dp"] == 8
    return jax.shard_map(
        local if quick else general,
        mesh=mesh,
        in_specs=placed,
        out_specs=(
            P(("dp", "fsdp"), None),
            P(),
            P(("dp", "fsdp"), None),
            P(("dp", "fsdp"), None),
            P(("dp", "fsdp"), None),
            P(("dp", "fsdp"), None),
            P(("dp", "fsdp"), None),
            P(("dp", "fsdp"), None),
            P(("dp", "fsdp"), None),
            P(("dp", "fsdp"), None),
            P(("dp", "fsdp")),
            P(("dp", "fsdp")),
            P(("dp", "fsdp")),
            P(("dp", "fsdp")),
            P(("dp", "fsdp")),
        ),
        check_vma=False,
    )
```

```python
import functools
import math

import jax
import jax.numpy as jnp
from jax import lax
from jax.experimental import pallas as pl
from jax.experimental.pallas import tpu as pltpu
from jax.sharding import PartitionSpec as P


D = 1280
HEADS = 20
HEAD_DIM = 64
FF = 5120
BLOCK = 128
DEPTH = 10


EPS = 1e-06


def unit_rows(vector):
    inverse = lax.rsqrt(jnp.sum(vector * vector, axis=-1, keepdims=True) + EPS)
    return (vector * inverse, inverse)


def unit_back(grad, unit, inverse):
    return (grad - unit * jnp.sum(grad * unit, axis=-1, keepdims=True)) * inverse


def project(left, right):
    return jnp.dot(left, right, preferred_element_type=jnp.float32)


def project_back(grad, weight):
    return jnp.einsum("te,de->td", grad, weight, preferred_element_type=jnp.float32)


def ancestors(local_parent):
    column = jnp.arange(local_parent.shape[0], dtype=jnp.int32)
    columns = [column]
    for depth_step in range(DEPTH - 1):
        column = jnp.where(column >= 0, local_parent[jnp.maximum(column, 0)], -1)
        columns.append(column)
    return jnp.stack(columns, axis=1)


def head_back(grad_flat, unit, inverse, scale):
    scaled = (grad_flat * scale).reshape(unit.shape)
    raw = unit_back(scaled, unit, inverse).reshape(grad_flat.shape)
    scale_grad = jnp.sum(grad_flat * unit.reshape(grad_flat.shape), axis=0)
    return (raw, scale_grad)


def general(
    states,
    teacher,
    parent_ids,
    valid_mask,
    w_query,
    w_key,
    w_value,
    w_out,
    w_up,
    w_gate,
    w_down,
    qk_scale,
    attn_rate,
    mlp_rate,
    up_scale,
    gate_scale,
):
    rows_dev = states.shape[0]
    blocks_dev = rows_dev // BLOCK
    width_rows = w_query.shape[0]
    span = DEPTH * BLOCK
    factor = math.sqrt(HEAD_DIM)
    root_width = math.sqrt(D)
    mask_f = valid_mask.astype(jnp.float32)
    qkv_local = jnp.concatenate((w_query, w_key, w_value), axis=1)
    scal_width_local = jnp.stack((qk_scale, attn_rate, mlp_rate), axis=1)
    piece_qkv = lax.all_gather(qkv_local, ("dp", "fsdp"), axis=0, tiled=True)
    piece_out = lax.all_gather(w_out, ("dp", "fsdp"), axis=0, tiled=True)
    piece_scal = lax.all_gather(scal_width_local, ("dp", "fsdp"), axis=0, tiled=True)
    lefts = states
    total = jnp.dot(lefts, piece_qkv, preferred_element_type=jnp.float32)
    scal_whole = piece_scal
    qkv_raw = total
    scal_width = scal_whole
    scale_qk = scal_width[:, 0].astype(jnp.float32)
    rate_attn = scal_width[:, 1].astype(jnp.float32)
    rate_mlp = scal_width[:, 2].astype(jnp.float32)
    query_raw = qkv_raw[:, :D]
    key_raw = qkv_raw[:, D : 2 * D]
    values = qkv_raw[:, 2 * D :].astype(jnp.bfloat16)
    query_unit, query_inv = unit_rows(query_raw.reshape(rows_dev, HEADS, HEAD_DIM))
    key_unit, key_inv = unit_rows(key_raw.reshape(rows_dev, HEADS, HEAD_DIM))
    query_n = (query_unit.reshape(rows_dev, D) * scale_qk).astype(jnp.bfloat16)
    key_n = (key_unit.reshape(rows_dev, D) * scale_qk).astype(jnp.bfloat16)
    key_group, value_group = (
        lax.all_gather(key_n, "fsdp", axis=0, tiled=True),
        lax.all_gather(values, "fsdp", axis=0, tiled=True),
    )
    group_blocks = parent_ids.shape[0]
    group_base = lax.axis_index("dp") * group_blocks
    local_parent = jnp.where(parent_ids >= 0, parent_ids - group_base, -1)
    paths_all = ancestors(local_parent)
    own_first = lax.axis_index("fsdp") * blocks_dev
    paths = lax.dynamic_slice_in_dim(paths_all, own_first, blocks_dev, 0)
    safe_paths = jnp.maximum(paths, 0)
    key_rows = key_group.reshape(group_blocks, BLOCK, D)[safe_paths].reshape(
        blocks_dev, span, HEADS, HEAD_DIM
    )
    value_rows = value_group.reshape(group_blocks, BLOCK, D)[safe_paths].reshape(
        blocks_dev, span, HEADS, HEAD_DIM
    )
    slot_of = jnp.arange(span, dtype=jnp.int32) // BLOCK
    offset = jnp.arange(span, dtype=jnp.int32) % BLOCK
    row_pos = jnp.arange(BLOCK, dtype=jnp.int32)
    causal = offset[None, :] <= row_pos[:, None]
    is_live = jnp.take(paths, slot_of, axis=1) >= 0
    allowed = jnp.where(slot_of[None, None, :] == 0, causal[None], is_live[:, None, :])[:, None]
    query_heads = query_n.reshape(blocks_dev, BLOCK, HEADS, HEAD_DIM)
    scores = factor * jnp.einsum(
        "bqhd,bkhd->bhqk", query_heads, key_rows, preferred_element_type=jnp.float32
    )
    scores = jnp.where(allowed, scores, jnp.float32(-1e30))
    row_max = jnp.max(scores, axis=-1, keepdims=True)
    powers = jnp.exp(scores - row_max)
    row_sum = jnp.sum(powers, axis=-1, keepdims=True)
    probs_b = (powers / row_sum).astype(jnp.bfloat16)
    log_total = row_max + jnp.log(row_sum)
    mixed = jnp.einsum("bhqk,bkhd->bqhd", probs_b, value_rows, preferred_element_type=jnp.float32)
    mixed = mixed.reshape(rows_dev, D).astype(jnp.bfloat16)
    inputs = states.astype(jnp.float32)
    attn = project(mixed, piece_out)
    attn_unit, attn_inv = unit_rows(attn)
    hidden, hidden_inv = unit_rows(inputs + rate_attn * (attn_unit - inputs))
    hidden_b = hidden.astype(jnp.bfloat16)
    ffn_local = jnp.concatenate((w_up, w_gate), axis=1)
    scal_hidden_local = jnp.concatenate(
        (up_scale.reshape(width_rows, 4), gate_scale.reshape(width_rows, 4)), axis=1
    )
    piece_ffn = lax.all_gather(ffn_local, ("dp", "fsdp"), axis=0, tiled=True)
    piece_scal = lax.all_gather(scal_hidden_local, ("dp", "fsdp"), axis=0, tiled=True)
    lefts = hidden_b
    total = jnp.dot(lefts, piece_ffn, preferred_element_type=jnp.float32)
    scal_whole = piece_scal
    scale_up = scal_whole[:, :4].reshape(FF).astype(jnp.float32)
    scale_gate = scal_whole[:, 4:].reshape(FF).astype(jnp.float32)
    up_proj = total[:, :FF]
    gate_proj = total[:, FF:]
    upscaled = up_proj * scale_up
    gated = gate_proj * scale_gate * root_width
    sigmoid_gate = jax.nn.sigmoid(gated)
    act = (upscaled * (gated * sigmoid_gate)).astype(jnp.bfloat16)
    lefts = act
    down = jnp.dot(
        lefts,
        lax.all_gather(w_down, ("dp", "fsdp"), axis=0, tiled=True),
        preferred_element_type=jnp.float32,
    )
    down_unit, down_inv = unit_rows(down)
    result, result_inv = unit_rows(hidden + rate_mlp * (down_unit - hidden))
    loss_local = jnp.sum(mask_f[:, None] * (result - teacher) ** 2)
    valid_count, loss_sum = lax.psum((jnp.sum(mask_f), loss_local), ("dp", "fsdp"))
    loss = loss_sum / valid_count
    g_result = 2.0 * mask_f[:, None] * (result - teacher) / valid_count
    g_last = unit_back(g_result, result, result_inv)
    g_hidden = g_last * (1.0 - rate_mlp)
    g_rate_mlp = jnp.sum(g_last * (down_unit - hidden), axis=0)
    g_down = unit_back(g_last * rate_mlp, down_unit, down_inv).astype(jnp.bfloat16)
    g_act = jnp.einsum(
        "te,fe->tf",
        g_down,
        lax.all_gather(w_down, ("dp", "fsdp"), axis=0, tiled=True),
        preferred_element_type=jnp.float32,
    )
    g_upscaled = g_act * (gated * sigmoid_gate)
    g_gated = g_act * upscaled * sigmoid_gate * (1.0 + gated * (1.0 - sigmoid_gate))
    grad_up_scale = jnp.sum(g_upscaled * up_proj, axis=0)
    grad_gate_scale = jnp.sum(g_gated * gate_proj * root_width, axis=0)
    g_up = (g_upscaled * scale_up).astype(jnp.bfloat16)
    g_gate = (g_gated * scale_gate * root_width).astype(jnp.bfloat16)
    g_both = jnp.concatenate((g_up, g_gate), axis=1)
    g_hidden = g_hidden + jnp.einsum(
        "tc,dc->td",
        g_both,
        lax.all_gather(ffn_local, ("dp", "fsdp"), axis=0, tiled=True),
        preferred_element_type=jnp.float32,
    )
    scal_terms = jnp.concatenate(
        (grad_up_scale.reshape(D, 4), grad_gate_scale.reshape(D, 4)), axis=1
    )
    lefts = hidden_b
    main = jnp.einsum("td,tc->dc", lefts, g_both, preferred_element_type=jnp.float32)
    ffn_share = lax.psum_scatter(
        jnp.concatenate((main, scal_terms), axis=1), ("dp", "fsdp"), scatter_dimension=0, tiled=True
    )
    lefts = act
    grad_down = lax.psum_scatter(
        jnp.einsum("tf,te->fe", lefts, g_down, preferred_element_type=jnp.float32),
        ("dp", "fsdp"),
        scatter_dimension=0,
        tiled=True,
    )
    g_pre = unit_back(g_hidden, hidden, hidden_inv)
    g_states = g_pre * (1.0 - rate_attn)
    g_rate_attn = jnp.sum(g_pre * (attn_unit - inputs), axis=0)
    g_attn = unit_back(g_pre * rate_attn, attn_unit, attn_inv).astype(jnp.bfloat16)
    g_mixed = project_back(g_attn, piece_out).astype(jnp.bfloat16)
    scores = factor * jnp.einsum(
        "bqhd,bkhd->bhqk", query_heads, key_rows, preferred_element_type=jnp.float32
    )
    probs = jnp.where(allowed, jnp.exp(scores - log_total), jnp.float32(0.0))
    probs_again = probs.astype(jnp.bfloat16)
    g_heads = g_mixed.reshape(blocks_dev, BLOCK, HEADS, HEAD_DIM)
    g_probs = jnp.einsum("bqhd,bkhd->bhqk", g_heads, value_rows, preferred_element_type=jnp.float32)
    delta = jnp.sum(probs * g_probs, axis=-1, keepdims=True)
    g_scores = (probs * (g_probs - delta)).astype(jnp.bfloat16)
    g_query_n = factor * jnp.einsum(
        "bhqk,bkhd->bqhd", g_scores, key_rows, preferred_element_type=jnp.float32
    )
    g_key_rows = factor * jnp.einsum(
        "bhqk,bqhd->bkhd", g_scores, query_heads, preferred_element_type=jnp.float32
    )
    g_value_rows = jnp.einsum(
        "bhqk,bqhd->bkhd", probs_again, g_heads, preferred_element_type=jnp.float32
    )
    flat_paths = safe_paths.reshape(blocks_dev * DEPTH)
    g_key_group = (
        jnp.zeros((group_blocks, BLOCK, D), jnp.float32)
        .at[flat_paths]
        .add(g_key_rows.reshape(blocks_dev * DEPTH, BLOCK, D))
    )
    g_value_group = (
        jnp.zeros((group_blocks, BLOCK, D), jnp.float32)
        .at[flat_paths]
        .add(g_value_rows.reshape(blocks_dev * DEPTH, BLOCK, D))
    )
    g_key_n, g_values = (
        lax.psum_scatter(
            g_key_group.reshape(group_blocks * BLOCK, D).astype(jnp.bfloat16),
            "fsdp",
            scatter_dimension=0,
            tiled=True,
        ).astype(jnp.float32),
        lax.psum_scatter(
            g_value_group.reshape(group_blocks * BLOCK, D).astype(jnp.bfloat16),
            "fsdp",
            scatter_dimension=0,
            tiled=True,
        ).astype(jnp.float32),
    )
    g_query_raw, scale_from_query = head_back(
        g_query_n.reshape(rows_dev, D), query_unit, query_inv, scale_qk
    )
    g_key_raw, scale_from_key = head_back(g_key_n, key_unit, key_inv, scale_qk)
    grad_qk_scale = scale_from_query + scale_from_key
    g_qkv = jnp.concatenate(
        (
            g_query_raw.astype(jnp.bfloat16),
            g_key_raw.astype(jnp.bfloat16),
            g_values.astype(jnp.bfloat16),
        ),
        axis=1,
    )
    g_states = g_states + jnp.einsum(
        "tc,dc->td",
        g_qkv,
        lax.all_gather(qkv_local, ("dp", "fsdp"), axis=0, tiled=True),
        preferred_element_type=jnp.float32,
    )
    vector_terms = jnp.stack((grad_qk_scale, g_rate_attn, g_rate_mlp), axis=1)
    lefts = states
    main = jnp.einsum("td,tc->dc", lefts, g_qkv, preferred_element_type=jnp.float32)
    outer = jnp.einsum("td,tc->dc", mixed, g_attn, preferred_element_type=jnp.float32)
    attn_share = lax.psum_scatter(
        jnp.concatenate((main, outer, vector_terms), axis=1),
        ("dp", "fsdp"),
        scatter_dimension=0,
        tiled=True,
    )
    return (
        result.astype(jnp.bfloat16),
        loss,
        g_states,
        attn_share[:, :D],
        attn_share[:, D : 2 * D],
        attn_share[:, 2 * D : 3 * D],
        attn_share[:, 3 * D : 4 * D],
        ffn_share[:, :FF],
        ffn_share[:, FF : 2 * FF],
        grad_down,
        attn_share[:, 4 * D],
        attn_share[:, 4 * D + 1],
        attn_share[:, 4 * D + 2],
        ffn_share[:, 2 * FF : 2 * FF + 4].reshape(-1),
        ffn_share[:, 2 * FF + 4 : 2 * FF + 8].reshape(-1),
    )

TRUNK = 8
NB = 20
TOK = NB * BLOCK
F32 = jnp.float32
BF = jnp.bfloat16


def head_norm(raw):
    inv = lax.rsqrt(jnp.sum(raw * raw, axis=0, keepdims=True) + EPS)
    return raw * inv, inv


def lanes_at(start, size):
    return pl.ds(pl.multiple_of(start, 128), size)


def rows_at(start, size):
    return pl.ds(pl.multiple_of(start, 16), size)


def early_chunks(visit):
    for j in range(TRUNK // 2):
        parts = [(0, 256 * j, "all")] if j else []
        visit(256 * j, parts + [(256 * j, 256, "causal")])
    trunk = TRUNK * BLOCK
    for start in (trunk, trunk + 256):
        visit(start, [(0, trunk, "all"), (start, 256, "pair")])


def late_chunks(visit):
    trunk = TRUNK * BLOCK
    for j in range(4):
        start = trunk + 4 * BLOCK + 256 * j
        visit(start, [(0, trunk, "all"), (trunk + BLOCK * j, BLOCK, "all"), (start, 256, "pair")])


def masked(kind, value):
    if kind == "all":
        return value
    key = lax.broadcasted_iota(jnp.int32, (256, 256), 0)
    query = lax.broadcasted_iota(jnp.int32, (256, 256), 1)
    keep = key <= query
    if kind == "pair":
        keep = keep & ((key < 128) == (query < 128))
    return jnp.where(keep, value, jnp.zeros_like(value))


def nn(a, b):
    return lax.dot_general(a, b, (((1,), (0,)), ((), ())), preferred_element_type=F32)


def nt(a, b):
    return lax.dot_general(a, b, (((1,), (1,)), ((), ())), preferred_element_type=F32)


def attention_back_kernel(order, qkv, scales, sums, mixed, ga_all, w_o, ht_all, gug_all,
                          g_qkv, g_scale, part_out, g_up, g_gate,
                          w_b, ga_b, ga, gm, raw, out_b, qT, q, k, kT, v, gT, g, dq, dk, dv, delta, inv,
                          gug_b, ht_r, ht_l, ring, own, hid_buf, hid_in,
                          ga_sem, gug_sem, row_sem, raw_sem, out_sem, ring_send, ring_recv, a2a_send, a2a_recv):
    me = lax.axis_index("fsdp")
    place = ring_place()
    peers = group_peers()
    right, left = {"dp": ring_dp(place + 1)}, {"dp": ring_dp(place - 1)}
    count, chunk, side = gug_b.shape[0], ring.shape[3], ring.shape[4]
    heads = g_scale.shape[0]
    rows_w = hid_buf.shape[1]

    def slices(step):
        slot = step % 2
        cut_r = rows_at(ring_dp(place - 1 - step) * chunk, chunk)
        cut_l = rows_at(ring_dp(place + 1 + step) * chunk, chunk)
        return [
            pltpu.make_async_copy(ht_all.at[:, cut_r], ht_r.at[slot], row_sem.at[0, slot]),
            pltpu.make_async_copy(ht_all.at[:, cut_l], ht_l.at[slot], row_sem.at[1, slot]),
        ]

    def raw_copy(head):
        slot = head % 2
        return pltpu.make_async_copy(
            qkv.at[:, rows_at(head * HEAD_DIM, HEAD_DIM)], raw.at[slot], raw_sem.at[slot]
        )

    def out_copy(head):
        slot = head % 2
        return pltpu.make_async_copy(
            out_b.at[slot], g_qkv.at[:, rows_at(head * HEAD_DIM, HEAD_DIM)], out_sem.at[slot]
        )

    load_ga = pltpu.make_async_copy(ga_all, ga_b, ga_sem.at[0])
    load_ga.start()
    load_w = pltpu.make_async_copy(w_o.at[0], w_b, ga_sem.at[1])
    load_w.start()
    raw_copy(0).start()
    for copy in slices(0):
        copy.start()
    loads = [pltpu.make_async_copy(gug_all.at[i], gug_b.at[i], gug_sem.at[i]) for i in range(count)]
    for copy in loads:
        copy.start()
    for copy in slices(1):
        copy.start()
    greet([*peers, right, left])
    load_ga.wait()
    load_w.wait()

    def pick(i, carry):
        ga[lanes_at(i * BLOCK, BLOCK)] = ga_b[order[0, i]]
        return carry

    lax.fori_loop(0, NB, pick, 0)

    def back(n, carry):
        gm[:, tile(n)] = nt(w_b[...], ga[tile(n)]).astype(BF)
        return carry

    lax.fori_loop(0, TOK // TILE, back, 0)

    def outer(n, carry):
        part_out[:, tile(n)] = nn(mixed[...], ga[:, tile(n)]).astype(BF)
        return carry

    lax.fori_loop(0, D // TILE, outer, 0)

    def parts(step, which):
        slot = step % 2

        @pl.when(which == 0)
        def _():
            for copy in slices(step):
                copy.wait()

        own[...] = jnp.zeros_like(own)

        def add(i, carry):
            for d, rows in enumerate((ht_r, ht_l)):
                cut = lanes_at((2 * d + which) * side, side)
                own[d] = own[d] + nn(rows[slot, i], gug_b[i, :, cut])
            return carry

        lax.fori_loop(0, count, add, 0)

        @pl.when((which == 1) & (step + 2 < 8))
        def _():
            for copy in slices(step + 2):
                copy.start()

    def hop_copies(step, which):
        return [
            send(ring.at[d, which, step], ring.at[d, which, step + 1], ring_send.at[d, which, step],
                 ring_recv.at[d, which, step], peer)
            for d, peer in enumerate((right, left))
        ]

    def exchange():
        return [
            send(hid_buf.at[peer["fsdp"]], hid_in.at[me], a2a_send.at[i], a2a_recv.at[i], peer)
            for i, peer in enumerate(peers)
        ]

    def poll(index):
        step, which = index // 2, index % 2
        parts(step + 1, which)
        for copy in hop_copies(step, which):
            copy.wait()

        @pl.when(step < 6)
        def _():
            for d in range(2):
                ring[d, which, step + 1] = (ring[d, which, step + 1].astype(F32) + own[d]).astype(BF)
            for copy in hop_copies(step + 1, which):
                copy.start()

        @pl.when(step == 6)
        def _():
            for d in range(2):
                total = ring[d, which, 7].astype(F32) + own[d]
                for i in range(4):
                    hid_buf[i, :, lanes_at((2 * d + which) * side, side)] = total[
                        i * rows_w : (i + 1) * rows_w
                    ].astype(BF)

        @pl.when(index == 13)
        def _():
            for copy in exchange():
                copy.start()

    for copy in loads:
        copy.wait()

    def begin(which, carry):
        parts(0, which)
        for d in range(2):
            ring[d, which, 0] = own[d].astype(BF)
        for copy in hop_copies(0, which):
            copy.start()
        return carry

    lax.fori_loop(0, 2, begin, 0)

    def open_head(head):
        slot = head % 2
        raw_copy(head).wait()

        @pl.when(head + 1 < heads)
        def _():
            raw_copy(head + 1).start()

        @pl.when(head >= 2)
        def _():
            out_copy(head - 2).wait()

        scale = scales[head]
        mine = rows_at(head * HEAD_DIM, HEAD_DIM)

        for i in range(NB):
            here = slice(i * BLOCK, (i + 1) * BLOCK)
            q_unit, _ = head_norm(raw[slot, 0, :, here])
            k_unit, _ = head_norm(raw[slot, 1, :, here])
            q8 = (q_unit * scale).astype(BF) * BF(8.0)
            qT[:, here] = q8
            q[here, :] = q8.T
            kn = (k_unit * scale).astype(BF)
            kT[:, here] = kn
            k[here, :] = kn.T
            v[here, :] = raw[slot, 2, :, here].astype(BF).T
            gh = gm[mine, here]
            gT[:, here] = gh
            g[here, :] = gh.T
            delta[:, here] = jnp.sum(gh.astype(F32) * mixed[mine, here].astype(F32), axis=0, keepdims=True)
            inv[:, here] = sums[head, 0:1, here]
        dk[...] = jnp.zeros_like(dk)
        dv[...] = jnp.zeros_like(dv)

    def visit(start, pieces):
        span = lanes_at(start, 256)
        query, grad = qT[:, span], gT[:, span]
        query_rows, grad_rows = q[span, :], g[span, :]
        scale_row, delta_row = inv[:, span], delta[:, span]
        acc = jnp.zeros((64, 256), F32)
        for kstart, size, kind in pieces:
            keys = lanes_at(kstart, size)
            probs = masked(kind, jnp.exp(nn(k[keys, :], query)) * scale_row)
            g_probs = nn(v[keys, :], grad)
            g_scores = (probs * (g_probs - delta_row)).astype(BF)
            dv[keys, :] += nn(probs.astype(BF), grad_rows)
            dk[keys, :] += nn(g_scores, query_rows)
            acc = acc + nn(kT[:, keys], g_scores)
        dq[:, span] = acc * 8.0


    def close_head(head):
        slot = head % 2
        scale = scales[head]
        total = jnp.zeros((64, BLOCK), F32)
        for i in range(NB):
            here = slice(i * BLOCK, (i + 1) * BLOCK)
            for which, grad in ((0, dq[:, here]), (1, dk[here, :].T)):
                unit, inverse = head_norm(raw[slot, which, :, here])
                total = total + grad * unit
                scaled = grad * scale
                value = (scaled - unit * jnp.sum(scaled * unit, axis=0, keepdims=True)) * inverse
                out_b[slot, which, :, here] = value.astype(BF)
            out_b[slot, 2, :, here] = dv[here, :].T.astype(BF)
        g_scale[head] = jnp.sum(total, axis=1, keepdims=True)
        out_copy(head).start()

    def work(i, carry):
        head, segment = i // 4, i % 4
        pl.when(segment == 0)(functools.partial(open_head, head))
        pl.when(segment == 1)(functools.partial(early_chunks, visit))
        pl.when(segment == 2)(functools.partial(late_chunks, visit))
        pl.when(segment == 3)(functools.partial(close_head, head))
        pl.when(i < 14)(functools.partial(poll, i))
        return carry

    lax.fori_loop(0, 4 * heads, work, 0)
    for copy in exchange():
        copy.wait()
    hid_in[me] = hid_buf[me]
    size = g_up.shape[1] // 32
    for which, out in enumerate((g_up, g_gate)):
        for d in range(8):
            start = (8 * which + d) * size
            block = [hid_in[i, :, start : start + size].astype(F32) for i in range(4)]
            out[:, d * 4 * size : (d + 1) * 4 * size] = jnp.concatenate(block, axis=1)
    for head in (heads - 2, heads - 1):
        out_copy(head).wait()


def attention_back(order, qkv, scales, sums, mixed, ga_all, w_o, ht_all, gug_all):
    heads = scales.shape[0]
    count, tokens, hidden_width = gug_all.shape
    chunk = ht_all.shape[1] // 8
    side = hidden_width // 4
    rows_w = chunk // 4
    vmem, hbm = pl.BlockSpec(memory_space=pltpu.VMEM), pl.BlockSpec(memory_space=pl.ANY)
    smem = pl.BlockSpec(memory_space=pltpu.SMEM)
    dma = pltpu.SemaphoreType.DMA
    return pl.pallas_call(
        attention_back_kernel,
        in_specs=[smem, hbm, vmem, vmem, vmem, hbm, hbm, hbm, hbm],
        out_specs=[hbm, vmem, vmem, vmem, vmem],
        out_shape=[
            jax.ShapeDtypeStruct(qkv.shape, BF),
            jax.ShapeDtypeStruct(scales.shape, F32),
            jax.ShapeDtypeStruct(w_o.shape[1:], BF),
            jax.ShapeDtypeStruct((rows_w, 2 * hidden_width), F32),
            jax.ShapeDtypeStruct((rows_w, 2 * hidden_width), F32),
        ],
        scratch_shapes=[
            pltpu.VMEM(w_o.shape[1:], BF),
            pltpu.VMEM(ga_all.shape, BF),
            pltpu.VMEM((TOK, w_o.shape[2]), BF),
            pltpu.VMEM(mixed.shape, BF),
            pltpu.VMEM((2, 3, HEAD_DIM, TOK), F32),
            pltpu.VMEM((2, 3, HEAD_DIM, TOK), BF),
            pltpu.VMEM((HEAD_DIM, TOK), BF),
            pltpu.VMEM((TOK, HEAD_DIM), BF),
            pltpu.VMEM((TOK, HEAD_DIM), BF),
            pltpu.VMEM((HEAD_DIM, TOK), BF),
            pltpu.VMEM((TOK, HEAD_DIM), BF),
            pltpu.VMEM((HEAD_DIM, TOK), BF),
            pltpu.VMEM((TOK, HEAD_DIM), BF),
            pltpu.VMEM((HEAD_DIM, TOK), F32),
            pltpu.VMEM((TOK, HEAD_DIM), F32),
            pltpu.VMEM((TOK, HEAD_DIM), F32),
            pltpu.VMEM((1, TOK), F32),
            pltpu.VMEM((1, TOK), F32),
            pltpu.VMEM(gug_all.shape, BF),
            pltpu.VMEM((2, count, chunk, tokens), BF),
            pltpu.VMEM((2, count, chunk, tokens), BF),
            pltpu.VMEM((2, 2, 8, chunk, side), BF),
            pltpu.VMEM((2, chunk, side), F32),
            pltpu.VMEM((4, rows_w, hidden_width), BF),
            pltpu.VMEM((4, rows_w, hidden_width), BF),
            dma((2,)),
            dma((count,)),
            dma((2, 2)),
            dma((2,)),
            dma((2,)),
            dma((2, 2, 7)),
            dma((2, 2, 7)),
            dma((3,)),
            dma((3,)),
        ],
        compiler_params=pltpu.CompilerParams(
            collective_id=5, has_side_effects=True, vmem_limit_bytes=62 << 20
        ),
        name="attention_back",
        cost_estimate=pl.CostEstimate(flops=40 * 10**9, bytes_accessed=60 << 20, transcendentals=14 << 20),
    )(order, qkv, scales, sums, mixed, ga_all, w_o, ht_all, gug_all)


MESH = pl.DeviceIdType.MESH


def ring_place():
    dp = lax.axis_index("dp")
    z, y = dp // 2, dp % 2
    return z + y * (7 - 2 * z)


def ring_dp(place):
    place = (place + 16) % 8
    y = place // 4
    return 2 * (place + y * (7 - 2 * place)) + y


def greet(peers):
    barrier = pltpu.get_barrier_semaphore()
    for peer in peers:
        pl.semaphore_signal(barrier, inc=1, device_id=peer, device_id_type=MESH)
    pl.semaphore_wait(barrier, len(peers))


def group_peers():
    me = lax.axis_index("fsdp")
    core = 1 - 2 * (me % 2)
    chip = 2 - 4 * (me // 2)
    return {"fsdp": me + core}, {"fsdp": me + chip}, {"fsdp": me + core + chip}


def send(src, dst, send_sem, recv_sem, peer):
    return pltpu.make_async_remote_copy(
        src_ref=src, dst_ref=dst, send_sem=send_sem, recv_sem=recv_sem, device_id=peer, device_id_type=MESH
    )


EARLY_HOPS = 5


def hidden_ring(ref, sends, recvs, step, base=0):
    place = ring_place()
    right, left = {"dp": ring_dp(place + 1)}, {"dp": ring_dp(place - 1)}
    chunk = ref.shape[0] // 8
    to_right, to_left = ring_dp(place - step) * chunk, ring_dp(place + step) * chunk
    first, size = 48, chunk // 2
    cuts = ((to_right, first, right), (to_left + size, first, left),
            (to_right + first, size - first, right), (to_left + size + first, size - first, left))
    return [
        send(ref.at[rows_at(start, rows)], ref.at[rows_at(start, rows)], sends.at[i, step - base],
             recvs.at[i, step - base], peer)
        for i, (start, rows, peer) in enumerate(cuts)
    ]


def forward_kernel(order, states, w_query, w_key, w_value, small, extra, out_piece, w_up, w_gate,
                   tokens_t, w_t, w_o, w_ug, qkv, mixed, sums, mixed_n,
                   qkv_send, ug_send, land, weights, tok, turned, tok_t, out_w, ug_land, ug_own, raw, qs, ks, vs, blocks, natural,
                   tok_send, tok_recv, a2a_send, a2a_recv, ring_send, ring_recv, ug_s, ug_r, local_sem, raw_sem,
                   w_send, w_recv):
    me, dp = lax.axis_index("fsdp"), lax.axis_index("dp")
    place = ring_place()
    sibling, across, corner = group_peers()
    right, left = {"dp": ring_dp(place + 1)}, {"dp": ring_dp(place - 1)}
    rows, width = states.shape
    piece = land.shape[1]
    chunk = 4 * piece
    half = chunk // 2
    cols = mixed.shape[0]
    heads = cols // HEAD_DIM
    own = pltpu.make_async_copy(states, tok.at[pl.ds(0, rows)], local_sem.at[0])
    own.start()
    for i in range(4):
        cut = slice(i * cols, (i + 1) * cols)
        block = [w[:, cut].astype(F32) for w in (w_query, w_key, w_value)] + [small[...].astype(F32)]
        qkv_send[i] = jnp.concatenate(block, axis=1).astype(BF)
    greet([sibling, across, corner, right, left])

    exchange, ug_exchange = [], []
    for i, peer in enumerate((sibling, across, corner)):
        copy = send(qkv_send.at[peer["fsdp"]], land.at[me], a2a_send.at[i], a2a_recv.at[i], peer)
        copy.start()
        exchange.append(copy)
    far = []
    for i in range(2):
        part = pl.ds(i * (rows // 2), rows // 2)
        here = pl.ds(2 * rows + i * (rows // 2), rows // 2)
        copy = send(states.at[part], tok.at[here], tok_send.at[i], tok_recv.at[i], across)
        copy.start()
        far.append(copy)
    near = send(states, tok.at[pl.ds(rows, rows)], tok_send.at[2], tok_recv.at[2], sibling)
    near.start()
    size = w_up.shape[1] // 32
    for i in range(4):
        for which, w in enumerate((w_up, w_gate)):
            for half_d in range(2):
                block = [
                    w[:, (4 * d + i) * size : (4 * d + i + 1) * size].astype(F32)
                    for d in range(4 * half_d, 4 * half_d + 4)
                ]
                start = (8 * which + 4 * half_d) * size
                ug_send[i, :, start : start + 4 * size] = jnp.concatenate(block, axis=1).astype(BF)
    land[me] = qkv_send[me]
    ug_land[me] = ug_send[me]
    out_w[dp] = out_piece[...]
    vs[HEAD_DIM:, :] = jnp.ones((vs.shape[0] - HEAD_DIM, TOK), BF)
    for copy in exchange:
        copy.wait()
    weights[rows_at(dp * chunk, chunk)] = jnp.concatenate([land[i].astype(F32) for i in range(4)], axis=0).astype(BF)
    last = pl.ds(weights.shape[1] - 128, 128)
    weights[rows_at(dp * chunk, chunk), last] = weights[rows_at(dp * chunk, chunk), last] + extra[...]

    def ring_copies(step):
        to_right, to_left = ring_dp(place - step), ring_dp(place + step)
        first, second = rows_at(to_right * chunk, half), rows_at(to_left * chunk + half, half)
        lanes_r, lanes_l = pl.ds(0, width // 2), pl.ds(width // 2, width // 2)
        return [
            send(ref, ref, ring_send.at[i, step], ring_recv.at[i, step], peer)
            for i, (ref, peer) in enumerate(
                (
                    (weights.at[first], right),
                    (weights.at[second], left),
                    (out_w.at[to_right, :, lanes_r], right),
                    (out_w.at[to_left, :, lanes_l], left),
                )
            )
        ]

    def hop(step, carry):
        for copy, later in zip(ring_copies(step), ring_copies(step + 1)):
            copy.wait()
            pl.when(step < 6)(later.start)
        return carry

    def ug_poll(index):
        step = index // 2
        now, late = hidden_ring(w_ug, ug_s, ug_r, step), hidden_ring(w_ug, ug_s, ug_r, step + 1)

        def pass_on(first):
            for copy, later in zip(now[first : first + 2], late[first : first + 2]):
                copy.wait()
                pl.when(step < EARLY_HOPS - 1)(later.start)

        pl.when(index % 2 == 0)(functools.partial(pass_on, 0))
        pl.when(index % 2 == 1)(functools.partial(pass_on, 2))

    for copy in ring_copies(0):
        copy.start()

    def turn(i, carry):
        turned[i] = tok[lanes_at(i * BLOCK, BLOCK)].T
        return carry

    lax.fori_loop(0, 1, hop, 0)
    near.wait()
    own.wait()
    lax.fori_loop(0, 4, turn, 0)
    lax.fori_loop(1, 2, hop, 0)
    lax.fori_loop(4, 7, turn, 0)
    lax.fori_loop(2, 3, hop, 0)
    lax.fori_loop(7, 10, turn, 0)
    lax.fori_loop(3, 5, hop, 0)
    passed = []
    for i in range(2):
        far[i].wait()
        here = pl.ds(2 * rows + i * (rows // 2), rows // 2)
        there = pl.ds(3 * rows + i * (rows // 2), rows // 2)
        copy = send(tok.at[here], tok.at[there], tok_send.at[3 + i], tok_recv.at[3 + i], sibling)
        copy.start()
        passed.append(copy)
    for i, peer in enumerate((sibling, across, corner)):
        copy = send(ug_send.at[peer["fsdp"]], ug_land.at[me], a2a_send.at[3 + i], a2a_recv.at[3 + i], peer)
        copy.start()
        ug_exchange.append(copy)
    lax.fori_loop(5, 6, hop, 0)
    lax.fori_loop(10, 15, turn, 0)
    lax.fori_loop(6, 7, hop, 0)
    for copy in passed:
        copy.wait()

    lax.fori_loop(15, NB, turn, 0)

    def arrange(i, carry):
        tok_t[:, lanes_at(i * BLOCK, BLOCK)] = turned[order[0, i]]
        return carry

    lax.fori_loop(0, NB, arrange, 0)
    keep = pltpu.make_async_copy(tok_t, tokens_t, local_sem.at[2])
    keep.start()

    def turn_weights(i, carry):
        w_t[:, lanes_at(i * BLOCK, BLOCK)] = weights[rows_at(i * BLOCK, BLOCK)].T
        return carry

    lax.fori_loop(0, width // BLOCK, turn_weights, 0)
    for copy in ug_exchange:
        copy.wait()
    ug_own[...] = jnp.concatenate([ug_land[i].astype(F32) for i in range(4)], axis=0).astype(BF)
    ug_store = pltpu.make_async_copy(ug_own, w_ug.at[rows_at(dp * chunk, chunk)], local_sem.at[1])
    ug_store.start()
    ug_store.wait()
    for copy in hidden_ring(w_ug, ug_s, ug_r, 0):
        copy.start()
    w_o[0] = jnp.concatenate([out_w[i].astype(F32) for i in range(8)], axis=0).astype(BF)
    w_copies = [
        send(w_o.at[0], w_o.at[i + 1], w_send.at[i], w_recv.at[i], peer)
        for i, peer in enumerate((sibling, across, corner))
    ]
    for copy in w_copies:
        copy.start()

    def raw_copies(head):
        slot = head % 2
        return [
            pltpu.make_async_copy(
                raw.at[slot, pl.ds(which * HEAD_DIM, HEAD_DIM)],
                qkv.at[which, rows_at(head * HEAD_DIM, HEAD_DIM)],
                raw_sem.at[slot, which],
            )
            for which in range(3)
        ]

    def open_head(head):
        slot = head % 2

        @pl.when(head >= 2)
        def _():
            for copy in raw_copies(head - 2):
                copy.wait()

        left_rows = jnp.concatenate(
            [w_t[rows_at(which * cols + head * HEAD_DIM, HEAD_DIM)] for which in range(3)], axis=0
        )

        def project_tile(n, carry):
            raw[slot, :, tile(n)] = nn(left_rows, tok_t[:, tile(n)])
            return carry

        lax.fori_loop(0, TOK // TILE, project_tile, 0, unroll=2)
        for copy in raw_copies(head):
            copy.start()
        scale = weights[rows_at(me * cols + head * HEAD_DIM, HEAD_DIM), last][:, HEAD_DIM : HEAD_DIM + 1].astype(F32)

        def prepare(i, carry):
            here = lanes_at(i * BLOCK, BLOCK)
            q_unit, _ = head_norm(raw[slot, pl.ds(0, HEAD_DIM), here])
            k_unit, _ = head_norm(raw[slot, pl.ds(HEAD_DIM, HEAD_DIM), here])
            qs[:, here] = (q_unit * scale).astype(BF) * BF(8.0)
            ks[here, :] = (k_unit * scale).astype(BF).T
            vs[0:HEAD_DIM, here] = raw[slot, pl.ds(2 * HEAD_DIM, HEAD_DIM), here].astype(BF)
            return carry

        lax.fori_loop(0, NB, prepare, 0, unroll=NB)

    def visit(head, start, parts):
        span = lanes_at(start, 256)
        query = qs[:, span]
        acc = jnp.zeros((vs.shape[0], 256), F32)
        for kstart, count, kind in parts:
            keys = lanes_at(kstart, count)
            powers = masked(kind, jnp.exp(nn(ks[keys, :], query))).astype(BF)
            acc = acc + nn(vs[:, keys], powers)
        total = 1.0 / acc[HEAD_DIM : HEAD_DIM + 1, :]
        mixed[rows_at(head * HEAD_DIM, HEAD_DIM), span] = (acc[0:HEAD_DIM, :] * total).astype(BF)
        sums[head, :, span] = jnp.broadcast_to(total, (8, 256))

    def work(i, carry):
        head, segment = i // 3, i % 3
        pl.when(segment == 0)(functools.partial(open_head, head))
        pl.when(segment == 1)(lambda: early_chunks(functools.partial(visit, head)))
        pl.when(segment == 2)(lambda: late_chunks(functools.partial(visit, head)))
        pl.when(i % 2 == 1)(lambda: ug_poll(i // 2))
        return carry

    lax.fori_loop(0, 3 * heads, work, 0)

    def split(i, carry):
        blocks[i] = mixed[:, lanes_at(i * BLOCK, BLOCK)]
        return carry

    def arrange_back(i, carry):
        natural[i] = blocks[order[1, i]]
        return carry

    lax.fori_loop(0, NB, split, 0)
    lax.fori_loop(0, NB, arrange_back, 0)
    keep_mixed = pltpu.make_async_copy(natural, mixed_n, local_sem.at[3])
    keep_mixed.start()
    lax.fori_loop(3 * heads // 2, 2 * EARLY_HOPS, lambda index, c: (ug_poll(index), c)[1], 0)
    keep.wait()
    keep_mixed.wait()
    for copy in w_copies:
        copy.wait()
    for head in (heads - 2, heads - 1):
        for copy in raw_copies(head):
            copy.wait()


def forward(order, states, w_query, w_key, w_value, small, extra, out_piece, w_up, w_gate):
    tps, rows_w = 4, w_query.shape[0]
    tokens, width = states.shape
    packed = 3 * width // tps + small.shape[1]
    hidden_width = 2 * w_up.shape[1] // tps
    cols = 8 * rows_w
    vmem, hbm = pl.BlockSpec(memory_space=pltpu.VMEM), pl.BlockSpec(memory_space=pl.ANY)
    smem = pl.BlockSpec(memory_space=pltpu.SMEM)
    dma = pltpu.SemaphoreType.DMA
    return pl.pallas_call(
        forward_kernel,
        in_specs=[smem, hbm] + [vmem] * 8,
        out_specs=[hbm, vmem, vmem, hbm, hbm, vmem, vmem, hbm],
        out_shape=[
            jax.ShapeDtypeStruct((width, TOK), BF),
            jax.ShapeDtypeStruct((packed, width), BF),
            jax.ShapeDtypeStruct((tps, cols, width), BF),
            jax.ShapeDtypeStruct((width, hidden_width), BF),
            jax.ShapeDtypeStruct((3, cols, TOK), F32),
            jax.ShapeDtypeStruct((cols, TOK), BF),
            jax.ShapeDtypeStruct((cols // HEAD_DIM, 8, TOK), F32),
            jax.ShapeDtypeStruct((NB, cols, BLOCK), BF),
        ],
        scratch_shapes=[
            pltpu.VMEM((tps, rows_w, packed), BF),
            pltpu.VMEM((tps, rows_w, hidden_width), BF),
            pltpu.VMEM((tps, rows_w, packed), BF),
            pltpu.VMEM((width, packed), BF),
            pltpu.VMEM((TOK, width), BF),
            pltpu.VMEM((NB, width, BLOCK), BF),
            pltpu.VMEM((width, TOK), BF),
            pltpu.VMEM((8, rows_w, width), BF),
            pltpu.VMEM((tps, rows_w, hidden_width), BF),
            pltpu.VMEM((tps * rows_w, hidden_width), BF),
            pltpu.VMEM((2, 3 * HEAD_DIM, TOK), F32),
            pltpu.VMEM((HEAD_DIM, TOK), BF),
            pltpu.VMEM((TOK, HEAD_DIM), BF),
            pltpu.VMEM((HEAD_DIM + 16, TOK), BF),
            pltpu.VMEM((NB, cols, BLOCK), BF),
            pltpu.VMEM((NB, cols, BLOCK), BF),
            dma((5,)),
            dma((5,)),
            dma((6,)),
            dma((6,)),
            dma((4, 7)),
            dma((4, 7)),
            dma((4, EARLY_HOPS)),
            dma((4, EARLY_HOPS)),
            dma((4,)),
            dma((2, 3)),
            dma((3,)),
            dma((3,)),
        ],
        compiler_params=pltpu.CompilerParams(
            collective_id=1, has_side_effects=True, vmem_limit_bytes=56 << 20
        ),
        cost_estimate=pl.CostEstimate(flops=12 * 10**9, bytes_accessed=200 << 20, transcendentals=14 << 20),
        name="forward",
    )(order, states, w_query, w_key, w_value, small, extra, out_piece, w_up, w_gate)


def last_kernel(order, base, tokens_t, g_qkv, w_t, part_out, vectors,
                g_states, g_query, g_key, g_value, out_rows, vec_own,
                gq_b, blocks, tok_r, tok_l, share, turned, core_buf, x_buf, base_b, gs_b,
                ring_r, ring_m, ring_l, ring_o, ring_v, next_r, next_l, row_buf, row_in, vec_part, vec_in,
                in_sem, row_sem, base_sem, core_send, core_recv, x_send, x_recv,
                ring_send, ring_recv, a2a_send, a2a_recv):
    me, dp = lax.axis_index("fsdp"), lax.axis_index("dp")
    place = ring_place()
    sibling, across, corner = group_peers()
    right, left = {"dp": ring_dp(place + 1)}, {"dp": ring_dp(place - 1)}
    chunk, side, cut = ring_r.shape[1], next_r.shape[1], ring_r.shape[2]
    rows = share.shape[1]
    quarter = rows // 4
    width = w_t.shape[1]
    heads_width = gq_b.shape[0]
    rows_w = row_buf.shape[1]

    def slices(step):
        slot = step % 2
        cut_r = rows_at(ring_dp(place - 1 - step) * chunk, chunk)
        cut_l = rows_at(ring_dp(place + 1 + step) * chunk, chunk)
        return [
            pltpu.make_async_copy(tokens_t.at[cut_r], tok_r.at[slot], row_sem.at[0, slot]),
            pltpu.make_async_copy(tokens_t.at[cut_l], tok_l.at[slot], row_sem.at[1, slot]),
        ]

    def base_copy(i):
        return pltpu.make_async_copy(base.at[pl.ds(i * quarter, quarter)], base_b.at[i % 2], base_sem.at[0, i % 2])

    def gs_copy(i):
        return pltpu.make_async_copy(gs_b.at[i % 2], g_states.at[pl.ds(i * quarter, quarter)], base_sem.at[1, i % 2])

    load_q = pltpu.make_async_copy(g_qkv, gq_b, in_sem.at[0])
    load_q.start()
    for step in (0, 1):
        for copy in slices(step):
            copy.start()
    greet([sibling, across, corner, right, left])

    def parts(step):
        slot = step % 2
        for copy in slices(step):
            copy.wait()
        next_r[...] = nt(tok_r[slot], gq_b[pl.ds(0, side)])
        next_l[...] = nt(tok_l[slot], gq_b[pl.ds(side, heads_width - side)])

        @pl.when(step + 2 < 8)
        def _():
            for copy in slices(step + 2):
                copy.start()

    def hop_copies(step):
        return [
            send(ring.at[step], ring.at[step + 1], ring_send.at[i, step], ring_recv.at[i, step], peer)
            for i, (ring, peer) in enumerate(
                ((ring_r, right), (ring_l, left), (ring_m, right), (ring_o, left), (ring_v, right))
            )
        ]

    def through(r, slot):
        for i in range(rows // BLOCK):
            turned[i * BLOCK : (i + 1) * BLOCK] = blocks[order[1, r * (rows // BLOCK) + i]].T

        def one(n, carry):
            share[slot, :, tile(n)] = nn(turned[...], w_t[pl.ds(0, heads_width), tile(n)]).astype(BF)
            return carry

        lax.fori_loop(0, width // TILE, one, 0)

    core = [
        send(share.at[0], core_buf.at[0], core_send.at[0], core_recv.at[0], sibling),
        send(share.at[2], core_buf.at[1], core_send.at[1], core_recv.at[1], sibling),
    ]
    far = [
        send(share.at[1, pl.ds(i * quarter, quarter)], x_buf.at[pl.ds(i * quarter, quarter)], x_send.at[i],
             x_recv.at[i], across)
        for i in range(4)
    ]
    load_q.wait()

    def split(i, carry):
        blocks[i] = gq_b[:, lanes_at(i * BLOCK, BLOCK)]
        return carry

    def hop(step, carry):
        parts(step)

        @pl.when(step == 0)
        def _():
            ring_r[0] = next_r[:, :cut].astype(BF)
            ring_m[0] = next_r[:, cut:].astype(BF)
            ring_l[0] = next_l[...].astype(BF)
            ring_o[0] = part_out[ring_dp(place + 1)]
            ring_v[0] = vectors[ring_dp(place - 1)]

        @pl.when(step > 0)
        def _():
            before, now = hop_copies(step - 1), hop_copies(step)
            before[0].wait()
            ring_r[step] = (ring_r[step].astype(F32) + next_r[:, :cut]).astype(BF)
            now[0].start()
            before[1].wait()
            ring_l[step] = (ring_l[step].astype(F32) + next_l[...]).astype(BF)
            now[1].start()
            before[2].wait()
            ring_m[step] = (ring_m[step].astype(F32) + next_r[:, cut:]).astype(BF)
            now[2].start()
            before[3].wait()
            ring_o[step] = (ring_o[step].astype(F32) + part_out[ring_dp(place + 1 + step)].astype(F32)).astype(BF)
            now[3].start()
            before[4].wait()
            ring_v[step] = ring_v[step] + vectors[ring_dp(place - 1 - step)]
            now[4].start()

        @pl.when(step == 0)
        def _():
            for copy in hop_copies(0):
                copy.start()

        @pl.when(step < 4)
        def _():
            @pl.when(step == 0)
            def _():
                lax.fori_loop(0, NB, split, 0)
                through(3, 0)
                core[0].start()

            @pl.when(step < 3)
            def _():
                through(2 - step, (step + 1) % 3)

            @pl.when(step == 0)
            def _():
                core[0].wait()
                for i in range(4):
                    span = pl.ds(i * quarter, quarter)
                    share[1, span] = (share[1, span].astype(F32) + core_buf[0, span].astype(F32)).astype(BF)
                    far[i].start()

            @pl.when(step == 1)
            def _():
                core[1].start()

        return carry

    lax.fori_loop(0, 7, hop, 0)
    base_copy(0).start()
    base_copy(1).start()
    parts(7)
    for copy in hop_copies(6):
        copy.wait()
    total = jnp.concatenate((ring_r[7], ring_m[7], ring_l[7]), axis=1).astype(F32)
    total = total + jnp.concatenate((next_r[...], next_l[...]), axis=1)
    for i in range(4):
        row_buf[i] = total[i * rows_w : (i + 1) * rows_w].astype(BF)
    vec_part[...] = ring_v[7] + vectors[dp]
    exchange = []
    for i, peer in enumerate((sibling, across, corner)):
        to = peer["fsdp"]
        copies = [
            send(row_buf.at[to], row_in.at[me], a2a_send.at[i], a2a_recv.at[i], peer),
            send(vec_part.at[to], vec_in.at[me], a2a_send.at[3 + i], a2a_recv.at[3 + i], peer),
        ]
        for copy in copies:
            copy.start()
        exchange += copies
    row_in[me] = row_buf[me]
    vec_in[me] = vec_part[me]
    out_rows[...] = ring_o[7].astype(F32) + part_out[dp].astype(F32)
    core[1].wait()
    for i in range(4):
        span = pl.ds(i * quarter, quarter)
        far[i].wait()
        base_copy(i).wait()
        if i >= 2:
            gs_copy(i - 2).wait()
        gs_b[i % 2] = base_b[i % 2] + (
            share[0, span].astype(F32) + core_buf[1, span].astype(F32) + x_buf[span].astype(F32)
        )
        gs_copy(i).start()
        if i < 2:
            base_copy(i + 2).start()
    for copy in exchange:
        copy.wait()
    vec_own[...] = vec_in[0] + vec_in[1] + vec_in[2] + vec_in[3]
    cols = heads_width // 3
    for which, out in enumerate((g_query, g_key, g_value)):
        out[...] = jnp.concatenate(
            [row_in[i, :, which * cols : (which + 1) * cols].astype(F32) for i in range(4)], axis=1
        )
    for i in (2, 3):
        gs_copy(i).wait()


def last_exchange(order, base, tokens_t, g_qkv, w_t, part_out, vectors):
    rows, width = base.shape
    heads_width = g_qkv.shape[0]
    rows_w = part_out.shape[1]
    chunk = 4 * rows_w
    side = 2 * heads_width // 3
    vmem, hbm = pl.BlockSpec(memory_space=pltpu.VMEM), pl.BlockSpec(memory_space=pl.ANY)
    dma = pltpu.SemaphoreType.DMA
    return pl.pallas_call(
        last_kernel,
        in_specs=[pl.BlockSpec(memory_space=pltpu.SMEM), hbm, hbm, hbm, vmem, vmem, vmem],
        out_specs=[hbm] + [vmem] * 5,
        out_shape=[jax.ShapeDtypeStruct((rows, width), F32)]
        + [jax.ShapeDtypeStruct((rows_w, width), F32)] * 4
        + [jax.ShapeDtypeStruct(vectors.shape[2:], F32)],
        scratch_shapes=[
            pltpu.VMEM(g_qkv.shape, BF),
            pltpu.VMEM((NB, heads_width, BLOCK), BF),
            pltpu.VMEM((2, chunk, tokens_t.shape[1]), BF),
            pltpu.VMEM((2, chunk, tokens_t.shape[1]), BF),
            pltpu.VMEM((3, rows, width), BF),
            pltpu.VMEM((rows, heads_width), BF),
            pltpu.VMEM((2, rows, width), BF),
            pltpu.VMEM((rows, width), BF),
            pltpu.VMEM((2, rows // 4, width), F32),
            pltpu.VMEM((2, rows // 4, width), F32),
            pltpu.VMEM((8, chunk, 384), BF),
            pltpu.VMEM((8, chunk, side - 384), BF),
            pltpu.VMEM((8, chunk, heads_width - side), BF),
            pltpu.VMEM((8, rows_w, width), BF),
            pltpu.VMEM(vectors.shape, F32),
            pltpu.VMEM((chunk, side), F32),
            pltpu.VMEM((chunk, heads_width - side), F32),
            pltpu.VMEM((4, rows_w, heads_width), BF),
            pltpu.VMEM((4, rows_w, heads_width), BF),
            pltpu.VMEM(vectors.shape[1:], F32),
            pltpu.VMEM(vectors.shape[1:], F32),
            dma((1,)),
            dma((2, 2)),
            dma((2, 2)),
            dma((2,)),
            dma((2,)),
            dma((4,)),
            dma((4,)),
            dma((5, 7)),
            dma((5, 7)),
            dma((6,)),
            dma((6,)),
        ],
        compiler_params=pltpu.CompilerParams(
            collective_id=2, has_side_effects=True, vmem_limit_bytes=48 << 20
        ),
        cost_estimate=pl.CostEstimate(flops=13 * 10**9, bytes_accessed=100 << 20, transcendentals=0),
        name="last_exchange",
    )(order, base, tokens_t, g_qkv, w_t, part_out, vectors)


CHUNK = 128
TILE = 256
LAG = 3


def tile(index, base=0):
    return pl.ds(pl.multiple_of(base + index * TILE, TILE), TILE)


def nt(a, b):
    return lax.dot_general(a, b, (((1,), (1,)), ((), ())), preferred_element_type=F32)


def middle_kernel(mixed_n, states, teacher, weight, mask, w_in, w_own, w_o, rates, scales,
                  w_ug_out, w_d_out, hidden_out, back_out, out_states, attn_unit, attn_inv, hidden_inv, sums, gd_all,
                  ht_all, act_all, ug_all, w_ug, w_d, hidden, back, target, mx, part, core, x_buf, tok, gd, act, act_t, ug, ht,
                  mx_send, mx_recv, mx_own, keep_sem, core_send, core_recv, x_send, x_recv, tok_send, tok_recv, gd_send, gd_recv, gd_own,
                  out_sem, ring_send, ring_recv, ug_s, ug_r, ug_sem):
    sibling, across, corner = group_peers()
    dp, place = lax.axis_index("dp"), ring_place()
    right, left = {"dp": ring_dp(place + 1)}, {"dp": ring_dp(place - 1)}
    piece = w_own.shape[0]
    count = x_buf.shape[0]
    width = hidden.shape[1]
    rate_attn, rate_mlp = rates[0:1], rates[1:2]

    def rows(i):
        return pl.ds(pl.multiple_of(i * CHUNK, CHUNK), CHUNK)

    def mx_copies(i):
        return [
            send(mixed_n.at[(r + 1) * count + i], mx.at[i, r + 1], mx_send.at[r, i], mx_recv.at[r, i], peer)
            for r, peer in enumerate((sibling, across, corner))
        ]

    def load_teacher(i):
        return pltpu.make_async_copy(teacher.at[rows(i)], target.at[i % 2], keep_sem.at[2, 2 + i % 2])

    def mx_local(i):
        return pltpu.make_async_copy(mixed_n.at[i], mx.at[i, 0], mx_own.at[i])

    def keep_rows(i):
        return [
            pltpu.make_async_copy(hidden.at[rows(i)], hidden_out.at[rows(i)], keep_sem.at[0, i]),
            pltpu.make_async_copy(back.at[rows(i)], back_out.at[rows(i)], keep_sem.at[1, i]),
        ]

    keep_w = [
        pltpu.make_async_copy(w_ug, w_ug_out, keep_sem.at[2, 0]),
        pltpu.make_async_copy(w_d, w_d_out, keep_sem.at[2, 1]),
    ]

    def core_a(stage, i):
        return send(part.at[i % 3, 3], core.at[0, i], core_send.at[stage, 0, i], core_recv.at[stage, 0, i], sibling)

    def core_b(stage, i):
        return send(part.at[i % 3, 1], core.at[1, i], core_send.at[stage, 1, i], core_recv.at[stage, 1, i], sibling)

    def chip(stage, i):
        return send(part.at[i % 3, 2], x_buf.at[i], x_send.at[stage, i], x_recv.at[stage, i], across)

    def spread(buf, own, sems, recvs, i):
        return [
            send(own, buf.at[i, 1], sems.at[0, i], recvs.at[0, i], sibling),
            send(own, buf.at[i, 2], sems.at[1, i], recvs.at[1, i], across),
            send(buf.at[i, 2], buf.at[i, 3], sems.at[2, i], recvs.at[2, i], sibling),
        ]

    def tok_copies(i):
        return spread(tok, tok.at[i, 0], tok_send, tok_recv, i)

    def gd_copies(i):
        return spread(gd_all, gd.at[i], gd_send, gd_recv, i)

    def gd_local(i):
        return pltpu.make_async_copy(gd.at[i], gd_all.at[i, 0], gd_own.at[i])

    def outs(i):
        slot = i % 2
        return [
            pltpu.make_async_copy(ht.at[slot], ht_all.at[i], out_sem.at[0, slot]),
            pltpu.make_async_copy(act_t.at[slot], act_all.at[i], out_sem.at[1, slot]),
            pltpu.make_async_copy(ug.at[slot], ug_all.at[i], out_sem.at[2, slot]),
        ]

    def hop(step):
        late = hidden_ring(w_d, ring_send, ring_recv, step + 1)
        for copy, later in zip(hidden_ring(w_d, ring_send, ring_recv, step), late):
            copy.wait()
            pl.when(step < 6)(later.start)

    def ug_hop(step):
        late = hidden_ring(w_ug, ug_s, ug_r, step + 1, EARLY_HOPS)
        for copy, later in zip(hidden_ring(w_ug, ug_s, ug_r, step, EARLY_HOPS), late):
            copy.wait()
            pl.when(step < 6)(later.start)

    def forward_far(stage, i):
        core_a(stage, i).wait_recv()
        part[i % 3, 2] = (part[i % 3, 2].astype(F32) + core[0, i].astype(F32)).astype(BF)
        chip(stage, i).start()

    def reduced(stage, i):
        core_b(stage, i).wait_recv()
        chip(stage, i).wait_recv()
        total = part[i % 3, 0].astype(F32) + core[1, i].astype(F32) + x_buf[i].astype(F32)
        core_a(stage, i).wait_send()
        core_b(stage, i).wait_send()
        chip(stage, i).wait_send()
        return total

    sums[...] = jnp.zeros_like(sums)
    load_teacher(0).start()
    load_teacher(1).start()
    w_d[rows_at(dp * piece, piece)] = w_own[...]
    chunk = w_ug.shape[0] // 8

    def load_w(i):
        cuts = rows_at(ring_dp(place - i) * chunk, chunk // 2), rows_at(
            ring_dp(place + i) * chunk + chunk // 2, chunk // 2
        )
        return [pltpu.make_async_copy(w_in.at[cut], w_ug.at[cut], ug_sem.at[d, i]) for d, cut in enumerate(cuts)]

    def start_w(i, carry):
        for copy in load_w(i):
            copy.start()
        return carry

    def wait_w(i, carry):
        for copy in load_w(i):
            copy.wait()
        return carry

    lax.fori_loop(0, EARLY_HOPS + 1, start_w, 0)
    greet([sibling, across, corner, right, left])
    for copy in hidden_ring(w_d, ring_send, ring_recv, 0):
        copy.start()

    def open_mixed(i, carry):
        mx_local(i).start()
        for copy in mx_copies(i):
            copy.start()
        return carry

    lax.fori_loop(0, count, open_mixed, 0)
    lax.fori_loop(0, EARLY_HOPS + 1, wait_w, 0)
    for copy in hidden_ring(w_ug, ug_s, ug_r, EARLY_HOPS, EARLY_HOPS):
        copy.start()

    def norm_hidden(i):
        mx_local(i).wait()
        for copy in mx_copies(i):
            copy.wait()
        attn = nn(mx[i, 0].T, w_o[0])
        for r in range(1, 4):
            attn = attn + nn(mx[i, r].T, w_o[r])
        unit, inverse = unit_rows(attn)
        own = states[rows(i)].astype(F32)
        value, value_inv = unit_rows(own + rate_attn * (unit - own))
        hidden[rows(i)] = value
        attn_unit[rows(i)] = unit.astype(BF)
        attn_inv[rows(i)] = inverse
        hidden_inv[rows(i)] = value_inv
        tok[i, 0] = value.astype(BF)
        copies = tok_copies(i)
        copies[0].start()
        copies[1].start()

    def pass_tokens(i):
        copies = tok_copies(i)
        copies[1].wait_recv()
        copies[2].start()

    def feed(i):
        copies = tok_copies(i)
        copies[0].wait()
        copies[1].wait_send()
        copies[2].wait()
        slot = i % 2

        @pl.when(i >= 2)
        def _():
            for copy in outs(i - 2):
                copy.wait()

        def up(n, carry):
            here = tok[i].reshape(4 * CHUNK, width)
            up_proj = nn(here, w_ug[:, tile(n)])
            gate_proj = nn(here, w_ug[:, tile(n, width)])
            gated = gate_proj * scales[1:2, tile(n)]
            value = up_proj * scales[0:1, tile(n)] * (gated * jax.nn.sigmoid(gated))
            act[slot, :, tile(n)] = value.astype(BF)
            act_t[slot, tile(n)] = value.astype(BF).T
            ug[slot, :, tile(n)] = up_proj.astype(BF)
            ug[slot, :, tile(n, width)] = gate_proj.astype(BF)
            return carry

        lax.fori_loop(0, width // TILE, up, 0)
        for copy in outs(i)[1:]:
            copy.start()

    def feed_down(i):
        slot = i % 2

        def down(n, carry):
            value = nn(act[slot], w_d[:, tile(n)])
            part[i % 3, :, :, tile(n)] = value.astype(BF).reshape(4, CHUNK, TILE)
            ht[slot, tile(n)] = tok[i, :, :, tile(n)].reshape(4 * CHUNK, TILE).T
            return carry

        lax.fori_loop(0, width // TILE, down, 0)
        core_a(0, i).start()
        core_b(0, i).start()
        outs(i)[0].start()
        forward_far(0, i)

    def finish(i):
        unit, inverse = unit_rows(reduced(0, i))
        own = hidden[rows(i)]
        result, result_inv = unit_rows(own + rate_mlp * (unit - own))
        out_states[rows(i)] = result.astype(BF)
        load_teacher(i).wait()
        diff = result - target[i % 2]

        @pl.when(i + 2 < count)
        def _():
            load_teacher(i + 2).start()

        sums[1:2] = sums[1:2] + jnp.sum(mask[rows(i)] * (diff * diff), axis=0, keepdims=True)
        g_last = unit_back(weight[rows(i)] * diff, result, result_inv)
        sums[0:1] = sums[0:1] + jnp.sum(g_last * (unit - own), axis=0, keepdims=True)
        back[rows(i)] = g_last * (1.0 - rate_mlp)
        gd[i] = unit_back(g_last * rate_mlp, unit, inverse).astype(BF)
        copies = gd_copies(i)
        copies[0].start()
        copies[1].start()
        gd_local(i).start()
        for copy in keep_rows(i):
            copy.start()

    def pass_grads(i):
        copies = gd_copies(i)
        copies[1].wait_recv()
        copies[2].start()

    stages = (norm_hidden, pass_tokens, feed, feed_down, finish, pass_grads)

    def step(t, carry):
        for lag, stage in enumerate(stages):
            if lag == 2:
                pl.when(t < 7 - EARLY_HOPS)(lambda: ug_hop(EARLY_HOPS + t))
            if lag == 3:
                pl.when(t < 4)(lambda: hop(jnp.maximum(2 * t - 1, 0)))
                pl.when((t >= 1) & (t < 4))(lambda: hop(2 * t))

                @pl.when(t == 3)
                def _():
                    for copy in keep_w:
                        copy.start()

            pl.when((t >= lag) & (t < lag + count))(functools.partial(stage, t - lag))
        return carry

    lax.fori_loop(0, count + len(stages) - 1, step, 0)

    def close(i, carry):
        copies = gd_copies(i)
        copies[0].wait()
        copies[1].wait_send()
        copies[2].wait()
        gd_local(i).wait()
        for copy in keep_rows(i):
            copy.wait()
        return carry

    lax.fori_loop(0, count, close, 0)
    for i in (count - 2, count - 1):
        for copy in outs(i):
            copy.wait()
    for copy in keep_w:
        copy.wait()


def middle(mixed_n, states, teacher, weight, mask, w_ug, w_own, w_o, rates, scales):
    rows, width = states.shape
    count = rows // CHUNK
    vmem, hbm = pl.BlockSpec(memory_space=pltpu.VMEM), pl.BlockSpec(memory_space=pl.ANY)
    dma = pltpu.SemaphoreType.DMA
    return pl.pallas_call(
        middle_kernel,
        in_specs=[hbm, vmem, hbm, vmem, vmem, hbm] + [vmem] * 4,
        out_specs=[hbm] * 4 + [vmem] * 5 + [hbm] * 4,
        out_shape=[
            jax.ShapeDtypeStruct(w_ug.shape, BF),
            jax.ShapeDtypeStruct((8 * w_own.shape[0], width), BF),
            jax.ShapeDtypeStruct((rows, width), F32),
            jax.ShapeDtypeStruct((rows, width), F32),
            jax.ShapeDtypeStruct((rows, width), BF),
            jax.ShapeDtypeStruct((rows, width), BF),
            jax.ShapeDtypeStruct((rows, 1), F32),
            jax.ShapeDtypeStruct((rows, 1), F32),
            jax.ShapeDtypeStruct((2, width), F32),
            jax.ShapeDtypeStruct((count, 4, CHUNK, width), BF),
            jax.ShapeDtypeStruct((count, width, 4 * CHUNK), BF),
            jax.ShapeDtypeStruct((count, width, 4 * CHUNK), BF),
            jax.ShapeDtypeStruct((count, 4 * CHUNK, 2 * width), BF),
        ],
        scratch_shapes=[
            pltpu.VMEM(w_ug.shape, BF),
            pltpu.VMEM((8 * w_own.shape[0], width), BF),
            pltpu.VMEM((rows, width), F32),
            pltpu.VMEM((rows, width), F32),
            pltpu.VMEM((2, CHUNK, width), F32),
            pltpu.VMEM((count, 4) + mixed_n.shape[1:], BF),
            pltpu.VMEM((3, 4, CHUNK, width), BF),
            pltpu.VMEM((2, count, CHUNK, width), BF),
            pltpu.VMEM((count, CHUNK, width), BF),
            pltpu.VMEM((count, 4, CHUNK, width), BF),
            pltpu.VMEM((count, CHUNK, width), BF),
            pltpu.VMEM((2, 4 * CHUNK, width), BF),
            pltpu.VMEM((2, width, 4 * CHUNK), BF),
            pltpu.VMEM((2, 4 * CHUNK, 2 * width), BF),
            pltpu.VMEM((2, width, 4 * CHUNK), BF),
            dma((3, count)),
            dma((3, count)),
            dma((count,)),
            dma((3, count)),
            dma((1, 2, count)),
            dma((1, 2, count)),
            dma((1, count)),
            dma((1, count)),
            dma((3, count)),
            dma((3, count)),
            dma((3, count)),
            dma((3, count)),
            dma((count,)),
            dma((3, 2)),
            dma((4, 7)),
            dma((4, 7)),
            dma((4, 7 - EARLY_HOPS)),
            dma((4, 7 - EARLY_HOPS)),
            dma((2, EARLY_HOPS + 1)),
        ],
        compiler_params=pltpu.CompilerParams(
            collective_id=3, has_side_effects=True, vmem_limit_bytes=62 << 20
        ),
        cost_estimate=pl.CostEstimate(flops=26 * 10**9, bytes_accessed=400 << 20, transcendentals=4 << 20),
        name="middle",
    )(mixed_n, states, teacher, weight, mask, w_ug, w_own, w_o, rates, scales)


def middle_back_kernel(gd_all, act_all, ug_all, hidden, attn_unit, states, back, attn_inv, hidden_inv, w_ug, w_d,
                       rates, scales, base, ga_all, gug_all, down_rows, sums, ff_sums,
                       w_ug_b, w_d_b, part, core, x_buf, ga, gd, act, ug, gug, own_f, own_b, base_buf, dwd, column, ring_buf,
                       gd_sem, act_sem, in_sem, own_sem, core_send, core_recv, x_send, x_recv, ga_send, ga_recv,
                       ga_own, base_sem, out_sem, w_sem, ring_send, ring_recv):
    sibling, across, _ = group_peers()
    dp, place = lax.axis_index("dp"), ring_place()
    right, left = {"dp": ring_dp(place + 1)}, {"dp": ring_dp(place - 1)}
    count = core.shape[1]
    width = w_d.shape[0]
    load_d = pltpu.make_async_copy(w_d, w_d_b, w_sem.at[0])
    load_u = pltpu.make_async_copy(w_ug, w_ug_b, w_sem.at[1])
    load_d.start()
    half = ring_buf.shape[2]
    rate_attn = rates[0:1]

    def rows(i):
        return pl.ds(pl.multiple_of(i * CHUNK, CHUNK), CHUNK)

    def load_gd(i):
        return pltpu.make_async_copy(gd_all.at[i], gd.at[i], gd_sem.at[i])

    def load_act(i):
        return pltpu.make_async_copy(act_all.at[i], act.at[i], act_sem.at[i])

    def load_ug(i):
        return pltpu.make_async_copy(ug_all.at[i], ug.at[i % 2], in_sem.at[i % 2])

    def store_gug(i):
        return pltpu.make_async_copy(gug.at[i % 2], gug_all.at[i], out_sem.at[i % 2])

    def own_rows(i):
        return [
            pltpu.make_async_copy(hidden.at[rows(i)], own_f.at[0], own_sem.at[0]),
            pltpu.make_async_copy(back.at[rows(i)], own_f.at[1], own_sem.at[1]),
            pltpu.make_async_copy(attn_unit.at[rows(i)], own_b.at[0], own_sem.at[2]),
            pltpu.make_async_copy(states.at[rows(i)], own_b.at[1], own_sem.at[3]),
        ]

    def core_a(i):
        return send(part.at[i % 3, 3], core.at[0, i], core_send.at[0, i], core_recv.at[0, i], sibling)

    def core_b(i):
        return send(part.at[i % 3, 1], core.at[1, i], core_send.at[1, i], core_recv.at[1, i], sibling)

    def chip(i):
        return send(part.at[i % 3, 2], x_buf.at[i], x_send.at[i], x_recv.at[i], across)

    def ga_copies(i):
        return [
            send(ga.at[i], ga_all.at[1, rows(i)], ga_send.at[0, i], ga_recv.at[0, i], sibling),
            send(ga.at[i], ga_all.at[2, rows(i)], ga_send.at[1, i], ga_recv.at[1, i], across),
            send(ga_all.at[2, rows(i)], ga_all.at[3, rows(i)], ga_send.at[2, i], ga_recv.at[2, i], sibling),
        ]

    def ga_local(i):
        return pltpu.make_async_copy(ga.at[i], ga_all.at[0, rows(i)], ga_own.at[i])

    def base_copy(i):
        return pltpu.make_async_copy(base_buf.at[i % 2], base.at[rows(i)], base_sem.at[i % 2])

    def right_half(step):
        return rows_at(ring_dp(place - 1 - step) * 2 * half, half)

    def left_half(step):
        return rows_at(ring_dp(place + 1 + step) * 2 * half + half, half)

    def ring(step):
        return [
            send(ring_buf.at[0, step], ring_buf.at[0, step + 1], ring_send.at[0, step], ring_recv.at[0, step], right),
            send(ring_buf.at[1, step], ring_buf.at[1, step + 1], ring_send.at[1, step], ring_recv.at[1, step], left),
        ]

    def hop(step, carry):
        for copy in ring(step):
            copy.wait()

        @pl.when(step < 6)
        def _():
            for side, cut in ((0, right_half(step + 1)), (1, left_half(step + 1))):
                ring_buf[side, step + 1] = (
                    ring_buf[side, step + 1].astype(F32) + dwd[cut].astype(F32)
                ).astype(BF)
            for copy in ring(step + 1):
                copy.start()

        return carry

    for copy in [load_ug(0)] + own_rows(0):
        copy.start()
    lax.fori_loop(0, count, lambda i, c: (load_gd(i).start(), c)[1], 0)
    load_u.start()
    lax.fori_loop(0, count, lambda i, c: (load_act(i).start(), c)[1], 0)
    sums[...] = jnp.zeros_like(sums)
    ff_sums[...] = jnp.zeros_like(ff_sums)
    greet([sibling, across, right, left])
    lax.fori_loop(0, count, lambda i, c: (load_gd(i).wait(), c)[1], 0)
    load_d.wait()

    def feed(i):
        slot = i % 2
        load_ug(i).wait()

        @pl.when(i + 1 < count)
        def _():
            load_ug(i + 1).start()

        @pl.when(i >= 2)
        def _():
            store_gug(i - 2).wait()

        def grads(n, carry):
            g_act = nt(gd[i].reshape(4 * CHUNK, width), w_d_b[tile(n)])
            up_proj = ug[slot, :, tile(n)].astype(F32)
            gate_proj = ug[slot, :, tile(n, width)].astype(F32)
            scale_up, scale_gate = scales[0:1, tile(n)], scales[1:2, tile(n)]
            gated = gate_proj * scale_gate
            sigmoid = jax.nn.sigmoid(gated)
            g_upscaled = g_act * (gated * sigmoid)
            g_gated = g_act * (up_proj * scale_up) * sigmoid * (1.0 + gated * (1.0 - sigmoid))
            ff_sums[0:1, tile(n)] = ff_sums[0:1, tile(n)] + jnp.sum(g_upscaled * up_proj, axis=0, keepdims=True)
            ff_sums[1:2, tile(n)] = ff_sums[1:2, tile(n)] + jnp.sum(g_gated * gate_proj, axis=0, keepdims=True)
            gug[slot, :, tile(n)] = (g_upscaled * scale_up).astype(BF)
            gug[slot, :, tile(n, width)] = (g_gated * scale_gate).astype(BF)
            return carry

        lax.fori_loop(0, width // TILE, grads, 0)
        store_gug(i).start()
        pl.when(i == 0)(load_u.wait)

        def through(n, carry):
            value = nt(gug[slot], w_ug_b[tile(n)])
            part[i % 3, :, :, tile(n)] = value.astype(BF).reshape(4, CHUNK, TILE)
            return carry

        lax.fori_loop(0, width // TILE, through, 0)
        core_a(i).start()
        core_b(i).start()
        core_a(i).wait_recv()
        part[i % 3, 2] = (part[i % 3, 2].astype(F32) + core[0, i].astype(F32)).astype(BF)
        chip(i).start()

    def down_grads():
        lax.fori_loop(0, count, lambda i, c: (load_act(i).wait(), c)[1], 0)

        def outer(n, carry):
            column[...] = jnp.zeros_like(column)

            def add(k, carry):
                column[...] = column[...] + nn(act[k], gd[k, :, :, tile(n)].reshape(4 * CHUNK, TILE))
                return carry

            lax.fori_loop(0, count, add, 0)
            dwd[:, tile(n)] = column[...].astype(BF)
            return carry

        lax.fori_loop(0, width // TILE, outer, 0)
        ring_buf[0, 0] = dwd[right_half(0)]
        ring_buf[1, 0] = dwd[left_half(0)]
        for copy in ring(0):
            copy.start()

    def finish(i):
        core_b(i).wait_recv()
        chip(i).wait_recv()
        through = part[i % 3, 0].astype(F32) + core[1, i].astype(F32) + x_buf[i].astype(F32)
        core_a(i).wait_send()
        core_b(i).wait_send()
        chip(i).wait_send()
        for copy in own_rows(i):
            copy.wait()
        value, unit, own = own_f[0], own_b[0].astype(F32), own_b[1].astype(F32)
        g_pre = unit_back(own_f[1] + through, value, hidden_inv[rows(i)])

        @pl.when(i + 1 < count)
        def _():
            for copy in own_rows(i + 1):
                copy.start()

        @pl.when(i >= 2)
        def _():
            base_copy(i - 2).wait()

        base_buf[i % 2] = g_pre * (1.0 - rate_attn)
        base_copy(i).start()
        sums[0:1] = sums[0:1] + jnp.sum(g_pre * (unit - own), axis=0, keepdims=True)
        ga[i] = unit_back(g_pre * rate_attn, unit, attn_inv[rows(i)]).astype(BF)
        copies = ga_copies(i)
        copies[0].start()
        copies[1].start()
        ga_local(i).start()

    def pass_grads(i):
        copies = ga_copies(i)
        copies[1].wait_recv()
        copies[2].start()

    stages = (feed, finish, pass_grads)

    def step(t, carry):
        for lag, stage in enumerate(stages):
            pl.when((t >= lag) & (t < lag + count))(functools.partial(stage, t - lag))
        pl.when(t == 0)(down_grads)

        @pl.when((t >= 1) & (t < 4))
        def _():
            lax.fori_loop(2 * t - 2, 2 * t, hop, 0)

        return carry

    lax.fori_loop(0, count + len(stages) - 1, step, 0)
    hop(6, 0)
    own = dp * 2 * half
    down_rows[pl.ds(0, half)] = ring_buf[0, 7].astype(F32) + dwd[rows_at(own, half)].astype(F32)
    down_rows[pl.ds(half, half)] = ring_buf[1, 7].astype(F32) + dwd[rows_at(own + half, half)].astype(F32)

    def close(i, carry):
        copies = ga_copies(i)
        copies[0].wait()
        copies[1].wait_send()
        copies[2].wait()
        ga_local(i).wait()
        return carry

    lax.fori_loop(0, count, close, 0)
    for i in (count - 2, count - 1):
        base_copy(i).wait()
        store_gug(i).wait()


def middle_back(gd_all, act_all, ug_all, hidden, attn_unit, states, back, attn_inv, hidden_inv, w_ug, w_d, rates,
                scales):
    rows, width = states.shape
    count = rows // CHUNK
    piece = width // 8
    vmem, hbm = pl.BlockSpec(memory_space=pltpu.VMEM), pl.BlockSpec(memory_space=pl.ANY)
    dma = pltpu.SemaphoreType.DMA
    return pl.pallas_call(
        middle_back_kernel,
        in_specs=[hbm] * 7 + [vmem] * 2 + [hbm] * 2 + [vmem] * 2,
        out_specs=[hbm, hbm, hbm, vmem, vmem, vmem],
        out_shape=[
            jax.ShapeDtypeStruct((rows, width), F32),
            jax.ShapeDtypeStruct((4, rows, width), BF),
            jax.ShapeDtypeStruct((count, 4 * CHUNK, 2 * width), BF),
            jax.ShapeDtypeStruct((piece, width), F32),
            jax.ShapeDtypeStruct((1, width), F32),
            jax.ShapeDtypeStruct((2, width), F32),
        ],
        scratch_shapes=[
            pltpu.VMEM(w_ug.shape, BF),
            pltpu.VMEM(w_d.shape, BF),
            pltpu.VMEM((3, 4, CHUNK, width), BF),
            pltpu.VMEM((2, count, CHUNK, width), BF),
            pltpu.VMEM((count, CHUNK, width), BF),
            pltpu.VMEM((count, CHUNK, width), BF),
            pltpu.VMEM((count, 4, CHUNK, width), BF),
            pltpu.VMEM((count, width, 4 * CHUNK), BF),
            pltpu.VMEM((2, 4 * CHUNK, 2 * width), BF),
            pltpu.VMEM((2, 4 * CHUNK, 2 * width), BF),
            pltpu.VMEM((2, CHUNK, width), F32),
            pltpu.VMEM((2, CHUNK, width), BF),
            pltpu.VMEM((2, CHUNK, width), F32),
            pltpu.VMEM((width, width), BF),
            pltpu.VMEM((width, TILE), F32),
            pltpu.VMEM((2, 8, piece // 2, width), BF),
            dma((count,)),
            dma((count,)),
            dma((2,)),
            dma((4,)),
            dma((2, count)),
            dma((2, count)),
            dma((count,)),
            dma((count,)),
            dma((3, count)),
            dma((3, count)),
            dma((count,)),
            dma((2,)),
            dma((2,)),
            dma((2,)),
            dma((2, 7)),
            dma((2, 7)),
        ],
        compiler_params=pltpu.CompilerParams(
            collective_id=4, has_side_effects=True, vmem_limit_bytes=60 << 20
        ),
        cost_estimate=pl.CostEstimate(flops=34 * 10**9, bytes_accessed=200 << 20, transcendentals=4 << 20),
        name="middle_back",
    )(gd_all, act_all, ug_all, hidden, attn_unit, states, back, attn_inv, hidden_inv, w_ug, w_d, rates, scales)


def order_kernel(where_ref, parent_ref, out_ref):
    base, me = where_ref[0], where_ref[1]
    shape = (128, 128)
    row = lax.broadcasted_iota(jnp.int32, shape, 0)
    block = lax.broadcasted_iota(jnp.int32, (8, 128), 1)
    real = block < NB
    parent = jnp.where(real & (parent_ref[...] >= 0), parent_ref[...] - base, -1)
    up = (row == parent[0:1]).astype(F32)
    up2 = nn(up, up)
    near = up + up2
    up4 = nn(up2, up2)
    near = near + nn(near, up2)
    near = near + nn(near, up4)
    above = near + nn(nn(up4, up4), up)
    depth = jnp.broadcast_to(jnp.sum(above, axis=0, keepdims=True), (8, 128)).astype(jnp.int32)
    before = (row < lax.broadcasted_iota(jnp.int32, shape, 1)).astype(F32)
    rank = nn(((depth == TRUNK) & real).astype(F32), before)
    parent_rank = nn(rank, up).astype(jnp.int32)
    sibling = jnp.sum(nn(up.T, up) * before, axis=0, keepdims=True).astype(jnp.int32)
    leaf = TRUNK + 4 + 2 * parent_rank + sibling
    slot = jnp.where(depth < TRUNK, depth, jnp.where(depth == TRUNK, TRUNK + rank.astype(jnp.int32), leaf))
    slot = jnp.where(real, slot, 127)
    mine = jnp.where(real, jnp.bitwise_xor(block // 5, me) * 5 + block % 5, 127)
    order = nt(mine.astype(F32), (row == slot[0:1]).astype(F32))
    back = nt(slot.astype(F32), (row == mine[0:1]).astype(F32))
    which = lax.broadcasted_iota(jnp.int32, (8, 128), 0)
    out_ref[...] = jnp.where(which == 0, order, back).astype(jnp.int32)


def tree_order(where, parents):
    return pl.pallas_call(
        order_kernel,
        in_specs=[pl.BlockSpec(memory_space=pltpu.SMEM), pl.BlockSpec(memory_space=pltpu.VMEM)],
        out_specs=pl.BlockSpec(memory_space=pltpu.VMEM),
        out_shape=jax.ShapeDtypeStruct((8, 128), jnp.int32),
        name="tree_order",
    )(where, jnp.broadcast_to(jnp.pad(parents, (0, 128 - NB), constant_values=-1), (8, 128)))


def local(
    states,
    teacher,
    parent_ids,
    valid_mask,
    w_query,
    w_key,
    w_value,
    w_out,
    w_up,
    w_gate,
    w_down,
    qk_scale,
    attn_rate,
    mlp_rate,
    up_scale,
    gate_scale,
):
    both = ("dp", "fsdp")
    dps, tps = 8, 4
    rows_w = w_query.shape[0]
    cols = D // tps
    hid = FF // tps
    ff_rows = FF // (dps * tps)
    me = lax.axis_index("fsdp")
    root_width = math.sqrt(D)
    mask_f = valid_mask.astype(F32)
    group_base = lax.axis_index("dp") * NB
    order = tree_order(jnp.stack((group_base, me)).astype(jnp.int32), parent_ids)

    count = jnp.sum(valid_mask)
    first_row = jnp.arange(rows_w, dtype=jnp.int32) == 0
    small = jnp.stack(
        (
            qk_scale,
            attn_rate,
            mlp_rate,
            jnp.where(first_row, count // 128, 0).astype(BF),
            jnp.where(first_row, count % 128, 0).astype(BF),
        ),
        axis=1,
    )
    small = jnp.pad(small, ((0, 0), (0, 59)))
    extra = jnp.pad(jnp.stack((up_scale, gate_scale), axis=1), ((0, 0), (69, 57)))
    spread = [(j, tps * (j % dps) + j // dps) for j in range(dps * tps)]
    tokens_t, w_t, w_o, w_ug, qkv, mixed, sums, mixed_n = forward(
        order, states, w_query, w_key, w_value, small, extra, lax.ppermute(w_out, both, spread), w_up, w_gate
    )
    small_all = w_t[3 * cols : 3 * cols + 8].astype(F32)
    rates = small_all[1:3]
    valid_count = 128.0 * jnp.sum(small_all[3]) + jnp.sum(small_all[4])
    scales = small_all[5:7] * jnp.array([[1.0], [root_width]], F32)
    scale_qk = lax.dynamic_slice_in_dim(small_all[0], me * cols, cols).reshape(cols // HEAD_DIM, HEAD_DIM, 1)

    mask_col = mask_f[:, None]
    w_ug, w_d, hidden, back, out_states, attn_unit, attn_inv, hidden_inv, sums_mid, gd_all, ht_all, act_all, ug_all = middle(
        mixed_n, states, teacher, mask_col * (2.0 / valid_count), mask_col, w_ug, w_down, w_o, rates, scales
    )
    base, ga_all, gug_all, grad_down, sums_back, ff_sums = middle_back(
        gd_all, act_all, ug_all, hidden, attn_unit, states, back, attn_inv, hidden_inv, w_ug, w_d, rates, scales
    )
    loss_local = jnp.sum(sums_mid[1])
    g_rate_mlp, g_rate_attn = sums_mid[0], sums_back[0]
    grad_up_scale, grad_gate_scale = ff_sums[0], ff_sums[1] * root_width
    g_qkv, g_scale, part_out, grad_up, grad_gate = attention_back(
        order, qkv, scale_qk, sums, mixed, ga_all.reshape(NB, BLOCK, D), w_o, ht_all, gug_all
    )
    g_qkv = g_qkv.reshape(3 * cols, TOK)
    slot = jnp.arange(tps, dtype=jnp.int32) == me
    qk_rows = jnp.where(slot[:, None], g_scale.reshape(1, cols), 0.0).reshape(dps * tps, rows_w)
    ff_terms = [
        jnp.where(slot[None, :, None], term.reshape(dps, 1, ff_rows), 0.0).reshape(dps * tps, ff_rows)
        for term in (grad_up_scale, grad_gate_scale)
    ]
    vectors = jnp.concatenate(
        [g_rate_attn.reshape(dps * tps, rows_w), g_rate_mlp.reshape(dps * tps, rows_w), qk_rows]
        + ff_terms
        + [jnp.broadcast_to(loss_local, (dps * tps, 512 - 3 * rows_w - 2 * ff_rows))],
        axis=1,
    ).reshape(dps, tps, 4, 128)
    part_out = part_out.reshape(dps, rows_w, D)
    grad_states, g_query, g_key, g_value, out_back, vector_share = last_exchange(
        order, base, tokens_t, g_qkv, w_t, part_out, vectors
    )
    vector_share = vector_share.reshape(512)
    grad_out = lax.ppermute(out_back, both, [(b, a) for a, b in spread])
    cuts = (0, rows_w, 2 * rows_w, 3 * rows_w, 3 * rows_w + ff_rows, 3 * rows_w + 2 * ff_rows)
    v = [vector_share[a:b] for a, b in zip(cuts, cuts[1:])]
    return (
        out_states,
        vector_share[-1] / valid_count,
        grad_states,
        g_query,
        g_key,
        g_value,
        grad_out,
        grad_up,
        grad_gate,
        grad_down,
        v[2],
        v[0],
        v[1],
        v[3],
        v[4],
    )


def solution(mesh):
    placed = (
        P(("dp", "fsdp"), None),
        P(("dp", "fsdp"), None),
        P("dp"),
        P(("dp", "fsdp")),
        P(("dp", "fsdp"), None),
        P(("dp", "fsdp"), None),
        P(("dp", "fsdp"), None),
        P(("dp", "fsdp"), None),
        P(("dp", "fsdp"), None),
        P(("dp", "fsdp"), None),
        P(("dp", "fsdp"), None),
        P(("dp", "fsdp")),
        P(("dp", "fsdp")),
        P(("dp", "fsdp")),
        P(("dp", "fsdp")),
        P(("dp", "fsdp")),
    )
    quick = mesh.shape["fsdp"] == 4 and mesh.shape["dp"] == 8
    return jax.shard_map(
        local if quick else general,
        mesh=mesh,
        in_specs=placed,
        out_specs=(
            P(("dp", "fsdp"), None),
            P(),
            P(("dp", "fsdp"), None),
            P(("dp", "fsdp"), None),
            P(("dp", "fsdp"), None),
            P(("dp", "fsdp"), None),
            P(("dp", "fsdp"), None),
            P(("dp", "fsdp"), None),
            P(("dp", "fsdp"), None),
            P(("dp", "fsdp"), None),
            P(("dp", "fsdp")),
            P(("dp", "fsdp")),
            P(("dp", "fsdp")),
            P(("dp", "fsdp")),
            P(("dp", "fsdp")),
        ),
        check_vma=False,
    )
```

```python
import functools
import math

import jax
import jax.numpy as jnp
from jax import lax
from jax.experimental import pallas as pl
from jax.experimental.pallas import tpu as pltpu
from jax.sharding import PartitionSpec as P


D = 1280
HEADS = 20
HEAD_DIM = 64
FF = 5120
BLOCK = 128
DEPTH = 10


EPS = 1e-06


def unit_rows(vector):
    inverse = lax.rsqrt(jnp.sum(vector * vector, axis=-1, keepdims=True) + EPS)
    return (vector * inverse, inverse)


def unit_back(grad, unit, inverse):
    return (grad - unit * jnp.sum(grad * unit, axis=-1, keepdims=True)) * inverse


def project(left, right):
    return jnp.dot(left, right, preferred_element_type=jnp.float32)


def project_back(grad, weight):
    return jnp.einsum("te,de->td", grad, weight, preferred_element_type=jnp.float32)


def ancestors(local_parent):
    column = jnp.arange(local_parent.shape[0], dtype=jnp.int32)
    columns = [column]
    for depth_step in range(DEPTH - 1):
        column = jnp.where(column >= 0, local_parent[jnp.maximum(column, 0)], -1)
        columns.append(column)
    return jnp.stack(columns, axis=1)


def head_back(grad_flat, unit, inverse, scale):
    scaled = (grad_flat * scale).reshape(unit.shape)
    raw = unit_back(scaled, unit, inverse).reshape(grad_flat.shape)
    scale_grad = jnp.sum(grad_flat * unit.reshape(grad_flat.shape), axis=0)
    return (raw, scale_grad)


def general(
    states,
    teacher,
    parent_ids,
    valid_mask,
    w_query,
    w_key,
    w_value,
    w_out,
    w_up,
    w_gate,
    w_down,
    qk_scale,
    attn_rate,
    mlp_rate,
    up_scale,
    gate_scale,
):
    rows_dev = states.shape[0]
    blocks_dev = rows_dev // BLOCK
    width_rows = w_query.shape[0]
    span = DEPTH * BLOCK
    factor = math.sqrt(HEAD_DIM)
    root_width = math.sqrt(D)
    mask_f = valid_mask.astype(jnp.float32)
    qkv_local = jnp.concatenate((w_query, w_key, w_value), axis=1)
    scal_width_local = jnp.stack((qk_scale, attn_rate, mlp_rate), axis=1)
    piece_qkv = lax.all_gather(qkv_local, ("dp", "fsdp"), axis=0, tiled=True)
    piece_out = lax.all_gather(w_out, ("dp", "fsdp"), axis=0, tiled=True)
    piece_scal = lax.all_gather(scal_width_local, ("dp", "fsdp"), axis=0, tiled=True)
    lefts = states
    total = jnp.dot(lefts, piece_qkv, preferred_element_type=jnp.float32)
    scal_whole = piece_scal
    qkv_raw = total
    scal_width = scal_whole
    scale_qk = scal_width[:, 0].astype(jnp.float32)
    rate_attn = scal_width[:, 1].astype(jnp.float32)
    rate_mlp = scal_width[:, 2].astype(jnp.float32)
    query_raw = qkv_raw[:, :D]
    key_raw = qkv_raw[:, D : 2 * D]
    values = qkv_raw[:, 2 * D :].astype(jnp.bfloat16)
    query_unit, query_inv = unit_rows(query_raw.reshape(rows_dev, HEADS, HEAD_DIM))
    key_unit, key_inv = unit_rows(key_raw.reshape(rows_dev, HEADS, HEAD_DIM))
    query_n = (query_unit.reshape(rows_dev, D) * scale_qk).astype(jnp.bfloat16)
    key_n = (key_unit.reshape(rows_dev, D) * scale_qk).astype(jnp.bfloat16)
    key_group, value_group = (
        lax.all_gather(key_n, "fsdp", axis=0, tiled=True),
        lax.all_gather(values, "fsdp", axis=0, tiled=True),
    )
    group_blocks = parent_ids.shape[0]
    group_base = lax.axis_index("dp") * group_blocks
    local_parent = jnp.where(parent_ids >= 0, parent_ids - group_base, -1)
    paths_all = ancestors(local_parent)
    own_first = lax.axis_index("fsdp") * blocks_dev
    paths = lax.dynamic_slice_in_dim(paths_all, own_first, blocks_dev, 0)
    safe_paths = jnp.maximum(paths, 0)
    key_rows = key_group.reshape(group_blocks, BLOCK, D)[safe_paths].reshape(
        blocks_dev, span, HEADS, HEAD_DIM
    )
    value_rows = value_group.reshape(group_blocks, BLOCK, D)[safe_paths].reshape(
        blocks_dev, span, HEADS, HEAD_DIM
    )
    slot_of = jnp.arange(span, dtype=jnp.int32) // BLOCK
    offset = jnp.arange(span, dtype=jnp.int32) % BLOCK
    row_pos = jnp.arange(BLOCK, dtype=jnp.int32)
    causal = offset[None, :] <= row_pos[:, None]
    is_live = jnp.take(paths, slot_of, axis=1) >= 0
    allowed = jnp.where(slot_of[None, None, :] == 0, causal[None], is_live[:, None, :])[:, None]
    query_heads = query_n.reshape(blocks_dev, BLOCK, HEADS, HEAD_DIM)
    scores = factor * jnp.einsum(
        "bqhd,bkhd->bhqk", query_heads, key_rows, preferred_element_type=jnp.float32
    )
    scores = jnp.where(allowed, scores, jnp.float32(-1e30))
    row_max = jnp.max(scores, axis=-1, keepdims=True)
    powers = jnp.exp(scores - row_max)
    row_sum = jnp.sum(powers, axis=-1, keepdims=True)
    probs_b = (powers / row_sum).astype(jnp.bfloat16)
    log_total = row_max + jnp.log(row_sum)
    mixed = jnp.einsum("bhqk,bkhd->bqhd", probs_b, value_rows, preferred_element_type=jnp.float32)
    mixed = mixed.reshape(rows_dev, D).astype(jnp.bfloat16)
    inputs = states.astype(jnp.float32)
    attn = project(mixed, piece_out)
    attn_unit, attn_inv = unit_rows(attn)
    hidden, hidden_inv = unit_rows(inputs + rate_attn * (attn_unit - inputs))
    hidden_b = hidden.astype(jnp.bfloat16)
    ffn_local = jnp.concatenate((w_up, w_gate), axis=1)
    scal_hidden_local = jnp.concatenate(
        (up_scale.reshape(width_rows, 4), gate_scale.reshape(width_rows, 4)), axis=1
    )
    piece_ffn = lax.all_gather(ffn_local, ("dp", "fsdp"), axis=0, tiled=True)
    piece_scal = lax.all_gather(scal_hidden_local, ("dp", "fsdp"), axis=0, tiled=True)
    lefts = hidden_b
    total = jnp.dot(lefts, piece_ffn, preferred_element_type=jnp.float32)
    scal_whole = piece_scal
    scale_up = scal_whole[:, :4].reshape(FF).astype(jnp.float32)
    scale_gate = scal_whole[:, 4:].reshape(FF).astype(jnp.float32)
    up_proj = total[:, :FF]
    gate_proj = total[:, FF:]
    upscaled = up_proj * scale_up
    gated = gate_proj * scale_gate * root_width
    sigmoid_gate = jax.nn.sigmoid(gated)
    act = (upscaled * (gated * sigmoid_gate)).astype(jnp.bfloat16)
    lefts = act
    down = jnp.dot(
        lefts,
        lax.all_gather(w_down, ("dp", "fsdp"), axis=0, tiled=True),
        preferred_element_type=jnp.float32,
    )
    down_unit, down_inv = unit_rows(down)
    result, result_inv = unit_rows(hidden + rate_mlp * (down_unit - hidden))
    loss_local = jnp.sum(mask_f[:, None] * (result - teacher) ** 2)
    valid_count, loss_sum = lax.psum((jnp.sum(mask_f), loss_local), ("dp", "fsdp"))
    loss = loss_sum / valid_count
    g_result = 2.0 * mask_f[:, None] * (result - teacher) / valid_count
    g_last = unit_back(g_result, result, result_inv)
    g_hidden = g_last * (1.0 - rate_mlp)
    g_rate_mlp = jnp.sum(g_last * (down_unit - hidden), axis=0)
    g_down = unit_back(g_last * rate_mlp, down_unit, down_inv).astype(jnp.bfloat16)
    g_act = jnp.einsum(
        "te,fe->tf",
        g_down,
        lax.all_gather(w_down, ("dp", "fsdp"), axis=0, tiled=True),
        preferred_element_type=jnp.float32,
    )
    g_upscaled = g_act * (gated * sigmoid_gate)
    g_gated = g_act * upscaled * sigmoid_gate * (1.0 + gated * (1.0 - sigmoid_gate))
    grad_up_scale = jnp.sum(g_upscaled * up_proj, axis=0)
    grad_gate_scale = jnp.sum(g_gated * gate_proj * root_width, axis=0)
    g_up = (g_upscaled * scale_up).astype(jnp.bfloat16)
    g_gate = (g_gated * scale_gate * root_width).astype(jnp.bfloat16)
    g_both = jnp.concatenate((g_up, g_gate), axis=1)
    g_hidden = g_hidden + jnp.einsum(
        "tc,dc->td",
        g_both,
        lax.all_gather(ffn_local, ("dp", "fsdp"), axis=0, tiled=True),
        preferred_element_type=jnp.float32,
    )
    scal_terms = jnp.concatenate(
        (grad_up_scale.reshape(D, 4), grad_gate_scale.reshape(D, 4)), axis=1
    )
    lefts = hidden_b
    main = jnp.einsum("td,tc->dc", lefts, g_both, preferred_element_type=jnp.float32)
    ffn_share = lax.psum_scatter(
        jnp.concatenate((main, scal_terms), axis=1), ("dp", "fsdp"), scatter_dimension=0, tiled=True
    )
    lefts = act
    grad_down = lax.psum_scatter(
        jnp.einsum("tf,te->fe", lefts, g_down, preferred_element_type=jnp.float32),
        ("dp", "fsdp"),
        scatter_dimension=0,
        tiled=True,
    )
    g_pre = unit_back(g_hidden, hidden, hidden_inv)
    g_states = g_pre * (1.0 - rate_attn)
    g_rate_attn = jnp.sum(g_pre * (attn_unit - inputs), axis=0)
    g_attn = unit_back(g_pre * rate_attn, attn_unit, attn_inv).astype(jnp.bfloat16)
    g_mixed = project_back(g_attn, piece_out).astype(jnp.bfloat16)
    scores = factor * jnp.einsum(
        "bqhd,bkhd->bhqk", query_heads, key_rows, preferred_element_type=jnp.float32
    )
    probs = jnp.where(allowed, jnp.exp(scores - log_total), jnp.float32(0.0))
    probs_again = probs.astype(jnp.bfloat16)
    g_heads = g_mixed.reshape(blocks_dev, BLOCK, HEADS, HEAD_DIM)
    g_probs = jnp.einsum("bqhd,bkhd->bhqk", g_heads, value_rows, preferred_element_type=jnp.float32)
    delta = jnp.sum(probs * g_probs, axis=-1, keepdims=True)
    g_scores = (probs * (g_probs - delta)).astype(jnp.bfloat16)
    g_query_n = factor * jnp.einsum(
        "bhqk,bkhd->bqhd", g_scores, key_rows, preferred_element_type=jnp.float32
    )
    g_key_rows = factor * jnp.einsum(
        "bhqk,bqhd->bkhd", g_scores, query_heads, preferred_element_type=jnp.float32
    )
    g_value_rows = jnp.einsum(
        "bhqk,bqhd->bkhd", probs_again, g_heads, preferred_element_type=jnp.float32
    )
    flat_paths = safe_paths.reshape(blocks_dev * DEPTH)
    g_key_group = (
        jnp.zeros((group_blocks, BLOCK, D), jnp.float32)
        .at[flat_paths]
        .add(g_key_rows.reshape(blocks_dev * DEPTH, BLOCK, D))
    )
    g_value_group = (
        jnp.zeros((group_blocks, BLOCK, D), jnp.float32)
        .at[flat_paths]
        .add(g_value_rows.reshape(blocks_dev * DEPTH, BLOCK, D))
    )
    g_key_n, g_values = (
        lax.psum_scatter(
            g_key_group.reshape(group_blocks * BLOCK, D).astype(jnp.bfloat16),
            "fsdp",
            scatter_dimension=0,
            tiled=True,
        ).astype(jnp.float32),
        lax.psum_scatter(
            g_value_group.reshape(group_blocks * BLOCK, D).astype(jnp.bfloat16),
            "fsdp",
            scatter_dimension=0,
            tiled=True,
        ).astype(jnp.float32),
    )
    g_query_raw, scale_from_query = head_back(
        g_query_n.reshape(rows_dev, D), query_unit, query_inv, scale_qk
    )
    g_key_raw, scale_from_key = head_back(g_key_n, key_unit, key_inv, scale_qk)
    grad_qk_scale = scale_from_query + scale_from_key
    g_qkv = jnp.concatenate(
        (
            g_query_raw.astype(jnp.bfloat16),
            g_key_raw.astype(jnp.bfloat16),
            g_values.astype(jnp.bfloat16),
        ),
        axis=1,
    )
    g_states = g_states + jnp.einsum(
        "tc,dc->td",
        g_qkv,
        lax.all_gather(qkv_local, ("dp", "fsdp"), axis=0, tiled=True),
        preferred_element_type=jnp.float32,
    )
    vector_terms = jnp.stack((grad_qk_scale, g_rate_attn, g_rate_mlp), axis=1)
    lefts = states
    main = jnp.einsum("td,tc->dc", lefts, g_qkv, preferred_element_type=jnp.float32)
    outer = jnp.einsum("td,tc->dc", mixed, g_attn, preferred_element_type=jnp.float32)
    attn_share = lax.psum_scatter(
        jnp.concatenate((main, outer, vector_terms), axis=1),
        ("dp", "fsdp"),
        scatter_dimension=0,
        tiled=True,
    )
    return (
        result.astype(jnp.bfloat16),
        loss,
        g_states,
        attn_share[:, :D],
        attn_share[:, D : 2 * D],
        attn_share[:, 2 * D : 3 * D],
        attn_share[:, 3 * D : 4 * D],
        ffn_share[:, :FF],
        ffn_share[:, FF : 2 * FF],
        grad_down,
        attn_share[:, 4 * D],
        attn_share[:, 4 * D + 1],
        attn_share[:, 4 * D + 2],
        ffn_share[:, 2 * FF : 2 * FF + 4].reshape(-1),
        ffn_share[:, 2 * FF + 4 : 2 * FF + 8].reshape(-1),
    )

TRUNK = 8
NB = 20
TOK = NB * BLOCK
F32 = jnp.float32
BF = jnp.bfloat16


def head_norm(raw):
    inv = lax.rsqrt(jnp.sum(raw * raw, axis=0, keepdims=True) + EPS)
    return raw * inv, inv


def lanes_at(start, size):
    return pl.ds(pl.multiple_of(start, 128), size)


def rows_at(start, size):
    return pl.ds(pl.multiple_of(start, 16), size)


def early_chunks(visit):
    for j in range(TRUNK // 2):
        parts = [(0, 256 * j, "all")] if j else []
        visit(256 * j, parts + [(256 * j, 256, "causal")])
    trunk = TRUNK * BLOCK
    for start in (trunk, trunk + 256):
        visit(start, [(0, trunk, "all"), (start, 256, "pair")])


def late_chunks(visit):
    trunk = TRUNK * BLOCK
    for j in range(4):
        start = trunk + 4 * BLOCK + 256 * j
        visit(start, [(0, trunk, "all"), (trunk + BLOCK * j, BLOCK, "all"), (start, 256, "pair")])


def masked(kind, value):
    if kind == "all":
        return value
    key = lax.broadcasted_iota(jnp.int32, (256, 256), 0)
    query = lax.broadcasted_iota(jnp.int32, (256, 256), 1)
    keep = key <= query
    if kind == "pair":
        keep = keep & ((key < 128) == (query < 128))
    return jnp.where(keep, value, jnp.zeros_like(value))


def nn(a, b):
    return lax.dot_general(a, b, (((1,), (0,)), ((), ())), preferred_element_type=F32)


def nt(a, b):
    return lax.dot_general(a, b, (((1,), (1,)), ((), ())), preferred_element_type=F32)


def attention_back_kernel(order, qkv, scales, sums, mixed, ga_all, w_o, ht_all, gug_all,
                          g_qkv, g_scale, part_out, g_up, g_gate,
                          w_b, ga_b, ga, gm, raw, out_b, qT, q, k, kT, v, gT, g, dq, dk, dv, delta, inv,
                          gug_b, ht_r, ht_l, ring, own, hid_buf, hid_in,
                          ga_sem, gug_sem, row_sem, raw_sem, out_sem, ring_send, ring_recv, a2a_send, a2a_recv):
    me = lax.axis_index("fsdp")
    place = ring_place()
    peers = group_peers()
    right, left = {"dp": ring_dp(place + 1)}, {"dp": ring_dp(place - 1)}
    count, chunk, side = gug_b.shape[0], ring.shape[3], ring.shape[4]
    heads = g_scale.shape[0]
    rows_w = hid_buf.shape[1]

    def slices(step):
        slot = step % 2
        cut_r = rows_at(ring_dp(place - 1 - step) * chunk, chunk)
        cut_l = rows_at(ring_dp(place + 1 + step) * chunk, chunk)
        return [
            pltpu.make_async_copy(ht_all.at[:, cut_r], ht_r.at[slot], row_sem.at[0, slot]),
            pltpu.make_async_copy(ht_all.at[:, cut_l], ht_l.at[slot], row_sem.at[1, slot]),
        ]

    def raw_copy(head):
        slot = head % 2
        return pltpu.make_async_copy(
            qkv.at[:, rows_at(head * HEAD_DIM, HEAD_DIM)], raw.at[slot], raw_sem.at[slot]
        )

    def out_copy(head):
        slot = head % 2
        return pltpu.make_async_copy(
            out_b.at[slot], g_qkv.at[:, rows_at(head * HEAD_DIM, HEAD_DIM)], out_sem.at[slot]
        )

    load_ga = pltpu.make_async_copy(ga_all, ga_b, ga_sem.at[0])
    load_ga.start()
    load_w = pltpu.make_async_copy(w_o.at[0], w_b, ga_sem.at[1])
    load_w.start()
    raw_copy(0).start()
    for copy in slices(0):
        copy.start()
    loads = [pltpu.make_async_copy(gug_all.at[i], gug_b.at[i], gug_sem.at[i]) for i in range(count)]
    for copy in loads:
        copy.start()
    for copy in slices(1):
        copy.start()
    greet([*peers, right, left])
    load_ga.wait()
    load_w.wait()

    def pick(i, carry):
        ga[lanes_at(i * BLOCK, BLOCK)] = ga_b[order[0, i]]
        return carry

    lax.fori_loop(0, NB, pick, 0)

    def back(n, carry):
        gm[:, tile(n)] = nt(w_b[...], ga[tile(n)]).astype(BF)
        return carry

    lax.fori_loop(0, TOK // TILE, back, 0)

    def outer(n, carry):
        part_out[:, tile(n)] = nn(mixed[...], ga[:, tile(n)]).astype(BF)
        return carry

    lax.fori_loop(0, D // TILE, outer, 0)

    def parts(step, which):
        slot = step % 2

        @pl.when(which == 0)
        def _():
            for copy in slices(step):
                copy.wait()

        own[...] = jnp.zeros_like(own)

        def add(i, carry):
            for d, rows in enumerate((ht_r, ht_l)):
                cut = lanes_at((2 * d + which) * side, side)
                own[d] = own[d] + nn(rows[slot, i], gug_b[i, :, cut])
            return carry

        lax.fori_loop(0, count, add, 0)

        @pl.when((which == 1) & (step + 2 < 8))
        def _():
            for copy in slices(step + 2):
                copy.start()

    def hop_copies(step, which):
        return [
            send(ring.at[d, which, step], ring.at[d, which, step + 1], ring_send.at[d, which, step],
                 ring_recv.at[d, which, step], peer)
            for d, peer in enumerate((right, left))
        ]

    def exchange():
        return [
            send(hid_buf.at[peer["fsdp"]], hid_in.at[me], a2a_send.at[i], a2a_recv.at[i], peer)
            for i, peer in enumerate(peers)
        ]

    def poll(index):
        step, which = index // 2, index % 2
        parts(step + 1, which)
        for copy in hop_copies(step, which):
            copy.wait()

        @pl.when(step < 6)
        def _():
            for d in range(2):
                ring[d, which, step + 1] = (ring[d, which, step + 1].astype(F32) + own[d]).astype(BF)
            for copy in hop_copies(step + 1, which):
                copy.start()

        @pl.when(step == 6)
        def _():
            for d in range(2):
                total = ring[d, which, 7].astype(F32) + own[d]
                for i in range(4):
                    hid_buf[i, :, lanes_at((2 * d + which) * side, side)] = total[
                        i * rows_w : (i + 1) * rows_w
                    ].astype(BF)

        @pl.when(index == 13)
        def _():
            for copy in exchange():
                copy.start()

    for copy in loads:
        copy.wait()

    def begin(which, carry):
        parts(0, which)
        for d in range(2):
            ring[d, which, 0] = own[d].astype(BF)
        for copy in hop_copies(0, which):
            copy.start()
        return carry

    lax.fori_loop(0, 2, begin, 0)

    def open_head(head):
        slot = head % 2
        raw_copy(head).wait()

        @pl.when(head + 1 < heads)
        def _():
            raw_copy(head + 1).start()

        @pl.when(head >= 2)
        def _():
            out_copy(head - 2).wait()

        scale = scales[head]
        mine = rows_at(head * HEAD_DIM, HEAD_DIM)

        for i in range(NB):
            here = slice(i * BLOCK, (i + 1) * BLOCK)
            q_unit, _ = head_norm(raw[slot, 0, :, here])
            k_unit, _ = head_norm(raw[slot, 1, :, here])
            q8 = (q_unit * scale).astype(BF) * BF(8.0)
            qT[:, here] = q8
            q[here, :] = q8.T
            kn = (k_unit * scale).astype(BF)
            kT[:, here] = kn
            k[here, :] = kn.T
            v[here, :] = raw[slot, 2, :, here].astype(BF).T
            gh = gm[mine, here]
            gT[:, here] = gh
            g[here, :] = gh.T
            delta[:, here] = jnp.sum(gh.astype(F32) * mixed[mine, here].astype(F32), axis=0, keepdims=True)
            inv[:, here] = sums[head, 0:1, here]
        dk[...] = jnp.zeros_like(dk)
        dv[...] = jnp.zeros_like(dv)

    def visit(start, pieces):
        span = lanes_at(start, 256)
        query, grad = qT[:, span], gT[:, span]
        query_rows, grad_rows = q[span, :], g[span, :]
        scale_row, delta_row = inv[:, span], delta[:, span]
        acc = jnp.zeros((64, 256), F32)
        for kstart, size, kind in pieces:
            keys = lanes_at(kstart, size)
            probs = masked(kind, jnp.exp(nn(k[keys, :], query)) * scale_row)
            g_probs = nn(v[keys, :], grad)
            g_scores = (probs * (g_probs - delta_row)).astype(BF)
            dv[keys, :] += nn(probs.astype(BF), grad_rows)
            dk[keys, :] += nn(g_scores, query_rows)
            acc = acc + nn(kT[:, keys], g_scores)
        dq[:, span] = acc * 8.0


    def close_head(head):
        slot = head % 2
        scale = scales[head]
        total = jnp.zeros((64, BLOCK), F32)
        for i in range(NB):
            here = slice(i * BLOCK, (i + 1) * BLOCK)
            for which, grad in ((0, dq[:, here]), (1, dk[here, :].T)):
                unit, inverse = head_norm(raw[slot, which, :, here])
                total = total + grad * unit
                scaled = grad * scale
                value = (scaled - unit * jnp.sum(scaled * unit, axis=0, keepdims=True)) * inverse
                out_b[slot, which, :, here] = value.astype(BF)
            out_b[slot, 2, :, here] = dv[here, :].T.astype(BF)
        g_scale[head] = jnp.sum(total, axis=1, keepdims=True)
        out_copy(head).start()

    def work(i, carry):
        head, segment = i // 4, i % 4
        pl.when(segment == 0)(functools.partial(open_head, head))
        pl.when(segment == 1)(functools.partial(early_chunks, visit))
        pl.when(segment == 2)(functools.partial(late_chunks, visit))
        pl.when(segment == 3)(functools.partial(close_head, head))
        pl.when(i < 14)(functools.partial(poll, i))
        return carry

    lax.fori_loop(0, 4 * heads, work, 0)
    for copy in exchange():
        copy.wait()
    hid_in[me] = hid_buf[me]
    size = g_up.shape[1] // 32
    for which, out in enumerate((g_up, g_gate)):
        for d in range(8):
            start = (8 * which + d) * size
            block = [hid_in[i, :, start : start + size].astype(F32) for i in range(4)]
            out[:, d * 4 * size : (d + 1) * 4 * size] = jnp.concatenate(block, axis=1)
    for head in (heads - 2, heads - 1):
        out_copy(head).wait()


def attention_back(order, qkv, scales, sums, mixed, ga_all, w_o, ht_all, gug_all):
    heads = scales.shape[0]
    count, tokens, hidden_width = gug_all.shape
    chunk = ht_all.shape[1] // 8
    side = hidden_width // 4
    rows_w = chunk // 4
    vmem, hbm = pl.BlockSpec(memory_space=pltpu.VMEM), pl.BlockSpec(memory_space=pl.ANY)
    smem = pl.BlockSpec(memory_space=pltpu.SMEM)
    dma = pltpu.SemaphoreType.DMA
    return pl.pallas_call(
        attention_back_kernel,
        in_specs=[smem, hbm, vmem, vmem, vmem, hbm, hbm, hbm, hbm],
        out_specs=[hbm, vmem, vmem, vmem, vmem],
        out_shape=[
            jax.ShapeDtypeStruct(qkv.shape, BF),
            jax.ShapeDtypeStruct(scales.shape, F32),
            jax.ShapeDtypeStruct(w_o.shape[1:], BF),
            jax.ShapeDtypeStruct((rows_w, 2 * hidden_width), F32),
            jax.ShapeDtypeStruct((rows_w, 2 * hidden_width), F32),
        ],
        scratch_shapes=[
            pltpu.VMEM(w_o.shape[1:], BF),
            pltpu.VMEM(ga_all.shape, BF),
            pltpu.VMEM((TOK, w_o.shape[2]), BF),
            pltpu.VMEM(mixed.shape, BF),
            pltpu.VMEM((2, 3, HEAD_DIM, TOK), F32),
            pltpu.VMEM((2, 3, HEAD_DIM, TOK), BF),
            pltpu.VMEM((HEAD_DIM, TOK), BF),
            pltpu.VMEM((TOK, HEAD_DIM), BF),
            pltpu.VMEM((TOK, HEAD_DIM), BF),
            pltpu.VMEM((HEAD_DIM, TOK), BF),
            pltpu.VMEM((TOK, HEAD_DIM), BF),
            pltpu.VMEM((HEAD_DIM, TOK), BF),
            pltpu.VMEM((TOK, HEAD_DIM), BF),
            pltpu.VMEM((HEAD_DIM, TOK), F32),
            pltpu.VMEM((TOK, HEAD_DIM), F32),
            pltpu.VMEM((TOK, HEAD_DIM), F32),
            pltpu.VMEM((1, TOK), F32),
            pltpu.VMEM((1, TOK), F32),
            pltpu.VMEM(gug_all.shape, BF),
            pltpu.VMEM((2, count, chunk, tokens), BF),
            pltpu.VMEM((2, count, chunk, tokens), BF),
            pltpu.VMEM((2, 2, 8, chunk, side), BF),
            pltpu.VMEM((2, chunk, side), F32),
            pltpu.VMEM((4, rows_w, hidden_width), BF),
            pltpu.VMEM((4, rows_w, hidden_width), BF),
            dma((2,)),
            dma((count,)),
            dma((2, 2)),
            dma((2,)),
            dma((2,)),
            dma((2, 2, 7)),
            dma((2, 2, 7)),
            dma((3,)),
            dma((3,)),
        ],
        compiler_params=pltpu.CompilerParams(
            collective_id=5, has_side_effects=True, vmem_limit_bytes=62 << 20
        ),
        name="attention_back",
        cost_estimate=pl.CostEstimate(flops=40 * 10**9, bytes_accessed=60 << 20, transcendentals=14 << 20),
    )(order, qkv, scales, sums, mixed, ga_all, w_o, ht_all, gug_all)


MESH = pl.DeviceIdType.MESH


def ring_place():
    dp = lax.axis_index("dp")
    z, y = dp // 2, dp % 2
    return z + y * (7 - 2 * z)


def ring_dp(place):
    place = (place + 16) % 8
    y = place // 4
    return 2 * (place + y * (7 - 2 * place)) + y


def greet(peers):
    barrier = pltpu.get_barrier_semaphore()
    for peer in peers:
        pl.semaphore_signal(barrier, inc=1, device_id=peer, device_id_type=MESH)
    pl.semaphore_wait(barrier, len(peers))


def group_peers():
    me = lax.axis_index("fsdp")
    core = 1 - 2 * (me % 2)
    chip = 2 - 4 * (me // 2)
    return {"fsdp": me + core}, {"fsdp": me + chip}, {"fsdp": me + core + chip}


def send(src, dst, send_sem, recv_sem, peer):
    return pltpu.make_async_remote_copy(
        src_ref=src, dst_ref=dst, send_sem=send_sem, recv_sem=recv_sem, device_id=peer, device_id_type=MESH
    )


EARLY_HOPS = 5


def hidden_ring(ref, sends, recvs, step, base=0):
    place = ring_place()
    right, left = {"dp": ring_dp(place + 1)}, {"dp": ring_dp(place - 1)}
    chunk = ref.shape[0] // 8
    to_right, to_left = ring_dp(place - step) * chunk, ring_dp(place + step) * chunk
    first, size = 48, chunk // 2
    cuts = ((to_right, first, right), (to_left + size, first, left),
            (to_right + first, size - first, right), (to_left + size + first, size - first, left))
    return [
        send(ref.at[rows_at(start, rows)], ref.at[rows_at(start, rows)], sends.at[i, step - base],
             recvs.at[i, step - base], peer)
        for i, (start, rows, peer) in enumerate(cuts)
    ]


def forward_kernel(order, states, w_query, w_key, w_value, small, extra, out_piece, w_up, w_gate,
                   tokens_t, w_t, w_o, w_ug, qkv, mixed, sums, mixed_n,
                   qkv_send, ug_send, land, weights, tok, turned, tok_t, out_w, ug_land, ug_own, raw, qs, ks, vs, blocks, natural,
                   tok_send, tok_recv, a2a_send, a2a_recv, ring_send, ring_recv, ug_s, ug_r, local_sem, raw_sem,
                   w_send, w_recv):
    me, dp = lax.axis_index("fsdp"), lax.axis_index("dp")
    place = ring_place()
    sibling, across, corner = group_peers()
    right, left = {"dp": ring_dp(place + 1)}, {"dp": ring_dp(place - 1)}
    rows, width = states.shape
    piece = land.shape[1]
    chunk = 4 * piece
    half = chunk // 2
    cols = mixed.shape[0]
    heads = cols // HEAD_DIM
    own = pltpu.make_async_copy(states, tok.at[pl.ds(0, rows)], local_sem.at[0])
    own.start()
    for i in range(4):
        cut = slice(i * cols, (i + 1) * cols)
        block = [w[:, cut].astype(F32) for w in (w_query, w_key, w_value)] + [small[...].astype(F32)]
        qkv_send[i] = jnp.concatenate(block, axis=1).astype(BF)
    greet([sibling, across, corner, right, left])

    exchange, ug_exchange = [], []
    for i, peer in enumerate((sibling, across, corner)):
        copy = send(qkv_send.at[peer["fsdp"]], land.at[me], a2a_send.at[i], a2a_recv.at[i], peer)
        copy.start()
        exchange.append(copy)
    far = []
    for i in range(2):
        part = pl.ds(i * (rows // 2), rows // 2)
        here = pl.ds(2 * rows + i * (rows // 2), rows // 2)
        copy = send(states.at[part], tok.at[here], tok_send.at[i], tok_recv.at[i], across)
        copy.start()
        far.append(copy)
    near = send(states, tok.at[pl.ds(rows, rows)], tok_send.at[2], tok_recv.at[2], sibling)
    near.start()
    size = w_up.shape[1] // 32
    for i in range(4):
        for which, w in enumerate((w_up, w_gate)):
            for half_d in range(2):
                block = [
                    w[:, (4 * d + i) * size : (4 * d + i + 1) * size].astype(F32)
                    for d in range(4 * half_d, 4 * half_d + 4)
                ]
                start = (8 * which + 4 * half_d) * size
                ug_send[i, :, start : start + 4 * size] = jnp.concatenate(block, axis=1).astype(BF)
    land[me] = qkv_send[me]
    ug_land[me] = ug_send[me]
    out_w[dp] = out_piece[...]
    vs[HEAD_DIM:, :] = jnp.ones((vs.shape[0] - HEAD_DIM, TOK), BF)
    for copy in exchange:
        copy.wait()
    weights[rows_at(dp * chunk, chunk)] = jnp.concatenate([land[i].astype(F32) for i in range(4)], axis=0).astype(BF)
    last = pl.ds(weights.shape[1] - 128, 128)
    weights[rows_at(dp * chunk, chunk), last] = weights[rows_at(dp * chunk, chunk), last] + extra[...]

    def ring_copies(step):
        to_right, to_left = ring_dp(place - step), ring_dp(place + step)
        first, second = rows_at(to_right * chunk, half), rows_at(to_left * chunk + half, half)
        lanes_r, lanes_l = pl.ds(0, width // 2), pl.ds(width // 2, width // 2)
        return [
            send(ref, ref, ring_send.at[i, step], ring_recv.at[i, step], peer)
            for i, (ref, peer) in enumerate(
                (
                    (weights.at[first], right),
                    (weights.at[second], left),
                    (out_w.at[to_right, :, lanes_r], right),
                    (out_w.at[to_left, :, lanes_l], left),
                )
            )
        ]

    def hop(step, carry):
        for copy, later in zip(ring_copies(step), ring_copies(step + 1)):
            copy.wait()
            pl.when(step < 6)(later.start)
        return carry

    def ug_poll(index):
        step = index // 2
        now, late = hidden_ring(w_ug, ug_s, ug_r, step), hidden_ring(w_ug, ug_s, ug_r, step + 1)

        def pass_on(first):
            for copy, later in zip(now[first : first + 2], late[first : first + 2]):
                copy.wait()
                pl.when(step < EARLY_HOPS - 1)(later.start)

        pl.when(index % 2 == 0)(functools.partial(pass_on, 0))
        pl.when(index % 2 == 1)(functools.partial(pass_on, 2))

    for copy in ring_copies(0):
        copy.start()

    def turn(i, carry):
        turned[i] = tok[lanes_at(i * BLOCK, BLOCK)].T
        return carry

    lax.fori_loop(0, 1, hop, 0)
    near.wait()
    own.wait()
    lax.fori_loop(0, 4, turn, 0)
    lax.fori_loop(1, 2, hop, 0)
    lax.fori_loop(4, 7, turn, 0)
    lax.fori_loop(2, 3, hop, 0)
    lax.fori_loop(7, 10, turn, 0)
    lax.fori_loop(3, 5, hop, 0)
    passed = []
    for i in range(2):
        far[i].wait()
        here = pl.ds(2 * rows + i * (rows // 2), rows // 2)
        there = pl.ds(3 * rows + i * (rows // 2), rows // 2)
        copy = send(tok.at[here], tok.at[there], tok_send.at[3 + i], tok_recv.at[3 + i], sibling)
        copy.start()
        passed.append(copy)
    for i, peer in enumerate((sibling, across, corner)):
        copy = send(ug_send.at[peer["fsdp"]], ug_land.at[me], a2a_send.at[3 + i], a2a_recv.at[3 + i], peer)
        copy.start()
        ug_exchange.append(copy)
    lax.fori_loop(5, 6, hop, 0)
    lax.fori_loop(10, 15, turn, 0)
    lax.fori_loop(6, 7, hop, 0)
    for copy in passed:
        copy.wait()

    lax.fori_loop(15, NB, turn, 0)

    def arrange(i, carry):
        tok_t[:, lanes_at(i * BLOCK, BLOCK)] = turned[order[0, i]]
        return carry

    lax.fori_loop(0, NB, arrange, 0)
    keep = pltpu.make_async_copy(tok_t, tokens_t, local_sem.at[2])
    keep.start()

    def turn_weights(i, carry):
        w_t[:, lanes_at(i * BLOCK, BLOCK)] = weights[rows_at(i * BLOCK, BLOCK)].T
        return carry

    lax.fori_loop(0, width // BLOCK, turn_weights, 0)
    for copy in ug_exchange:
        copy.wait()
    ug_own[...] = jnp.concatenate([ug_land[i].astype(F32) for i in range(4)], axis=0).astype(BF)
    ug_store = pltpu.make_async_copy(ug_own, w_ug.at[rows_at(dp * chunk, chunk)], local_sem.at[1])
    ug_store.start()
    ug_store.wait()
    for copy in hidden_ring(w_ug, ug_s, ug_r, 0):
        copy.start()
    w_o[0] = jnp.concatenate([out_w[i].astype(F32) for i in range(8)], axis=0).astype(BF)
    w_copies = [
        send(w_o.at[0], w_o.at[i + 1], w_send.at[i], w_recv.at[i], peer)
        for i, peer in enumerate((sibling, across, corner))
    ]
    for copy in w_copies:
        copy.start()

    def raw_copies(head):
        slot = head % 2
        return [
            pltpu.make_async_copy(
                raw.at[slot, pl.ds(which * HEAD_DIM, HEAD_DIM)],
                qkv.at[which, rows_at(head * HEAD_DIM, HEAD_DIM)],
                raw_sem.at[slot, which],
            )
            for which in range(3)
        ]

    def open_head(head):
        slot = head % 2

        @pl.when(head >= 2)
        def _():
            for copy in raw_copies(head - 2):
                copy.wait()

        left_rows = jnp.concatenate(
            [w_t[rows_at(which * cols + head * HEAD_DIM, HEAD_DIM)] for which in range(3)], axis=0
        )

        def project_tile(n, carry):
            raw[slot, :, tile(n)] = nn(left_rows, tok_t[:, tile(n)])
            return carry

        lax.fori_loop(0, TOK // TILE, project_tile, 0, unroll=2)
        for copy in raw_copies(head):
            copy.start()
        scale = weights[rows_at(me * cols + head * HEAD_DIM, HEAD_DIM), last][:, HEAD_DIM : HEAD_DIM + 1].astype(F32)

        def prepare(i, carry):
            here = lanes_at(i * BLOCK, BLOCK)
            q_unit, _ = head_norm(raw[slot, pl.ds(0, HEAD_DIM), here])
            k_unit, _ = head_norm(raw[slot, pl.ds(HEAD_DIM, HEAD_DIM), here])
            qs[:, here] = (q_unit * scale).astype(BF) * BF(8.0)
            ks[here, :] = (k_unit * scale).astype(BF).T
            vs[0:HEAD_DIM, here] = raw[slot, pl.ds(2 * HEAD_DIM, HEAD_DIM), here].astype(BF)
            return carry

        lax.fori_loop(0, NB, prepare, 0, unroll=NB)

    def visit(head, start, parts):
        span = lanes_at(start, 256)
        query = qs[:, span]
        acc = jnp.zeros((vs.shape[0], 256), F32)
        for kstart, count, kind in parts:
            keys = lanes_at(kstart, count)
            powers = masked(kind, jnp.exp(nn(ks[keys, :], query))).astype(BF)
            acc = acc + nn(vs[:, keys], powers)
        total = 1.0 / acc[HEAD_DIM : HEAD_DIM + 1, :]
        mixed[rows_at(head * HEAD_DIM, HEAD_DIM), span] = (acc[0:HEAD_DIM, :] * total).astype(BF)
        sums[head, :, span] = jnp.broadcast_to(total, (8, 256))

    def work(i, carry):
        head, segment = i // 3, i % 3
        pl.when(segment == 0)(functools.partial(open_head, head))
        pl.when(segment == 1)(lambda: early_chunks(functools.partial(visit, head)))
        pl.when(segment == 2)(lambda: late_chunks(functools.partial(visit, head)))
        pl.when(i % 2 == 1)(lambda: ug_poll(i // 2))
        return carry

    lax.fori_loop(0, 3 * heads, work, 0)

    def split(i, carry):
        blocks[i] = mixed[:, lanes_at(i * BLOCK, BLOCK)]
        return carry

    def arrange_back(i, carry):
        natural[i] = blocks[order[1, i]]
        return carry

    lax.fori_loop(0, NB, split, 0)
    lax.fori_loop(0, NB, arrange_back, 0)
    keep_mixed = pltpu.make_async_copy(natural, mixed_n, local_sem.at[3])
    keep_mixed.start()
    lax.fori_loop(3 * heads // 2, 2 * EARLY_HOPS, lambda index, c: (ug_poll(index), c)[1], 0)
    keep.wait()
    keep_mixed.wait()
    for copy in w_copies:
        copy.wait()
    for head in (heads - 2, heads - 1):
        for copy in raw_copies(head):
            copy.wait()


def forward(order, states, w_query, w_key, w_value, small, extra, out_piece, w_up, w_gate):
    tps, rows_w = 4, w_query.shape[0]
    tokens, width = states.shape
    packed = 3 * width // tps + small.shape[1]
    hidden_width = 2 * w_up.shape[1] // tps
    cols = 8 * rows_w
    vmem, hbm = pl.BlockSpec(memory_space=pltpu.VMEM), pl.BlockSpec(memory_space=pl.ANY)
    smem = pl.BlockSpec(memory_space=pltpu.SMEM)
    dma = pltpu.SemaphoreType.DMA
    return pl.pallas_call(
        forward_kernel,
        in_specs=[smem, hbm] + [vmem] * 8,
        out_specs=[hbm, vmem, vmem, hbm, hbm, vmem, vmem, hbm],
        out_shape=[
            jax.ShapeDtypeStruct((width, TOK), BF),
            jax.ShapeDtypeStruct((packed, width), BF),
            jax.ShapeDtypeStruct((tps, cols, width), BF),
            jax.ShapeDtypeStruct((width, hidden_width), BF),
            jax.ShapeDtypeStruct((3, cols, TOK), F32),
            jax.ShapeDtypeStruct((cols, TOK), BF),
            jax.ShapeDtypeStruct((cols // HEAD_DIM, 8, TOK), F32),
            jax.ShapeDtypeStruct((NB, cols, BLOCK), BF),
        ],
        scratch_shapes=[
            pltpu.VMEM((tps, rows_w, packed), BF),
            pltpu.VMEM((tps, rows_w, hidden_width), BF),
            pltpu.VMEM((tps, rows_w, packed), BF),
            pltpu.VMEM((width, packed), BF),
            pltpu.VMEM((TOK, width), BF),
            pltpu.VMEM((NB, width, BLOCK), BF),
            pltpu.VMEM((width, TOK), BF),
            pltpu.VMEM((8, rows_w, width), BF),
            pltpu.VMEM((tps, rows_w, hidden_width), BF),
            pltpu.VMEM((tps * rows_w, hidden_width), BF),
            pltpu.VMEM((2, 3 * HEAD_DIM, TOK), F32),
            pltpu.VMEM((HEAD_DIM, TOK), BF),
            pltpu.VMEM((TOK, HEAD_DIM), BF),
            pltpu.VMEM((HEAD_DIM + 16, TOK), BF),
            pltpu.VMEM((NB, cols, BLOCK), BF),
            pltpu.VMEM((NB, cols, BLOCK), BF),
            dma((5,)),
            dma((5,)),
            dma((6,)),
            dma((6,)),
            dma((4, 7)),
            dma((4, 7)),
            dma((4, EARLY_HOPS)),
            dma((4, EARLY_HOPS)),
            dma((4,)),
            dma((2, 3)),
            dma((3,)),
            dma((3,)),
        ],
        compiler_params=pltpu.CompilerParams(
            collective_id=1, has_side_effects=True, vmem_limit_bytes=56 << 20
        ),
        cost_estimate=pl.CostEstimate(flops=12 * 10**9, bytes_accessed=200 << 20, transcendentals=14 << 20),
        name="forward",
    )(order, states, w_query, w_key, w_value, small, extra, out_piece, w_up, w_gate)


def last_kernel(order, base, tokens_t, g_qkv, w_t, part_out, vectors,
                g_states, g_query, g_key, g_value, out_rows, vec_own,
                gq_b, blocks, tok_r, tok_l, share, turned, core_buf, x_buf, base_b, gs_b,
                ring_r, ring_m, ring_l, ring_o, ring_v, next_r, next_l, row_buf, row_in, vec_part, vec_in,
                in_sem, row_sem, base_sem, core_send, core_recv, x_send, x_recv,
                ring_send, ring_recv, a2a_send, a2a_recv):
    me, dp = lax.axis_index("fsdp"), lax.axis_index("dp")
    place = ring_place()
    sibling, across, corner = group_peers()
    right, left = {"dp": ring_dp(place + 1)}, {"dp": ring_dp(place - 1)}
    chunk, side, cut = ring_r.shape[1], next_r.shape[1], ring_r.shape[2]
    rows = share.shape[1]
    quarter = rows // 4
    width = w_t.shape[1]
    heads_width = gq_b.shape[0]
    rows_w = row_buf.shape[1]

    def slices(step):
        slot = step % 2
        cut_r = rows_at(ring_dp(place - 1 - step) * chunk, chunk)
        cut_l = rows_at(ring_dp(place + 1 + step) * chunk, chunk)
        return [
            pltpu.make_async_copy(tokens_t.at[cut_r], tok_r.at[slot], row_sem.at[0, slot]),
            pltpu.make_async_copy(tokens_t.at[cut_l], tok_l.at[slot], row_sem.at[1, slot]),
        ]

    def base_copy(i):
        return pltpu.make_async_copy(base.at[pl.ds(i * quarter, quarter)], base_b.at[i % 2], base_sem.at[0, i % 2])

    def gs_copy(i):
        return pltpu.make_async_copy(gs_b.at[i % 2], g_states.at[pl.ds(i * quarter, quarter)], base_sem.at[1, i % 2])

    load_q = pltpu.make_async_copy(g_qkv, gq_b, in_sem.at[0])
    load_q.start()
    for step in (0, 1):
        for copy in slices(step):
            copy.start()
    greet([sibling, across, corner, right, left])

    def parts(step):
        slot = step % 2
        for copy in slices(step):
            copy.wait()
        next_r[...] = nt(tok_r[slot], gq_b[pl.ds(0, side)])
        next_l[...] = nt(tok_l[slot], gq_b[pl.ds(side, heads_width - side)])

        @pl.when(step + 2 < 8)
        def _():
            for copy in slices(step + 2):
                copy.start()

    def hop_copies(step):
        return [
            send(ring.at[step], ring.at[step + 1], ring_send.at[i, step], ring_recv.at[i, step], peer)
            for i, (ring, peer) in enumerate(
                ((ring_r, right), (ring_l, left), (ring_m, right), (ring_o, left), (ring_v, right))
            )
        ]

    def through(r, slot):
        for i in range(rows // BLOCK):
            turned[i * BLOCK : (i + 1) * BLOCK] = blocks[order[1, r * (rows // BLOCK) + i]].T

        def one(n, carry):
            share[slot, :, tile(n)] = nn(turned[...], w_t[pl.ds(0, heads_width), tile(n)]).astype(BF)
            return carry

        lax.fori_loop(0, width // TILE, one, 0)

    core = [
        send(share.at[0], core_buf.at[0], core_send.at[0], core_recv.at[0], sibling),
        send(share.at[2], core_buf.at[1], core_send.at[1], core_recv.at[1], sibling),
    ]
    far = [
        send(share.at[1, pl.ds(i * quarter, quarter)], x_buf.at[pl.ds(i * quarter, quarter)], x_send.at[i],
             x_recv.at[i], across)
        for i in range(4)
    ]
    load_q.wait()

    def split(i, carry):
        blocks[i] = gq_b[:, lanes_at(i * BLOCK, BLOCK)]
        return carry

    def hop(step, carry):
        parts(step)

        @pl.when(step == 0)
        def _():
            ring_r[0] = next_r[:, :cut].astype(BF)
            ring_m[0] = next_r[:, cut:].astype(BF)
            ring_l[0] = next_l[...].astype(BF)
            ring_o[0] = part_out[ring_dp(place + 1)]
            ring_v[0] = vectors[ring_dp(place - 1)]

        @pl.when(step > 0)
        def _():
            before, now = hop_copies(step - 1), hop_copies(step)
            before[0].wait()
            ring_r[step] = (ring_r[step].astype(F32) + next_r[:, :cut]).astype(BF)
            now[0].start()
            before[1].wait()
            ring_l[step] = (ring_l[step].astype(F32) + next_l[...]).astype(BF)
            now[1].start()
            before[2].wait()
            ring_m[step] = (ring_m[step].astype(F32) + next_r[:, cut:]).astype(BF)
            now[2].start()
            before[3].wait()
            ring_o[step] = (ring_o[step].astype(F32) + part_out[ring_dp(place + 1 + step)].astype(F32)).astype(BF)
            now[3].start()
            before[4].wait()
            ring_v[step] = ring_v[step] + vectors[ring_dp(place - 1 - step)]
            now[4].start()

        @pl.when(step == 0)
        def _():
            for copy in hop_copies(0):
                copy.start()

        @pl.when(step < 4)
        def _():
            @pl.when(step == 0)
            def _():
                lax.fori_loop(0, NB, split, 0)
                through(3, 0)
                core[0].start()

            @pl.when(step < 3)
            def _():
                through(2 - step, (step + 1) % 3)

            @pl.when(step == 0)
            def _():
                core[0].wait()
                for i in range(4):
                    span = pl.ds(i * quarter, quarter)
                    share[1, span] = (share[1, span].astype(F32) + core_buf[0, span].astype(F32)).astype(BF)
                    far[i].start()

            @pl.when(step == 1)
            def _():
                core[1].start()

        return carry

    lax.fori_loop(0, 7, hop, 0)
    base_copy(0).start()
    base_copy(1).start()
    parts(7)
    for copy in hop_copies(6):
        copy.wait()
    total = jnp.concatenate((ring_r[7], ring_m[7], ring_l[7]), axis=1).astype(F32)
    total = total + jnp.concatenate((next_r[...], next_l[...]), axis=1)
    for i in range(4):
        row_buf[i] = total[i * rows_w : (i + 1) * rows_w].astype(BF)
    vec_part[...] = ring_v[7] + vectors[dp]
    exchange = []
    for i, peer in enumerate((sibling, across, corner)):
        to = peer["fsdp"]
        copies = [
            send(row_buf.at[to], row_in.at[me], a2a_send.at[i], a2a_recv.at[i], peer),
            send(vec_part.at[to], vec_in.at[me], a2a_send.at[3 + i], a2a_recv.at[3 + i], peer),
        ]
        for copy in copies:
            copy.start()
        exchange += copies
    row_in[me] = row_buf[me]
    vec_in[me] = vec_part[me]
    out_rows[...] = ring_o[7].astype(F32) + part_out[dp].astype(F32)
    core[1].wait()
    for i in range(4):
        span = pl.ds(i * quarter, quarter)
        far[i].wait()
        base_copy(i).wait()
        if i >= 2:
            gs_copy(i - 2).wait()
        gs_b[i % 2] = base_b[i % 2] + (
            share[0, span].astype(F32) + core_buf[1, span].astype(F32) + x_buf[span].astype(F32)
        )
        gs_copy(i).start()
        if i < 2:
            base_copy(i + 2).start()
    for copy in exchange:
        copy.wait()
    vec_own[...] = vec_in[0] + vec_in[1] + vec_in[2] + vec_in[3]
    cols = heads_width // 3
    for which, out in enumerate((g_query, g_key, g_value)):
        out[...] = jnp.concatenate(
            [row_in[i, :, which * cols : (which + 1) * cols].astype(F32) for i in range(4)], axis=1
        )
    for i in (2, 3):
        gs_copy(i).wait()


def last_exchange(order, base, tokens_t, g_qkv, w_t, part_out, vectors):
    rows, width = base.shape
    heads_width = g_qkv.shape[0]
    rows_w = part_out.shape[1]
    chunk = 4 * rows_w
    side = 2 * heads_width // 3
    vmem, hbm = pl.BlockSpec(memory_space=pltpu.VMEM), pl.BlockSpec(memory_space=pl.ANY)
    dma = pltpu.SemaphoreType.DMA
    return pl.pallas_call(
        last_kernel,
        in_specs=[pl.BlockSpec(memory_space=pltpu.SMEM), hbm, hbm, hbm, vmem, vmem, vmem],
        out_specs=[hbm] + [vmem] * 5,
        out_shape=[jax.ShapeDtypeStruct((rows, width), F32)]
        + [jax.ShapeDtypeStruct((rows_w, width), F32)] * 4
        + [jax.ShapeDtypeStruct(vectors.shape[2:], F32)],
        scratch_shapes=[
            pltpu.VMEM(g_qkv.shape, BF),
            pltpu.VMEM((NB, heads_width, BLOCK), BF),
            pltpu.VMEM((2, chunk, tokens_t.shape[1]), BF),
            pltpu.VMEM((2, chunk, tokens_t.shape[1]), BF),
            pltpu.VMEM((3, rows, width), BF),
            pltpu.VMEM((rows, heads_width), BF),
            pltpu.VMEM((2, rows, width), BF),
            pltpu.VMEM((rows, width), BF),
            pltpu.VMEM((2, rows // 4, width), F32),
            pltpu.VMEM((2, rows // 4, width), F32),
            pltpu.VMEM((8, chunk, 384), BF),
            pltpu.VMEM((8, chunk, side - 384), BF),
            pltpu.VMEM((8, chunk, heads_width - side), BF),
            pltpu.VMEM((8, rows_w, width), BF),
            pltpu.VMEM(vectors.shape, F32),
            pltpu.VMEM((chunk, side), F32),
            pltpu.VMEM((chunk, heads_width - side), F32),
            pltpu.VMEM((4, rows_w, heads_width), BF),
            pltpu.VMEM((4, rows_w, heads_width), BF),
            pltpu.VMEM(vectors.shape[1:], F32),
            pltpu.VMEM(vectors.shape[1:], F32),
            dma((1,)),
            dma((2, 2)),
            dma((2, 2)),
            dma((2,)),
            dma((2,)),
            dma((4,)),
            dma((4,)),
            dma((5, 7)),
            dma((5, 7)),
            dma((6,)),
            dma((6,)),
        ],
        compiler_params=pltpu.CompilerParams(
            collective_id=2, has_side_effects=True, vmem_limit_bytes=48 << 20
        ),
        cost_estimate=pl.CostEstimate(flops=13 * 10**9, bytes_accessed=100 << 20, transcendentals=0),
        name="last_exchange",
    )(order, base, tokens_t, g_qkv, w_t, part_out, vectors)


CHUNK = 128
TILE = 256
LAG = 3


def tile(index, base=0):
    return pl.ds(pl.multiple_of(base + index * TILE, TILE), TILE)


def nt(a, b):
    return lax.dot_general(a, b, (((1,), (1,)), ((), ())), preferred_element_type=F32)


def middle_kernel(mixed_n, states, teacher, weight, mask, w_in, w_own, w_o, rates, scales,
                  w_ug_out, w_d_out, hidden_out, back_out, out_states, attn_unit, attn_inv, hidden_inv, sums, gd_all,
                  ht_all, act_all, ug_all, w_ug, w_d, hidden, back, target, mx, part, core, x_buf, tok, gd, act, act_t, ug, ht,
                  mx_send, mx_recv, mx_own, keep_sem, core_send, core_recv, x_send, x_recv, tok_send, tok_recv, gd_send, gd_recv, gd_own,
                  out_sem, ring_send, ring_recv, ug_s, ug_r, ug_sem):
    sibling, across, corner = group_peers()
    dp, place = lax.axis_index("dp"), ring_place()
    right, left = {"dp": ring_dp(place + 1)}, {"dp": ring_dp(place - 1)}
    piece = w_own.shape[0]
    count = x_buf.shape[0]
    width = hidden.shape[1]
    rate_attn, rate_mlp = rates[0:1], rates[1:2]

    def rows(i):
        return pl.ds(pl.multiple_of(i * CHUNK, CHUNK), CHUNK)

    def mx_copies(i):
        return [
            send(mixed_n.at[(r + 1) * count + i], mx.at[i, r + 1], mx_send.at[r, i], mx_recv.at[r, i], peer)
            for r, peer in enumerate((sibling, across, corner))
        ]

    def load_teacher(i):
        return pltpu.make_async_copy(teacher.at[rows(i)], target.at[i % 2], keep_sem.at[2, 2 + i % 2])

    def mx_local(i):
        return pltpu.make_async_copy(mixed_n.at[i], mx.at[i, 0], mx_own.at[i])

    def keep_rows(i):
        return [
            pltpu.make_async_copy(hidden.at[rows(i)], hidden_out.at[rows(i)], keep_sem.at[0, i]),
            pltpu.make_async_copy(back.at[rows(i)], back_out.at[rows(i)], keep_sem.at[1, i]),
        ]

    keep_w = [
        pltpu.make_async_copy(w_ug, w_ug_out, keep_sem.at[2, 0]),
        pltpu.make_async_copy(w_d, w_d_out, keep_sem.at[2, 1]),
    ]

    def core_a(stage, i):
        return send(part.at[i % 3, 3], core.at[0, i], core_send.at[stage, 0, i], core_recv.at[stage, 0, i], sibling)

    def core_b(stage, i):
        return send(part.at[i % 3, 1], core.at[1, i], core_send.at[stage, 1, i], core_recv.at[stage, 1, i], sibling)

    def chip(stage, i):
        return send(part.at[i % 3, 2], x_buf.at[i], x_send.at[stage, i], x_recv.at[stage, i], across)

    def spread(buf, own, sems, recvs, i):
        return [
            send(own, buf.at[i, 1], sems.at[0, i], recvs.at[0, i], sibling),
            send(own, buf.at[i, 2], sems.at[1, i], recvs.at[1, i], across),
            send(buf.at[i, 2], buf.at[i, 3], sems.at[2, i], recvs.at[2, i], sibling),
        ]

    def tok_copies(i):
        return spread(tok, tok.at[i, 0], tok_send, tok_recv, i)

    def gd_copies(i):
        return spread(gd_all, gd.at[i], gd_send, gd_recv, i)

    def gd_local(i):
        return pltpu.make_async_copy(gd.at[i], gd_all.at[i, 0], gd_own.at[i])

    def outs(i):
        slot = i % 2
        return [
            pltpu.make_async_copy(ht.at[slot], ht_all.at[i], out_sem.at[0, slot]),
            pltpu.make_async_copy(act_t.at[slot], act_all.at[i], out_sem.at[1, slot]),
            pltpu.make_async_copy(ug.at[slot], ug_all.at[i], out_sem.at[2, slot]),
        ]

    def hop(step):
        late = hidden_ring(w_d, ring_send, ring_recv, step + 1)
        for copy, later in zip(hidden_ring(w_d, ring_send, ring_recv, step), late):
            copy.wait()
            pl.when(step < 6)(later.start)

    def ug_hop(step):
        late = hidden_ring(w_ug, ug_s, ug_r, step + 1, EARLY_HOPS)
        for copy, later in zip(hidden_ring(w_ug, ug_s, ug_r, step, EARLY_HOPS), late):
            copy.wait()
            pl.when(step < 6)(later.start)

    def forward_far(stage, i):
        core_a(stage, i).wait_recv()
        part[i % 3, 2] = (part[i % 3, 2].astype(F32) + core[0, i].astype(F32)).astype(BF)
        chip(stage, i).start()

    def reduced(stage, i):
        core_b(stage, i).wait_recv()
        chip(stage, i).wait_recv()
        total = part[i % 3, 0].astype(F32) + core[1, i].astype(F32) + x_buf[i].astype(F32)
        core_a(stage, i).wait_send()
        core_b(stage, i).wait_send()
        chip(stage, i).wait_send()
        return total

    sums[...] = jnp.zeros_like(sums)
    load_teacher(0).start()
    load_teacher(1).start()
    w_d[rows_at(dp * piece, piece)] = w_own[...]
    chunk = w_ug.shape[0] // 8

    def load_w(i):
        cuts = rows_at(ring_dp(place - i) * chunk, chunk // 2), rows_at(
            ring_dp(place + i) * chunk + chunk // 2, chunk // 2
        )
        return [pltpu.make_async_copy(w_in.at[cut], w_ug.at[cut], ug_sem.at[d, i]) for d, cut in enumerate(cuts)]

    def start_w(i, carry):
        for copy in load_w(i):
            copy.start()
        return carry

    def wait_w(i, carry):
        for copy in load_w(i):
            copy.wait()
        return carry

    lax.fori_loop(0, EARLY_HOPS + 1, start_w, 0)
    greet([sibling, across, corner, right, left])
    for copy in hidden_ring(w_d, ring_send, ring_recv, 0):
        copy.start()

    def open_mixed(i, carry):
        mx_local(i).start()
        for copy in mx_copies(i):
            copy.start()
        return carry

    lax.fori_loop(0, count, open_mixed, 0)
    lax.fori_loop(0, EARLY_HOPS + 1, wait_w, 0)
    for copy in hidden_ring(w_ug, ug_s, ug_r, EARLY_HOPS, EARLY_HOPS):
        copy.start()

    def norm_hidden(i):
        mx_local(i).wait()
        for copy in mx_copies(i):
            copy.wait()
        attn = nn(mx[i, 0].T, w_o[0])
        for r in range(1, 4):
            attn = attn + nn(mx[i, r].T, w_o[r])
        unit, inverse = unit_rows(attn)
        own = states[rows(i)].astype(F32)
        value, value_inv = unit_rows(own + rate_attn * (unit - own))
        hidden[rows(i)] = value
        attn_unit[rows(i)] = unit.astype(BF)
        attn_inv[rows(i)] = inverse
        hidden_inv[rows(i)] = value_inv
        tok[i, 0] = value.astype(BF)
        copies = tok_copies(i)
        copies[0].start()
        copies[1].start()

    def pass_tokens(i):
        copies = tok_copies(i)
        copies[1].wait_recv()
        copies[2].start()

    def feed(i):
        copies = tok_copies(i)
        copies[0].wait()
        copies[1].wait_send()
        copies[2].wait()
        slot = i % 2

        @pl.when(i >= 2)
        def _():
            for copy in outs(i - 2):
                copy.wait()

        def up(n, carry):
            here = tok[i].reshape(4 * CHUNK, width)
            up_proj = nn(here, w_ug[:, tile(n)])
            gate_proj = nn(here, w_ug[:, tile(n, width)])
            gated = gate_proj * scales[1:2, tile(n)]
            value = up_proj * scales[0:1, tile(n)] * (gated * jax.nn.sigmoid(gated))
            act[slot, :, tile(n)] = value.astype(BF)
            act_t[slot, tile(n)] = value.astype(BF).T
            ug[slot, :, tile(n)] = up_proj.astype(BF)
            ug[slot, :, tile(n, width)] = gate_proj.astype(BF)
            return carry

        lax.fori_loop(0, width // TILE, up, 0)
        for copy in outs(i)[1:]:
            copy.start()

    def feed_down(i):
        slot = i % 2

        def down(n, carry):
            value = nn(act[slot], w_d[:, tile(n)])
            part[i % 3, :, :, tile(n)] = value.astype(BF).reshape(4, CHUNK, TILE)
            ht[slot, tile(n)] = tok[i, :, :, tile(n)].reshape(4 * CHUNK, TILE).T
            return carry

        lax.fori_loop(0, width // TILE, down, 0)
        core_a(0, i).start()
        core_b(0, i).start()
        outs(i)[0].start()
        forward_far(0, i)

    def finish(i):
        unit, inverse = unit_rows(reduced(0, i))
        own = hidden[rows(i)]
        result, result_inv = unit_rows(own + rate_mlp * (unit - own))
        out_states[rows(i)] = result.astype(BF)
        load_teacher(i).wait()
        diff = result - target[i % 2]

        @pl.when(i + 2 < count)
        def _():
            load_teacher(i + 2).start()

        sums[1:2] = sums[1:2] + jnp.sum(mask[rows(i)] * (diff * diff), axis=0, keepdims=True)
        g_last = unit_back(weight[rows(i)] * diff, result, result_inv)
        sums[0:1] = sums[0:1] + jnp.sum(g_last * (unit - own), axis=0, keepdims=True)
        back[rows(i)] = g_last * (1.0 - rate_mlp)
        gd[i] = unit_back(g_last * rate_mlp, unit, inverse).astype(BF)
        copies = gd_copies(i)
        copies[0].start()
        copies[1].start()
        gd_local(i).start()
        for copy in keep_rows(i):
            copy.start()

    def pass_grads(i):
        copies = gd_copies(i)
        copies[1].wait_recv()
        copies[2].start()

    stages = (norm_hidden, pass_tokens, feed, feed_down, finish, pass_grads)

    def step(t, carry):
        for lag, stage in enumerate(stages):
            if lag == 2:
                pl.when(t < 7 - EARLY_HOPS)(lambda: ug_hop(EARLY_HOPS + t))
            if lag == 3:
                pl.when(t < 4)(lambda: hop(jnp.maximum(2 * t - 1, 0)))
                pl.when((t >= 1) & (t < 4))(lambda: hop(2 * t))

                @pl.when(t == 3)
                def _():
                    for copy in keep_w:
                        copy.start()

            pl.when((t >= lag) & (t < lag + count))(functools.partial(stage, t - lag))
        return carry

    lax.fori_loop(0, count + len(stages) - 1, step, 0)

    def close(i, carry):
        copies = gd_copies(i)
        copies[0].wait()
        copies[1].wait_send()
        copies[2].wait()
        gd_local(i).wait()
        for copy in keep_rows(i):
            copy.wait()
        return carry

    lax.fori_loop(0, count, close, 0)
    for i in (count - 2, count - 1):
        for copy in outs(i):
            copy.wait()
    for copy in keep_w:
        copy.wait()


def middle(mixed_n, states, teacher, weight, mask, w_ug, w_own, w_o, rates, scales):
    rows, width = states.shape
    count = rows // CHUNK
    vmem, hbm = pl.BlockSpec(memory_space=pltpu.VMEM), pl.BlockSpec(memory_space=pl.ANY)
    dma = pltpu.SemaphoreType.DMA
    return pl.pallas_call(
        middle_kernel,
        in_specs=[hbm, vmem, hbm, vmem, vmem, hbm] + [vmem] * 4,
        out_specs=[hbm] * 4 + [vmem] * 5 + [hbm] * 4,
        out_shape=[
            jax.ShapeDtypeStruct(w_ug.shape, BF),
            jax.ShapeDtypeStruct((8 * w_own.shape[0], width), BF),
            jax.ShapeDtypeStruct((rows, width), F32),
            jax.ShapeDtypeStruct((rows, width), F32),
            jax.ShapeDtypeStruct((rows, width), BF),
            jax.ShapeDtypeStruct((rows, width), BF),
            jax.ShapeDtypeStruct((rows, 1), F32),
            jax.ShapeDtypeStruct((rows, 1), F32),
            jax.ShapeDtypeStruct((2, width), F32),
            jax.ShapeDtypeStruct((count, 4, CHUNK, width), BF),
            jax.ShapeDtypeStruct((count, width, 4 * CHUNK), BF),
            jax.ShapeDtypeStruct((count, width, 4 * CHUNK), BF),
            jax.ShapeDtypeStruct((count, 4 * CHUNK, 2 * width), BF),
        ],
        scratch_shapes=[
            pltpu.VMEM(w_ug.shape, BF),
            pltpu.VMEM((8 * w_own.shape[0], width), BF),
            pltpu.VMEM((rows, width), F32),
            pltpu.VMEM((rows, width), F32),
            pltpu.VMEM((2, CHUNK, width), F32),
            pltpu.VMEM((count, 4) + mixed_n.shape[1:], BF),
            pltpu.VMEM((3, 4, CHUNK, width), BF),
            pltpu.VMEM((2, count, CHUNK, width), BF),
            pltpu.VMEM((count, CHUNK, width), BF),
            pltpu.VMEM((count, 4, CHUNK, width), BF),
            pltpu.VMEM((count, CHUNK, width), BF),
            pltpu.VMEM((2, 4 * CHUNK, width), BF),
            pltpu.VMEM((2, width, 4 * CHUNK), BF),
            pltpu.VMEM((2, 4 * CHUNK, 2 * width), BF),
            pltpu.VMEM((2, width, 4 * CHUNK), BF),
            dma((3, count)),
            dma((3, count)),
            dma((count,)),
            dma((3, count)),
            dma((1, 2, count)),
            dma((1, 2, count)),
            dma((1, count)),
            dma((1, count)),
            dma((3, count)),
            dma((3, count)),
            dma((3, count)),
            dma((3, count)),
            dma((count,)),
            dma((3, 2)),
            dma((4, 7)),
            dma((4, 7)),
            dma((4, 7 - EARLY_HOPS)),
            dma((4, 7 - EARLY_HOPS)),
            dma((2, EARLY_HOPS + 1)),
        ],
        compiler_params=pltpu.CompilerParams(
            collective_id=3, has_side_effects=True, vmem_limit_bytes=62 << 20
        ),
        cost_estimate=pl.CostEstimate(flops=26 * 10**9, bytes_accessed=400 << 20, transcendentals=4 << 20),
        name="middle",
    )(mixed_n, states, teacher, weight, mask, w_ug, w_own, w_o, rates, scales)


def middle_back_kernel(gd_all, act_all, ug_all, hidden, attn_unit, states, back, attn_inv, hidden_inv, w_ug, w_d,
                       rates, scales, base, ga_all, gug_all, down_rows, sums, ff_sums,
                       w_ug_b, w_d_b, part, core, x_buf, ga, gd, act, ug, gug, own_f, own_b, base_buf, dwd, column, ring_buf,
                       gd_sem, act_sem, in_sem, own_sem, core_send, core_recv, x_send, x_recv, ga_send, ga_recv,
                       ga_own, base_sem, out_sem, w_sem, ring_send, ring_recv):
    sibling, across, _ = group_peers()
    dp, place = lax.axis_index("dp"), ring_place()
    right, left = {"dp": ring_dp(place + 1)}, {"dp": ring_dp(place - 1)}
    count = core.shape[1]
    width = w_d.shape[0]
    load_d = pltpu.make_async_copy(w_d, w_d_b, w_sem.at[0])
    load_u = pltpu.make_async_copy(w_ug, w_ug_b, w_sem.at[1])
    load_d.start()
    half = ring_buf.shape[2]
    rate_attn = rates[0:1]

    def rows(i):
        return pl.ds(pl.multiple_of(i * CHUNK, CHUNK), CHUNK)

    def load_gd(i):
        return pltpu.make_async_copy(gd_all.at[i], gd.at[i], gd_sem.at[i])

    def load_act(i):
        return pltpu.make_async_copy(act_all.at[i], act.at[i], act_sem.at[i])

    def load_ug(i):
        return pltpu.make_async_copy(ug_all.at[i], ug.at[i % 2], in_sem.at[i % 2])

    def store_gug(i):
        return pltpu.make_async_copy(gug.at[i % 2], gug_all.at[i], out_sem.at[i % 2])

    def own_rows(i):
        return [
            pltpu.make_async_copy(hidden.at[rows(i)], own_f.at[0], own_sem.at[0]),
            pltpu.make_async_copy(back.at[rows(i)], own_f.at[1], own_sem.at[1]),
            pltpu.make_async_copy(attn_unit.at[rows(i)], own_b.at[0], own_sem.at[2]),
            pltpu.make_async_copy(states.at[rows(i)], own_b.at[1], own_sem.at[3]),
        ]

    def core_a(i):
        return send(part.at[i % 3, 3], core.at[0, i], core_send.at[0, i], core_recv.at[0, i], sibling)

    def core_b(i):
        return send(part.at[i % 3, 1], core.at[1, i], core_send.at[1, i], core_recv.at[1, i], sibling)

    def chip(i):
        return send(part.at[i % 3, 2], x_buf.at[i], x_send.at[i], x_recv.at[i], across)

    def ga_copies(i):
        return [
            send(ga.at[i], ga_all.at[1, rows(i)], ga_send.at[0, i], ga_recv.at[0, i], sibling),
            send(ga.at[i], ga_all.at[2, rows(i)], ga_send.at[1, i], ga_recv.at[1, i], across),
            send(ga_all.at[2, rows(i)], ga_all.at[3, rows(i)], ga_send.at[2, i], ga_recv.at[2, i], sibling),
        ]

    def ga_local(i):
        return pltpu.make_async_copy(ga.at[i], ga_all.at[0, rows(i)], ga_own.at[i])

    def base_copy(i):
        return pltpu.make_async_copy(base_buf.at[i % 2], base.at[rows(i)], base_sem.at[i % 2])

    def right_half(step):
        return rows_at(ring_dp(place - 1 - step) * 2 * half, half)

    def left_half(step):
        return rows_at(ring_dp(place + 1 + step) * 2 * half + half, half)

    def ring(step):
        return [
            send(ring_buf.at[0, step], ring_buf.at[0, step + 1], ring_send.at[0, step], ring_recv.at[0, step], right),
            send(ring_buf.at[1, step], ring_buf.at[1, step + 1], ring_send.at[1, step], ring_recv.at[1, step], left),
        ]

    def hop(step, carry):
        for copy in ring(step):
            copy.wait()

        @pl.when(step < 6)
        def _():
            for side, cut in ((0, right_half(step + 1)), (1, left_half(step + 1))):
                ring_buf[side, step + 1] = (
                    ring_buf[side, step + 1].astype(F32) + dwd[cut].astype(F32)
                ).astype(BF)
            for copy in ring(step + 1):
                copy.start()

        return carry

    for copy in [load_ug(0)] + own_rows(0):
        copy.start()
    lax.fori_loop(0, count, lambda i, c: (load_gd(i).start(), c)[1], 0)
    load_u.start()
    lax.fori_loop(0, count, lambda i, c: (load_act(i).start(), c)[1], 0)
    sums[...] = jnp.zeros_like(sums)
    ff_sums[...] = jnp.zeros_like(ff_sums)
    greet([sibling, across, right, left])
    lax.fori_loop(0, count, lambda i, c: (load_gd(i).wait(), c)[1], 0)
    load_d.wait()

    def feed(i):
        slot = i % 2
        load_ug(i).wait()

        @pl.when(i + 1 < count)
        def _():
            load_ug(i + 1).start()

        @pl.when(i >= 2)
        def _():
            store_gug(i - 2).wait()

        def grads(n, carry):
            g_act = nt(gd[i].reshape(4 * CHUNK, width), w_d_b[tile(n)])
            up_proj = ug[slot, :, tile(n)].astype(F32)
            gate_proj = ug[slot, :, tile(n, width)].astype(F32)
            scale_up, scale_gate = scales[0:1, tile(n)], scales[1:2, tile(n)]
            gated = gate_proj * scale_gate
            sigmoid = jax.nn.sigmoid(gated)
            g_upscaled = g_act * (gated * sigmoid)
            g_gated = g_act * (up_proj * scale_up) * sigmoid * (1.0 + gated * (1.0 - sigmoid))
            ff_sums[0:1, tile(n)] = ff_sums[0:1, tile(n)] + jnp.sum(g_upscaled * up_proj, axis=0, keepdims=True)
            ff_sums[1:2, tile(n)] = ff_sums[1:2, tile(n)] + jnp.sum(g_gated * gate_proj, axis=0, keepdims=True)
            gug[slot, :, tile(n)] = (g_upscaled * scale_up).astype(BF)
            gug[slot, :, tile(n, width)] = (g_gated * scale_gate).astype(BF)
            return carry

        lax.fori_loop(0, width // TILE, grads, 0)
        store_gug(i).start()
        pl.when(i == 0)(load_u.wait)

        def through(n, carry):
            value = nt(gug[slot], w_ug_b[tile(n)])
            part[i % 3, :, :, tile(n)] = value.astype(BF).reshape(4, CHUNK, TILE)
            return carry

        lax.fori_loop(0, width // TILE, through, 0)
        core_a(i).start()
        core_b(i).start()
        core_a(i).wait_recv()
        part[i % 3, 2] = (part[i % 3, 2].astype(F32) + core[0, i].astype(F32)).astype(BF)
        chip(i).start()

    def down_grads():
        lax.fori_loop(0, count, lambda i, c: (load_act(i).wait(), c)[1], 0)

        def outer(n, carry):
            column[...] = jnp.zeros_like(column)

            def add(k, carry):
                column[...] = column[...] + nn(act[k], gd[k, :, :, tile(n)].reshape(4 * CHUNK, TILE))
                return carry

            lax.fori_loop(0, count, add, 0)
            dwd[:, tile(n)] = column[...].astype(BF)
            return carry

        lax.fori_loop(0, width // TILE, outer, 0)
        ring_buf[0, 0] = dwd[right_half(0)]
        ring_buf[1, 0] = dwd[left_half(0)]
        for copy in ring(0):
            copy.start()

    def finish(i):
        core_b(i).wait_recv()
        chip(i).wait_recv()
        through = part[i % 3, 0].astype(F32) + core[1, i].astype(F32) + x_buf[i].astype(F32)
        core_a(i).wait_send()
        core_b(i).wait_send()
        chip(i).wait_send()
        for copy in own_rows(i):
            copy.wait()
        value, unit, own = own_f[0], own_b[0].astype(F32), own_b[1].astype(F32)
        g_pre = unit_back(own_f[1] + through, value, hidden_inv[rows(i)])

        @pl.when(i + 1 < count)
        def _():
            for copy in own_rows(i + 1):
                copy.start()

        @pl.when(i >= 2)
        def _():
            base_copy(i - 2).wait()

        base_buf[i % 2] = g_pre * (1.0 - rate_attn)
        base_copy(i).start()
        sums[0:1] = sums[0:1] + jnp.sum(g_pre * (unit - own), axis=0, keepdims=True)
        ga[i] = unit_back(g_pre * rate_attn, unit, attn_inv[rows(i)]).astype(BF)
        copies = ga_copies(i)
        copies[0].start()
        copies[1].start()
        ga_local(i).start()

    def pass_grads(i):
        copies = ga_copies(i)
        copies[1].wait_recv()
        copies[2].start()

    stages = (feed, finish, pass_grads)

    def step(t, carry):
        for lag, stage in enumerate(stages):
            pl.when((t >= lag) & (t < lag + count))(functools.partial(stage, t - lag))
        pl.when(t == 2)(down_grads)

        @pl.when((t >= 3) & (t < 6))
        def _():
            lax.fori_loop(2 * t - 6, 2 * t - 4, hop, 0)

        return carry

    lax.fori_loop(0, count + len(stages) - 1, step, 0)
    hop(6, 0)
    own = dp * 2 * half
    down_rows[pl.ds(0, half)] = ring_buf[0, 7].astype(F32) + dwd[rows_at(own, half)].astype(F32)
    down_rows[pl.ds(half, half)] = ring_buf[1, 7].astype(F32) + dwd[rows_at(own + half, half)].astype(F32)

    def close(i, carry):
        copies = ga_copies(i)
        copies[0].wait()
        copies[1].wait_send()
        copies[2].wait()
        ga_local(i).wait()
        return carry

    lax.fori_loop(0, count, close, 0)
    for i in (count - 2, count - 1):
        base_copy(i).wait()
        store_gug(i).wait()


def middle_back(gd_all, act_all, ug_all, hidden, attn_unit, states, back, attn_inv, hidden_inv, w_ug, w_d, rates,
                scales):
    rows, width = states.shape
    count = rows // CHUNK
    piece = width // 8
    vmem, hbm = pl.BlockSpec(memory_space=pltpu.VMEM), pl.BlockSpec(memory_space=pl.ANY)
    dma = pltpu.SemaphoreType.DMA
    return pl.pallas_call(
        middle_back_kernel,
        in_specs=[hbm] * 7 + [vmem] * 2 + [hbm] * 2 + [vmem] * 2,
        out_specs=[hbm, hbm, hbm, vmem, vmem, vmem],
        out_shape=[
            jax.ShapeDtypeStruct((rows, width), F32),
            jax.ShapeDtypeStruct((4, rows, width), BF),
            jax.ShapeDtypeStruct((count, 4 * CHUNK, 2 * width), BF),
            jax.ShapeDtypeStruct((piece, width), F32),
            jax.ShapeDtypeStruct((1, width), F32),
            jax.ShapeDtypeStruct((2, width), F32),
        ],
        scratch_shapes=[
            pltpu.VMEM(w_ug.shape, BF),
            pltpu.VMEM(w_d.shape, BF),
            pltpu.VMEM((3, 4, CHUNK, width), BF),
            pltpu.VMEM((2, count, CHUNK, width), BF),
            pltpu.VMEM((count, CHUNK, width), BF),
            pltpu.VMEM((count, CHUNK, width), BF),
            pltpu.VMEM((count, 4, CHUNK, width), BF),
            pltpu.VMEM((count, width, 4 * CHUNK), BF),
            pltpu.VMEM((2, 4 * CHUNK, 2 * width), BF),
            pltpu.VMEM((2, 4 * CHUNK, 2 * width), BF),
            pltpu.VMEM((2, CHUNK, width), F32),
            pltpu.VMEM((2, CHUNK, width), BF),
            pltpu.VMEM((2, CHUNK, width), F32),
            pltpu.VMEM((width, width), BF),
            pltpu.VMEM((width, TILE), F32),
            pltpu.VMEM((2, 8, piece // 2, width), BF),
            dma((count,)),
            dma((count,)),
            dma((2,)),
            dma((4,)),
            dma((2, count)),
            dma((2, count)),
            dma((count,)),
            dma((count,)),
            dma((3, count)),
            dma((3, count)),
            dma((count,)),
            dma((2,)),
            dma((2,)),
            dma((2,)),
            dma((2, 7)),
            dma((2, 7)),
        ],
        compiler_params=pltpu.CompilerParams(
            collective_id=4, has_side_effects=True, vmem_limit_bytes=60 << 20
        ),
        cost_estimate=pl.CostEstimate(flops=34 * 10**9, bytes_accessed=200 << 20, transcendentals=4 << 20),
        name="middle_back",
    )(gd_all, act_all, ug_all, hidden, attn_unit, states, back, attn_inv, hidden_inv, w_ug, w_d, rates, scales)


def order_kernel(where_ref, parent_ref, out_ref):
    base, me = where_ref[0], where_ref[1]
    shape = (128, 128)
    row = lax.broadcasted_iota(jnp.int32, shape, 0)
    block = lax.broadcasted_iota(jnp.int32, (8, 128), 1)
    real = block < NB
    parent = jnp.where(real & (parent_ref[...] >= 0), parent_ref[...] - base, -1)
    up = (row == parent[0:1]).astype(F32)
    up2 = nn(up, up)
    near = up + up2
    up4 = nn(up2, up2)
    near = near + nn(near, up2)
    near = near + nn(near, up4)
    above = near + nn(nn(up4, up4), up)
    depth = jnp.broadcast_to(jnp.sum(above, axis=0, keepdims=True), (8, 128)).astype(jnp.int32)
    before = (row < lax.broadcasted_iota(jnp.int32, shape, 1)).astype(F32)
    rank = nn(((depth == TRUNK) & real).astype(F32), before)
    parent_rank = nn(rank, up).astype(jnp.int32)
    sibling = jnp.sum(nn(up.T, up) * before, axis=0, keepdims=True).astype(jnp.int32)
    leaf = TRUNK + 4 + 2 * parent_rank + sibling
    slot = jnp.where(depth < TRUNK, depth, jnp.where(depth == TRUNK, TRUNK + rank.astype(jnp.int32), leaf))
    slot = jnp.where(real, slot, 127)
    mine = jnp.where(real, jnp.bitwise_xor(block // 5, me) * 5 + block % 5, 127)
    order = nt(mine.astype(F32), (row == slot[0:1]).astype(F32))
    back = nt(slot.astype(F32), (row == mine[0:1]).astype(F32))
    which = lax.broadcasted_iota(jnp.int32, (8, 128), 0)
    out_ref[...] = jnp.where(which == 0, order, back).astype(jnp.int32)


def tree_order(where, parents):
    return pl.pallas_call(
        order_kernel,
        in_specs=[pl.BlockSpec(memory_space=pltpu.SMEM), pl.BlockSpec(memory_space=pltpu.VMEM)],
        out_specs=pl.BlockSpec(memory_space=pltpu.VMEM),
        out_shape=jax.ShapeDtypeStruct((8, 128), jnp.int32),
        name="tree_order",
    )(where, jnp.broadcast_to(jnp.pad(parents, (0, 128 - NB), constant_values=-1), (8, 128)))


def local(
    states,
    teacher,
    parent_ids,
    valid_mask,
    w_query,
    w_key,
    w_value,
    w_out,
    w_up,
    w_gate,
    w_down,
    qk_scale,
    attn_rate,
    mlp_rate,
    up_scale,
    gate_scale,
):
    both = ("dp", "fsdp")
    dps, tps = 8, 4
    rows_w = w_query.shape[0]
    cols = D // tps
    hid = FF // tps
    ff_rows = FF // (dps * tps)
    me = lax.axis_index("fsdp")
    root_width = math.sqrt(D)
    mask_f = valid_mask.astype(F32)
    group_base = lax.axis_index("dp") * NB
    order = tree_order(jnp.stack((group_base, me)).astype(jnp.int32), parent_ids)

    count = jnp.sum(valid_mask)
    first_row = jnp.arange(rows_w, dtype=jnp.int32) == 0
    small = jnp.stack(
        (
            qk_scale,
            attn_rate,
            mlp_rate,
            jnp.where(first_row, count // 128, 0).astype(BF),
            jnp.where(first_row, count % 128, 0).astype(BF),
        ),
        axis=1,
    )
    small = jnp.pad(small, ((0, 0), (0, 59)))
    extra = jnp.pad(jnp.stack((up_scale, gate_scale), axis=1), ((0, 0), (69, 57)))
    spread = [(j, tps * (j % dps) + j // dps) for j in range(dps * tps)]
    tokens_t, w_t, w_o, w_ug, qkv, mixed, sums, mixed_n = forward(
        order, states, w_query, w_key, w_value, small, extra, lax.ppermute(w_out, both, spread), w_up, w_gate
    )
    small_all = w_t[3 * cols : 3 * cols + 8].astype(F32)
    rates = small_all[1:3]
    valid_count = 128.0 * jnp.sum(small_all[3]) + jnp.sum(small_all[4])
    scales = small_all[5:7] * jnp.array([[1.0], [root_width]], F32)
    scale_qk = lax.dynamic_slice_in_dim(small_all[0], me * cols, cols).reshape(cols // HEAD_DIM, HEAD_DIM, 1)

    mask_col = mask_f[:, None]
    w_ug, w_d, hidden, back, out_states, attn_unit, attn_inv, hidden_inv, sums_mid, gd_all, ht_all, act_all, ug_all = middle(
        mixed_n, states, teacher, mask_col * (2.0 / valid_count), mask_col, w_ug, w_down, w_o, rates, scales
    )
    base, ga_all, gug_all, grad_down, sums_back, ff_sums = middle_back(
        gd_all, act_all, ug_all, hidden, attn_unit, states, back, attn_inv, hidden_inv, w_ug, w_d, rates, scales
    )
    loss_local = jnp.sum(sums_mid[1])
    g_rate_mlp, g_rate_attn = sums_mid[0], sums_back[0]
    grad_up_scale, grad_gate_scale = ff_sums[0], ff_sums[1] * root_width
    g_qkv, g_scale, part_out, grad_up, grad_gate = attention_back(
        order, qkv, scale_qk, sums, mixed, ga_all.reshape(NB, BLOCK, D), w_o, ht_all, gug_all
    )
    g_qkv = g_qkv.reshape(3 * cols, TOK)
    slot = jnp.arange(tps, dtype=jnp.int32) == me
    qk_rows = jnp.where(slot[:, None], g_scale.reshape(1, cols), 0.0).reshape(dps * tps, rows_w)
    ff_terms = [
        jnp.where(slot[None, :, None], term.reshape(dps, 1, ff_rows), 0.0).reshape(dps * tps, ff_rows)
        for term in (grad_up_scale, grad_gate_scale)
    ]
    vectors = jnp.concatenate(
        [g_rate_attn.reshape(dps * tps, rows_w), g_rate_mlp.reshape(dps * tps, rows_w), qk_rows]
        + ff_terms
        + [jnp.broadcast_to(loss_local, (dps * tps, 512 - 3 * rows_w - 2 * ff_rows))],
        axis=1,
    ).reshape(dps, tps, 4, 128)
    part_out = part_out.reshape(dps, rows_w, D)
    grad_states, g_query, g_key, g_value, out_back, vector_share = last_exchange(
        order, base, tokens_t, g_qkv, w_t, part_out, vectors
    )
    vector_share = vector_share.reshape(512)
    grad_out = lax.ppermute(out_back, both, [(b, a) for a, b in spread])
    cuts = (0, rows_w, 2 * rows_w, 3 * rows_w, 3 * rows_w + ff_rows, 3 * rows_w + 2 * ff_rows)
    v = [vector_share[a:b] for a, b in zip(cuts, cuts[1:])]
    return (
        out_states,
        vector_share[-1] / valid_count,
        grad_states,
        g_query,
        g_key,
        g_value,
        grad_out,
        grad_up,
        grad_gate,
        grad_down,
        v[2],
        v[0],
        v[1],
        v[3],
        v[4],
    )


def solution(mesh):
    placed = (
        P(("dp", "fsdp"), None),
        P(("dp", "fsdp"), None),
        P("dp"),
        P(("dp", "fsdp")),
        P(("dp", "fsdp"), None),
        P(("dp", "fsdp"), None),
        P(("dp", "fsdp"), None),
        P(("dp", "fsdp"), None),
        P(("dp", "fsdp"), None),
        P(("dp", "fsdp"), None),
        P(("dp", "fsdp"), None),
        P(("dp", "fsdp")),
        P(("dp", "fsdp")),
        P(("dp", "fsdp")),
        P(("dp", "fsdp")),
        P(("dp", "fsdp")),
    )
    quick = mesh.shape["fsdp"] == 4 and mesh.shape["dp"] == 8
    return jax.shard_map(
        local if quick else general,
        mesh=mesh,
        in_specs=placed,
        out_specs=(
            P(("dp", "fsdp"), None),
            P(),
            P(("dp", "fsdp"), None),
            P(("dp", "fsdp"), None),
            P(("dp", "fsdp"), None),
            P(("dp", "fsdp"), None),
            P(("dp", "fsdp"), None),
            P(("dp", "fsdp"), None),
            P(("dp", "fsdp"), None),
            P(("dp", "fsdp"), None),
            P(("dp", "fsdp")),
            P(("dp", "fsdp")),
            P(("dp", "fsdp")),
            P(("dp", "fsdp")),
            P(("dp", "fsdp")),
        ),
        check_vma=False,
    )
```

```python
import functools
import math

import jax
import jax.numpy as jnp
from jax import lax
from jax.experimental import pallas as pl
from jax.experimental.pallas import tpu as pltpu
from jax.sharding import PartitionSpec as P


D = 1280
HEADS = 20
HEAD_DIM = 64
FF = 5120
BLOCK = 128
DEPTH = 10


EPS = 1e-06


def unit_rows(vector):
    inverse = lax.rsqrt(jnp.sum(vector * vector, axis=-1, keepdims=True) + EPS)
    return (vector * inverse, inverse)


def unit_back(grad, unit, inverse):
    return (grad - unit * jnp.sum(grad * unit, axis=-1, keepdims=True)) * inverse


def project(left, right):
    return jnp.dot(left, right, preferred_element_type=jnp.float32)


def project_back(grad, weight):
    return jnp.einsum("te,de->td", grad, weight, preferred_element_type=jnp.float32)


def ancestors(local_parent):
    column = jnp.arange(local_parent.shape[0], dtype=jnp.int32)
    columns = [column]
    for depth_step in range(DEPTH - 1):
        column = jnp.where(column >= 0, local_parent[jnp.maximum(column, 0)], -1)
        columns.append(column)
    return jnp.stack(columns, axis=1)


def head_back(grad_flat, unit, inverse, scale):
    scaled = (grad_flat * scale).reshape(unit.shape)
    raw = unit_back(scaled, unit, inverse).reshape(grad_flat.shape)
    scale_grad = jnp.sum(grad_flat * unit.reshape(grad_flat.shape), axis=0)
    return (raw, scale_grad)


def general(
    states,
    teacher,
    parent_ids,
    valid_mask,
    w_query,
    w_key,
    w_value,
    w_out,
    w_up,
    w_gate,
    w_down,
    qk_scale,
    attn_rate,
    mlp_rate,
    up_scale,
    gate_scale,
):
    rows_dev = states.shape[0]
    blocks_dev = rows_dev // BLOCK
    width_rows = w_query.shape[0]
    span = DEPTH * BLOCK
    factor = math.sqrt(HEAD_DIM)
    root_width = math.sqrt(D)
    mask_f = valid_mask.astype(jnp.float32)
    qkv_local = jnp.concatenate((w_query, w_key, w_value), axis=1)
    scal_width_local = jnp.stack((qk_scale, attn_rate, mlp_rate), axis=1)
    piece_qkv = lax.all_gather(qkv_local, ("dp", "fsdp"), axis=0, tiled=True)
    piece_out = lax.all_gather(w_out, ("dp", "fsdp"), axis=0, tiled=True)
    piece_scal = lax.all_gather(scal_width_local, ("dp", "fsdp"), axis=0, tiled=True)
    lefts = states
    total = jnp.dot(lefts, piece_qkv, preferred_element_type=jnp.float32)
    scal_whole = piece_scal
    qkv_raw = total
    scal_width = scal_whole
    scale_qk = scal_width[:, 0].astype(jnp.float32)
    rate_attn = scal_width[:, 1].astype(jnp.float32)
    rate_mlp = scal_width[:, 2].astype(jnp.float32)
    query_raw = qkv_raw[:, :D]
    key_raw = qkv_raw[:, D : 2 * D]
    values = qkv_raw[:, 2 * D :].astype(jnp.bfloat16)
    query_unit, query_inv = unit_rows(query_raw.reshape(rows_dev, HEADS, HEAD_DIM))
    key_unit, key_inv = unit_rows(key_raw.reshape(rows_dev, HEADS, HEAD_DIM))
    query_n = (query_unit.reshape(rows_dev, D) * scale_qk).astype(jnp.bfloat16)
    key_n = (key_unit.reshape(rows_dev, D) * scale_qk).astype(jnp.bfloat16)
    key_group, value_group = (
        lax.all_gather(key_n, "fsdp", axis=0, tiled=True),
        lax.all_gather(values, "fsdp", axis=0, tiled=True),
    )
    group_blocks = parent_ids.shape[0]
    group_base = lax.axis_index("dp") * group_blocks
    local_parent = jnp.where(parent_ids >= 0, parent_ids - group_base, -1)
    paths_all = ancestors(local_parent)
    own_first = lax.axis_index("fsdp") * blocks_dev
    paths = lax.dynamic_slice_in_dim(paths_all, own_first, blocks_dev, 0)
    safe_paths = jnp.maximum(paths, 0)
    key_rows = key_group.reshape(group_blocks, BLOCK, D)[safe_paths].reshape(
        blocks_dev, span, HEADS, HEAD_DIM
    )
    value_rows = value_group.reshape(group_blocks, BLOCK, D)[safe_paths].reshape(
        blocks_dev, span, HEADS, HEAD_DIM
    )
    slot_of = jnp.arange(span, dtype=jnp.int32) // BLOCK
    offset = jnp.arange(span, dtype=jnp.int32) % BLOCK
    row_pos = jnp.arange(BLOCK, dtype=jnp.int32)
    causal = offset[None, :] <= row_pos[:, None]
    is_live = jnp.take(paths, slot_of, axis=1) >= 0
    allowed = jnp.where(slot_of[None, None, :] == 0, causal[None], is_live[:, None, :])[:, None]
    query_heads = query_n.reshape(blocks_dev, BLOCK, HEADS, HEAD_DIM)
    scores = factor * jnp.einsum(
        "bqhd,bkhd->bhqk", query_heads, key_rows, preferred_element_type=jnp.float32
    )
    scores = jnp.where(allowed, scores, jnp.float32(-1e30))
    row_max = jnp.max(scores, axis=-1, keepdims=True)
    powers = jnp.exp(scores - row_max)
    row_sum = jnp.sum(powers, axis=-1, keepdims=True)
    probs_b = (powers / row_sum).astype(jnp.bfloat16)
    log_total = row_max + jnp.log(row_sum)
    mixed = jnp.einsum("bhqk,bkhd->bqhd", probs_b, value_rows, preferred_element_type=jnp.float32)
    mixed = mixed.reshape(rows_dev, D).astype(jnp.bfloat16)
    inputs = states.astype(jnp.float32)
    attn = project(mixed, piece_out)
    attn_unit, attn_inv = unit_rows(attn)
    hidden, hidden_inv = unit_rows(inputs + rate_attn * (attn_unit - inputs))
    hidden_b = hidden.astype(jnp.bfloat16)
    ffn_local = jnp.concatenate((w_up, w_gate), axis=1)
    scal_hidden_local = jnp.concatenate(
        (up_scale.reshape(width_rows, 4), gate_scale.reshape(width_rows, 4)), axis=1
    )
    piece_ffn = lax.all_gather(ffn_local, ("dp", "fsdp"), axis=0, tiled=True)
    piece_scal = lax.all_gather(scal_hidden_local, ("dp", "fsdp"), axis=0, tiled=True)
    lefts = hidden_b
    total = jnp.dot(lefts, piece_ffn, preferred_element_type=jnp.float32)
    scal_whole = piece_scal
    scale_up = scal_whole[:, :4].reshape(FF).astype(jnp.float32)
    scale_gate = scal_whole[:, 4:].reshape(FF).astype(jnp.float32)
    up_proj = total[:, :FF]
    gate_proj = total[:, FF:]
    upscaled = up_proj * scale_up
    gated = gate_proj * scale_gate * root_width
    sigmoid_gate = jax.nn.sigmoid(gated)
    act = (upscaled * (gated * sigmoid_gate)).astype(jnp.bfloat16)
    lefts = act
    down = jnp.dot(
        lefts,
        lax.all_gather(w_down, ("dp", "fsdp"), axis=0, tiled=True),
        preferred_element_type=jnp.float32,
    )
    down_unit, down_inv = unit_rows(down)
    result, result_inv = unit_rows(hidden + rate_mlp * (down_unit - hidden))
    loss_local = jnp.sum(mask_f[:, None] * (result - teacher) ** 2)
    valid_count, loss_sum = lax.psum((jnp.sum(mask_f), loss_local), ("dp", "fsdp"))
    loss = loss_sum / valid_count
    g_result = 2.0 * mask_f[:, None] * (result - teacher) / valid_count
    g_last = unit_back(g_result, result, result_inv)
    g_hidden = g_last * (1.0 - rate_mlp)
    g_rate_mlp = jnp.sum(g_last * (down_unit - hidden), axis=0)
    g_down = unit_back(g_last * rate_mlp, down_unit, down_inv).astype(jnp.bfloat16)
    g_act = jnp.einsum(
        "te,fe->tf",
        g_down,
        lax.all_gather(w_down, ("dp", "fsdp"), axis=0, tiled=True),
        preferred_element_type=jnp.float32,
    )
    g_upscaled = g_act * (gated * sigmoid_gate)
    g_gated = g_act * upscaled * sigmoid_gate * (1.0 + gated * (1.0 - sigmoid_gate))
    grad_up_scale = jnp.sum(g_upscaled * up_proj, axis=0)
    grad_gate_scale = jnp.sum(g_gated * gate_proj * root_width, axis=0)
    g_up = (g_upscaled * scale_up).astype(jnp.bfloat16)
    g_gate = (g_gated * scale_gate * root_width).astype(jnp.bfloat16)
    g_both = jnp.concatenate((g_up, g_gate), axis=1)
    g_hidden = g_hidden + jnp.einsum(
        "tc,dc->td",
        g_both,
        lax.all_gather(ffn_local, ("dp", "fsdp"), axis=0, tiled=True),
        preferred_element_type=jnp.float32,
    )
    scal_terms = jnp.concatenate(
        (grad_up_scale.reshape(D, 4), grad_gate_scale.reshape(D, 4)), axis=1
    )
    lefts = hidden_b
    main = jnp.einsum("td,tc->dc", lefts, g_both, preferred_element_type=jnp.float32)
    ffn_share = lax.psum_scatter(
        jnp.concatenate((main, scal_terms), axis=1), ("dp", "fsdp"), scatter_dimension=0, tiled=True
    )
    lefts = act
    grad_down = lax.psum_scatter(
        jnp.einsum("tf,te->fe", lefts, g_down, preferred_element_type=jnp.float32),
        ("dp", "fsdp"),
        scatter_dimension=0,
        tiled=True,
    )
    g_pre = unit_back(g_hidden, hidden, hidden_inv)
    g_states = g_pre * (1.0 - rate_attn)
    g_rate_attn = jnp.sum(g_pre * (attn_unit - inputs), axis=0)
    g_attn = unit_back(g_pre * rate_attn, attn_unit, attn_inv).astype(jnp.bfloat16)
    g_mixed = project_back(g_attn, piece_out).astype(jnp.bfloat16)
    scores = factor * jnp.einsum(
        "bqhd,bkhd->bhqk", query_heads, key_rows, preferred_element_type=jnp.float32
    )
    probs = jnp.where(allowed, jnp.exp(scores - log_total), jnp.float32(0.0))
    probs_again = probs.astype(jnp.bfloat16)
    g_heads = g_mixed.reshape(blocks_dev, BLOCK, HEADS, HEAD_DIM)
    g_probs = jnp.einsum("bqhd,bkhd->bhqk", g_heads, value_rows, preferred_element_type=jnp.float32)
    delta = jnp.sum(probs * g_probs, axis=-1, keepdims=True)
    g_scores = (probs * (g_probs - delta)).astype(jnp.bfloat16)
    g_query_n = factor * jnp.einsum(
        "bhqk,bkhd->bqhd", g_scores, key_rows, preferred_element_type=jnp.float32
    )
    g_key_rows = factor * jnp.einsum(
        "bhqk,bqhd->bkhd", g_scores, query_heads, preferred_element_type=jnp.float32
    )
    g_value_rows = jnp.einsum(
        "bhqk,bqhd->bkhd", probs_again, g_heads, preferred_element_type=jnp.float32
    )
    flat_paths = safe_paths.reshape(blocks_dev * DEPTH)
    g_key_group = (
        jnp.zeros((group_blocks, BLOCK, D), jnp.float32)
        .at[flat_paths]
        .add(g_key_rows.reshape(blocks_dev * DEPTH, BLOCK, D))
    )
    g_value_group = (
        jnp.zeros((group_blocks, BLOCK, D), jnp.float32)
        .at[flat_paths]
        .add(g_value_rows.reshape(blocks_dev * DEPTH, BLOCK, D))
    )
    g_key_n, g_values = (
        lax.psum_scatter(
            g_key_group.reshape(group_blocks * BLOCK, D).astype(jnp.bfloat16),
            "fsdp",
            scatter_dimension=0,
            tiled=True,
        ).astype(jnp.float32),
        lax.psum_scatter(
            g_value_group.reshape(group_blocks * BLOCK, D).astype(jnp.bfloat16),
            "fsdp",
            scatter_dimension=0,
            tiled=True,
        ).astype(jnp.float32),
    )
    g_query_raw, scale_from_query = head_back(
        g_query_n.reshape(rows_dev, D), query_unit, query_inv, scale_qk
    )
    g_key_raw, scale_from_key = head_back(g_key_n, key_unit, key_inv, scale_qk)
    grad_qk_scale = scale_from_query + scale_from_key
    g_qkv = jnp.concatenate(
        (
            g_query_raw.astype(jnp.bfloat16),
            g_key_raw.astype(jnp.bfloat16),
            g_values.astype(jnp.bfloat16),
        ),
        axis=1,
    )
    g_states = g_states + jnp.einsum(
        "tc,dc->td",
        g_qkv,
        lax.all_gather(qkv_local, ("dp", "fsdp"), axis=0, tiled=True),
        preferred_element_type=jnp.float32,
    )
    vector_terms = jnp.stack((grad_qk_scale, g_rate_attn, g_rate_mlp), axis=1)
    lefts = states
    main = jnp.einsum("td,tc->dc", lefts, g_qkv, preferred_element_type=jnp.float32)
    outer = jnp.einsum("td,tc->dc", mixed, g_attn, preferred_element_type=jnp.float32)
    attn_share = lax.psum_scatter(
        jnp.concatenate((main, outer, vector_terms), axis=1),
        ("dp", "fsdp"),
        scatter_dimension=0,
        tiled=True,
    )
    return (
        result.astype(jnp.bfloat16),
        loss,
        g_states,
        attn_share[:, :D],
        attn_share[:, D : 2 * D],
        attn_share[:, 2 * D : 3 * D],
        attn_share[:, 3 * D : 4 * D],
        ffn_share[:, :FF],
        ffn_share[:, FF : 2 * FF],
        grad_down,
        attn_share[:, 4 * D],
        attn_share[:, 4 * D + 1],
        attn_share[:, 4 * D + 2],
        ffn_share[:, 2 * FF : 2 * FF + 4].reshape(-1),
        ffn_share[:, 2 * FF + 4 : 2 * FF + 8].reshape(-1),
    )

TRUNK = 8
NB = 20
TOK = NB * BLOCK
F32 = jnp.float32
BF = jnp.bfloat16


def head_norm(raw):
    inv = lax.rsqrt(jnp.sum(raw * raw, axis=0, keepdims=True) + EPS)
    return raw * inv, inv


def lanes_at(start, size):
    return pl.ds(pl.multiple_of(start, 128), size)


def rows_at(start, size):
    return pl.ds(pl.multiple_of(start, 16), size)


def early_chunks(visit):
    for j in range(TRUNK // 2):
        parts = [(0, 256 * j, "all")] if j else []
        visit(256 * j, parts + [(256 * j, 256, "causal")])
    trunk = TRUNK * BLOCK
    for start in (trunk, trunk + 256):
        visit(start, [(0, trunk, "all"), (start, 256, "pair")])


def late_chunks(visit):
    trunk = TRUNK * BLOCK
    for j in range(4):
        start = trunk + 4 * BLOCK + 256 * j
        visit(start, [(0, trunk, "all"), (trunk + BLOCK * j, BLOCK, "all"), (start, 256, "pair")])


def masked(kind, value):
    if kind == "all":
        return value
    key = lax.broadcasted_iota(jnp.int32, (256, 256), 0)
    query = lax.broadcasted_iota(jnp.int32, (256, 256), 1)
    keep = key <= query
    if kind == "pair":
        keep = keep & ((key < 128) == (query < 128))
    return jnp.where(keep, value, jnp.zeros_like(value))


def nn(a, b):
    return lax.dot_general(a, b, (((1,), (0,)), ((), ())), preferred_element_type=F32)


def nt(a, b):
    return lax.dot_general(a, b, (((1,), (1,)), ((), ())), preferred_element_type=F32)


def attention_back_kernel(order, qkv, scales, sums, mixed, ga_all, w_o, ht_all, gug_all,
                          g_qkv, g_scale, part_out, g_up, g_gate,
                          w_b, ga_b, ga, gm, raw, out_b, qT, q, k, kT, v, gT, g, dq, dk, dv, delta, inv,
                          gug_b, ht_r, ht_l, ring, own, hid_buf, hid_in,
                          ga_sem, gug_sem, row_sem, raw_sem, out_sem, ring_send, ring_recv, a2a_send, a2a_recv):
    me = lax.axis_index("fsdp")
    place = ring_place()
    peers = group_peers()
    right, left = {"dp": ring_dp(place + 1)}, {"dp": ring_dp(place - 1)}
    count, chunk, side = gug_b.shape[0], ring.shape[3], ring.shape[4]
    heads = g_scale.shape[0]
    rows_w = hid_buf.shape[1]

    def slices(step):
        slot = step % 2
        cut_r = rows_at(ring_dp(place - 1 - step) * chunk, chunk)
        cut_l = rows_at(ring_dp(place + 1 + step) * chunk, chunk)
        return [
            pltpu.make_async_copy(ht_all.at[:, cut_r], ht_r.at[slot], row_sem.at[0, slot]),
            pltpu.make_async_copy(ht_all.at[:, cut_l], ht_l.at[slot], row_sem.at[1, slot]),
        ]

    def raw_copy(head):
        slot = head % 2
        return pltpu.make_async_copy(
            qkv.at[:, rows_at(head * HEAD_DIM, HEAD_DIM)], raw.at[slot], raw_sem.at[slot]
        )

    def out_copy(head):
        slot = head % 2
        return pltpu.make_async_copy(
            out_b.at[slot], g_qkv.at[:, rows_at(head * HEAD_DIM, HEAD_DIM)], out_sem.at[slot]
        )

    load_ga = pltpu.make_async_copy(ga_all, ga_b, ga_sem.at[0])
    load_ga.start()
    load_w = pltpu.make_async_copy(w_o.at[0], w_b, ga_sem.at[1])
    load_w.start()
    raw_copy(0).start()
    for copy in slices(0):
        copy.start()
    loads = [pltpu.make_async_copy(gug_all.at[i], gug_b.at[i], gug_sem.at[i]) for i in range(count)]
    for copy in loads:
        copy.start()
    for copy in slices(1):
        copy.start()
    greet([*peers, right, left])
    load_ga.wait()
    load_w.wait()

    def pick(i, carry):
        ga[lanes_at(i * BLOCK, BLOCK)] = ga_b[order[0, i]]
        return carry

    lax.fori_loop(0, NB, pick, 0)

    def back(n, carry):
        gm[:, tile(n)] = nt(w_b[...], ga[tile(n)]).astype(BF)
        return carry

    lax.fori_loop(0, TOK // TILE, back, 0)

    def outer(n, carry):
        part_out[:, tile(n)] = nn(mixed[...], ga[:, tile(n)]).astype(BF)
        return carry

    lax.fori_loop(0, D // TILE, outer, 0)

    def parts(step, which):
        slot = step % 2

        @pl.when(which == 0)
        def _():
            for copy in slices(step):
                copy.wait()

        own[...] = jnp.zeros_like(own)

        def add(i, carry):
            for d, rows in enumerate((ht_r, ht_l)):
                cut = lanes_at((2 * d + which) * side, side)
                own[d] = own[d] + nn(rows[slot, i], gug_b[i, :, cut])
            return carry

        lax.fori_loop(0, count, add, 0)

        @pl.when((which == 1) & (step + 2 < 8))
        def _():
            for copy in slices(step + 2):
                copy.start()

    def hop_copies(step, which):
        return [
            send(ring.at[d, which, step], ring.at[d, which, step + 1], ring_send.at[d, which, step],
                 ring_recv.at[d, which, step], peer)
            for d, peer in enumerate((right, left))
        ]

    def exchange():
        return [
            send(hid_buf.at[peer["fsdp"]], hid_in.at[me], a2a_send.at[i], a2a_recv.at[i], peer)
            for i, peer in enumerate(peers)
        ]

    def poll(index):
        step, which = index // 2, index % 2
        parts(step + 1, which)
        for copy in hop_copies(step, which):
            copy.wait()

        @pl.when(step < 6)
        def _():
            for d in range(2):
                ring[d, which, step + 1] = (ring[d, which, step + 1].astype(F32) + own[d]).astype(BF)
            for copy in hop_copies(step + 1, which):
                copy.start()

        @pl.when(step == 6)
        def _():
            for d in range(2):
                total = ring[d, which, 7].astype(F32) + own[d]
                for i in range(4):
                    hid_buf[i, :, lanes_at((2 * d + which) * side, side)] = total[
                        i * rows_w : (i + 1) * rows_w
                    ].astype(BF)

        @pl.when(index == 13)
        def _():
            for copy in exchange():
                copy.start()

    for copy in loads:
        copy.wait()

    def begin(which, carry):
        parts(0, which)
        for d in range(2):
            ring[d, which, 0] = own[d].astype(BF)
        for copy in hop_copies(0, which):
            copy.start()
        return carry

    lax.fori_loop(0, 2, begin, 0)

    def open_head(head):
        slot = head % 2
        raw_copy(head).wait()

        @pl.when(head + 1 < heads)
        def _():
            raw_copy(head + 1).start()

        @pl.when(head >= 2)
        def _():
            out_copy(head - 2).wait()

        scale = scales[head]
        mine = rows_at(head * HEAD_DIM, HEAD_DIM)

        for i in range(NB):
            here = slice(i * BLOCK, (i + 1) * BLOCK)
            q_unit, _ = head_norm(raw[slot, 0, :, here])
            k_unit, _ = head_norm(raw[slot, 1, :, here])
            q8 = (q_unit * scale).astype(BF) * BF(8.0)
            qT[:, here] = q8
            q[here, :] = q8.T
            kn = (k_unit * scale).astype(BF)
            kT[:, here] = kn
            k[here, :] = kn.T
            v[here, :] = raw[slot, 2, :, here].astype(BF).T
            gh = gm[mine, here]
            gT[:, here] = gh
            g[here, :] = gh.T
            delta[:, here] = jnp.sum(gh.astype(F32) * mixed[mine, here].astype(F32), axis=0, keepdims=True)
            inv[:, here] = sums[head, 0:1, here]
        dk[...] = jnp.zeros_like(dk)
        dv[...] = jnp.zeros_like(dv)

    def visit(start, pieces):
        span = lanes_at(start, 256)
        query, grad = qT[:, span], gT[:, span]
        query_rows, grad_rows = q[span, :], g[span, :]
        scale_row, delta_row = inv[:, span], delta[:, span]
        acc = jnp.zeros((64, 256), F32)
        for kstart, size, kind in pieces:
            keys = lanes_at(kstart, size)
            probs = masked(kind, jnp.exp(nn(k[keys, :], query)) * scale_row)
            g_probs = nn(v[keys, :], grad)
            g_scores = (probs * (g_probs - delta_row)).astype(BF)
            dv[keys, :] += nn(probs.astype(BF), grad_rows)
            dk[keys, :] += nn(g_scores, query_rows)
            acc = acc + nn(kT[:, keys], g_scores)
        dq[:, span] = acc * 8.0


    def close_head(head):
        slot = head % 2
        scale = scales[head]
        total = jnp.zeros((64, BLOCK), F32)
        for i in range(NB):
            here = slice(i * BLOCK, (i + 1) * BLOCK)
            for which, grad in ((0, dq[:, here]), (1, dk[here, :].T)):
                unit, inverse = head_norm(raw[slot, which, :, here])
                total = total + grad * unit
                scaled = grad * scale
                value = (scaled - unit * jnp.sum(scaled * unit, axis=0, keepdims=True)) * inverse
                out_b[slot, which, :, here] = value.astype(BF)
            out_b[slot, 2, :, here] = dv[here, :].T.astype(BF)
        g_scale[head] = jnp.sum(total, axis=1, keepdims=True)
        out_copy(head).start()

    def work(i, carry):
        head, segment = i // 4, i % 4
        pl.when(segment == 0)(functools.partial(open_head, head))
        pl.when(segment == 1)(functools.partial(early_chunks, visit))
        pl.when(segment == 2)(functools.partial(late_chunks, visit))
        pl.when(segment == 3)(functools.partial(close_head, head))
        pl.when(i < 14)(functools.partial(poll, i))
        return carry

    lax.fori_loop(0, 4 * heads, work, 0)
    for copy in exchange():
        copy.wait()
    hid_in[me] = hid_buf[me]
    size = g_up.shape[1] // 32
    for which, out in enumerate((g_up, g_gate)):
        for d in range(8):
            start = (8 * which + d) * size
            block = [hid_in[i, :, start : start + size].astype(F32) for i in range(4)]
            out[:, d * 4 * size : (d + 1) * 4 * size] = jnp.concatenate(block, axis=1)
    for head in (heads - 2, heads - 1):
        out_copy(head).wait()


def attention_back(order, qkv, scales, sums, mixed, ga_all, w_o, ht_all, gug_all):
    heads = scales.shape[0]
    count, tokens, hidden_width = gug_all.shape
    chunk = ht_all.shape[1] // 8
    side = hidden_width // 4
    rows_w = chunk // 4
    vmem, hbm = pl.BlockSpec(memory_space=pltpu.VMEM), pl.BlockSpec(memory_space=pl.ANY)
    smem = pl.BlockSpec(memory_space=pltpu.SMEM)
    dma = pltpu.SemaphoreType.DMA
    return pl.pallas_call(
        attention_back_kernel,
        in_specs=[smem, hbm, vmem, vmem, vmem, hbm, hbm, hbm, hbm],
        out_specs=[hbm, vmem, vmem, vmem, vmem],
        out_shape=[
            jax.ShapeDtypeStruct(qkv.shape, BF),
            jax.ShapeDtypeStruct(scales.shape, F32),
            jax.ShapeDtypeStruct(w_o.shape[1:], BF),
            jax.ShapeDtypeStruct((rows_w, 2 * hidden_width), F32),
            jax.ShapeDtypeStruct((rows_w, 2 * hidden_width), F32),
        ],
        scratch_shapes=[
            pltpu.VMEM(w_o.shape[1:], BF),
            pltpu.VMEM(ga_all.shape, BF),
            pltpu.VMEM((TOK, w_o.shape[2]), BF),
            pltpu.VMEM(mixed.shape, BF),
            pltpu.VMEM((2, 3, HEAD_DIM, TOK), F32),
            pltpu.VMEM((2, 3, HEAD_DIM, TOK), BF),
            pltpu.VMEM((HEAD_DIM, TOK), BF),
            pltpu.VMEM((TOK, HEAD_DIM), BF),
            pltpu.VMEM((TOK, HEAD_DIM), BF),
            pltpu.VMEM((HEAD_DIM, TOK), BF),
            pltpu.VMEM((TOK, HEAD_DIM), BF),
            pltpu.VMEM((HEAD_DIM, TOK), BF),
            pltpu.VMEM((TOK, HEAD_DIM), BF),
            pltpu.VMEM((HEAD_DIM, TOK), F32),
            pltpu.VMEM((TOK, HEAD_DIM), F32),
            pltpu.VMEM((TOK, HEAD_DIM), F32),
            pltpu.VMEM((1, TOK), F32),
            pltpu.VMEM((1, TOK), F32),
            pltpu.VMEM(gug_all.shape, BF),
            pltpu.VMEM((2, count, chunk, tokens), BF),
            pltpu.VMEM((2, count, chunk, tokens), BF),
            pltpu.VMEM((2, 2, 8, chunk, side), BF),
            pltpu.VMEM((2, chunk, side), F32),
            pltpu.VMEM((4, rows_w, hidden_width), BF),
            pltpu.VMEM((4, rows_w, hidden_width), BF),
            dma((2,)),
            dma((count,)),
            dma((2, 2)),
            dma((2,)),
            dma((2,)),
            dma((2, 2, 7)),
            dma((2, 2, 7)),
            dma((3,)),
            dma((3,)),
        ],
        compiler_params=pltpu.CompilerParams(
            collective_id=5, has_side_effects=True, vmem_limit_bytes=62 << 20
        ),
        name="attention_back",
        cost_estimate=pl.CostEstimate(flops=40 * 10**9, bytes_accessed=60 << 20, transcendentals=14 << 20),
    )(order, qkv, scales, sums, mixed, ga_all, w_o, ht_all, gug_all)


MESH = pl.DeviceIdType.MESH


def ring_place():
    dp = lax.axis_index("dp")
    z, y = dp // 2, dp % 2
    return z + y * (7 - 2 * z)


def ring_dp(place):
    place = (place + 16) % 8
    y = place // 4
    return 2 * (place + y * (7 - 2 * place)) + y


def greet(peers):
    barrier = pltpu.get_barrier_semaphore()
    for peer in peers:
        pl.semaphore_signal(barrier, inc=1, device_id=peer, device_id_type=MESH)
    pl.semaphore_wait(barrier, len(peers))


def group_peers():
    me = lax.axis_index("fsdp")
    core = 1 - 2 * (me % 2)
    chip = 2 - 4 * (me // 2)
    return {"fsdp": me + core}, {"fsdp": me + chip}, {"fsdp": me + core + chip}


def send(src, dst, send_sem, recv_sem, peer):
    return pltpu.make_async_remote_copy(
        src_ref=src, dst_ref=dst, send_sem=send_sem, recv_sem=recv_sem, device_id=peer, device_id_type=MESH
    )


EARLY_HOPS = 5


def hidden_ring(ref, sends, recvs, step, base=0):
    place = ring_place()
    right, left = {"dp": ring_dp(place + 1)}, {"dp": ring_dp(place - 1)}
    chunk = ref.shape[0] // 8
    to_right, to_left = ring_dp(place - step) * chunk, ring_dp(place + step) * chunk
    first, size = 48, chunk // 2
    cuts = ((to_right, first, right), (to_left + size, first, left),
            (to_right + first, size - first, right), (to_left + size + first, size - first, left))
    return [
        send(ref.at[rows_at(start, rows)], ref.at[rows_at(start, rows)], sends.at[i, step - base],
             recvs.at[i, step - base], peer)
        for i, (start, rows, peer) in enumerate(cuts)
    ]


def forward_kernel(order, states, w_query, w_key, w_value, small, extra, out_piece, w_up, w_gate,
                   tokens_t, w_t, w_o, w_ug, qkv, mixed, sums, mixed_n,
                   qkv_send, ug_send, land, weights, tok, turned, tok_t, out_w, ug_land, ug_own, raw, qs, ks, vs, blocks, natural,
                   tok_send, tok_recv, a2a_send, a2a_recv, ring_send, ring_recv, ug_s, ug_r, local_sem, raw_sem,
                   w_send, w_recv):
    me, dp = lax.axis_index("fsdp"), lax.axis_index("dp")
    place = ring_place()
    sibling, across, corner = group_peers()
    right, left = {"dp": ring_dp(place + 1)}, {"dp": ring_dp(place - 1)}
    rows, width = states.shape
    piece = land.shape[1]
    chunk = 4 * piece
    half = chunk // 2
    cols = mixed.shape[0]
    heads = cols // HEAD_DIM
    own = pltpu.make_async_copy(states, tok.at[pl.ds(0, rows)], local_sem.at[0])
    own.start()
    for i in range(4):
        cut = slice(i * cols, (i + 1) * cols)
        block = [w[:, cut].astype(F32) for w in (w_query, w_key, w_value)] + [small[...].astype(F32)]
        qkv_send[i] = jnp.concatenate(block, axis=1).astype(BF)
    greet([sibling, across, corner, right, left])

    exchange, ug_exchange = [], []
    for i, peer in enumerate((sibling, across, corner)):
        copy = send(qkv_send.at[peer["fsdp"]], land.at[me], a2a_send.at[i], a2a_recv.at[i], peer)
        copy.start()
        exchange.append(copy)
    far = []
    for i in range(2):
        part = pl.ds(i * (rows // 2), rows // 2)
        here = pl.ds(2 * rows + i * (rows // 2), rows // 2)
        copy = send(states.at[part], tok.at[here], tok_send.at[i], tok_recv.at[i], across)
        copy.start()
        far.append(copy)
    near = send(states, tok.at[pl.ds(rows, rows)], tok_send.at[2], tok_recv.at[2], sibling)
    near.start()
    size = w_up.shape[1] // 32
    for i in range(4):
        for which, w in enumerate((w_up, w_gate)):
            for half_d in range(2):
                block = [
                    w[:, (4 * d + i) * size : (4 * d + i + 1) * size].astype(F32)
                    for d in range(4 * half_d, 4 * half_d + 4)
                ]
                start = (8 * which + 4 * half_d) * size
                ug_send[i, :, start : start + 4 * size] = jnp.concatenate(block, axis=1).astype(BF)
    land[me] = qkv_send[me]
    ug_land[me] = ug_send[me]
    out_w[dp] = out_piece[...]
    vs[HEAD_DIM:, :] = jnp.ones((vs.shape[0] - HEAD_DIM, TOK), BF)
    for copy in exchange:
        copy.wait()
    weights[rows_at(dp * chunk, chunk)] = jnp.concatenate([land[i].astype(F32) for i in range(4)], axis=0).astype(BF)
    last = pl.ds(weights.shape[1] - 128, 128)
    weights[rows_at(dp * chunk, chunk), last] = weights[rows_at(dp * chunk, chunk), last] + extra[...]

    def ring_copies(step):
        to_right, to_left = ring_dp(place - step), ring_dp(place + step)
        first, second = rows_at(to_right * chunk, half), rows_at(to_left * chunk + half, half)
        lanes_r, lanes_l = pl.ds(0, width // 2), pl.ds(width // 2, width // 2)
        return [
            send(ref, ref, ring_send.at[i, step], ring_recv.at[i, step], peer)
            for i, (ref, peer) in enumerate(
                (
                    (weights.at[first], right),
                    (weights.at[second], left),
                    (out_w.at[to_right, :, lanes_r], right),
                    (out_w.at[to_left, :, lanes_l], left),
                )
            )
        ]

    def hop(step, carry):
        for copy, later in zip(ring_copies(step), ring_copies(step + 1)):
            copy.wait()
            pl.when(step < 6)(later.start)
        return carry

    def ug_poll(index):
        step = index // 2
        now, late = hidden_ring(w_ug, ug_s, ug_r, step), hidden_ring(w_ug, ug_s, ug_r, step + 1)

        def pass_on(first):
            for copy, later in zip(now[first : first + 2], late[first : first + 2]):
                copy.wait()
                pl.when(step < EARLY_HOPS - 1)(later.start)

        pl.when(index % 2 == 0)(functools.partial(pass_on, 0))
        pl.when(index % 2 == 1)(functools.partial(pass_on, 2))

    for copy in ring_copies(0):
        copy.start()

    def turn(i, carry):
        turned[i] = tok[lanes_at(i * BLOCK, BLOCK)].T
        return carry

    lax.fori_loop(0, 1, hop, 0)
    near.wait()
    own.wait()
    lax.fori_loop(0, 4, turn, 0)
    lax.fori_loop(1, 2, hop, 0)
    lax.fori_loop(4, 7, turn, 0)
    lax.fori_loop(2, 3, hop, 0)
    lax.fori_loop(7, 10, turn, 0)
    lax.fori_loop(3, 5, hop, 0)
    passed = []
    for i in range(2):
        far[i].wait()
        here = pl.ds(2 * rows + i * (rows // 2), rows // 2)
        there = pl.ds(3 * rows + i * (rows // 2), rows // 2)
        copy = send(tok.at[here], tok.at[there], tok_send.at[3 + i], tok_recv.at[3 + i], sibling)
        copy.start()
        passed.append(copy)
    for i, peer in enumerate((sibling, across, corner)):
        copy = send(ug_send.at[peer["fsdp"]], ug_land.at[me], a2a_send.at[3 + i], a2a_recv.at[3 + i], peer)
        copy.start()
        ug_exchange.append(copy)
    lax.fori_loop(5, 6, hop, 0)
    lax.fori_loop(10, 15, turn, 0)
    lax.fori_loop(6, 7, hop, 0)
    for copy in passed:
        copy.wait()

    lax.fori_loop(15, NB, turn, 0)

    def arrange(i, carry):
        tok_t[:, lanes_at(i * BLOCK, BLOCK)] = turned[order[0, i]]
        return carry

    lax.fori_loop(0, NB, arrange, 0)
    keep = pltpu.make_async_copy(tok_t, tokens_t, local_sem.at[2])
    keep.start()

    def turn_weights(i, carry):
        w_t[:, lanes_at(i * BLOCK, BLOCK)] = weights[rows_at(i * BLOCK, BLOCK)].T
        return carry

    lax.fori_loop(0, width // BLOCK, turn_weights, 0)
    for copy in ug_exchange:
        copy.wait()
    ug_own[...] = jnp.concatenate([ug_land[i].astype(F32) for i in range(4)], axis=0).astype(BF)
    ug_store = pltpu.make_async_copy(ug_own, w_ug.at[rows_at(dp * chunk, chunk)], local_sem.at[1])
    ug_store.start()
    ug_store.wait()
    for copy in hidden_ring(w_ug, ug_s, ug_r, 0):
        copy.start()
    w_o[0] = jnp.concatenate([out_w[i].astype(F32) for i in range(8)], axis=0).astype(BF)
    w_copies = [
        send(w_o.at[0], w_o.at[i + 1], w_send.at[i], w_recv.at[i], peer)
        for i, peer in enumerate((sibling, across, corner))
    ]
    for copy in w_copies:
        copy.start()

    def raw_copies(head):
        slot = head % 2
        return [
            pltpu.make_async_copy(
                raw.at[slot, pl.ds(which * HEAD_DIM, HEAD_DIM)],
                qkv.at[which, rows_at(head * HEAD_DIM, HEAD_DIM)],
                raw_sem.at[slot, which],
            )
            for which in range(3)
        ]

    def open_head(head):
        slot = head % 2

        @pl.when(head >= 2)
        def _():
            for copy in raw_copies(head - 2):
                copy.wait()

        left_rows = jnp.concatenate(
            [w_t[rows_at(which * cols + head * HEAD_DIM, HEAD_DIM)] for which in range(3)], axis=0
        )

        def project_tile(n, carry):
            raw[slot, :, tile(n)] = nn(left_rows, tok_t[:, tile(n)])
            return carry

        lax.fori_loop(0, TOK // TILE, project_tile, 0, unroll=2)
        for copy in raw_copies(head):
            copy.start()
        scale = weights[rows_at(me * cols + head * HEAD_DIM, HEAD_DIM), last][:, HEAD_DIM : HEAD_DIM + 1].astype(F32)

        def prepare(i, carry):
            here = lanes_at(i * BLOCK, BLOCK)
            q_unit, _ = head_norm(raw[slot, pl.ds(0, HEAD_DIM), here])
            k_unit, _ = head_norm(raw[slot, pl.ds(HEAD_DIM, HEAD_DIM), here])
            qs[:, here] = (q_unit * scale).astype(BF) * BF(8.0)
            ks[here, :] = (k_unit * scale).astype(BF).T
            vs[0:HEAD_DIM, here] = raw[slot, pl.ds(2 * HEAD_DIM, HEAD_DIM), here].astype(BF)
            return carry

        lax.fori_loop(0, NB, prepare, 0, unroll=NB)

    def visit(head, start, parts):
        span = lanes_at(start, 256)
        query = qs[:, span]
        acc = jnp.zeros((vs.shape[0], 256), F32)
        for kstart, count, kind in parts:
            keys = lanes_at(kstart, count)
            powers = masked(kind, jnp.exp(nn(ks[keys, :], query))).astype(BF)
            acc = acc + nn(vs[:, keys], powers)
        total = 1.0 / acc[HEAD_DIM : HEAD_DIM + 1, :]
        mixed[rows_at(head * HEAD_DIM, HEAD_DIM), span] = (acc[0:HEAD_DIM, :] * total).astype(BF)
        sums[head, :, span] = jnp.broadcast_to(total, (8, 256))

    def work(i, carry):
        head, segment = i // 3, i % 3
        pl.when(segment == 0)(functools.partial(open_head, head))
        pl.when(segment == 1)(lambda: early_chunks(functools.partial(visit, head)))
        pl.when(segment == 2)(lambda: late_chunks(functools.partial(visit, head)))
        pl.when(i % 2 == 1)(lambda: ug_poll(i // 2))
        return carry

    lax.fori_loop(0, 3 * heads, work, 0)

    def split(i, carry):
        blocks[i] = mixed[:, lanes_at(i * BLOCK, BLOCK)]
        return carry

    def arrange_back(i, carry):
        natural[i] = blocks[order[1, i]]
        return carry

    lax.fori_loop(0, NB, split, 0)
    lax.fori_loop(0, NB, arrange_back, 0)
    keep_mixed = pltpu.make_async_copy(natural, mixed_n, local_sem.at[3])
    keep_mixed.start()
    lax.fori_loop(3 * heads // 2, 2 * EARLY_HOPS, lambda index, c: (ug_poll(index), c)[1], 0)
    keep.wait()
    keep_mixed.wait()
    for copy in w_copies:
        copy.wait()
    for head in (heads - 2, heads - 1):
        for copy in raw_copies(head):
            copy.wait()


def forward(order, states, w_query, w_key, w_value, small, extra, out_piece, w_up, w_gate):
    tps, rows_w = 4, w_query.shape[0]
    tokens, width = states.shape
    packed = 3 * width // tps + small.shape[1]
    hidden_width = 2 * w_up.shape[1] // tps
    cols = 8 * rows_w
    vmem, hbm = pl.BlockSpec(memory_space=pltpu.VMEM), pl.BlockSpec(memory_space=pl.ANY)
    smem = pl.BlockSpec(memory_space=pltpu.SMEM)
    dma = pltpu.SemaphoreType.DMA
    return pl.pallas_call(
        forward_kernel,
        in_specs=[smem, hbm] + [vmem] * 8,
        out_specs=[hbm, vmem, vmem, hbm, hbm, vmem, vmem, hbm],
        out_shape=[
            jax.ShapeDtypeStruct((width, TOK), BF),
            jax.ShapeDtypeStruct((packed, width), BF),
            jax.ShapeDtypeStruct((tps, cols, width), BF),
            jax.ShapeDtypeStruct((width, hidden_width), BF),
            jax.ShapeDtypeStruct((3, cols, TOK), F32),
            jax.ShapeDtypeStruct((cols, TOK), BF),
            jax.ShapeDtypeStruct((cols // HEAD_DIM, 8, TOK), F32),
            jax.ShapeDtypeStruct((NB, cols, BLOCK), BF),
        ],
        scratch_shapes=[
            pltpu.VMEM((tps, rows_w, packed), BF),
            pltpu.VMEM((tps, rows_w, hidden_width), BF),
            pltpu.VMEM((tps, rows_w, packed), BF),
            pltpu.VMEM((width, packed), BF),
            pltpu.VMEM((TOK, width), BF),
            pltpu.VMEM((NB, width, BLOCK), BF),
            pltpu.VMEM((width, TOK), BF),
            pltpu.VMEM((8, rows_w, width), BF),
            pltpu.VMEM((tps, rows_w, hidden_width), BF),
            pltpu.VMEM((tps * rows_w, hidden_width), BF),
            pltpu.VMEM((2, 3 * HEAD_DIM, TOK), F32),
            pltpu.VMEM((HEAD_DIM, TOK), BF),
            pltpu.VMEM((TOK, HEAD_DIM), BF),
            pltpu.VMEM((HEAD_DIM + 16, TOK), BF),
            pltpu.VMEM((NB, cols, BLOCK), BF),
            pltpu.VMEM((NB, cols, BLOCK), BF),
            dma((5,)),
            dma((5,)),
            dma((6,)),
            dma((6,)),
            dma((4, 7)),
            dma((4, 7)),
            dma((4, EARLY_HOPS)),
            dma((4, EARLY_HOPS)),
            dma((4,)),
            dma((2, 3)),
            dma((3,)),
            dma((3,)),
        ],
        compiler_params=pltpu.CompilerParams(
            collective_id=1, has_side_effects=True, vmem_limit_bytes=56 << 20
        ),
        cost_estimate=pl.CostEstimate(flops=12 * 10**9, bytes_accessed=200 << 20, transcendentals=14 << 20),
        name="forward",
    )(order, states, w_query, w_key, w_value, small, extra, out_piece, w_up, w_gate)


def last_kernel(order, base, tokens_t, g_qkv, w_t, part_out, vectors,
                g_states, g_query, g_key, g_value, out_rows, vec_own,
                w_b, gq_b, blocks, tok_r, tok_l, share, turned, core_buf, x_buf, base_b, gs_b,
                ring_r, ring_m, ring_l, ring_o, ring_v, next_r, next_l, row_buf, row_in, vec_part, vec_in,
                in_sem, row_sem, base_sem, core_send, core_recv, x_send, x_recv,
                ring_send, ring_recv, a2a_send, a2a_recv):
    me, dp = lax.axis_index("fsdp"), lax.axis_index("dp")
    place = ring_place()
    sibling, across, corner = group_peers()
    right, left = {"dp": ring_dp(place + 1)}, {"dp": ring_dp(place - 1)}
    chunk, side, cut = ring_r.shape[1], next_r.shape[1], ring_r.shape[2]
    rows = share.shape[1]
    quarter = rows // 4
    width = w_t.shape[1]
    heads_width = gq_b.shape[0]
    rows_w = row_buf.shape[1]

    def slices(step):
        slot = step % 2
        cut_r = rows_at(ring_dp(place - 1 - step) * chunk, chunk)
        cut_l = rows_at(ring_dp(place + 1 + step) * chunk, chunk)
        return [
            pltpu.make_async_copy(tokens_t.at[cut_r], tok_r.at[slot], row_sem.at[0, slot]),
            pltpu.make_async_copy(tokens_t.at[cut_l], tok_l.at[slot], row_sem.at[1, slot]),
        ]

    def base_copy(i):
        return pltpu.make_async_copy(base.at[pl.ds(i * quarter, quarter)], base_b.at[i % 2], base_sem.at[0, i % 2])

    def gs_copy(i):
        return pltpu.make_async_copy(gs_b.at[i % 2], g_states.at[pl.ds(i * quarter, quarter)], base_sem.at[1, i % 2])

    load_q = pltpu.make_async_copy(g_qkv, gq_b, in_sem.at[0])
    load_q.start()
    load_w = pltpu.make_async_copy(w_t.at[pl.ds(0, g_qkv.shape[0])], w_b, in_sem.at[1])
    for step in (0, 1):
        for copy in slices(step):
            copy.start()
    load_w.start()
    greet([sibling, across, corner, right, left])

    def parts(step):
        slot = step % 2
        for copy in slices(step):
            copy.wait()
        next_r[...] = nt(tok_r[slot], gq_b[pl.ds(0, side)])
        next_l[...] = nt(tok_l[slot], gq_b[pl.ds(side, heads_width - side)])

        @pl.when(step + 2 < 8)
        def _():
            for copy in slices(step + 2):
                copy.start()

    def hop_copies(step):
        return [
            send(ring.at[step], ring.at[step + 1], ring_send.at[i, step], ring_recv.at[i, step], peer)
            for i, (ring, peer) in enumerate(
                ((ring_r, right), (ring_l, left), (ring_m, right), (ring_o, left), (ring_v, right))
            )
        ]

    def through(r, slot):
        for i in range(rows // BLOCK):
            turned[i * BLOCK : (i + 1) * BLOCK] = blocks[order[1, r * (rows // BLOCK) + i]].T

        def one(n, carry):
            share[slot, :, tile(n)] = nn(turned[...], w_b[:, tile(n)]).astype(BF)
            return carry

        lax.fori_loop(0, width // TILE, one, 0)

    core = [
        send(share.at[0], core_buf.at[0], core_send.at[0], core_recv.at[0], sibling),
        send(share.at[2], core_buf.at[1], core_send.at[1], core_recv.at[1], sibling),
    ]
    far = [
        send(share.at[1, pl.ds(i * quarter, quarter)], x_buf.at[pl.ds(i * quarter, quarter)], x_send.at[i],
             x_recv.at[i], across)
        for i in range(4)
    ]
    load_q.wait()

    def split(i, carry):
        blocks[i] = gq_b[:, lanes_at(i * BLOCK, BLOCK)]
        return carry

    def hop(step, carry):
        parts(step)

        @pl.when(step == 0)
        def _():
            ring_r[0] = next_r[:, :cut].astype(BF)
            ring_m[0] = next_r[:, cut:].astype(BF)
            ring_l[0] = next_l[...].astype(BF)
            ring_o[0] = part_out[ring_dp(place + 1)]
            ring_v[0] = vectors[ring_dp(place - 1)]

        @pl.when(step > 0)
        def _():
            before, now = hop_copies(step - 1), hop_copies(step)
            before[0].wait()
            ring_r[step] = (ring_r[step].astype(F32) + next_r[:, :cut]).astype(BF)
            now[0].start()
            before[1].wait()
            ring_l[step] = (ring_l[step].astype(F32) + next_l[...]).astype(BF)
            now[1].start()
            before[2].wait()
            ring_m[step] = (ring_m[step].astype(F32) + next_r[:, cut:]).astype(BF)
            now[2].start()
            before[3].wait()
            ring_o[step] = (ring_o[step].astype(F32) + part_out[ring_dp(place + 1 + step)].astype(F32)).astype(BF)
            now[3].start()
            before[4].wait()
            ring_v[step] = ring_v[step] + vectors[ring_dp(place - 1 - step)]
            now[4].start()

        @pl.when(step == 0)
        def _():
            for copy in hop_copies(0):
                copy.start()

        @pl.when(step < 4)
        def _():
            @pl.when(step == 0)
            def _():
                lax.fori_loop(0, NB, split, 0)
                load_w.wait()
                through(3, 0)
                core[0].start()

            @pl.when(step < 3)
            def _():
                through(2 - step, (step + 1) % 3)

            @pl.when(step == 0)
            def _():
                core[0].wait()
                for i in range(4):
                    span = pl.ds(i * quarter, quarter)
                    share[1, span] = (share[1, span].astype(F32) + core_buf[0, span].astype(F32)).astype(BF)
                    far[i].start()

            @pl.when(step == 1)
            def _():
                core[1].start()

        return carry

    lax.fori_loop(0, 7, hop, 0)
    base_copy(0).start()
    base_copy(1).start()
    parts(7)
    for copy in hop_copies(6):
        copy.wait()
    total = jnp.concatenate((ring_r[7], ring_m[7], ring_l[7]), axis=1).astype(F32)
    total = total + jnp.concatenate((next_r[...], next_l[...]), axis=1)
    for i in range(4):
        row_buf[i] = total[i * rows_w : (i + 1) * rows_w].astype(BF)
    vec_part[...] = ring_v[7] + vectors[dp]
    exchange = []
    for i, peer in enumerate((sibling, across, corner)):
        to = peer["fsdp"]
        copies = [
            send(row_buf.at[to], row_in.at[me], a2a_send.at[i], a2a_recv.at[i], peer),
            send(vec_part.at[to], vec_in.at[me], a2a_send.at[3 + i], a2a_recv.at[3 + i], peer),
        ]
        for copy in copies:
            copy.start()
        exchange += copies
    row_in[me] = row_buf[me]
    vec_in[me] = vec_part[me]
    out_rows[...] = ring_o[7].astype(F32) + part_out[dp].astype(F32)
    core[1].wait()
    for i in range(4):
        span = pl.ds(i * quarter, quarter)
        far[i].wait()
        base_copy(i).wait()
        if i >= 2:
            gs_copy(i - 2).wait()
        gs_b[i % 2] = base_b[i % 2] + (
            share[0, span].astype(F32) + core_buf[1, span].astype(F32) + x_buf[span].astype(F32)
        )
        gs_copy(i).start()
        if i < 2:
            base_copy(i + 2).start()
    for copy in exchange:
        copy.wait()
    vec_own[...] = vec_in[0] + vec_in[1] + vec_in[2] + vec_in[3]
    cols = heads_width // 3
    for which, out in enumerate((g_query, g_key, g_value)):
        out[...] = jnp.concatenate(
            [row_in[i, :, which * cols : (which + 1) * cols].astype(F32) for i in range(4)], axis=1
        )
    for i in (2, 3):
        gs_copy(i).wait()


def last_exchange(order, base, tokens_t, g_qkv, w_t, part_out, vectors):
    rows, width = base.shape
    heads_width = g_qkv.shape[0]
    rows_w = part_out.shape[1]
    chunk = 4 * rows_w
    side = 2 * heads_width // 3
    vmem, hbm = pl.BlockSpec(memory_space=pltpu.VMEM), pl.BlockSpec(memory_space=pl.ANY)
    dma = pltpu.SemaphoreType.DMA
    return pl.pallas_call(
        last_kernel,
        in_specs=[pl.BlockSpec(memory_space=pltpu.SMEM), hbm, hbm, hbm, hbm, vmem, vmem],
        out_specs=[hbm] + [vmem] * 5,
        out_shape=[jax.ShapeDtypeStruct((rows, width), F32)]
        + [jax.ShapeDtypeStruct((rows_w, width), F32)] * 4
        + [jax.ShapeDtypeStruct(vectors.shape[2:], F32)],
        scratch_shapes=[
            pltpu.VMEM((heads_width, width), BF),
            pltpu.VMEM(g_qkv.shape, BF),
            pltpu.VMEM((NB, heads_width, BLOCK), BF),
            pltpu.VMEM((2, chunk, tokens_t.shape[1]), BF),
            pltpu.VMEM((2, chunk, tokens_t.shape[1]), BF),
            pltpu.VMEM((3, rows, width), BF),
            pltpu.VMEM((rows, heads_width), BF),
            pltpu.VMEM((2, rows, width), BF),
            pltpu.VMEM((rows, width), BF),
            pltpu.VMEM((2, rows // 4, width), F32),
            pltpu.VMEM((2, rows // 4, width), F32),
            pltpu.VMEM((8, chunk, 384), BF),
            pltpu.VMEM((8, chunk, side - 384), BF),
            pltpu.VMEM((8, chunk, heads_width - side), BF),
            pltpu.VMEM((8, rows_w, width), BF),
            pltpu.VMEM(vectors.shape, F32),
            pltpu.VMEM((chunk, side), F32),
            pltpu.VMEM((chunk, heads_width - side), F32),
            pltpu.VMEM((4, rows_w, heads_width), BF),
            pltpu.VMEM((4, rows_w, heads_width), BF),
            pltpu.VMEM(vectors.shape[1:], F32),
            pltpu.VMEM(vectors.shape[1:], F32),
            dma((2,)),
            dma((2, 2)),
            dma((2, 2)),
            dma((2,)),
            dma((2,)),
            dma((4,)),
            dma((4,)),
            dma((5, 7)),
            dma((5, 7)),
            dma((6,)),
            dma((6,)),
        ],
        compiler_params=pltpu.CompilerParams(
            collective_id=2, has_side_effects=True, vmem_limit_bytes=48 << 20
        ),
        cost_estimate=pl.CostEstimate(flops=13 * 10**9, bytes_accessed=100 << 20, transcendentals=0),
        name="last_exchange",
    )(order, base, tokens_t, g_qkv, w_t, part_out, vectors)


CHUNK = 128
TILE = 256
LAG = 3


def tile(index, base=0):
    return pl.ds(pl.multiple_of(base + index * TILE, TILE), TILE)


def nt(a, b):
    return lax.dot_general(a, b, (((1,), (1,)), ((), ())), preferred_element_type=F32)


def middle_kernel(mixed_n, states, teacher, weight, mask, w_in, w_own, w_o, rates, scales,
                  w_ug_out, w_d_out, hidden_out, back_out, out_states, attn_unit, attn_inv, hidden_inv, sums, gd_all,
                  ht_all, act_all, ug_all, w_ob, w_ug, w_d, hidden, back, target, mx, part, core, x_buf, tok, gd, act, act_t, ug, ht,
                  mx_send, mx_recv, mx_own, keep_sem, core_send, core_recv, x_send, x_recv, tok_send, tok_recv, gd_send, gd_recv, gd_own,
                  out_sem, ring_send, ring_recv, ug_s, ug_r, ug_sem):
    sibling, across, corner = group_peers()
    dp, place = lax.axis_index("dp"), ring_place()
    right, left = {"dp": ring_dp(place + 1)}, {"dp": ring_dp(place - 1)}
    piece = w_own.shape[0]
    count = x_buf.shape[0]
    width = hidden.shape[1]
    rate_attn, rate_mlp = rates[0:1], rates[1:2]

    def rows(i):
        return pl.ds(pl.multiple_of(i * CHUNK, CHUNK), CHUNK)

    def mx_copies(i):
        return [
            send(mixed_n.at[(r + 1) * count + i], mx.at[i, r + 1], mx_send.at[r, i], mx_recv.at[r, i], peer)
            for r, peer in enumerate((sibling, across, corner))
        ]

    def load_teacher(i):
        return pltpu.make_async_copy(teacher.at[rows(i)], target.at[i % 2], keep_sem.at[2, 2 + i % 2])

    def mx_local(i):
        return pltpu.make_async_copy(mixed_n.at[i], mx.at[i, 0], mx_own.at[i])

    def keep_rows(i):
        return [
            pltpu.make_async_copy(hidden.at[rows(i)], hidden_out.at[rows(i)], keep_sem.at[0, i]),
            pltpu.make_async_copy(back.at[rows(i)], back_out.at[rows(i)], keep_sem.at[1, i]),
        ]

    keep_w = [
        pltpu.make_async_copy(w_ug, w_ug_out, keep_sem.at[2, 0]),
        pltpu.make_async_copy(w_d, w_d_out, keep_sem.at[2, 1]),
    ]

    def core_a(stage, i):
        return send(part.at[i % 3, 3], core.at[0, i], core_send.at[stage, 0, i], core_recv.at[stage, 0, i], sibling)

    def core_b(stage, i):
        return send(part.at[i % 3, 1], core.at[1, i], core_send.at[stage, 1, i], core_recv.at[stage, 1, i], sibling)

    def chip(stage, i):
        return send(part.at[i % 3, 2], x_buf.at[i], x_send.at[stage, i], x_recv.at[stage, i], across)

    def spread(buf, own, sems, recvs, i):
        return [
            send(own, buf.at[i, 1], sems.at[0, i], recvs.at[0, i], sibling),
            send(own, buf.at[i, 2], sems.at[1, i], recvs.at[1, i], across),
            send(buf.at[i, 2], buf.at[i, 3], sems.at[2, i], recvs.at[2, i], sibling),
        ]

    def tok_copies(i):
        return spread(tok, tok.at[i, 0], tok_send, tok_recv, i)

    def gd_copies(i):
        return spread(gd_all, gd.at[i], gd_send, gd_recv, i)

    def gd_local(i):
        return pltpu.make_async_copy(gd.at[i], gd_all.at[i, 0], gd_own.at[i])

    def outs(i):
        slot = i % 2
        return [
            pltpu.make_async_copy(ht.at[slot], ht_all.at[i], out_sem.at[0, slot]),
            pltpu.make_async_copy(act_t.at[slot], act_all.at[i], out_sem.at[1, slot]),
            pltpu.make_async_copy(ug.at[slot], ug_all.at[i], out_sem.at[2, slot]),
        ]

    def hop(step):
        late = hidden_ring(w_d, ring_send, ring_recv, step + 1)
        for copy, later in zip(hidden_ring(w_d, ring_send, ring_recv, step), late):
            copy.wait()
            pl.when(step < 6)(later.start)

    def ug_hop(step):
        late = hidden_ring(w_ug, ug_s, ug_r, step + 1, EARLY_HOPS)
        for copy, later in zip(hidden_ring(w_ug, ug_s, ug_r, step, EARLY_HOPS), late):
            copy.wait()
            pl.when(step < 6)(later.start)

    def forward_far(stage, i):
        core_a(stage, i).wait_recv()
        part[i % 3, 2] = (part[i % 3, 2].astype(F32) + core[0, i].astype(F32)).astype(BF)
        chip(stage, i).start()

    def reduced(stage, i):
        core_b(stage, i).wait_recv()
        chip(stage, i).wait_recv()
        total = part[i % 3, 0].astype(F32) + core[1, i].astype(F32) + x_buf[i].astype(F32)
        core_a(stage, i).wait_send()
        core_b(stage, i).wait_send()
        chip(stage, i).wait_send()
        return total

    sums[...] = jnp.zeros_like(sums)
    load_o = pltpu.make_async_copy(w_o, w_ob, keep_sem.at[2, 4])
    load_o.start()
    load_teacher(0).start()
    load_teacher(1).start()
    w_d[rows_at(dp * piece, piece)] = w_own[...]
    chunk = w_ug.shape[0] // 8

    def load_w(i):
        cuts = rows_at(ring_dp(place - i) * chunk, chunk // 2), rows_at(
            ring_dp(place + i) * chunk + chunk // 2, chunk // 2
        )
        return [pltpu.make_async_copy(w_in.at[cut], w_ug.at[cut], ug_sem.at[d, i]) for d, cut in enumerate(cuts)]

    def start_w(i, carry):
        for copy in load_w(i):
            copy.start()
        return carry

    def wait_w(i, carry):
        for copy in load_w(i):
            copy.wait()
        return carry

    lax.fori_loop(0, EARLY_HOPS + 1, start_w, 0)
    greet([sibling, across, corner, right, left])
    for copy in hidden_ring(w_d, ring_send, ring_recv, 0):
        copy.start()

    def open_mixed(i, carry):
        mx_local(i).start()
        for copy in mx_copies(i):
            copy.start()
        return carry

    lax.fori_loop(0, count, open_mixed, 0)
    load_o.wait()
    lax.fori_loop(0, EARLY_HOPS + 1, wait_w, 0)
    for copy in hidden_ring(w_ug, ug_s, ug_r, EARLY_HOPS, EARLY_HOPS):
        copy.start()

    def norm_hidden(i):
        mx_local(i).wait()
        for copy in mx_copies(i):
            copy.wait()
        attn = nn(mx[i, 0].T, w_ob[0])
        for r in range(1, 4):
            attn = attn + nn(mx[i, r].T, w_ob[r])
        unit, inverse = unit_rows(attn)
        own = states[rows(i)].astype(F32)
        value, value_inv = unit_rows(own + rate_attn * (unit - own))
        hidden[rows(i)] = value
        attn_unit[rows(i)] = unit.astype(BF)
        attn_inv[rows(i)] = inverse
        hidden_inv[rows(i)] = value_inv
        tok[i, 0] = value.astype(BF)
        copies = tok_copies(i)
        copies[0].start()
        copies[1].start()

    def pass_tokens(i):
        copies = tok_copies(i)
        copies[1].wait_recv()
        copies[2].start()

    def feed(i):
        copies = tok_copies(i)
        copies[0].wait()
        copies[1].wait_send()
        copies[2].wait()
        slot = i % 2

        @pl.when(i >= 2)
        def _():
            for copy in outs(i - 2):
                copy.wait()

        def up(n, carry):
            here = tok[i].reshape(4 * CHUNK, width)
            up_proj = nn(here, w_ug[:, tile(n)])
            gate_proj = nn(here, w_ug[:, tile(n, width)])
            gated = gate_proj * scales[1:2, tile(n)]
            value = up_proj * scales[0:1, tile(n)] * (gated * jax.nn.sigmoid(gated))
            act[slot, :, tile(n)] = value.astype(BF)
            act_t[slot, tile(n)] = value.astype(BF).T
            ug[slot, :, tile(n)] = up_proj.astype(BF)
            ug[slot, :, tile(n, width)] = gate_proj.astype(BF)
            return carry

        lax.fori_loop(0, width // TILE, up, 0)
        for copy in outs(i)[1:]:
            copy.start()

    def feed_down(i):
        slot = i % 2

        def down(n, carry):
            value = nn(act[slot], w_d[:, tile(n)])
            part[i % 3, :, :, tile(n)] = value.astype(BF).reshape(4, CHUNK, TILE)
            ht[slot, tile(n)] = tok[i, :, :, tile(n)].reshape(4 * CHUNK, TILE).T
            return carry

        lax.fori_loop(0, width // TILE, down, 0)
        core_a(0, i).start()
        core_b(0, i).start()
        outs(i)[0].start()
        forward_far(0, i)

    def finish(i):
        unit, inverse = unit_rows(reduced(0, i))
        own = hidden[rows(i)]
        result, result_inv = unit_rows(own + rate_mlp * (unit - own))
        out_states[rows(i)] = result.astype(BF)
        load_teacher(i).wait()
        diff = result - target[i % 2]

        @pl.when(i + 2 < count)
        def _():
            load_teacher(i + 2).start()

        sums[1:2] = sums[1:2] + jnp.sum(mask[rows(i)] * (diff * diff), axis=0, keepdims=True)
        g_last = unit_back(weight[rows(i)] * diff, result, result_inv)
        sums[0:1] = sums[0:1] + jnp.sum(g_last * (unit - own), axis=0, keepdims=True)
        back[rows(i)] = g_last * (1.0 - rate_mlp)
        gd[i] = unit_back(g_last * rate_mlp, unit, inverse).astype(BF)
        copies = gd_copies(i)
        copies[0].start()
        copies[1].start()
        gd_local(i).start()
        for copy in keep_rows(i):
            copy.start()

    def pass_grads(i):
        copies = gd_copies(i)
        copies[1].wait_recv()
        copies[2].start()

    stages = (norm_hidden, pass_tokens, feed, feed_down, finish, pass_grads)

    def step(t, carry):
        for lag, stage in enumerate(stages):
            if lag == 2:
                pl.when(t < 7 - EARLY_HOPS)(lambda: ug_hop(EARLY_HOPS + t))
            if lag == 3:
                pl.when(t < 4)(lambda: hop(jnp.maximum(2 * t - 1, 0)))
                pl.when((t >= 1) & (t < 4))(lambda: hop(2 * t))

                @pl.when(t == 3)
                def _():
                    for copy in keep_w:
                        copy.start()

            pl.when((t >= lag) & (t < lag + count))(functools.partial(stage, t - lag))
        return carry

    lax.fori_loop(0, count + len(stages) - 1, step, 0)

    def close(i, carry):
        copies = gd_copies(i)
        copies[0].wait()
        copies[1].wait_send()
        copies[2].wait()
        gd_local(i).wait()
        for copy in keep_rows(i):
            copy.wait()
        return carry

    lax.fori_loop(0, count, close, 0)
    for i in (count - 2, count - 1):
        for copy in outs(i):
            copy.wait()
    for copy in keep_w:
        copy.wait()


def middle(mixed_n, states, teacher, weight, mask, w_ug, w_own, w_o, rates, scales):
    rows, width = states.shape
    count = rows // CHUNK
    vmem, hbm = pl.BlockSpec(memory_space=pltpu.VMEM), pl.BlockSpec(memory_space=pl.ANY)
    dma = pltpu.SemaphoreType.DMA
    return pl.pallas_call(
        middle_kernel,
        in_specs=[hbm, vmem, hbm, vmem, vmem, hbm, vmem, hbm, vmem, vmem],
        out_specs=[hbm] * 4 + [vmem] * 5 + [hbm] * 4,
        out_shape=[
            jax.ShapeDtypeStruct(w_ug.shape, BF),
            jax.ShapeDtypeStruct((8 * w_own.shape[0], width), BF),
            jax.ShapeDtypeStruct((rows, width), F32),
            jax.ShapeDtypeStruct((rows, width), F32),
            jax.ShapeDtypeStruct((rows, width), BF),
            jax.ShapeDtypeStruct((rows, width), BF),
            jax.ShapeDtypeStruct((rows, 1), F32),
            jax.ShapeDtypeStruct((rows, 1), F32),
            jax.ShapeDtypeStruct((2, width), F32),
            jax.ShapeDtypeStruct((count, 4, CHUNK, width), BF),
            jax.ShapeDtypeStruct((count, width, 4 * CHUNK), BF),
            jax.ShapeDtypeStruct((count, width, 4 * CHUNK), BF),
            jax.ShapeDtypeStruct((count, 4 * CHUNK, 2 * width), BF),
        ],
        scratch_shapes=[
            pltpu.VMEM(w_o.shape, BF),
            pltpu.VMEM(w_ug.shape, BF),
            pltpu.VMEM((8 * w_own.shape[0], width), BF),
            pltpu.VMEM((rows, width), F32),
            pltpu.VMEM((rows, width), F32),
            pltpu.VMEM((2, CHUNK, width), F32),
            pltpu.VMEM((count, 4) + mixed_n.shape[1:], BF),
            pltpu.VMEM((3, 4, CHUNK, width), BF),
            pltpu.VMEM((2, count, CHUNK, width), BF),
            pltpu.VMEM((count, CHUNK, width), BF),
            pltpu.VMEM((count, 4, CHUNK, width), BF),
            pltpu.VMEM((count, CHUNK, width), BF),
            pltpu.VMEM((2, 4 * CHUNK, width), BF),
            pltpu.VMEM((2, width, 4 * CHUNK), BF),
            pltpu.VMEM((2, 4 * CHUNK, 2 * width), BF),
            pltpu.VMEM((2, width, 4 * CHUNK), BF),
            dma((3, count)),
            dma((3, count)),
            dma((count,)),
            dma((3, count)),
            dma((1, 2, count)),
            dma((1, 2, count)),
            dma((1, count)),
            dma((1, count)),
            dma((3, count)),
            dma((3, count)),
            dma((3, count)),
            dma((3, count)),
            dma((count,)),
            dma((3, 2)),
            dma((4, 7)),
            dma((4, 7)),
            dma((4, 7 - EARLY_HOPS)),
            dma((4, 7 - EARLY_HOPS)),
            dma((2, EARLY_HOPS + 1)),
        ],
        compiler_params=pltpu.CompilerParams(
            collective_id=3, has_side_effects=True, vmem_limit_bytes=62 << 20
        ),
        cost_estimate=pl.CostEstimate(flops=26 * 10**9, bytes_accessed=400 << 20, transcendentals=4 << 20),
        name="middle",
    )(mixed_n, states, teacher, weight, mask, w_ug, w_own, w_o, rates, scales)


def middle_back_kernel(gd_all, act_all, ug_all, hidden, attn_unit, states, back, attn_inv, hidden_inv, w_ug, w_d,
                       rates, scales, base, ga_all, gug_all, down_rows, sums, ff_sums,
                       w_ug_b, w_d_b, part, core, x_buf, ga, gd, act, ug, gug, own_f, own_b, base_buf, dwd, column, ring_buf,
                       gd_sem, act_sem, in_sem, own_sem, core_send, core_recv, x_send, x_recv, ga_send, ga_recv,
                       ga_own, base_sem, out_sem, w_sem, ring_send, ring_recv):
    sibling, across, _ = group_peers()
    dp, place = lax.axis_index("dp"), ring_place()
    right, left = {"dp": ring_dp(place + 1)}, {"dp": ring_dp(place - 1)}
    count = core.shape[1]
    width = w_d.shape[0]
    load_d = pltpu.make_async_copy(w_d, w_d_b, w_sem.at[0])
    load_u = pltpu.make_async_copy(w_ug, w_ug_b, w_sem.at[1])
    load_d.start()
    half = ring_buf.shape[2]
    rate_attn = rates[0:1]

    def rows(i):
        return pl.ds(pl.multiple_of(i * CHUNK, CHUNK), CHUNK)

    def load_gd(i):
        return pltpu.make_async_copy(gd_all.at[i], gd.at[i], gd_sem.at[i])

    def load_act(i):
        return pltpu.make_async_copy(act_all.at[i], act.at[i], act_sem.at[i])

    def load_ug(i):
        return pltpu.make_async_copy(ug_all.at[i], ug.at[i % 2], in_sem.at[i % 2])

    def store_gug(i):
        return pltpu.make_async_copy(gug.at[i % 2], gug_all.at[i], out_sem.at[i % 2])

    def own_rows(i):
        return [
            pltpu.make_async_copy(hidden.at[rows(i)], own_f.at[0], own_sem.at[0]),
            pltpu.make_async_copy(back.at[rows(i)], own_f.at[1], own_sem.at[1]),
            pltpu.make_async_copy(attn_unit.at[rows(i)], own_b.at[0], own_sem.at[2]),
            pltpu.make_async_copy(states.at[rows(i)], own_b.at[1], own_sem.at[3]),
        ]

    def core_a(i):
        return send(part.at[i % 3, 3], core.at[0, i], core_send.at[0, i], core_recv.at[0, i], sibling)

    def core_b(i):
        return send(part.at[i % 3, 1], core.at[1, i], core_send.at[1, i], core_recv.at[1, i], sibling)

    def chip(i):
        return send(part.at[i % 3, 2], x_buf.at[i], x_send.at[i], x_recv.at[i], across)

    def ga_copies(i):
        return [
            send(ga.at[i], ga_all.at[1, rows(i)], ga_send.at[0, i], ga_recv.at[0, i], sibling),
            send(ga.at[i], ga_all.at[2, rows(i)], ga_send.at[1, i], ga_recv.at[1, i], across),
            send(ga_all.at[2, rows(i)], ga_all.at[3, rows(i)], ga_send.at[2, i], ga_recv.at[2, i], sibling),
        ]

    def ga_local(i):
        return pltpu.make_async_copy(ga.at[i], ga_all.at[0, rows(i)], ga_own.at[i])

    def base_copy(i):
        return pltpu.make_async_copy(base_buf.at[i % 2], base.at[rows(i)], base_sem.at[i % 2])

    def right_half(step):
        return rows_at(ring_dp(place - 1 - step) * 2 * half, half)

    def left_half(step):
        return rows_at(ring_dp(place + 1 + step) * 2 * half + half, half)

    def ring(step):
        return [
            send(ring_buf.at[0, step], ring_buf.at[0, step + 1], ring_send.at[0, step], ring_recv.at[0, step], right),
            send(ring_buf.at[1, step], ring_buf.at[1, step + 1], ring_send.at[1, step], ring_recv.at[1, step], left),
        ]

    def hop(step, carry):
        for copy in ring(step):
            copy.wait()

        @pl.when(step < 6)
        def _():
            for side, cut in ((0, right_half(step + 1)), (1, left_half(step + 1))):
                ring_buf[side, step + 1] = (
                    ring_buf[side, step + 1].astype(F32) + dwd[cut].astype(F32)
                ).astype(BF)
            for copy in ring(step + 1):
                copy.start()

        return carry

    for copy in [load_ug(0)] + own_rows(0):
        copy.start()
    lax.fori_loop(0, count, lambda i, c: (load_gd(i).start(), c)[1], 0)
    load_u.start()
    lax.fori_loop(0, count, lambda i, c: (load_act(i).start(), c)[1], 0)
    sums[...] = jnp.zeros_like(sums)
    ff_sums[...] = jnp.zeros_like(ff_sums)
    greet([sibling, across, right, left])
    lax.fori_loop(0, count, lambda i, c: (load_gd(i).wait(), c)[1], 0)
    load_d.wait()

    def feed(i):
        slot = i % 2
        load_ug(i).wait()

        @pl.when(i + 1 < count)
        def _():
            load_ug(i + 1).start()

        @pl.when(i >= 2)
        def _():
            store_gug(i - 2).wait()

        def grads(n, carry):
            g_act = nt(gd[i].reshape(4 * CHUNK, width), w_d_b[tile(n)])
            up_proj = ug[slot, :, tile(n)].astype(F32)
            gate_proj = ug[slot, :, tile(n, width)].astype(F32)
            scale_up, scale_gate = scales[0:1, tile(n)], scales[1:2, tile(n)]
            gated = gate_proj * scale_gate
            sigmoid = jax.nn.sigmoid(gated)
            g_upscaled = g_act * (gated * sigmoid)
            g_gated = g_act * (up_proj * scale_up) * sigmoid * (1.0 + gated * (1.0 - sigmoid))
            ff_sums[0:1, tile(n)] = ff_sums[0:1, tile(n)] + jnp.sum(g_upscaled * up_proj, axis=0, keepdims=True)
            ff_sums[1:2, tile(n)] = ff_sums[1:2, tile(n)] + jnp.sum(g_gated * gate_proj, axis=0, keepdims=True)
            gug[slot, :, tile(n)] = (g_upscaled * scale_up).astype(BF)
            gug[slot, :, tile(n, width)] = (g_gated * scale_gate).astype(BF)
            return carry

        lax.fori_loop(0, width // TILE, grads, 0)
        store_gug(i).start()
        pl.when(i == 0)(load_u.wait)

        def through(n, carry):
            value = nt(gug[slot], w_ug_b[tile(n)])
            part[i % 3, :, :, tile(n)] = value.astype(BF).reshape(4, CHUNK, TILE)
            return carry

        lax.fori_loop(0, width // TILE, through, 0)
        core_a(i).start()
        core_b(i).start()
        core_a(i).wait_recv()
        part[i % 3, 2] = (part[i % 3, 2].astype(F32) + core[0, i].astype(F32)).astype(BF)
        chip(i).start()

    def down_grads():
        lax.fori_loop(0, count, lambda i, c: (load_act(i).wait(), c)[1], 0)

        def outer(n, carry):
            column[...] = jnp.zeros_like(column)

            def add(k, carry):
                column[...] = column[...] + nn(act[k], gd[k, :, :, tile(n)].reshape(4 * CHUNK, TILE))
                return carry

            lax.fori_loop(0, count, add, 0)
            dwd[:, tile(n)] = column[...].astype(BF)
            return carry

        lax.fori_loop(0, width // TILE, outer, 0)
        ring_buf[0, 0] = dwd[right_half(0)]
        ring_buf[1, 0] = dwd[left_half(0)]
        for copy in ring(0):
            copy.start()

    def finish(i):
        core_b(i).wait_recv()
        chip(i).wait_recv()
        through = part[i % 3, 0].astype(F32) + core[1, i].astype(F32) + x_buf[i].astype(F32)
        core_a(i).wait_send()
        core_b(i).wait_send()
        chip(i).wait_send()
        for copy in own_rows(i):
            copy.wait()
        value, unit, own = own_f[0], own_b[0].astype(F32), own_b[1].astype(F32)
        g_pre = unit_back(own_f[1] + through, value, hidden_inv[rows(i)])

        @pl.when(i + 1 < count)
        def _():
            for copy in own_rows(i + 1):
                copy.start()

        @pl.when(i >= 2)
        def _():
            base_copy(i - 2).wait()

        base_buf[i % 2] = g_pre * (1.0 - rate_attn)
        base_copy(i).start()
        sums[0:1] = sums[0:1] + jnp.sum(g_pre * (unit - own), axis=0, keepdims=True)
        ga[i] = unit_back(g_pre * rate_attn, unit, attn_inv[rows(i)]).astype(BF)
        copies = ga_copies(i)
        copies[0].start()
        copies[1].start()
        ga_local(i).start()

    def pass_grads(i):
        copies = ga_copies(i)
        copies[1].wait_recv()
        copies[2].start()

    stages = (feed, finish, pass_grads)

    def step(t, carry):
        for lag, stage in enumerate(stages):
            pl.when((t >= lag) & (t < lag + count))(functools.partial(stage, t - lag))
        pl.when(t == 2)(down_grads)

        @pl.when((t >= 3) & (t < 6))
        def _():
            lax.fori_loop(2 * t - 6, 2 * t - 4, hop, 0)

        return carry

    lax.fori_loop(0, count + len(stages) - 1, step, 0)
    hop(6, 0)
    own = dp * 2 * half
    down_rows[pl.ds(0, half)] = ring_buf[0, 7].astype(F32) + dwd[rows_at(own, half)].astype(F32)
    down_rows[pl.ds(half, half)] = ring_buf[1, 7].astype(F32) + dwd[rows_at(own + half, half)].astype(F32)

    def close(i, carry):
        copies = ga_copies(i)
        copies[0].wait()
        copies[1].wait_send()
        copies[2].wait()
        ga_local(i).wait()
        return carry

    lax.fori_loop(0, count, close, 0)
    for i in (count - 2, count - 1):
        base_copy(i).wait()
        store_gug(i).wait()


def middle_back(gd_all, act_all, ug_all, hidden, attn_unit, states, back, attn_inv, hidden_inv, w_ug, w_d, rates,
                scales):
    rows, width = states.shape
    count = rows // CHUNK
    piece = width // 8
    vmem, hbm = pl.BlockSpec(memory_space=pltpu.VMEM), pl.BlockSpec(memory_space=pl.ANY)
    dma = pltpu.SemaphoreType.DMA
    return pl.pallas_call(
        middle_back_kernel,
        in_specs=[hbm] * 7 + [vmem] * 2 + [hbm] * 2 + [vmem] * 2,
        out_specs=[hbm, hbm, hbm, vmem, vmem, vmem],
        out_shape=[
            jax.ShapeDtypeStruct((rows, width), F32),
            jax.ShapeDtypeStruct((4, rows, width), BF),
            jax.ShapeDtypeStruct((count, 4 * CHUNK, 2 * width), BF),
            jax.ShapeDtypeStruct((piece, width), F32),
            jax.ShapeDtypeStruct((1, width), F32),
            jax.ShapeDtypeStruct((2, width), F32),
        ],
        scratch_shapes=[
            pltpu.VMEM(w_ug.shape, BF),
            pltpu.VMEM(w_d.shape, BF),
            pltpu.VMEM((3, 4, CHUNK, width), BF),
            pltpu.VMEM((2, count, CHUNK, width), BF),
            pltpu.VMEM((count, CHUNK, width), BF),
            pltpu.VMEM((count, CHUNK, width), BF),
            pltpu.VMEM((count, 4, CHUNK, width), BF),
            pltpu.VMEM((count, width, 4 * CHUNK), BF),
            pltpu.VMEM((2, 4 * CHUNK, 2 * width), BF),
            pltpu.VMEM((2, 4 * CHUNK, 2 * width), BF),
            pltpu.VMEM((2, CHUNK, width), F32),
            pltpu.VMEM((2, CHUNK, width), BF),
            pltpu.VMEM((2, CHUNK, width), F32),
            pltpu.VMEM((width, width), BF),
            pltpu.VMEM((width, TILE), F32),
            pltpu.VMEM((2, 8, piece // 2, width), BF),
            dma((count,)),
            dma((count,)),
            dma((2,)),
            dma((4,)),
            dma((2, count)),
            dma((2, count)),
            dma((count,)),
            dma((count,)),
            dma((3, count)),
            dma((3, count)),
            dma((count,)),
            dma((2,)),
            dma((2,)),
            dma((2,)),
            dma((2, 7)),
            dma((2, 7)),
        ],
        compiler_params=pltpu.CompilerParams(
            collective_id=4, has_side_effects=True, vmem_limit_bytes=60 << 20
        ),
        cost_estimate=pl.CostEstimate(flops=34 * 10**9, bytes_accessed=200 << 20, transcendentals=4 << 20),
        name="middle_back",
    )(gd_all, act_all, ug_all, hidden, attn_unit, states, back, attn_inv, hidden_inv, w_ug, w_d, rates, scales)


def order_kernel(where_ref, parent_ref, out_ref):
    base, me = where_ref[0], where_ref[1]
    shape = (128, 128)
    row = lax.broadcasted_iota(jnp.int32, shape, 0)
    block = lax.broadcasted_iota(jnp.int32, (8, 128), 1)
    real = block < NB
    parent = jnp.where(real & (parent_ref[...] >= 0), parent_ref[...] - base, -1)
    up = (row == parent[0:1]).astype(F32)
    up2 = nn(up, up)
    near = up + up2
    up4 = nn(up2, up2)
    near = near + nn(near, up2)
    near = near + nn(near, up4)
    above = near + nn(nn(up4, up4), up)
    depth = jnp.broadcast_to(jnp.sum(above, axis=0, keepdims=True), (8, 128)).astype(jnp.int32)
    before = (row < lax.broadcasted_iota(jnp.int32, shape, 1)).astype(F32)
    rank = nn(((depth == TRUNK) & real).astype(F32), before)
    parent_rank = nn(rank, up).astype(jnp.int32)
    sibling = jnp.sum(nn(up.T, up) * before, axis=0, keepdims=True).astype(jnp.int32)
    leaf = TRUNK + 4 + 2 * parent_rank + sibling
    slot = jnp.where(depth < TRUNK, depth, jnp.where(depth == TRUNK, TRUNK + rank.astype(jnp.int32), leaf))
    slot = jnp.where(real, slot, 127)
    mine = jnp.where(real, jnp.bitwise_xor(block // 5, me) * 5 + block % 5, 127)
    order = nt(mine.astype(F32), (row == slot[0:1]).astype(F32))
    back = nt(slot.astype(F32), (row == mine[0:1]).astype(F32))
    which = lax.broadcasted_iota(jnp.int32, (8, 128), 0)
    out_ref[...] = jnp.where(which == 0, order, back).astype(jnp.int32)


def tree_order(where, parents):
    return pl.pallas_call(
        order_kernel,
        in_specs=[pl.BlockSpec(memory_space=pltpu.SMEM), pl.BlockSpec(memory_space=pltpu.VMEM)],
        out_specs=pl.BlockSpec(memory_space=pltpu.VMEM),
        out_shape=jax.ShapeDtypeStruct((8, 128), jnp.int32),
        name="tree_order",
    )(where, jnp.broadcast_to(jnp.pad(parents, (0, 128 - NB), constant_values=-1), (8, 128)))


def local(
    states,
    teacher,
    parent_ids,
    valid_mask,
    w_query,
    w_key,
    w_value,
    w_out,
    w_up,
    w_gate,
    w_down,
    qk_scale,
    attn_rate,
    mlp_rate,
    up_scale,
    gate_scale,
):
    both = ("dp", "fsdp")
    dps, tps = 8, 4
    rows_w = w_query.shape[0]
    cols = D // tps
    hid = FF // tps
    ff_rows = FF // (dps * tps)
    me = lax.axis_index("fsdp")
    root_width = math.sqrt(D)
    mask_f = valid_mask.astype(F32)
    group_base = lax.axis_index("dp") * NB
    order = tree_order(jnp.stack((group_base, me)).astype(jnp.int32), parent_ids)

    count = jnp.sum(valid_mask)
    first_row = jnp.arange(rows_w, dtype=jnp.int32) == 0
    small = jnp.stack(
        (
            qk_scale,
            attn_rate,
            mlp_rate,
            jnp.where(first_row, count // 128, 0).astype(BF),
            jnp.where(first_row, count % 128, 0).astype(BF),
        ),
        axis=1,
    )
    small = jnp.pad(small, ((0, 0), (0, 59)))
    extra = jnp.pad(jnp.stack((up_scale, gate_scale), axis=1), ((0, 0), (69, 57)))
    spread = [(j, tps * (j % dps) + j // dps) for j in range(dps * tps)]
    tokens_t, w_t, w_o, w_ug, qkv, mixed, sums, mixed_n = forward(
        order, states, w_query, w_key, w_value, small, extra, lax.ppermute(w_out, both, spread), w_up, w_gate
    )
    small_all = w_t[3 * cols : 3 * cols + 8].astype(F32)
    rates = small_all[1:3]
    valid_count = 128.0 * jnp.sum(small_all[3]) + jnp.sum(small_all[4])
    scales = small_all[5:7] * jnp.array([[1.0], [root_width]], F32)
    scale_qk = lax.dynamic_slice_in_dim(small_all[0], me * cols, cols).reshape(cols // HEAD_DIM, HEAD_DIM, 1)

    mask_col = mask_f[:, None]
    w_ug, w_d, hidden, back, out_states, attn_unit, attn_inv, hidden_inv, sums_mid, gd_all, ht_all, act_all, ug_all = middle(
        mixed_n, states, teacher, mask_col * (2.0 / valid_count), mask_col, w_ug, w_down, w_o, rates, scales
    )
    base, ga_all, gug_all, grad_down, sums_back, ff_sums = middle_back(
        gd_all, act_all, ug_all, hidden, attn_unit, states, back, attn_inv, hidden_inv, w_ug, w_d, rates, scales
    )
    loss_local = jnp.sum(sums_mid[1])
    g_rate_mlp, g_rate_attn = sums_mid[0], sums_back[0]
    grad_up_scale, grad_gate_scale = ff_sums[0], ff_sums[1] * root_width
    g_qkv, g_scale, part_out, grad_up, grad_gate = attention_back(
        order, qkv, scale_qk, sums, mixed, ga_all.reshape(NB, BLOCK, D), w_o, ht_all, gug_all
    )
    g_qkv = g_qkv.reshape(3 * cols, TOK)
    slot = jnp.arange(tps, dtype=jnp.int32) == me
    qk_rows = jnp.where(slot[:, None], g_scale.reshape(1, cols), 0.0).reshape(dps * tps, rows_w)
    ff_terms = [
        jnp.where(slot[None, :, None], term.reshape(dps, 1, ff_rows), 0.0).reshape(dps * tps, ff_rows)
        for term in (grad_up_scale, grad_gate_scale)
    ]
    vectors = jnp.concatenate(
        [g_rate_attn.reshape(dps * tps, rows_w), g_rate_mlp.reshape(dps * tps, rows_w), qk_rows]
        + ff_terms
        + [jnp.broadcast_to(loss_local, (dps * tps, 512 - 3 * rows_w - 2 * ff_rows))],
        axis=1,
    ).reshape(dps, tps, 4, 128)
    part_out = part_out.reshape(dps, rows_w, D)
    grad_states, g_query, g_key, g_value, out_back, vector_share = last_exchange(
        order, base, tokens_t, g_qkv, w_t, part_out, vectors
    )
    vector_share = vector_share.reshape(512)
    grad_out = lax.ppermute(out_back, both, [(b, a) for a, b in spread])
    cuts = (0, rows_w, 2 * rows_w, 3 * rows_w, 3 * rows_w + ff_rows, 3 * rows_w + 2 * ff_rows)
    v = [vector_share[a:b] for a, b in zip(cuts, cuts[1:])]
    return (
        out_states,
        vector_share[-1] / valid_count,
        grad_states,
        g_query,
        g_key,
        g_value,
        grad_out,
        grad_up,
        grad_gate,
        grad_down,
        v[2],
        v[0],
        v[1],
        v[3],
        v[4],
    )


def solution(mesh):
    placed = (
        P(("dp", "fsdp"), None),
        P(("dp", "fsdp"), None),
        P("dp"),
        P(("dp", "fsdp")),
        P(("dp", "fsdp"), None),
        P(("dp", "fsdp"), None),
        P(("dp", "fsdp"), None),
        P(("dp", "fsdp"), None),
        P(("dp", "fsdp"), None),
        P(("dp", "fsdp"), None),
        P(("dp", "fsdp"), None),
        P(("dp", "fsdp")),
        P(("dp", "fsdp")),
        P(("dp", "fsdp")),
        P(("dp", "fsdp")),
        P(("dp", "fsdp")),
    )
    quick = mesh.shape["fsdp"] == 4 and mesh.shape["dp"] == 8
    return jax.shard_map(
        local if quick else general,
        mesh=mesh,
        in_specs=placed,
        out_specs=(
            P(("dp", "fsdp"), None),
            P(),
            P(("dp", "fsdp"), None),
            P(("dp", "fsdp"), None),
            P(("dp", "fsdp"), None),
            P(("dp", "fsdp"), None),
            P(("dp", "fsdp"), None),
            P(("dp", "fsdp"), None),
            P(("dp", "fsdp"), None),
            P(("dp", "fsdp"), None),
            P(("dp", "fsdp")),
            P(("dp", "fsdp")),
            P(("dp", "fsdp")),
            P(("dp", "fsdp")),
            P(("dp", "fsdp")),
        ),
        check_vma=False,
    )
```
